128 devices in a mesh: seq: 32 (over z, x, core), batch: 4 (over y).
Axes of the slice: x: 4, y: 4, z: 4, core: 2. Of those that a mesh axis runs over, the one named last changes fastest.
Arguments:
- sequence_input: bfloat16 [32768, 1536], P(('batch', 'seq')), parts along dimension 0, may hold values from -6 to 6
- conv_first: bfloat16 [5, 1536, 768], replicated, may hold values from -0.0625 to 0.0625
- conv_second: bfloat16 [5, 768, 768], replicated, may hold values from -0.09375 to 0.09375
- qkv_weight: bfloat16 [768, 1536], replicated, may hold values from -0.21875 to 0.21875
- out_weight: bfloat16 [512, 768], replicated, may hold values from -0.25 to 0.25
- logit_scale: float32 [4], replicated, may hold values from 2.5 to 30, as said below
Outputs:
- block_output: bfloat16 [32768, 768], P(('batch', 'seq')), parts along dimension 0
The draws below stay inside these ranges and needn't reach their ends.
There are 4 independent parts, one for each index of `batch`. The reference program is written for one: setup_inputs(seed, part) draws one part's arguments, and reference() takes and returns one part's arrays. A program takes and returns all parts, laid end to end along the dimension named above; an argument that names none is the same for every part. Nothing has to cross between parts.
Inputs may be any that keep to these rules, and one draw needn't show every extreme that they name: `logit_scale`: one positive scale a head.
All inputs are finite; a program needn't handle non-finite values.
Results may differ from the reference program's by a relative error of at most 0.023.
Values may be sent and summed in bfloat16 or wider, within the bound.
A program may use at most 256 MiB of HBM per device.

```python
import math
import jax
import jax.numpy as jnp
from jax import lax

C = 1536
CW = 768
HEADS = 4
DH = 128
TOKENS = 8192


def draw_logit_scale(key, part):
    return jnp.exp(jax.random.uniform(key, (HEADS,), jnp.float32, math.log(2.5), math.log(10.0)))


def level_of(own_key, extent, shards, least, top_value):
    gain = 1.0
    for position, parts in shards:
        draws = jax.random.uniform(jax.random.fold_in(jax.random.fold_in(own_key, 6), position), (parts,), jnp.float32, least / len(shards), top_value / len(shards))
        gain = gain * jnp.repeat(jnp.exp(draws), extent[position] // parts).reshape((-1,) + (1,) * (len(extent) - 1 - position))
    return gain


def gaussian(stream_key, shape, scale, reach, pieces=(), dtype=jnp.bfloat16):
    factor_of = level_of(stream_key, shape, pieces, -0.22, 0.18) if pieces else 1.0
    drawn = jax.random.normal(stream_key, shape, jnp.float32) * scale * factor_of
    return jnp.minimum(jnp.maximum(drawn, -reach), reach).astype(dtype)


def setup_inputs(seed: int = 0, part: int = 0) -> dict:
    seeds = jax.random.split(jax.random.key(seed), 7)
    own_keys = jax.random.split(jax.random.fold_in(seeds[6], part), 7)
    return {
        "sequence_input": gaussian(own_keys[0], (TOKENS, C), 1.0, 6.0, ((0, 32),)),
        "conv_first": gaussian(seeds[1], (5, C, CW), (5 * C) ** -0.5, 0.0625),
        "conv_second": gaussian(seeds[2], (5, CW, CW), (5 * CW) ** -0.5, 0.09375),
        "qkv_weight": gaussian(seeds[3], (CW, 3 * HEADS * DH), CW ** -0.5, 0.21875),
        "out_weight": gaussian(seeds[4], (HEADS * DH, CW), (HEADS * DH) ** -0.5, 0.25),
        "logit_scale": draw_logit_scale(jax.random.fold_in(seeds[6], 71), part),
    }


def convolve(source, weight):
    row_count = source.shape[0]
    padded = jnp.pad(source, ((2, 2), (0, 0)))
    conv_sum = jnp.dot(padded[0:row_count], weight[0], preferred_element_type=jnp.float32)
    for offset in range(1, 5):
        conv_sum = conv_sum + jnp.dot(padded[offset:offset + row_count], weight[offset], preferred_element_type=jnp.float32)
    return conv_sum

def head_rms(tensor):
    return tensor * lax.rsqrt(lax.optimization_barrier(jnp.mean(tensor * tensor, axis=-1, keepdims=True)) + 1e-06)

def reference(sequence_input, conv_first, conv_second, qkv_weight, out_weight, logit_scale):
    first_out = jax.nn.gelu(convolve(sequence_input, conv_first)).astype(jnp.bfloat16)
    hidden = (first_out.astype(jnp.float32) + convolve(first_out, conv_second)).astype(jnp.bfloat16)
    width_all = HEADS * DH
    projected = jnp.dot(hidden, qkv_weight, preferred_element_type=jnp.float32)
    query_part = projected[:, :width_all].reshape(TOKENS, HEADS, DH)
    key_part = projected[:, width_all:2 * width_all].reshape(TOKENS, HEADS, DH)
    value_part = projected[:, 2 * width_all:].reshape(TOKENS, HEADS, DH)
    queries = (head_rms(query_part) * (logit_scale / math.sqrt(DH))[None, :, None]).astype(jnp.bfloat16)
    key_wide = head_rms(key_part).astype(jnp.bfloat16).astype(jnp.float32)
    value_wide = value_part.astype(jnp.bfloat16).astype(jnp.float32)
    block_rows = math.gcd(TOKENS, 512)

    def attend(query_block):
        scores = jnp.einsum('qhd,khd->hqk', query_block.astype(jnp.float32), key_wide)
        row_max = lax.optimization_barrier(jnp.max(scores, axis=2, keepdims=True))
        exponent = jnp.exp(scores - row_max)
        denominators = lax.optimization_barrier(jnp.sum(exponent, axis=2))
        probabilities = lax.optimization_barrier(exponent.astype(jnp.bfloat16)).astype(jnp.float32)
        mixed_out = jnp.einsum('hqk,khd->qhd', probabilities, value_wide)
        return mixed_out / denominators.T[:, :, None]
    blocks = queries.reshape(TOKENS // block_rows, block_rows, HEADS, DH)
    attended = lax.map(attend, blocks).reshape(TOKENS, width_all).astype(jnp.bfloat16)
    return (hidden.astype(jnp.float32) + jnp.dot(attended, out_weight, preferred_element_type=jnp.float32)).astype(jnp.bfloat16)
```

```python
import functools
import math

import jax
import jax.numpy as jnp
import numpy as np
from jax import lax
from jax.experimental import pallas as pl
from jax.experimental.pallas import tpu as pltpu
from jax.sharding import Mesh
from jax.sharding import PartitionSpec as P

SEQ_AXES = ("zx", "core")


def padded_2(block, width):
    count = lax.axis_size(SEQ_AXES)
    forward = [(i, i + 1) for i in range(count - 1)]
    backward = [(target, source) for source, target in forward]
    low = lax.ppermute(lax.slice_in_dim(block, block.shape[0] - width, None, axis=0), SEQ_AXES, forward)
    high = lax.ppermute(lax.slice_in_dim(block, 0, width, axis=0), SEQ_AXES, backward)
    return jnp.concatenate([low, block, high], axis=0)


def convolve(padded, weight, row_count):
    conv_sum = jnp.dot(padded[0:row_count], weight[0], preferred_element_type=jnp.float32)
    for offset in range(1, weight.shape[0]):
        conv_sum = conv_sum + jnp.dot(
            padded[offset : offset + row_count], weight[offset], preferred_element_type=jnp.float32
        )
    return conv_sum


def head_rms(tensor):
    return tensor * lax.rsqrt(jnp.mean(tensor * tensor, axis=-1, keepdims=True) + 1e-06)


def flash_kernel(nk, q_ref, k_ref, v_ref, o_ref, m_ref, l_ref, m_sc, l_sc, acc_sc):
    kb = pl.program_id(2)

    @pl.when(kb == 0)
    def _():
        m_sc[...] = jnp.full(m_sc.shape, -jnp.inf, jnp.float32)
        l_sc[...] = jnp.zeros(l_sc.shape, jnp.float32)
        acc_sc[...] = jnp.zeros(acc_sc.shape, jnp.float32)

    s = lax.dot_general(
        q_ref[...], k_ref[...], (((1,), (1,)), ((), ())), preferred_element_type=jnp.float32
    )
    m_prev = m_sc[...]
    m_new = jnp.maximum(m_prev, jnp.max(s, axis=1, keepdims=True))
    alpha = jnp.exp(m_prev - m_new)
    p = jnp.exp(s - m_new)
    l_sc[...] = alpha * l_sc[...] + jnp.sum(p, axis=1, keepdims=True)
    acc_sc[...] = alpha * acc_sc[...] + jnp.dot(
        p.astype(jnp.bfloat16), v_ref[...], preferred_element_type=jnp.float32
    )
    m_sc[...] = m_new

    @pl.when(kb == nk - 1)
    def _():
        o_ref[...] = acc_sc[...]
        m_ref[...] = m_sc[...]
        l_ref[...] = l_sc[...]


def flash_partial(queries, kv, heads, head_size, tq=256, tk=1024):
    q_rows = queries.shape[0]
    k_rows = kv.shape[0]
    nq, nk = q_rows // tq, k_rows // tk
    return pl.pallas_call(
        functools.partial(flash_kernel, nk),
        grid=(heads, nq, nk),
        in_specs=[
            pl.BlockSpec((tq, head_size), lambda h, i, j: (i, h)),
            pl.BlockSpec((tk, head_size), lambda h, i, j: (j, h)),
            pl.BlockSpec((tk, head_size), lambda h, i, j: (j, heads + h)),
        ],
        out_specs=[
            pl.BlockSpec((tq, head_size), lambda h, i, j: (i, h)),
            pl.BlockSpec((None, tq, 1), lambda h, i, j: (h, i, 0)),
            pl.BlockSpec((None, tq, 1), lambda h, i, j: (h, i, 0)),
        ],
        out_shape=[
            jax.ShapeDtypeStruct((q_rows, heads * head_size), jnp.float32),
            jax.ShapeDtypeStruct((heads, q_rows, 1), jnp.float32),
            jax.ShapeDtypeStruct((heads, q_rows, 1), jnp.float32),
        ],
        scratch_shapes=[
            pltpu.VMEM((tq, 1), jnp.float32),
            pltpu.VMEM((tq, 1), jnp.float32),
            pltpu.VMEM((tq, head_size), jnp.float32),
        ],
        compiler_params=pltpu.CompilerParams(
            dimension_semantics=("arbitrary", "arbitrary", "arbitrary")
        ),
        cost_estimate=pl.CostEstimate(
            flops=4 * q_rows * k_rows * heads * head_size,
            transcendentals=q_rows * k_rows * heads,
            bytes_accessed=(k_rows * 2 * heads * head_size * 2) * nq + q_rows * heads * head_size * 6,
        ),
    )(queries, kv, kv)


def body(sequence_input, conv_first, conv_second, qkv_weight, out_weight, logit_scale):
    row_count = sequence_input.shape[0]
    padded_input = padded_2(sequence_input, 2)
    first_out = jax.nn.gelu(convolve(padded_input, conv_first, row_count)).astype(jnp.bfloat16)
    padded_first = padded_2(first_out, 2)
    second = convolve(padded_first, conv_second, row_count)
    hidden = (first_out.astype(jnp.float32) + second).astype(jnp.bfloat16)
    head_count = logit_scale.shape[0]
    width_all = qkv_weight.shape[1] // 3
    head_size = width_all // head_count
    projected = jnp.dot(hidden, qkv_weight, preferred_element_type=jnp.float32)
    query_part = projected[:, :width_all].reshape(row_count, head_count, head_size)
    queries = (head_rms(query_part) * (logit_scale / math.sqrt(head_size))[None, :, None]).astype(
        jnp.bfloat16
    ).reshape(row_count, width_all)
    key_part = projected[:, width_all : 2 * width_all].reshape(row_count, head_count, head_size)
    keys = head_rms(key_part).astype(jnp.bfloat16).reshape(row_count, width_all)
    values = projected[:, 2 * width_all :].astype(jnp.bfloat16)
    kv_local = jnp.concatenate([keys, values], axis=1)

    kv_all = lax.all_gather(kv_local, "zx", axis=0, tiled=True)
    pair_queries = lax.all_gather(queries, "core", axis=0, tiled=True)
    o_part, m_part, l_part = flash_partial(pair_queries, kv_all, head_count, head_size)

    core = lax.axis_index("core")
    other = 1 - core
    send_o = lax.dynamic_slice_in_dim(o_part, other * row_count, row_count, axis=0)
    send_m = lax.dynamic_slice_in_dim(m_part, other * row_count, row_count, axis=1)
    send_l = lax.dynamic_slice_in_dim(l_part, other * row_count, row_count, axis=1)
    own_o = lax.dynamic_slice_in_dim(o_part, core * row_count, row_count, axis=0)
    own_m = lax.dynamic_slice_in_dim(m_part, core * row_count, row_count, axis=1)
    own_l = lax.dynamic_slice_in_dim(l_part, core * row_count, row_count, axis=1)
    swap = [(0, 1), (1, 0)]
    got_o, got_m, got_l = lax.ppermute((send_o, send_m, send_l), "core", swap)

    m_all = jnp.maximum(own_m, got_m)
    w_own = jnp.exp(own_m - m_all)
    w_got = jnp.exp(got_m - m_all)
    denom = own_l * w_own + got_l * w_got
    w_own_t = w_own[:, :, 0].T[:, :, None]
    w_got_t = w_got[:, :, 0].T[:, :, None]
    denom_t = denom[:, :, 0].T[:, :, None]
    mixed = (
        own_o.reshape(row_count, head_count, head_size) * w_own_t
        + got_o.reshape(row_count, head_count, head_size) * w_got_t
    )
    attended = (mixed / denom_t).reshape(row_count, width_all).astype(jnp.bfloat16)
    return (
        hidden.astype(jnp.float32)
        + jnp.dot(attended, out_weight, preferred_element_type=jnp.float32)
    ).astype(jnp.bfloat16)


def solution(mesh):
    devices = np.asarray(mesh.devices)
    seq_size = mesh.shape["seq"]
    batch_size = mesh.shape["batch"]
    order = [mesh.axis_names.index("seq"), mesh.axis_names.index("batch")]
    devices = devices.transpose(order).reshape(seq_size // 2, 2, batch_size)
    split_mesh = Mesh(devices, ("zx", "core", "batch"))
    rows = P(("batch", "zx", "core"), None)
    in_specs = (rows, P(), P(), P(), P(), P())
    return jax.shard_map(body, mesh=split_mesh, in_specs=in_specs, out_specs=rows, check_vma=False)
```

```python
import functools
import math

import jax
import jax.numpy as jnp
import numpy as np
from jax import lax
from jax.experimental import pallas as pl
from jax.experimental.pallas import tpu as pltpu
from jax.sharding import Mesh
from jax.sharding import PartitionSpec as P

SEQ_AXES = ("zx", "core")


def padded_2(block, width):
    count = lax.axis_size(SEQ_AXES)
    forward = [(i, i + 1) for i in range(count - 1)]
    backward = [(target, source) for source, target in forward]
    low = lax.ppermute(lax.slice_in_dim(block, block.shape[0] - width, None, axis=0), SEQ_AXES, forward)
    high = lax.ppermute(lax.slice_in_dim(block, 0, width, axis=0), SEQ_AXES, backward)
    return jnp.concatenate([low, block, high], axis=0)


def convolve(padded, weight, row_count):
    conv_sum = jnp.dot(padded[0:row_count], weight[0], preferred_element_type=jnp.float32)
    for offset in range(1, weight.shape[0]):
        conv_sum = conv_sum + jnp.dot(
            padded[offset : offset + row_count], weight[offset], preferred_element_type=jnp.float32
        )
    return conv_sum


def head_rms(tensor):
    return tensor * lax.rsqrt(jnp.mean(tensor * tensor, axis=-1, keepdims=True) + 1e-06)


def head_norm(block, heads, head_size):
    parts = []
    for h in range(heads):
        part = block[:, h * head_size : (h + 1) * head_size]
        mean_sq = jnp.mean(part * part, axis=1, keepdims=True)
        parts.append(part * lax.rsqrt(mean_sq + 1e-06))
    return parts


def attend_kernel(heads, head_size, nk, hq_ref, hkv_ref, wq_ref, wkv_ref, scale_ref,
                  o_ref, st_ref, q_sc, m_sc, l_sc, acc_sc):
    j = pl.program_id(0)
    width = heads * head_size

    @pl.when(j == 0)
    def _():
        proj = jnp.dot(hq_ref[...], wq_ref[...], preferred_element_type=jnp.float32)
        normed = head_norm(proj, heads, head_size)
        scale = scale_ref[...]
        for h in range(heads):
            cols = slice(h * head_size, (h + 1) * head_size)
            q_sc[:, cols] = (normed[h] * scale[:, cols]).astype(jnp.bfloat16)
        m_sc[...] = jnp.full(m_sc.shape, -jnp.inf, jnp.float32)
        l_sc[...] = jnp.zeros(l_sc.shape, jnp.float32)
        acc_sc[...] = jnp.zeros(acc_sc.shape, jnp.float32)

    kv = jnp.dot(hkv_ref[...], wkv_ref[...], preferred_element_type=jnp.float32)
    keys = head_norm(kv[:, :width], heads, head_size)
    for h in range(heads):
        cols = slice(h * head_size, (h + 1) * head_size)
        k_h = keys[h].astype(jnp.bfloat16)
        v_h = kv[:, width + h * head_size : width + (h + 1) * head_size].astype(jnp.bfloat16)
        s = lax.dot_general(
            q_sc[:, cols], k_h, (((1,), (1,)), ((), ())), preferred_element_type=jnp.float32
        )
        m_prev = m_sc[h]
        m_next = jnp.maximum(m_prev, jnp.max(s, axis=1, keepdims=True))
        alpha = jnp.exp(m_prev - m_next)
        p = jnp.exp(s - m_next[:, 0:1])
        l_sc[h] = alpha * l_sc[h] + jnp.sum(p, axis=1, keepdims=True)
        acc_sc[:, cols] = alpha[:, 0:1] * acc_sc[:, cols] + jnp.dot(
            p.astype(jnp.bfloat16), v_h, preferred_element_type=jnp.float32
        )
        m_sc[h] = m_next

    @pl.when(j == nk - 1)
    def _():
        o_ref[...] = acc_sc[...]
        lane = lax.broadcasted_iota(jnp.int32, st_ref.shape, 1)
        packed = jnp.zeros(st_ref.shape, jnp.float32)
        for h in range(heads):
            packed = jnp.where(lane == h, m_sc[h], packed)
            packed = jnp.where(lane == 64 + h, l_sc[h], packed)
        st_ref[...] = packed


def attend_partial(hidden_q, hidden_kv, wq, wkv, scale_row, heads, head_size, tk=512):
    q_rows, channels = hidden_q.shape
    k_rows = hidden_kv.shape[0]
    width = heads * head_size
    nk = k_rows // tk
    whole = lambda j: (0, 0)
    return pl.pallas_call(
        functools.partial(attend_kernel, heads, head_size, nk),
        grid=(nk,),
        in_specs=[
            pl.BlockSpec((q_rows, channels), whole),
            pl.BlockSpec((tk, channels), lambda j: (j, 0)),
            pl.BlockSpec((channels, width), whole),
            pl.BlockSpec((channels, 2 * width), whole),
            pl.BlockSpec((1, width), whole),
        ],
        out_specs=[
            pl.BlockSpec((q_rows, width), whole),
            pl.BlockSpec((q_rows, 128), whole),
        ],
        out_shape=[
            jax.ShapeDtypeStruct((q_rows, width), jnp.float32),
            jax.ShapeDtypeStruct((q_rows, 128), jnp.float32),
        ],
        scratch_shapes=[
            pltpu.VMEM((q_rows, width), jnp.bfloat16),
            pltpu.VMEM((heads, q_rows, 128), jnp.float32),
            pltpu.VMEM((heads, q_rows, 128), jnp.float32),
            pltpu.VMEM((q_rows, width), jnp.float32),
        ],
        compiler_params=pltpu.CompilerParams(dimension_semantics=("arbitrary",)),
        cost_estimate=pl.CostEstimate(
            flops=4 * q_rows * k_rows * width + 2 * k_rows * channels * 2 * width,
            transcendentals=q_rows * k_rows * heads,
            bytes_accessed=k_rows * channels * 2 + q_rows * width * 8,
        ),
    )(hidden_q, hidden_kv, wq, wkv, scale_row)


def finish_kernel(heads, head_size, o_ref, st_ref, og_ref, sg_ref, hid_ref, wo_ref, out_ref):
    st_own = st_ref[...]
    st_got = sg_ref[...]
    mixed = []
    for h in range(heads):
        cols = slice(h * head_size, (h + 1) * head_size)
        m_own = st_own[:, h : h + 1]
        m_got = st_got[:, h : h + 1]
        m_all = jnp.maximum(m_own, m_got)
        w_own = jnp.exp(m_own - m_all)
        w_got = jnp.exp(m_got - m_all)
        denom = st_own[:, 64 + h : 65 + h] * w_own + st_got[:, 64 + h : 65 + h] * w_got
        part = (o_ref[:, cols] * w_own + og_ref[:, cols] * w_got) / denom
        mixed.append(part.astype(jnp.bfloat16))
    attended = jnp.concatenate(mixed, axis=1)
    out = hid_ref[...].astype(jnp.float32) + jnp.dot(
        attended, wo_ref[...], preferred_element_type=jnp.float32
    )
    out_ref[...] = out.astype(out_ref.dtype)


def finish(o_part, st_part, o_got, st_got, hidden, out_weight, heads, head_size):
    rows, width_out = hidden.shape
    width = heads * head_size
    whole = lambda i: (0, 0)
    return pl.pallas_call(
        functools.partial(finish_kernel, heads, head_size),
        grid=(1,),
        in_specs=[
            pl.BlockSpec((rows, width), whole),
            pl.BlockSpec((rows, 128), whole),
            pl.BlockSpec((rows, width), whole),
            pl.BlockSpec((rows, 128), whole),
            pl.BlockSpec((rows, width_out), whole),
            pl.BlockSpec((width, width_out), whole),
        ],
        out_specs=pl.BlockSpec((rows, width_out), whole),
        out_shape=jax.ShapeDtypeStruct((rows, width_out), jnp.bfloat16),
    )(o_part, st_part, o_got, st_got, hidden, out_weight)


def body(sequence_input, conv_first, conv_second, qkv_weight, out_weight, logit_scale):
    row_count = sequence_input.shape[0]
    padded_input = padded_2(sequence_input, 2)
    first_out = jax.nn.gelu(convolve(padded_input, conv_first, row_count)).astype(jnp.bfloat16)
    padded_first = padded_2(first_out, 2)
    second = convolve(padded_first, conv_second, row_count)
    hidden = (first_out.astype(jnp.float32) + second).astype(jnp.bfloat16)
    head_count = logit_scale.shape[0]
    width_all = qkv_weight.shape[1] // 3
    head_size = width_all // head_count
    scale_row = jnp.repeat(logit_scale / math.sqrt(head_size), head_size)[None, :]
    wq = qkv_weight[:, :width_all]
    wkv = qkv_weight[:, width_all:]

    swap = [(0, 1), (1, 0)]
    hidden_all = lax.all_gather(hidden, "zx", axis=0, tiled=True)
    hidden_other = lax.ppermute(hidden, "core", swap)
    hidden_q = jnp.concatenate([hidden, hidden_other], axis=0)
    o_part, st_part = attend_partial(hidden_q, hidden_all, wq, wkv, scale_row, head_count, head_size)
    o_got, st_got = lax.ppermute((o_part[row_count:], st_part[row_count:]), "core", swap)
    return finish(o_part, st_part, o_got, st_got, hidden, out_weight, head_count, head_size)


def solution(mesh):
    devices = np.asarray(mesh.devices)
    seq_size = mesh.shape["seq"]
    batch_size = mesh.shape["batch"]
    order = [mesh.axis_names.index("seq"), mesh.axis_names.index("batch")]
    devices = devices.transpose(order).reshape(seq_size // 2, 2, batch_size)
    split_mesh = Mesh(devices, ("zx", "core", "batch"))
    rows = P(("batch", "zx", "core"), None)
    in_specs = (rows, P(), P(), P(), P(), P())
    return jax.shard_map(body, mesh=split_mesh, in_specs=in_specs, out_specs=rows, check_vma=False)
```

```python
import functools
import math

import jax
import jax.numpy as jnp
import numpy as np
from jax import lax
from jax.experimental import pallas as pl
from jax.experimental.pallas import tpu as pltpu
from jax.sharding import Mesh
from jax.sharding import PartitionSpec as P

SEQ_AXES = ("zx", "core")


def padded_2(block, width):
    count = lax.axis_size(SEQ_AXES)
    forward = [(i, i + 1) for i in range(count - 1)]
    backward = [(target, source) for source, target in forward]
    low = lax.ppermute(lax.slice_in_dim(block, block.shape[0] - width, None, axis=0), SEQ_AXES, forward)
    high = lax.ppermute(lax.slice_in_dim(block, 0, width, axis=0), SEQ_AXES, backward)
    return jnp.concatenate([low, block, high], axis=0)


def convolve(padded, weight, row_count):
    conv_sum = jnp.dot(padded[0:row_count], weight[0], preferred_element_type=jnp.float32)
    for offset in range(1, weight.shape[0]):
        conv_sum = conv_sum + jnp.dot(
            padded[offset : offset + row_count], weight[offset], preferred_element_type=jnp.float32
        )
    return conv_sum


def head_rms(tensor):
    return tensor * lax.rsqrt(jnp.mean(tensor * tensor, axis=-1, keepdims=True) + 1e-06)


def head_norm(block, heads, head_size):
    parts = []
    for h in range(heads):
        part = block[:, h * head_size : (h + 1) * head_size]
        mean_sq = jnp.mean(part * part, axis=1, keepdims=True)
        parts.append(part * lax.rsqrt(mean_sq + 1e-06))
    return parts


def attend_kernel(first, heads, head_size, nk, *refs):
    if first:
        hq_ref, hkv_ref, wq_ref, wkv_ref, scale_ref, q_out, o_ref, st_ref = refs[:8]
    else:
        q_in, hkv_ref, wkv_ref, o_in, st_in, o_ref, st_ref = refs[:7]
    q_sc, m_sc, l_sc, acc_sc = refs[-4:]
    j = pl.program_id(0)
    width = heads * head_size

    @pl.when(j == 0)
    def _():
        if first:
            proj = jnp.dot(hq_ref[...], wq_ref[...], preferred_element_type=jnp.float32)
            normed = head_norm(proj, heads, head_size)
            scale = scale_ref[...]
            for h in range(heads):
                cols = slice(h * head_size, (h + 1) * head_size)
                q_sc[:, cols] = (normed[h] * scale[:, cols]).astype(jnp.bfloat16)
            q_out[...] = q_sc[...]
            m_sc[...] = jnp.full(m_sc.shape, -jnp.inf, jnp.float32)
            l_sc[...] = jnp.zeros(l_sc.shape, jnp.float32)
            acc_sc[...] = jnp.zeros(acc_sc.shape, jnp.float32)
        else:
            q_sc[...] = q_in[...]
            acc_sc[...] = o_in[...]
            st = st_in[...]
            for h in range(heads):
                m_sc[h] = jnp.broadcast_to(st[:, h : h + 1], m_sc.shape[1:])
                l_sc[h] = jnp.broadcast_to(st[:, 64 + h : 65 + h], l_sc.shape[1:])

    kv = jnp.dot(hkv_ref[...], wkv_ref[...], preferred_element_type=jnp.float32)
    keys = head_norm(kv[:, :width], heads, head_size)
    for h in range(heads):
        cols = slice(h * head_size, (h + 1) * head_size)
        k_h = keys[h].astype(jnp.bfloat16)
        v_h = kv[:, width + h * head_size : width + (h + 1) * head_size].astype(jnp.bfloat16)
        s = lax.dot_general(
            q_sc[:, cols], k_h, (((1,), (1,)), ((), ())), preferred_element_type=jnp.float32
        )
        m_prev = m_sc[h]
        m_next = jnp.maximum(m_prev, jnp.max(s, axis=1, keepdims=True))
        alpha = jnp.exp(m_prev - m_next)
        p = jnp.exp(s - m_next[:, 0:1])
        l_sc[h] = alpha * l_sc[h] + jnp.sum(p, axis=1, keepdims=True)
        acc_sc[:, cols] = alpha[:, 0:1] * acc_sc[:, cols] + jnp.dot(
            p.astype(jnp.bfloat16), v_h, preferred_element_type=jnp.float32
        )
        m_sc[h] = m_next

    @pl.when(j == nk - 1)
    def _():
        o_ref[...] = acc_sc[...]
        lane = lax.broadcasted_iota(jnp.int32, st_ref.shape, 1)
        packed = jnp.zeros(st_ref.shape, jnp.float32)
        for h in range(heads):
            packed = jnp.where(lane == h, m_sc[h], packed)
            packed = jnp.where(lane == 64 + h, l_sc[h], packed)
        st_ref[...] = packed


def attend_chunk(state, hidden_kv, wkv, heads, head_size, tk=512, first=None):
    k_rows, channels = hidden_kv.shape
    width = heads * head_size
    nk = k_rows // tk
    whole = lambda j: (0, 0)
    if state is None:
        hidden_q, wq, scale_row = first
        q_rows = hidden_q.shape[0]
        args = (hidden_q, hidden_kv, wq, wkv, scale_row)
        in_specs = [
            pl.BlockSpec((q_rows, channels), whole),
            pl.BlockSpec((tk, channels), lambda j: (j, 0)),
            pl.BlockSpec((channels, width), whole),
            pl.BlockSpec((channels, 2 * width), whole),
            pl.BlockSpec((1, width), whole),
        ]
        out_specs = [pl.BlockSpec((q_rows, width), whole)]
        out_shape = [jax.ShapeDtypeStruct((q_rows, width), jnp.bfloat16)]
        aliases = {}
    else:
        queries, o_prev, st_prev = state
        q_rows = queries.shape[0]
        args = (queries, hidden_kv, wkv, o_prev, st_prev)
        in_specs = [
            pl.BlockSpec((q_rows, width), whole),
            pl.BlockSpec((tk, channels), lambda j: (j, 0)),
            pl.BlockSpec((channels, 2 * width), whole),
            pl.BlockSpec((q_rows, width), whole),
            pl.BlockSpec((q_rows, 128), whole),
        ]
        out_specs, out_shape = [], []
        aliases = {3: 0, 4: 1}
    out_specs += [pl.BlockSpec((q_rows, width), whole), pl.BlockSpec((q_rows, 128), whole)]
    out_shape += [
        jax.ShapeDtypeStruct((q_rows, width), jnp.float32),
        jax.ShapeDtypeStruct((q_rows, 128), jnp.float32),
    ]
    outs = pl.pallas_call(
        functools.partial(attend_kernel, state is None, heads, head_size, nk),
        grid=(nk,),
        in_specs=in_specs,
        out_specs=out_specs,
        out_shape=out_shape,
        input_output_aliases=aliases,
        scratch_shapes=[
            pltpu.VMEM((q_rows, width), jnp.bfloat16),
            pltpu.VMEM((heads, q_rows, 128), jnp.float32),
            pltpu.VMEM((heads, q_rows, 128), jnp.float32),
            pltpu.VMEM((q_rows, width), jnp.float32),
        ],
        compiler_params=pltpu.CompilerParams(dimension_semantics=("arbitrary",)),
        cost_estimate=pl.CostEstimate(
            flops=4 * q_rows * k_rows * width + 2 * k_rows * channels * 2 * width,
            transcendentals=q_rows * k_rows * heads,
            bytes_accessed=k_rows * channels * 2 + q_rows * width * 8,
        ),
    )(*args)
    if state is None:
        return tuple(outs)
    return (queries,) + tuple(outs)


def finish_kernel(heads, head_size, o_ref, st_ref, og_ref, sg_ref, hid_ref, wo_ref, out_ref):
    st_own = st_ref[...]
    st_got = sg_ref[...]
    mixed = []
    for h in range(heads):
        cols = slice(h * head_size, (h + 1) * head_size)
        m_own = st_own[:, h : h + 1]
        m_got = st_got[:, h : h + 1]
        m_all = jnp.maximum(m_own, m_got)
        w_own = jnp.exp(m_own - m_all)
        w_got = jnp.exp(m_got - m_all)
        denom = st_own[:, 64 + h : 65 + h] * w_own + st_got[:, 64 + h : 65 + h] * w_got
        part = (o_ref[:, cols] * w_own + og_ref[:, cols] * w_got) / denom
        mixed.append(part.astype(jnp.bfloat16))
    attended = jnp.concatenate(mixed, axis=1)
    out = hid_ref[...].astype(jnp.float32) + jnp.dot(
        attended, wo_ref[...], preferred_element_type=jnp.float32
    )
    out_ref[...] = out.astype(out_ref.dtype)


def finish(o_part, st_part, o_got, st_got, hidden, out_weight, heads, head_size):
    rows, width_out = hidden.shape
    width = heads * head_size
    whole = lambda i: (0, 0)
    return pl.pallas_call(
        functools.partial(finish_kernel, heads, head_size),
        grid=(1,),
        in_specs=[
            pl.BlockSpec((rows, width), whole),
            pl.BlockSpec((rows, 128), whole),
            pl.BlockSpec((rows, width), whole),
            pl.BlockSpec((rows, 128), whole),
            pl.BlockSpec((rows, width_out), whole),
            pl.BlockSpec((width, width_out), whole),
        ],
        out_specs=pl.BlockSpec((rows, width_out), whole),
        out_shape=jax.ShapeDtypeStruct((rows, width_out), jnp.bfloat16),
    )(o_part, st_part, o_got, st_got, hidden, out_weight)


def body(sequence_input, conv_first, conv_second, qkv_weight, out_weight, logit_scale):
    row_count = sequence_input.shape[0]
    padded_input = padded_2(sequence_input, 2)
    first_out = jax.nn.gelu(convolve(padded_input, conv_first, row_count)).astype(jnp.bfloat16)
    padded_first = padded_2(first_out, 2)
    second = convolve(padded_first, conv_second, row_count)
    hidden = (first_out.astype(jnp.float32) + second).astype(jnp.bfloat16)
    head_count = logit_scale.shape[0]
    width_all = qkv_weight.shape[1] // 3
    head_size = width_all // head_count
    scale_row = jnp.repeat(logit_scale / math.sqrt(head_size), head_size)[None, :]
    wq = qkv_weight[:, :width_all]
    wkv = qkv_weight[:, width_all:]

    swap = [(0, 1), (1, 0)]
    hidden_other = lax.ppermute(hidden, "core", swap)
    hidden_q = jnp.concatenate([hidden, hidden_other], axis=0)
    chunks = 4
    piece = row_count // chunks
    state = None
    for c in range(chunks):
        gathered = lax.all_gather(hidden[c * piece : (c + 1) * piece], "zx", axis=0, tiled=True)
        state = attend_chunk(state, gathered, wkv, head_count, head_size, first=(hidden_q, wq, scale_row))
    _, o_part, st_part = state
    o_got, st_got = lax.ppermute((o_part[row_count:], st_part[row_count:]), "core", swap)
    return finish(o_part, st_part, o_got, st_got, hidden, out_weight, head_count, head_size)


def solution(mesh):
    devices = np.asarray(mesh.devices)
    seq_size = mesh.shape["seq"]
    batch_size = mesh.shape["batch"]
    order = [mesh.axis_names.index("seq"), mesh.axis_names.index("batch")]
    devices = devices.transpose(order).reshape(seq_size // 2, 2, batch_size)
    split_mesh = Mesh(devices, ("zx", "core", "batch"))
    rows = P(("batch", "zx", "core"), None)
    in_specs = (rows, P(), P(), P(), P(), P())
    return jax.shard_map(body, mesh=split_mesh, in_specs=in_specs, out_specs=rows, check_vma=False)
```

```python
import functools
import math

import jax
import jax.numpy as jnp
import numpy as np
from jax import lax
from jax.experimental import pallas as pl
from jax.experimental.pallas import tpu as pltpu
from jax.sharding import Mesh
from jax.sharding import PartitionSpec as P

SEQ_AXES = ("zx", "core")


def padded_2(block, width):
    count = lax.axis_size(SEQ_AXES)
    forward = [(i, i + 1) for i in range(count - 1)]
    backward = [(target, source) for source, target in forward]
    low = lax.ppermute(lax.slice_in_dim(block, block.shape[0] - width, None, axis=0), SEQ_AXES, forward)
    high = lax.ppermute(lax.slice_in_dim(block, 0, width, axis=0), SEQ_AXES, backward)
    return jnp.concatenate([low, block, high], axis=0)


def convolve(padded, weight, row_count):
    conv_sum = jnp.dot(padded[0:row_count], weight[0], preferred_element_type=jnp.float32)
    for offset in range(1, weight.shape[0]):
        conv_sum = conv_sum + jnp.dot(
            padded[offset : offset + row_count], weight[offset], preferred_element_type=jnp.float32
        )
    return conv_sum


def head_rms(tensor):
    return tensor * lax.rsqrt(jnp.mean(tensor * tensor, axis=-1, keepdims=True) + 1e-06)


def head_norm(block, heads, head_size):
    parts = []
    for h in range(heads):
        part = block[:, h * head_size : (h + 1) * head_size]
        mean_sq = jnp.mean(part * part, axis=1, keepdims=True)
        parts.append(part * lax.rsqrt(mean_sq + 1e-06))
    return parts


def attend_kernel(heads, head_size, nk, hq_ref, hkv_ref, wqt_ref, wk_ref, wvt_ref, scale_ref,
                  o_ref, st_ref, qt_sc, m_sc, l_sc, acc_sc):
    j = pl.program_id(0)
    contract_last = (((1,), (1,)), ((), ()))

    @pl.when(j == 0)
    def _():
        proj_t = lax.dot_general(
            wqt_ref[...], hq_ref[...], contract_last, preferred_element_type=jnp.float32
        )
        for h in range(heads):
            rows = slice(h * head_size, (h + 1) * head_size)
            part = proj_t[rows, :]
            mean_sq = jnp.mean(part * part, axis=0, keepdims=True)
            normed = part * lax.rsqrt(mean_sq + 1e-06)
            qt_sc[rows, :] = (normed * scale_ref[rows, :]).astype(jnp.bfloat16)
        m_sc[...] = jnp.full(m_sc.shape, -jnp.inf, jnp.float32)
        l_sc[...] = jnp.zeros(l_sc.shape, jnp.float32)
        acc_sc[...] = jnp.zeros(acc_sc.shape, jnp.float32)

    hkv = hkv_ref[...]
    k_all = jnp.dot(hkv, wk_ref[...], preferred_element_type=jnp.float32)
    v_t = lax.dot_general(wvt_ref[...], hkv, contract_last, preferred_element_type=jnp.float32)
    for h in range(heads):
        rows = slice(h * head_size, (h + 1) * head_size)
        k_h = k_all[:, rows]
        k_h = (k_h * lax.rsqrt(jnp.mean(k_h * k_h, axis=1, keepdims=True) + 1e-06)).astype(
            jnp.bfloat16
        )
        s_t = jnp.dot(k_h, qt_sc[rows, :], preferred_element_type=jnp.float32)
        m_prev = m_sc[h]
        m_next = jnp.maximum(m_prev, jnp.max(s_t, axis=0, keepdims=True))
        alpha = jnp.exp(m_prev - m_next)
        p_t = jnp.exp(s_t - m_next)
        l_sc[h] = alpha * l_sc[h] + jnp.sum(p_t, axis=0, keepdims=True)
        acc_sc[rows, :] = alpha * acc_sc[rows, :] + jnp.dot(
            v_t[rows, :].astype(jnp.bfloat16), p_t.astype(jnp.bfloat16),
            preferred_element_type=jnp.float32,
        )
        m_sc[h] = m_next

    @pl.when(j == nk - 1)
    def _():
        o_ref[...] = acc_sc[...]
        for h in range(heads):
            st_ref[h : h + 1, :] = m_sc[h]
            st_ref[heads + h : heads + h + 1, :] = l_sc[h]


def attend_partial(hidden_q, hidden_kv, wqt, wk, wvt, scale_col, heads, head_size, tk=512):
    q_rows, channels = hidden_q.shape
    k_rows = hidden_kv.shape[0]
    width = heads * head_size
    nk = k_rows // tk
    whole = lambda j: (0, 0)
    return pl.pallas_call(
        functools.partial(attend_kernel, heads, head_size, nk),
        grid=(nk,),
        in_specs=[
            pl.BlockSpec((q_rows, channels), whole),
            pl.BlockSpec((tk, channels), lambda j: (j, 0)),
            pl.BlockSpec((width, channels), whole),
            pl.BlockSpec((channels, width), whole),
            pl.BlockSpec((width, channels), whole),
            pl.BlockSpec((width, 1), whole),
        ],
        out_specs=[
            pl.BlockSpec((width, q_rows), whole),
            pl.BlockSpec((2 * heads, q_rows), whole),
        ],
        out_shape=[
            jax.ShapeDtypeStruct((width, q_rows), jnp.float32),
            jax.ShapeDtypeStruct((2 * heads, q_rows), jnp.float32),
        ],
        scratch_shapes=[
            pltpu.VMEM((width, q_rows), jnp.bfloat16),
            pltpu.VMEM((heads, 1, q_rows), jnp.float32),
            pltpu.VMEM((heads, 1, q_rows), jnp.float32),
            pltpu.VMEM((width, q_rows), jnp.float32),
        ],
        compiler_params=pltpu.CompilerParams(dimension_semantics=("arbitrary",)),
        cost_estimate=pl.CostEstimate(
            flops=4 * q_rows * k_rows * width + 2 * k_rows * channels * 2 * width,
            transcendentals=q_rows * k_rows * heads,
            bytes_accessed=k_rows * channels * 2 + q_rows * width * 8,
        ),
    )(hidden_q, hidden_kv, wqt, wk, wvt, scale_col)


def finish_kernel(heads, head_size, o_ref, st_ref, og_ref, sg_ref, hid_ref, wo_ref, out_ref):
    st_own = st_ref[...]
    st_got = sg_ref[...]
    mixed = []
    for h in range(heads):
        rows = slice(h * head_size, (h + 1) * head_size)
        m_own = st_own[h : h + 1, :]
        m_got = st_got[h : h + 1, :]
        m_all = jnp.maximum(m_own, m_got)
        w_own = jnp.exp(m_own - m_all)
        w_got = jnp.exp(m_got - m_all)
        denom = st_own[heads + h : heads + h + 1, :] * w_own + st_got[heads + h : heads + h + 1, :] * w_got
        mixed.append((o_ref[rows, :] * w_own + og_ref[rows, :] * w_got) / denom)
    attended = jnp.concatenate(mixed, axis=0).T.astype(jnp.bfloat16)
    out = hid_ref[...].astype(jnp.float32) + jnp.dot(
        attended, wo_ref[...], preferred_element_type=jnp.float32
    )
    out_ref[...] = out.astype(out_ref.dtype)


def finish(o_part, st_part, o_got, st_got, hidden, out_weight, heads, head_size):
    rows, width_out = hidden.shape
    width = heads * head_size
    whole = lambda i: (0, 0)
    return pl.pallas_call(
        functools.partial(finish_kernel, heads, head_size),
        grid=(1,),
        in_specs=[
            pl.BlockSpec((width, rows), whole),
            pl.BlockSpec((2 * heads, rows), whole),
            pl.BlockSpec((width, rows), whole),
            pl.BlockSpec((2 * heads, rows), whole),
            pl.BlockSpec((rows, width_out), whole),
            pl.BlockSpec((width, width_out), whole),
        ],
        out_specs=pl.BlockSpec((rows, width_out), whole),
        out_shape=jax.ShapeDtypeStruct((rows, width_out), jnp.bfloat16),
    )(o_part, st_part, o_got, st_got, hidden, out_weight)


def body(sequence_input, conv_first, conv_second, qkv_weight, out_weight, logit_scale):
    row_count = sequence_input.shape[0]
    padded_input = padded_2(sequence_input, 2)
    first_out = jax.nn.gelu(convolve(padded_input, conv_first, row_count)).astype(jnp.bfloat16)
    padded_first = padded_2(first_out, 2)
    second = convolve(padded_first, conv_second, row_count)
    hidden = (first_out.astype(jnp.float32) + second).astype(jnp.bfloat16)
    head_count = logit_scale.shape[0]
    width_all = qkv_weight.shape[1] // 3
    head_size = width_all // head_count
    scale_col = jnp.repeat(logit_scale / math.sqrt(head_size), head_size)[:, None]
    wqt = qkv_weight[:, :width_all].T
    wk = qkv_weight[:, width_all : 2 * width_all]
    wvt = qkv_weight[:, 2 * width_all :].T

    swap = [(0, 1), (1, 0)]
    hidden_all = lax.all_gather(hidden, "zx", axis=0, tiled=True)
    hidden_other = lax.ppermute(hidden, "core", swap)
    hidden_q = jnp.concatenate([hidden, hidden_other], axis=0)
    o_part, st_part = attend_partial(hidden_q, hidden_all, wqt, wk, wvt, scale_col, head_count, head_size)
    o_got, st_got = lax.ppermute((o_part[:, row_count:], st_part[:, row_count:]), "core", swap)
    return finish(o_part, st_part, o_got, st_got, hidden, out_weight, head_count, head_size)


def solution(mesh):
    devices = np.asarray(mesh.devices)
    seq_size = mesh.shape["seq"]
    batch_size = mesh.shape["batch"]
    order = [mesh.axis_names.index("seq"), mesh.axis_names.index("batch")]
    devices = devices.transpose(order).reshape(seq_size // 2, 2, batch_size)
    split_mesh = Mesh(devices, ("zx", "core", "batch"))
    rows = P(("batch", "zx", "core"), None)
    in_specs = (rows, P(), P(), P(), P(), P())
    return jax.shard_map(body, mesh=split_mesh, in_specs=in_specs, out_specs=rows, check_vma=False)
```

```python
import functools
import math

import jax
import jax.numpy as jnp
import numpy as np
from jax import lax
from jax.experimental import pallas as pl
from jax.experimental.pallas import tpu as pltpu
from jax.sharding import Mesh
from jax.sharding import PartitionSpec as P

SEQ_AXES = ("z", "x", "core")


def padded_2(block, width):
    count = lax.axis_size(SEQ_AXES)
    forward = [(i, i + 1) for i in range(count - 1)]
    backward = [(target, source) for source, target in forward]
    low = lax.ppermute(lax.slice_in_dim(block, block.shape[0] - width, None, axis=0), SEQ_AXES, forward)
    high = lax.ppermute(lax.slice_in_dim(block, 0, width, axis=0), SEQ_AXES, backward)
    return jnp.concatenate([low, block, high], axis=0)


def convolve(padded, weight, row_count):
    conv_sum = jnp.dot(padded[0:row_count], weight[0], preferred_element_type=jnp.float32)
    for offset in range(1, weight.shape[0]):
        conv_sum = conv_sum + jnp.dot(
            padded[offset : offset + row_count], weight[offset], preferred_element_type=jnp.float32
        )
    return conv_sum


def head_rms(tensor):
    return tensor * lax.rsqrt(jnp.mean(tensor * tensor, axis=-1, keepdims=True) + 1e-06)


def head_norm(block, heads, head_size):
    parts = []
    for h in range(heads):
        part = block[:, h * head_size : (h + 1) * head_size]
        mean_sq = jnp.mean(part * part, axis=1, keepdims=True)
        parts.append(part * lax.rsqrt(mean_sq + 1e-06))
    return parts


def attend_kernel(heads, head_size, nk, hq_ref, hkv_ref, wqt_ref, wk_ref, wvt_ref, scale_ref,
                  o_ref, st_ref, qt_sc, m_sc, l_sc, acc_sc):
    j = pl.program_id(0)
    contract_last = (((1,), (1,)), ((), ()))

    @pl.when(j == 0)
    def _():
        proj_t = lax.dot_general(
            wqt_ref[...], hq_ref[...], contract_last, preferred_element_type=jnp.float32
        )
        for h in range(heads):
            rows = slice(h * head_size, (h + 1) * head_size)
            part = proj_t[rows, :]
            mean_sq = jnp.mean(part * part, axis=0, keepdims=True)
            normed = part * lax.rsqrt(mean_sq + 1e-06)
            qt_sc[rows, :] = (normed * scale_ref[rows, :]).astype(jnp.bfloat16)
        m_sc[...] = jnp.full(m_sc.shape, -jnp.inf, jnp.float32)
        l_sc[...] = jnp.zeros(l_sc.shape, jnp.float32)
        acc_sc[...] = jnp.zeros(acc_sc.shape, jnp.float32)

    hkv = hkv_ref[...]
    k_all = jnp.dot(hkv, wk_ref[...], preferred_element_type=jnp.float32)
    v_t = lax.dot_general(wvt_ref[...], hkv, contract_last, preferred_element_type=jnp.float32)
    for h in range(heads):
        rows = slice(h * head_size, (h + 1) * head_size)
        k_h = k_all[:, rows]
        k_h = (k_h * lax.rsqrt(jnp.mean(k_h * k_h, axis=1, keepdims=True) + 1e-06)).astype(
            jnp.bfloat16
        )
        s_t = jnp.dot(k_h, qt_sc[rows, :], preferred_element_type=jnp.float32)
        m_prev = m_sc[h]
        m_next = jnp.maximum(m_prev, jnp.max(s_t, axis=0, keepdims=True))
        alpha = jnp.exp(m_prev - m_next)
        p_t = jnp.exp(s_t - m_next)
        l_sc[h] = alpha * l_sc[h] + jnp.sum(p_t, axis=0, keepdims=True)
        acc_sc[rows, :] = alpha * acc_sc[rows, :] + jnp.dot(
            v_t[rows, :].astype(jnp.bfloat16), p_t.astype(jnp.bfloat16),
            preferred_element_type=jnp.float32,
        )
        m_sc[h] = m_next

    @pl.when(j == nk - 1)
    def _():
        o_ref[...] = acc_sc[...]
        for h in range(heads):
            st_ref[h : h + 1, :] = m_sc[h]
            st_ref[heads + h : heads + h + 1, :] = l_sc[h]


def attend_partial(hidden_q, hidden_kv, wqt, wk, wvt, scale_col, heads, head_size, tk=512):
    q_rows, channels = hidden_q.shape
    k_rows = hidden_kv.shape[0]
    width = heads * head_size
    nk = k_rows // tk
    whole = lambda j: (0, 0)
    return pl.pallas_call(
        functools.partial(attend_kernel, heads, head_size, nk),
        grid=(nk,),
        in_specs=[
            pl.BlockSpec((q_rows, channels), whole),
            pl.BlockSpec((tk, channels), lambda j: (j, 0)),
            pl.BlockSpec((width, channels), whole),
            pl.BlockSpec((channels, width), whole),
            pl.BlockSpec((width, channels), whole),
            pl.BlockSpec((width, 1), whole),
        ],
        out_specs=[
            pl.BlockSpec((width, q_rows), whole),
            pl.BlockSpec((2 * heads, q_rows), whole),
        ],
        out_shape=[
            jax.ShapeDtypeStruct((width, q_rows), jnp.float32),
            jax.ShapeDtypeStruct((2 * heads, q_rows), jnp.float32),
        ],
        scratch_shapes=[
            pltpu.VMEM((width, q_rows), jnp.bfloat16),
            pltpu.VMEM((heads, 1, q_rows), jnp.float32),
            pltpu.VMEM((heads, 1, q_rows), jnp.float32),
            pltpu.VMEM((width, q_rows), jnp.float32),
        ],
        compiler_params=pltpu.CompilerParams(dimension_semantics=("arbitrary",)),
        cost_estimate=pl.CostEstimate(
            flops=4 * q_rows * k_rows * width + 2 * k_rows * channels * 2 * width,
            transcendentals=q_rows * k_rows * heads,
            bytes_accessed=k_rows * channels * 2 + q_rows * width * 8,
        ),
    )(hidden_q, hidden_kv, wqt, wk, wvt, scale_col)


def finish_kernel(heads, head_size, o_ref, st_ref, og_ref, sg_ref, hid_ref, wo_ref, out_ref):
    st_own = st_ref[...]
    st_got = sg_ref[...]
    mixed = []
    for h in range(heads):
        rows = slice(h * head_size, (h + 1) * head_size)
        m_own = st_own[h : h + 1, :]
        m_got = st_got[h : h + 1, :]
        m_all = jnp.maximum(m_own, m_got)
        w_own = jnp.exp(m_own - m_all)
        w_got = jnp.exp(m_got - m_all)
        denom = st_own[heads + h : heads + h + 1, :] * w_own + st_got[heads + h : heads + h + 1, :] * w_got
        mixed.append((o_ref[rows, :] * w_own + og_ref[rows, :] * w_got) / denom)
    attended = jnp.concatenate(mixed, axis=0).T.astype(jnp.bfloat16)
    out = hid_ref[...].astype(jnp.float32) + jnp.dot(
        attended, wo_ref[...], preferred_element_type=jnp.float32
    )
    out_ref[...] = out.astype(out_ref.dtype)


def finish(o_part, st_part, o_got, st_got, hidden, out_weight, heads, head_size):
    rows, width_out = hidden.shape
    width = heads * head_size
    whole = lambda i: (0, 0)
    return pl.pallas_call(
        functools.partial(finish_kernel, heads, head_size),
        grid=(1,),
        in_specs=[
            pl.BlockSpec((width, rows), whole),
            pl.BlockSpec((2 * heads, rows), whole),
            pl.BlockSpec((width, rows), whole),
            pl.BlockSpec((2 * heads, rows), whole),
            pl.BlockSpec((rows, width_out), whole),
            pl.BlockSpec((width, width_out), whole),
        ],
        out_specs=pl.BlockSpec((rows, width_out), whole),
        out_shape=jax.ShapeDtypeStruct((rows, width_out), jnp.bfloat16),
    )(o_part, st_part, o_got, st_got, hidden, out_weight)


def body(sequence_input, conv_first, conv_second, qkv_weight, out_weight, logit_scale):
    row_count = sequence_input.shape[0]
    padded_input = padded_2(sequence_input, 2)
    first_out = jax.nn.gelu(convolve(padded_input, conv_first, row_count)).astype(jnp.bfloat16)
    padded_first = padded_2(first_out, 2)
    second = convolve(padded_first, conv_second, row_count)
    hidden = (first_out.astype(jnp.float32) + second).astype(jnp.bfloat16)
    head_count = logit_scale.shape[0]
    width_all = qkv_weight.shape[1] // 3
    head_size = width_all // head_count
    scale_col = jnp.repeat(logit_scale / math.sqrt(head_size), head_size)[:, None]
    wqt = qkv_weight[:, :width_all].T
    wk = qkv_weight[:, width_all : 2 * width_all]
    wvt = qkv_weight[:, 2 * width_all :].T

    swap = [(0, 1), (1, 0)]
    hidden_all = lax.all_gather(lax.all_gather(hidden, "x", axis=0, tiled=True), "z", axis=0, tiled=True)
    hidden_other = lax.ppermute(hidden, "core", swap)
    hidden_q = jnp.concatenate([hidden, hidden_other], axis=0)
    o_part, st_part = attend_partial(hidden_q, hidden_all, wqt, wk, wvt, scale_col, head_count, head_size)
    o_got, st_got = lax.ppermute((o_part[:, row_count:], st_part[:, row_count:]), "core", swap)
    return finish(o_part, st_part, o_got, st_got, hidden, out_weight, head_count, head_size)


def solution(mesh):
    devices = np.asarray(mesh.devices)
    seq_size = mesh.shape["seq"]
    batch_size = mesh.shape["batch"]
    order = [mesh.axis_names.index("seq"), mesh.axis_names.index("batch")]
    side = math.isqrt(seq_size // 2)
    devices = devices.transpose(order).reshape(seq_size // 2 // side, side, 2, batch_size)
    split_mesh = Mesh(devices, ("z", "x", "core", "batch"))
    rows = P(("batch", "z", "x", "core"), None)
    in_specs = (rows, P(), P(), P(), P(), P())
    return jax.shard_map(body, mesh=split_mesh, in_specs=in_specs, out_specs=rows, check_vma=False)
```

```python
import functools
import math

import jax
import jax.numpy as jnp
import numpy as np
from jax import lax
from jax.experimental import pallas as pl
from jax.experimental.pallas import tpu as pltpu
from jax.sharding import Mesh
from jax.sharding import PartitionSpec as P

SEQ_AXES = ("zx", "core")


def padded_2(block, width):
    count = lax.axis_size(SEQ_AXES)
    forward = [(i, i + 1) for i in range(count - 1)]
    backward = [(target, source) for source, target in forward]
    low = lax.ppermute(lax.slice_in_dim(block, block.shape[0] - width, None, axis=0), SEQ_AXES, forward)
    high = lax.ppermute(lax.slice_in_dim(block, 0, width, axis=0), SEQ_AXES, backward)
    return jnp.concatenate([low, block, high], axis=0)


def convolve(padded, weight, row_count):
    conv_sum = jnp.dot(padded[0:row_count], weight[0], preferred_element_type=jnp.float32)
    for offset in range(1, weight.shape[0]):
        conv_sum = conv_sum + jnp.dot(
            padded[offset : offset + row_count], weight[offset], preferred_element_type=jnp.float32
        )
    return conv_sum


def head_rms(tensor):
    return tensor * lax.rsqrt(jnp.mean(tensor * tensor, axis=-1, keepdims=True) + 1e-06)


def head_norm(block, heads, head_size):
    parts = []
    for h in range(heads):
        part = block[:, h * head_size : (h + 1) * head_size]
        mean_sq = jnp.mean(part * part, axis=1, keepdims=True)
        parts.append(part * lax.rsqrt(mean_sq + 1e-06))
    return parts


def attend_kernel(heads, head_size, nk, hq_ref, hkv_ref, wqt_ref, wk_ref, wvt_ref, scale_ref,
                  o_ref, st_ref, qt_sc, m_sc, l_sc, acc_sc):
    j = pl.program_id(0)
    contract_last = (((1,), (1,)), ((), ()))

    @pl.when(j == 0)
    def _():
        proj_t = lax.dot_general(
            wqt_ref[...], hq_ref[...], contract_last, preferred_element_type=jnp.float32
        )
        for h in range(heads):
            rows = slice(h * head_size, (h + 1) * head_size)
            part = proj_t[rows, :]
            mean_sq = jnp.mean(part * part, axis=0, keepdims=True)
            normed = part * lax.rsqrt(mean_sq + 1e-06)
            qt_sc[rows, :] = (normed * scale_ref[rows, :]).astype(jnp.bfloat16)
        m_sc[...] = jnp.full(m_sc.shape, -jnp.inf, jnp.float32)
        l_sc[...] = jnp.zeros(l_sc.shape, jnp.float32)
        acc_sc[...] = jnp.zeros(acc_sc.shape, jnp.float32)

    hkv = hkv_ref[...]
    k_all = jnp.dot(hkv, wk_ref[...], preferred_element_type=jnp.float32)
    v_t = lax.dot_general(wvt_ref[...], hkv, contract_last, preferred_element_type=jnp.float32)
    for h in range(heads):
        rows = slice(h * head_size, (h + 1) * head_size)
        k_h = k_all[:, rows]
        k_h = (k_h * lax.rsqrt(jnp.mean(k_h * k_h, axis=1, keepdims=True) + 1e-06)).astype(
            jnp.bfloat16
        )
        s_t = jnp.dot(k_h, qt_sc[rows, :], preferred_element_type=jnp.float32)
        m_prev = m_sc[h]
        m_next = jnp.maximum(m_prev, jnp.max(s_t, axis=0, keepdims=True))
        alpha = jnp.exp(m_prev - m_next)
        p_t = jnp.exp(s_t - m_next)
        l_sc[h] = alpha * l_sc[h] + jnp.sum(p_t, axis=0, keepdims=True)
        acc_sc[rows, :] = alpha * acc_sc[rows, :] + jnp.dot(
            v_t[rows, :].astype(jnp.bfloat16), p_t.astype(jnp.bfloat16),
            preferred_element_type=jnp.float32,
        )
        m_sc[h] = m_next

    @pl.when(j == nk - 1)
    def _():
        o_ref[...] = acc_sc[...]
        for h in range(heads):
            st_ref[h : h + 1, :] = m_sc[h]
            st_ref[heads + h : heads + h + 1, :] = l_sc[h]


def attend_partial(hidden_q, hidden_kv, wqt, wk, wvt, scale_col, heads, head_size, tk=512):
    q_rows, channels = hidden_q.shape
    k_rows = hidden_kv.shape[0]
    width = heads * head_size
    nk = k_rows // tk
    whole = lambda j: (0, 0)
    return pl.pallas_call(
        functools.partial(attend_kernel, heads, head_size, nk),
        grid=(nk,),
        in_specs=[
            pl.BlockSpec((q_rows, channels), whole),
            pl.BlockSpec((tk, channels), lambda j: (j, 0)),
            pl.BlockSpec((width, channels), whole),
            pl.BlockSpec((channels, width), whole),
            pl.BlockSpec((width, channels), whole),
            pl.BlockSpec((width, 1), whole),
        ],
        out_specs=[
            pl.BlockSpec((width, q_rows), whole),
            pl.BlockSpec((2 * heads, q_rows), whole),
        ],
        out_shape=[
            jax.ShapeDtypeStruct((width, q_rows), jnp.float32),
            jax.ShapeDtypeStruct((2 * heads, q_rows), jnp.float32),
        ],
        scratch_shapes=[
            pltpu.VMEM((width, q_rows), jnp.bfloat16),
            pltpu.VMEM((heads, 1, q_rows), jnp.float32),
            pltpu.VMEM((heads, 1, q_rows), jnp.float32),
            pltpu.VMEM((width, q_rows), jnp.float32),
        ],
        compiler_params=pltpu.CompilerParams(dimension_semantics=("arbitrary",)),
        cost_estimate=pl.CostEstimate(
            flops=4 * q_rows * k_rows * width + 2 * k_rows * channels * 2 * width,
            transcendentals=q_rows * k_rows * heads,
            bytes_accessed=k_rows * channels * 2 + q_rows * width * 8,
        ),
    )(hidden_q, hidden_kv, wqt, wk, wvt, scale_col)


def finish_kernel(heads, head_size, o_ref, st_ref, og_ref, sg_ref, hid_ref, wo_ref, out_ref):
    st_own = st_ref[...]
    st_got = sg_ref[...]
    mixed = []
    for h in range(heads):
        rows = slice(h * head_size, (h + 1) * head_size)
        m_own = st_own[h : h + 1, :]
        m_got = st_got[h : h + 1, :]
        m_all = jnp.maximum(m_own, m_got)
        w_own = jnp.exp(m_own - m_all)
        w_got = jnp.exp(m_got - m_all)
        denom = st_own[heads + h : heads + h + 1, :] * w_own + st_got[heads + h : heads + h + 1, :] * w_got
        mixed.append((o_ref[rows, :] * w_own + og_ref[rows, :] * w_got) / denom)
    attended = jnp.concatenate(mixed, axis=0).T.astype(jnp.bfloat16)
    out = hid_ref[...].astype(jnp.float32) + jnp.dot(
        attended, wo_ref[...], preferred_element_type=jnp.float32
    )
    out_ref[...] = out.astype(out_ref.dtype)


def finish(o_part, st_part, o_got, st_got, hidden, out_weight, heads, head_size):
    rows, width_out = hidden.shape
    width = heads * head_size
    whole = lambda i: (0, 0)
    return pl.pallas_call(
        functools.partial(finish_kernel, heads, head_size),
        grid=(1,),
        in_specs=[
            pl.BlockSpec((width, rows), whole),
            pl.BlockSpec((2 * heads, rows), whole),
            pl.BlockSpec((width, rows), whole),
            pl.BlockSpec((2 * heads, rows), whole),
            pl.BlockSpec((rows, width_out), whole),
            pl.BlockSpec((width, width_out), whole),
        ],
        out_specs=pl.BlockSpec((rows, width_out), whole),
        out_shape=jax.ShapeDtypeStruct((rows, width_out), jnp.bfloat16),
    )(o_part, st_part, o_got, st_got, hidden, out_weight)


def gather_kernel(axis, n, x_ref, out_ref, send_sem, recv_sem, local_sem):
    me = lax.axis_index(axis)
    rows = x_ref.shape[0]
    mesh_ids = pl.DeviceIdType.MESH
    barrier = pltpu.get_barrier_semaphore()
    for i in range(1, n):
        pl.semaphore_signal(barrier, inc=1, device_id={axis: lax.rem(me + i, n)}, device_id_type=mesh_ids)
    pl.semaphore_wait(barrier, n - 1)
    own_slot = out_ref.at[pl.ds(pl.multiple_of(me * rows, rows), rows)]
    local = pltpu.make_async_copy(x_ref, own_slot, local_sem)
    local.start()
    sends = []
    for i in range(1, n):
        copy = pltpu.make_async_remote_copy(
            src_ref=x_ref,
            dst_ref=own_slot,
            send_sem=send_sem.at[i],
            recv_sem=recv_sem.at[i],
            device_id={axis: lax.rem(me + i, n)},
            device_id_type=mesh_ids,
        )
        copy.start()
        sends.append(copy)
    local.wait()
    for i in range(1, n):
        sends[i - 1].wait_send()
        source = lax.rem(me + n - i, n)
        pltpu.make_async_remote_copy(
            src_ref=x_ref,
            dst_ref=out_ref.at[pl.ds(pl.multiple_of(source * rows, rows), rows)],
            send_sem=send_sem.at[i],
            recv_sem=recv_sem.at[i],
            device_id={axis: source},
            device_id_type=mesh_ids,
        ).wait_recv()


def gather_rows(block, axis):
    n = lax.axis_size(axis)
    rows, width = block.shape
    return pl.pallas_call(
        functools.partial(gather_kernel, axis, n),
        in_specs=[pl.BlockSpec(memory_space=pl.ANY)],
        out_specs=pl.BlockSpec(memory_space=pl.ANY),
        out_shape=jax.ShapeDtypeStruct((n * rows, width), block.dtype),
        scratch_shapes=[
            pltpu.SemaphoreType.DMA((n,)),
            pltpu.SemaphoreType.DMA((n,)),
            pltpu.SemaphoreType.DMA,
        ],
        compiler_params=pltpu.CompilerParams(collective_id=0, has_side_effects=True),
    )(block)


def body(sequence_input, conv_first, conv_second, qkv_weight, out_weight, logit_scale):
    row_count = sequence_input.shape[0]
    padded_input = padded_2(sequence_input, 2)
    first_out = jax.nn.gelu(convolve(padded_input, conv_first, row_count)).astype(jnp.bfloat16)
    padded_first = padded_2(first_out, 2)
    second = convolve(padded_first, conv_second, row_count)
    hidden = (first_out.astype(jnp.float32) + second).astype(jnp.bfloat16)
    head_count = logit_scale.shape[0]
    width_all = qkv_weight.shape[1] // 3
    head_size = width_all // head_count
    scale_col = jnp.repeat(logit_scale / math.sqrt(head_size), head_size)[:, None]
    wqt = qkv_weight[:, :width_all].T
    wk = qkv_weight[:, width_all : 2 * width_all]
    wvt = qkv_weight[:, 2 * width_all :].T

    swap = [(0, 1), (1, 0)]
    hidden_all = gather_rows(hidden, "zx")
    hidden_other = lax.ppermute(hidden, "core", swap)
    hidden_q = jnp.concatenate([hidden, hidden_other], axis=0)
    o_part, st_part = attend_partial(hidden_q, hidden_all, wqt, wk, wvt, scale_col, head_count, head_size)
    o_got, st_got = lax.ppermute((o_part[:, row_count:], st_part[:, row_count:]), "core", swap)
    return finish(o_part, st_part, o_got, st_got, hidden, out_weight, head_count, head_size)


def solution(mesh):
    devices = np.asarray(mesh.devices)
    seq_size = mesh.shape["seq"]
    batch_size = mesh.shape["batch"]
    order = [mesh.axis_names.index("seq"), mesh.axis_names.index("batch")]
    devices = devices.transpose(order).reshape(seq_size // 2, 2, batch_size)
    split_mesh = Mesh(devices, ("zx", "core", "batch"))
    rows = P(("batch", "zx", "core"), None)
    in_specs = (rows, P(), P(), P(), P(), P())
    return jax.shard_map(body, mesh=split_mesh, in_specs=in_specs, out_specs=rows, check_vma=False)
```

```python
import functools
import math

import jax
import jax.numpy as jnp
import numpy as np
from jax import lax
from jax.experimental import pallas as pl
from jax.experimental.pallas import tpu as pltpu
from jax.sharding import Mesh
from jax.sharding import PartitionSpec as P

SEQ_AXES = ("zx", "core")


def padded_2(block, width):
    count = lax.axis_size(SEQ_AXES)
    forward = [(i, i + 1) for i in range(count - 1)]
    backward = [(target, source) for source, target in forward]
    low = lax.ppermute(lax.slice_in_dim(block, block.shape[0] - width, None, axis=0), SEQ_AXES, forward)
    high = lax.ppermute(lax.slice_in_dim(block, 0, width, axis=0), SEQ_AXES, backward)
    return jnp.concatenate([low, block, high], axis=0)


def convolve(padded, weight, row_count):
    conv_sum = jnp.dot(padded[0:row_count], weight[0], preferred_element_type=jnp.float32)
    for offset in range(1, weight.shape[0]):
        conv_sum = conv_sum + jnp.dot(
            padded[offset : offset + row_count], weight[offset], preferred_element_type=jnp.float32
        )
    return conv_sum


def head_rms(tensor):
    return tensor * lax.rsqrt(jnp.mean(tensor * tensor, axis=-1, keepdims=True) + 1e-06)


def head_norm(block, heads, head_size):
    parts = []
    for h in range(heads):
        part = block[:, h * head_size : (h + 1) * head_size]
        mean_sq = jnp.mean(part * part, axis=1, keepdims=True)
        parts.append(part * lax.rsqrt(mean_sq + 1e-06))
    return parts


def attend_kernel(heads, head_size, nk, hq_ref, hkv_ref, wqt_ref, wk_ref, wvt_ref, scale_ref,
                  o_ref, st_ref, qt_sc, m_sc, l_sc, acc_sc):
    j = pl.program_id(0)
    contract_last = (((1,), (1,)), ((), ()))

    @pl.when(j == 0)
    def _():
        proj_t = lax.dot_general(
            wqt_ref[...], hq_ref[...], contract_last, preferred_element_type=jnp.float32
        )
        for h in range(heads):
            rows = slice(h * head_size, (h + 1) * head_size)
            part = proj_t[rows, :]
            mean_sq = jnp.mean(part * part, axis=0, keepdims=True)
            normed = part * lax.rsqrt(mean_sq + 1e-06)
            qt_sc[rows, :] = (normed * scale_ref[rows, :]).astype(jnp.bfloat16)
        m_sc[...] = jnp.full(m_sc.shape, -jnp.inf, jnp.float32)
        l_sc[...] = jnp.zeros(l_sc.shape, jnp.float32)
        acc_sc[...] = jnp.zeros(acc_sc.shape, jnp.float32)

    hkv = hkv_ref[...]
    k_all = jnp.dot(hkv, wk_ref[...], preferred_element_type=jnp.float32)
    v_t = lax.dot_general(wvt_ref[...], hkv, contract_last, preferred_element_type=jnp.float32)
    for h in range(heads):
        rows = slice(h * head_size, (h + 1) * head_size)
        k_h = k_all[:, rows]
        k_h = (k_h * lax.rsqrt(jnp.mean(k_h * k_h, axis=1, keepdims=True) + 1e-06)).astype(
            jnp.bfloat16
        )
        s_t = jnp.dot(k_h, qt_sc[rows, :], preferred_element_type=jnp.float32)
        m_prev = m_sc[h]
        m_next = jnp.maximum(m_prev, jnp.max(s_t, axis=0, keepdims=True))
        alpha = jnp.exp(m_prev - m_next)
        p_t = jnp.exp(s_t - m_next)
        l_sc[h] = alpha * l_sc[h] + jnp.sum(p_t, axis=0, keepdims=True)
        acc_sc[rows, :] = alpha * acc_sc[rows, :] + jnp.dot(
            v_t[rows, :].astype(jnp.bfloat16), p_t.astype(jnp.bfloat16),
            preferred_element_type=jnp.float32,
        )
        m_sc[h] = m_next

    @pl.when(j == nk - 1)
    def _():
        o_ref[...] = acc_sc[...]
        for h in range(heads):
            st_ref[h : h + 1, :] = m_sc[h]
            st_ref[heads + h : heads + h + 1, :] = l_sc[h]


def attend_partial(hidden_q, hidden_kv, wqt, wk, wvt, scale_col, heads, head_size, tk=512):
    q_rows, channels = hidden_q.shape
    k_rows = hidden_kv.shape[0]
    width = heads * head_size
    nk = k_rows // tk
    whole = lambda j: (0, 0)
    return pl.pallas_call(
        functools.partial(attend_kernel, heads, head_size, nk),
        grid=(nk,),
        in_specs=[
            pl.BlockSpec((q_rows, channels), whole),
            pl.BlockSpec((tk, channels), lambda j: (j, 0)),
            pl.BlockSpec((width, channels), whole),
            pl.BlockSpec((channels, width), whole),
            pl.BlockSpec((width, channels), whole),
            pl.BlockSpec((width, 1), whole),
        ],
        out_specs=[
            pl.BlockSpec((width, q_rows), whole),
            pl.BlockSpec((2 * heads, q_rows), whole),
        ],
        out_shape=[
            jax.ShapeDtypeStruct((width, q_rows), jnp.float32),
            jax.ShapeDtypeStruct((2 * heads, q_rows), jnp.float32),
        ],
        scratch_shapes=[
            pltpu.VMEM((width, q_rows), jnp.bfloat16),
            pltpu.VMEM((heads, 1, q_rows), jnp.float32),
            pltpu.VMEM((heads, 1, q_rows), jnp.float32),
            pltpu.VMEM((width, q_rows), jnp.float32),
        ],
        compiler_params=pltpu.CompilerParams(dimension_semantics=("arbitrary",)),
        cost_estimate=pl.CostEstimate(
            flops=4 * q_rows * k_rows * width + 2 * k_rows * channels * 2 * width,
            transcendentals=q_rows * k_rows * heads,
            bytes_accessed=k_rows * channels * 2 + q_rows * width * 8,
        ),
    )(hidden_q, hidden_kv, wqt, wk, wvt, scale_col)


def finish_kernel(heads, head_size, o_ref, st_ref, og_ref, sg_ref, hid_ref, wo_ref, out_ref):
    st_own = st_ref[...]
    st_got = sg_ref[...]
    mixed = []
    for h in range(heads):
        rows = slice(h * head_size, (h + 1) * head_size)
        m_own = st_own[h : h + 1, :]
        m_got = st_got[h : h + 1, :]
        m_all = jnp.maximum(m_own, m_got)
        w_own = jnp.exp(m_own - m_all)
        w_got = jnp.exp(m_got - m_all)
        denom = st_own[heads + h : heads + h + 1, :] * w_own + st_got[heads + h : heads + h + 1, :] * w_got
        mixed.append((o_ref[rows, :] * w_own + og_ref[rows, :] * w_got) / denom)
    attended = jnp.concatenate(mixed, axis=0).T.astype(jnp.bfloat16)
    out = hid_ref[...].astype(jnp.float32) + jnp.dot(
        attended, wo_ref[...], preferred_element_type=jnp.float32
    )
    out_ref[...] = out.astype(out_ref.dtype)


def finish(o_part, st_part, o_got, st_got, hidden, out_weight, heads, head_size):
    rows, width_out = hidden.shape
    width = heads * head_size
    whole = lambda i: (0, 0)
    return pl.pallas_call(
        functools.partial(finish_kernel, heads, head_size),
        grid=(1,),
        in_specs=[
            pl.BlockSpec((width, rows), whole),
            pl.BlockSpec((2 * heads, rows), whole),
            pl.BlockSpec((width, rows), whole),
            pl.BlockSpec((2 * heads, rows), whole),
            pl.BlockSpec((rows, width_out), whole),
            pl.BlockSpec((width, width_out), whole),
        ],
        out_specs=pl.BlockSpec((rows, width_out), whole),
        out_shape=jax.ShapeDtypeStruct((rows, width_out), jnp.bfloat16),
    )(o_part, st_part, o_got, st_got, hidden, out_weight)


def ring_gather_kernel(side, x_ref, out_ref, send_sem, recv_sem, local_sem):
    me = lax.axis_index("zx")
    z, x = me // side, me % side
    half = x_ref.shape[1]
    q = half // 2
    mesh_ids = pl.DeviceIdType.MESH

    def slot(stream, a, b):
        a = lax.rem(a + side, side)
        b = lax.rem(b + side, side)
        return b * side + a if stream == 0 else a * side + b

    own = [(x, z), (z, x)]
    barrier = pltpu.get_barrier_semaphore()
    for target in (slot(0, x + 1, z), slot(0, x - 1, z), slot(1, z + 1, x), slot(1, z - 1, x)):
        pl.semaphore_signal(barrier, inc=1, device_id={"zx": target}, device_id_type=mesh_ids)
    pl.semaphore_wait(barrier, 4)
    local = pltpu.make_async_copy(x_ref, out_ref.at[me], local_sem)
    local.start()

    sends = []
    index = {}

    def send(key, src, view, target):
        idx = len(index)
        index[key] = idx
        copy = pltpu.make_async_remote_copy(
            src_ref=src, dst_ref=view, send_sem=send_sem.at[idx], recv_sem=recv_sem.at[idx],
            device_id={"zx": target}, device_id_type=mesh_ids,
        )
        copy.start()
        sends.append(copy)

    def recv(key, view, source):
        idx = index[key]
        pltpu.make_async_remote_copy(
            src_ref=view, dst_ref=view, send_sem=send_sem.at[idx], recv_sem=recv_sem.at[idx],
            device_id={"zx": source}, device_id_type=mesh_ids,
        ).wait_recv()

    def part(stream, a, b, lo=None):
        view = out_ref.at[slot(stream, a, b), stream]
        return view if lo is None else view.at[pl.ds(lo, q)]

    for st in range(2):
        a0, b0 = own[st]
        send((st, 1, 1), x_ref.at[st], part(st, a0, b0), slot(st, a0 + 1, b0))
        send((st, 1, -1), x_ref.at[st], part(st, a0, b0), slot(st, a0 - 1, b0))
    for st in range(2):
        a0, b0 = own[st]
        recv((st, 1, 1), part(st, a0 - 1, b0), slot(st, a0 - 1, b0))
        recv((st, 1, -1), part(st, a0 + 1, b0), slot(st, a0 + 1, b0))
        send((st, 2, 1), part(st, a0 - 1, b0, 0), part(st, a0 - 1, b0, 0), slot(st, a0 + 1, b0))
        send((st, 2, -1), part(st, a0 + 1, b0, q), part(st, a0 + 1, b0, q), slot(st, a0 - 1, b0))
    for st in range(2):
        a0, b0 = own[st]
        recv((st, 2, 1), part(st, a0 - 2, b0, 0), slot(st, a0 - 1, b0))
        recv((st, 2, -1), part(st, a0 + 2, b0, q), slot(st, a0 + 1, b0))
        for k in range(side):
            src = x_ref.at[st] if k == 0 else part(st, a0 + k, b0)
            send((st, 3, 1, k), src, part(st, a0 + k, b0), slot(st, a0, b0 + 1))
            send((st, 3, -1, k), src, part(st, a0 + k, b0), slot(st, a0, b0 - 1))
    for st in range(2):
        a0, b0 = own[st]
        for k in range(side):
            recv((st, 3, 1, k), part(st, a0 + k, b0 - 1), slot(st, a0, b0 - 1))
            recv((st, 3, -1, k), part(st, a0 + k, b0 + 1), slot(st, a0, b0 + 1))
            send((st, 4, 1, k), part(st, a0 + k, b0 - 1, 0), part(st, a0 + k, b0 - 1, 0), slot(st, a0, b0 + 1))
            send((st, 4, -1, k), part(st, a0 + k, b0 + 1, q), part(st, a0 + k, b0 + 1, q), slot(st, a0, b0 - 1))
    for st in range(2):
        a0, b0 = own[st]
        for k in range(side):
            recv((st, 4, 1, k), part(st, a0 + k, b0 - 2, 0), slot(st, a0, b0 - 1))
            recv((st, 4, -1, k), part(st, a0 + k, b0 + 2, q), slot(st, a0, b0 + 1))
    local.wait()
    for copy in sends:
        copy.wait_send()


def gather_rows(block, axis):
    n = lax.axis_size(axis)
    side = math.isqrt(n)
    rows, width = block.shape
    copies = 2 * (2 + 2 + 4 * side)
    out = pl.pallas_call(
        functools.partial(ring_gather_kernel, side),
        in_specs=[pl.BlockSpec(memory_space=pl.ANY)],
        out_specs=pl.BlockSpec(memory_space=pl.ANY),
        out_shape=jax.ShapeDtypeStruct((n, 2, rows // 2, width), block.dtype),
        scratch_shapes=[
            pltpu.SemaphoreType.DMA((copies,)),
            pltpu.SemaphoreType.DMA((copies,)),
            pltpu.SemaphoreType.DMA,
        ],
        compiler_params=pltpu.CompilerParams(collective_id=0, has_side_effects=True),
    )(block.reshape(2, rows // 2, width))
    return out.reshape(n * rows, width)


def body(sequence_input, conv_first, conv_second, qkv_weight, out_weight, logit_scale):
    row_count = sequence_input.shape[0]
    padded_input = padded_2(sequence_input, 2)
    first_out = jax.nn.gelu(convolve(padded_input, conv_first, row_count)).astype(jnp.bfloat16)
    padded_first = padded_2(first_out, 2)
    second = convolve(padded_first, conv_second, row_count)
    hidden = (first_out.astype(jnp.float32) + second).astype(jnp.bfloat16)
    head_count = logit_scale.shape[0]
    width_all = qkv_weight.shape[1] // 3
    head_size = width_all // head_count
    scale_col = jnp.repeat(logit_scale / math.sqrt(head_size), head_size)[:, None]
    wqt = qkv_weight[:, :width_all].T
    wk = qkv_weight[:, width_all : 2 * width_all]
    wvt = qkv_weight[:, 2 * width_all :].T

    swap = [(0, 1), (1, 0)]
    hidden_all = gather_rows(hidden, "zx")
    hidden_other = lax.ppermute(hidden, "core", swap)
    hidden_q = jnp.concatenate([hidden, hidden_other], axis=0)
    o_part, st_part = attend_partial(hidden_q, hidden_all, wqt, wk, wvt, scale_col, head_count, head_size)
    o_got, st_got = lax.ppermute((o_part[:, row_count:], st_part[:, row_count:]), "core", swap)
    return finish(o_part, st_part, o_got, st_got, hidden, out_weight, head_count, head_size)


def solution(mesh):
    devices = np.asarray(mesh.devices)
    seq_size = mesh.shape["seq"]
    batch_size = mesh.shape["batch"]
    order = [mesh.axis_names.index("seq"), mesh.axis_names.index("batch")]
    devices = devices.transpose(order).reshape(seq_size // 2, 2, batch_size)
    split_mesh = Mesh(devices, ("zx", "core", "batch"))
    rows = P(("batch", "zx", "core"), None)
    in_specs = (rows, P(), P(), P(), P(), P())
    return jax.shard_map(body, mesh=split_mesh, in_specs=in_specs, out_specs=rows, check_vma=False)
```

```python
import functools
import math

import jax
import jax.numpy as jnp
import numpy as np
from jax import lax
from jax.experimental import pallas as pl
from jax.experimental.pallas import tpu as pltpu
from jax.sharding import Mesh
from jax.sharding import PartitionSpec as P

SEQ_AXES = ("zx", "core")


def padded_2(block, width):
    count = lax.axis_size(SEQ_AXES)
    forward = [(i, i + 1) for i in range(count - 1)]
    backward = [(target, source) for source, target in forward]
    low = lax.ppermute(lax.slice_in_dim(block, block.shape[0] - width, None, axis=0), SEQ_AXES, forward)
    high = lax.ppermute(lax.slice_in_dim(block, 0, width, axis=0), SEQ_AXES, backward)
    return jnp.concatenate([low, block, high], axis=0)


def convolve(padded, weight, row_count):
    conv_sum = jnp.dot(padded[0:row_count], weight[0], preferred_element_type=jnp.float32)
    for offset in range(1, weight.shape[0]):
        conv_sum = conv_sum + jnp.dot(
            padded[offset : offset + row_count], weight[offset], preferred_element_type=jnp.float32
        )
    return conv_sum


def head_rms(tensor):
    return tensor * lax.rsqrt(jnp.mean(tensor * tensor, axis=-1, keepdims=True) + 1e-06)


def head_norm(block, heads, head_size):
    parts = []
    for h in range(heads):
        part = block[:, h * head_size : (h + 1) * head_size]
        mean_sq = jnp.mean(part * part, axis=1, keepdims=True)
        parts.append(part * lax.rsqrt(mean_sq + 1e-06))
    return parts


def attend_kernel(heads, head_size, nk, hq_ref, hkv_ref, wqt_ref, wk_ref, wvt_ref, scale_ref,
                  o_ref, st_ref, qt_sc, m_sc, l_sc, acc_sc):
    j = pl.program_id(0)
    contract_last = (((1,), (1,)), ((), ()))

    @pl.when(j == 0)
    def _():
        proj_t = lax.dot_general(
            wqt_ref[...], hq_ref[...], contract_last, preferred_element_type=jnp.float32
        )
        for h in range(heads):
            rows = slice(h * head_size, (h + 1) * head_size)
            part = proj_t[rows, :]
            mean_sq = jnp.mean(part * part, axis=0, keepdims=True)
            normed = part * lax.rsqrt(mean_sq + 1e-06)
            qt_sc[rows, :] = (normed * scale_ref[rows, :]).astype(jnp.bfloat16)
        m_sc[...] = jnp.full(m_sc.shape, -jnp.inf, jnp.float32)
        l_sc[...] = jnp.zeros(l_sc.shape, jnp.float32)
        acc_sc[...] = jnp.zeros(acc_sc.shape, jnp.float32)

    hkv = hkv_ref[...]
    k_all = jnp.dot(hkv, wk_ref[...], preferred_element_type=jnp.float32)
    v_t = lax.dot_general(wvt_ref[...], hkv, contract_last, preferred_element_type=jnp.float32)
    for h in range(heads):
        rows = slice(h * head_size, (h + 1) * head_size)
        k_h = k_all[:, rows]
        k_h = (k_h * lax.rsqrt(jnp.mean(k_h * k_h, axis=1, keepdims=True) + 1e-06)).astype(
            jnp.bfloat16
        )
        s_t = jnp.dot(k_h, qt_sc[rows, :], preferred_element_type=jnp.float32)
        m_prev = m_sc[h]
        m_next = jnp.maximum(m_prev, jnp.max(s_t, axis=0, keepdims=True))
        alpha = jnp.exp(m_prev - m_next)
        p_t = jnp.exp(s_t - m_next)
        l_sc[h] = alpha * l_sc[h] + jnp.sum(p_t, axis=0, keepdims=True)
        acc_sc[rows, :] = alpha * acc_sc[rows, :] + jnp.dot(
            v_t[rows, :].astype(jnp.bfloat16), p_t.astype(jnp.bfloat16),
            preferred_element_type=jnp.float32,
        )
        m_sc[h] = m_next

    @pl.when(j == nk - 1)
    def _():
        o_ref[...] = acc_sc[...]
        for h in range(heads):
            st_ref[h : h + 1, :] = m_sc[h]
            st_ref[heads + h : heads + h + 1, :] = l_sc[h]


def attend_partial(hidden_q, hidden_kv, wqt, wk, wvt, scale_col, heads, head_size, tk=512):
    q_rows, channels = hidden_q.shape
    k_rows = hidden_kv.shape[0]
    width = heads * head_size
    nk = k_rows // tk
    whole = lambda j: (0, 0)
    return pl.pallas_call(
        functools.partial(attend_kernel, heads, head_size, nk),
        grid=(nk,),
        in_specs=[
            pl.BlockSpec((q_rows, channels), whole),
            pl.BlockSpec((tk, channels), lambda j: (j, 0)),
            pl.BlockSpec((width, channels), whole),
            pl.BlockSpec((channels, width), whole),
            pl.BlockSpec((width, channels), whole),
            pl.BlockSpec((width, 1), whole),
        ],
        out_specs=[
            pl.BlockSpec((width, q_rows), whole),
            pl.BlockSpec((2 * heads, q_rows), whole),
        ],
        out_shape=[
            jax.ShapeDtypeStruct((width, q_rows), jnp.float32),
            jax.ShapeDtypeStruct((2 * heads, q_rows), jnp.float32),
        ],
        scratch_shapes=[
            pltpu.VMEM((width, q_rows), jnp.bfloat16),
            pltpu.VMEM((heads, 1, q_rows), jnp.float32),
            pltpu.VMEM((heads, 1, q_rows), jnp.float32),
            pltpu.VMEM((width, q_rows), jnp.float32),
        ],
        compiler_params=pltpu.CompilerParams(dimension_semantics=("arbitrary",)),
        cost_estimate=pl.CostEstimate(
            flops=4 * q_rows * k_rows * width + 2 * k_rows * channels * 2 * width,
            transcendentals=q_rows * k_rows * heads,
            bytes_accessed=k_rows * channels * 2 + q_rows * width * 8,
        ),
    )(hidden_q, hidden_kv, wqt, wk, wvt, scale_col)


def finish_kernel(heads, head_size, o_ref, st_ref, og_ref, sg_ref, hid_ref, wo_ref, out_ref):
    st_own = st_ref[...]
    st_got = sg_ref[...]
    mixed = []
    for h in range(heads):
        rows = slice(h * head_size, (h + 1) * head_size)
        m_own = st_own[h : h + 1, :]
        m_got = st_got[h : h + 1, :]
        m_all = jnp.maximum(m_own, m_got)
        w_own = jnp.exp(m_own - m_all)
        w_got = jnp.exp(m_got - m_all)
        denom = st_own[heads + h : heads + h + 1, :] * w_own + st_got[heads + h : heads + h + 1, :] * w_got
        mixed.append((o_ref[rows, :] * w_own + og_ref[rows, :] * w_got) / denom)
    attended = jnp.concatenate(mixed, axis=0).T.astype(jnp.bfloat16)
    out = hid_ref[...].astype(jnp.float32) + jnp.dot(
        attended, wo_ref[...], preferred_element_type=jnp.float32
    )
    out_ref[...] = out.astype(out_ref.dtype)


def finish(o_part, st_part, o_got, st_got, hidden, out_weight, heads, head_size):
    rows, width_out = hidden.shape
    width = heads * head_size
    whole = lambda i: (0, 0)
    return pl.pallas_call(
        functools.partial(finish_kernel, heads, head_size),
        grid=(1,),
        in_specs=[
            pl.BlockSpec((width, rows), whole),
            pl.BlockSpec((2 * heads, rows), whole),
            pl.BlockSpec((width, rows), whole),
            pl.BlockSpec((2 * heads, rows), whole),
            pl.BlockSpec((rows, width_out), whole),
            pl.BlockSpec((width, width_out), whole),
        ],
        out_specs=pl.BlockSpec((rows, width_out), whole),
        out_shape=jax.ShapeDtypeStruct((rows, width_out), jnp.bfloat16),
    )(o_part, st_part, o_got, st_got, hidden, out_weight)


def ring_gather_kernel(side, x_ref, out_ref, send_sem, recv_sem, local_sem):
    me = lax.axis_index("zx")
    z, x = me // side, me % side
    half = x_ref.shape[1]
    q = half // 2
    mesh_ids = pl.DeviceIdType.MESH

    def slot(stream, a, b):
        a = lax.rem(a + side, side)
        b = lax.rem(b + side, side)
        return b * side + a if stream == 0 else a * side + b

    own = [(x, z), (z, x)]
    barrier = pltpu.get_barrier_semaphore()
    for target in (slot(0, x + 1, z), slot(0, x - 1, z), slot(1, z + 1, x), slot(1, z - 1, x)):
        pl.semaphore_signal(barrier, inc=1, device_id={"zx": target}, device_id_type=mesh_ids)
    pl.semaphore_wait(barrier, 4)
    local = pltpu.make_async_copy(x_ref, out_ref.at[me], local_sem)
    local.start()

    sends = []
    index = {}

    def send(key, src, view, target):
        idx = len(index)
        index[key] = idx
        copy = pltpu.make_async_remote_copy(
            src_ref=src, dst_ref=view, send_sem=send_sem.at[idx], recv_sem=recv_sem.at[idx],
            device_id={"zx": target}, device_id_type=mesh_ids,
        )
        copy.start()
        sends.append(copy)

    def recv(key, view, source):
        idx = index[key]
        pltpu.make_async_remote_copy(
            src_ref=view, dst_ref=view, send_sem=send_sem.at[idx], recv_sem=recv_sem.at[idx],
            device_id={"zx": source}, device_id_type=mesh_ids,
        ).wait_recv()

    def part(stream, a, b, lo=None):
        view = out_ref.at[slot(stream, a, b), stream]
        return view if lo is None else view.at[pl.ds(lo, q)]

    for st in range(2):
        a0, b0 = own[st]
        send((st, 1, 1), x_ref.at[st], part(st, a0, b0), slot(st, a0 + 1, b0))
        send((st, 1, -1), x_ref.at[st], part(st, a0, b0), slot(st, a0 - 1, b0))
    for st in range(2):
        a0, b0 = own[st]
        recv((st, 1, 1), part(st, a0 - 1, b0), slot(st, a0 - 1, b0))
        recv((st, 1, -1), part(st, a0 + 1, b0), slot(st, a0 + 1, b0))
        send((st, 2, 1), part(st, a0 - 1, b0, 0), part(st, a0 - 1, b0, 0), slot(st, a0 + 1, b0))
        send((st, 2, -1), part(st, a0 + 1, b0, q), part(st, a0 + 1, b0, q), slot(st, a0 - 1, b0))
    for st in range(2):
        a0, b0 = own[st]
        recv((st, 2, 1), part(st, a0 - 2, b0, 0), slot(st, a0 - 1, b0))
        recv((st, 2, -1), part(st, a0 + 2, b0, q), slot(st, a0 + 1, b0))
        for k in range(side):
            src = x_ref.at[st] if k == 0 else part(st, a0 + k, b0)
            send((st, 3, 1, k), src, part(st, a0 + k, b0), slot(st, a0, b0 + 1))
            send((st, 3, -1, k), src, part(st, a0 + k, b0), slot(st, a0, b0 - 1))
    for st in range(2):
        a0, b0 = own[st]
        for k in range(side):
            recv((st, 3, 1, k), part(st, a0 + k, b0 - 1), slot(st, a0, b0 - 1))
            recv((st, 3, -1, k), part(st, a0 + k, b0 + 1), slot(st, a0, b0 + 1))
            send((st, 4, 1, k), part(st, a0 + k, b0 - 1, 0), part(st, a0 + k, b0 - 1, 0), slot(st, a0, b0 + 1))
            send((st, 4, -1, k), part(st, a0 + k, b0 + 1, q), part(st, a0 + k, b0 + 1, q), slot(st, a0, b0 - 1))
    for st in range(2):
        a0, b0 = own[st]
        for k in range(side):
            recv((st, 4, 1, k), part(st, a0 + k, b0 - 2, 0), slot(st, a0, b0 - 1))
            recv((st, 4, -1, k), part(st, a0 + k, b0 + 2, q), slot(st, a0, b0 + 1))
    local.wait()
    for copy in sends:
        copy.wait_send()


def gather_rows(block, axis):
    n = lax.axis_size(axis)
    side = math.isqrt(n)
    rows, width = block.shape
    copies = 2 * (2 + 2 + 4 * side)
    out = pl.pallas_call(
        functools.partial(ring_gather_kernel, side),
        in_specs=[pl.BlockSpec(memory_space=pl.ANY)],
        out_specs=pl.BlockSpec(memory_space=pl.ANY),
        out_shape=jax.ShapeDtypeStruct((n, 2, rows // 2, width), block.dtype),
        scratch_shapes=[
            pltpu.SemaphoreType.DMA((copies,)),
            pltpu.SemaphoreType.DMA((copies,)),
            pltpu.SemaphoreType.DMA,
        ],
        compiler_params=pltpu.CompilerParams(collective_id=0, has_side_effects=True),
    )(block.reshape(2, rows // 2, width))
    return out.reshape(n * rows, width)


def conv_gelu_kernel(taps, rows, x_ref, w_ref, o_ref, acc_sc):
    j = pl.program_id(0)
    product = jnp.dot(x_ref[...], w_ref[...], preferred_element_type=jnp.float32)
    for t in range(taps):

        @pl.when(j == t)
        def _():
            if t == 0:
                acc_sc[...] = product[t : t + rows]
            else:
                acc_sc[...] = acc_sc[...] + product[t : t + rows]

    @pl.when(j == taps - 1)
    def _():
        o_ref[...] = jax.nn.gelu(acc_sc[...]).astype(o_ref.dtype)


def conv_gelu(padded, weight, rows):
    taps, channels, width = weight.shape
    extra = (-padded.shape[0]) % 8
    padded = jnp.pad(padded, ((0, extra), (0, 0)))
    whole = lambda j: (0, 0)
    return pl.pallas_call(
        functools.partial(conv_gelu_kernel, taps, rows),
        grid=(taps,),
        in_specs=[
            pl.BlockSpec(padded.shape, whole),
            pl.BlockSpec((None, channels, width), lambda j: (j, 0, 0)),
        ],
        out_specs=pl.BlockSpec((rows, width), whole),
        out_shape=jax.ShapeDtypeStruct((rows, width), jnp.bfloat16),
        scratch_shapes=[pltpu.VMEM((rows, width), jnp.float32)],
        compiler_params=pltpu.CompilerParams(dimension_semantics=("arbitrary",)),
        cost_estimate=pl.CostEstimate(
            flops=2 * taps * padded.shape[0] * channels * width,
            transcendentals=rows * width,
            bytes_accessed=taps * channels * width * 2 + padded.size * 2 + rows * width * 2,
        ),
    )(padded, weight)


def body(sequence_input, conv_first, conv_second, qkv_weight, out_weight, logit_scale):
    row_count = sequence_input.shape[0]
    padded_input = padded_2(sequence_input, 2)
    first_out = conv_gelu(padded_input, conv_first, row_count)
    padded_first = padded_2(first_out, 2)
    second = convolve(padded_first, conv_second, row_count)
    hidden = (first_out.astype(jnp.float32) + second).astype(jnp.bfloat16)
    head_count = logit_scale.shape[0]
    width_all = qkv_weight.shape[1] // 3
    head_size = width_all // head_count
    scale_col = jnp.repeat(logit_scale / math.sqrt(head_size), head_size)[:, None]
    wqt = qkv_weight[:, :width_all].T
    wk = qkv_weight[:, width_all : 2 * width_all]
    wvt = qkv_weight[:, 2 * width_all :].T

    swap = [(0, 1), (1, 0)]
    hidden_all = gather_rows(hidden, "zx")
    hidden_other = lax.ppermute(hidden, "core", swap)
    hidden_q = jnp.concatenate([hidden, hidden_other], axis=0)
    o_part, st_part = attend_partial(hidden_q, hidden_all, wqt, wk, wvt, scale_col, head_count, head_size)
    o_got, st_got = lax.ppermute((o_part[:, row_count:], st_part[:, row_count:]), "core", swap)
    return finish(o_part, st_part, o_got, st_got, hidden, out_weight, head_count, head_size)


def solution(mesh):
    devices = np.asarray(mesh.devices)
    seq_size = mesh.shape["seq"]
    batch_size = mesh.shape["batch"]
    order = [mesh.axis_names.index("seq"), mesh.axis_names.index("batch")]
    devices = devices.transpose(order).reshape(seq_size // 2, 2, batch_size)
    split_mesh = Mesh(devices, ("zx", "core", "batch"))
    rows = P(("batch", "zx", "core"), None)
    in_specs = (rows, P(), P(), P(), P(), P())
    return jax.shard_map(body, mesh=split_mesh, in_specs=in_specs, out_specs=rows, check_vma=False)
```

```python
import functools
import math

import jax
import jax.numpy as jnp
import numpy as np
from jax import lax
from jax.experimental import pallas as pl
from jax.experimental.pallas import tpu as pltpu
from jax.sharding import Mesh
from jax.sharding import PartitionSpec as P

SEQ_AXES = ("zx", "core")


def padded_2(block, width):
    count = lax.axis_size(SEQ_AXES)
    forward = [(i, i + 1) for i in range(count - 1)]
    backward = [(target, source) for source, target in forward]
    low = lax.ppermute(lax.slice_in_dim(block, block.shape[0] - width, None, axis=0), SEQ_AXES, forward)
    high = lax.ppermute(lax.slice_in_dim(block, 0, width, axis=0), SEQ_AXES, backward)
    return jnp.concatenate([low, block, high], axis=0)


def convolve(padded, weight, row_count):
    conv_sum = jnp.dot(padded[0:row_count], weight[0], preferred_element_type=jnp.float32)
    for offset in range(1, weight.shape[0]):
        conv_sum = conv_sum + jnp.dot(
            padded[offset : offset + row_count], weight[offset], preferred_element_type=jnp.float32
        )
    return conv_sum


def head_rms(tensor):
    return tensor * lax.rsqrt(jnp.mean(tensor * tensor, axis=-1, keepdims=True) + 1e-06)


def head_norm(block, heads, head_size):
    parts = []
    for h in range(heads):
        part = block[:, h * head_size : (h + 1) * head_size]
        mean_sq = jnp.mean(part * part, axis=1, keepdims=True)
        parts.append(part * lax.rsqrt(mean_sq + 1e-06))
    return parts


def attend_kernel(heads, head_size, nk, qa_ref, qb_ref, hkv_ref, wk_ref, wvt_ref,
                  o_ref, st_ref, qt_sc, m_sc, l_sc, acc_sc):
    j = pl.program_id(0)
    contract_last = (((1,), (1,)), ((), ()))

    @pl.when(j == 0)
    def _():
        own = qa_ref.shape[1]
        qt_sc[:, :own] = qa_ref[...]
        qt_sc[:, own:] = qb_ref[...]
        m_sc[...] = jnp.full(m_sc.shape, -jnp.inf, jnp.float32)
        l_sc[...] = jnp.zeros(l_sc.shape, jnp.float32)
        acc_sc[...] = jnp.zeros(acc_sc.shape, jnp.float32)

    hkv = hkv_ref[...]
    k_all = jnp.dot(hkv, wk_ref[...], preferred_element_type=jnp.float32)
    v_t = lax.dot_general(wvt_ref[...], hkv, contract_last, preferred_element_type=jnp.float32)
    for h in range(heads):
        rows = slice(h * head_size, (h + 1) * head_size)
        k_h = k_all[:, rows]
        k_h = (k_h * lax.rsqrt(jnp.mean(k_h * k_h, axis=1, keepdims=True) + 1e-06)).astype(
            jnp.bfloat16
        )
        s_t = jnp.dot(k_h, qt_sc[rows, :], preferred_element_type=jnp.float32)
        m_prev = m_sc[h]
        m_next = jnp.maximum(m_prev, jnp.max(s_t, axis=0, keepdims=True))
        alpha = jnp.exp(m_prev - m_next)
        p_t = jnp.exp(s_t - m_next)
        l_sc[h] = alpha * l_sc[h] + jnp.sum(p_t, axis=0, keepdims=True)
        acc_sc[rows, :] = alpha * acc_sc[rows, :] + jnp.dot(
            v_t[rows, :].astype(jnp.bfloat16), p_t.astype(jnp.bfloat16),
            preferred_element_type=jnp.float32,
        )
        m_sc[h] = m_next

    @pl.when(j == nk - 1)
    def _():
        o_ref[...] = acc_sc[...]
        for h in range(heads):
            st_ref[h : h + 1, :] = m_sc[h]
            st_ref[heads + h : heads + h + 1, :] = l_sc[h]


def attend_partial(qt_own, qt_other, hidden_kv, qkv_weight, wvt, heads, head_size, tk=512):
    width, own = qt_own.shape
    q_rows = 2 * own
    k_rows, channels = hidden_kv.shape
    nk = k_rows // tk
    whole = lambda j: (0, 0)
    return pl.pallas_call(
        functools.partial(attend_kernel, heads, head_size, nk),
        grid=(nk,),
        in_specs=[
            pl.BlockSpec((width, own), whole),
            pl.BlockSpec((width, own), whole),
            pl.BlockSpec((tk, channels), lambda j: (j, 0)),
            pl.BlockSpec((channels, width), lambda j: (0, 1)),
            pl.BlockSpec((width, channels), whole),
        ],
        out_specs=[
            pl.BlockSpec((width, q_rows), whole),
            pl.BlockSpec((2 * heads, q_rows), whole),
        ],
        out_shape=[
            jax.ShapeDtypeStruct((width, q_rows), jnp.float32),
            jax.ShapeDtypeStruct((2 * heads, q_rows), jnp.float32),
        ],
        scratch_shapes=[
            pltpu.VMEM((width, q_rows), jnp.bfloat16),
            pltpu.VMEM((heads, 1, q_rows), jnp.float32),
            pltpu.VMEM((heads, 1, q_rows), jnp.float32),
            pltpu.VMEM((width, q_rows), jnp.float32),
        ],
        compiler_params=pltpu.CompilerParams(dimension_semantics=("arbitrary",)),
        cost_estimate=pl.CostEstimate(
            flops=4 * q_rows * k_rows * width + 2 * k_rows * channels * 2 * width,
            transcendentals=q_rows * k_rows * heads,
            bytes_accessed=k_rows * channels * 2 + q_rows * width * 8,
        ),
    )(qt_own, qt_other, hidden_kv, qkv_weight, wvt)


def finish_kernel(heads, head_size, o_ref, st_ref, og_ref, sg_ref, hid_ref, wo_ref, out_ref):
    st_own = st_ref[...]
    st_got = sg_ref[...]
    mixed = []
    for h in range(heads):
        rows = slice(h * head_size, (h + 1) * head_size)
        m_own = st_own[h : h + 1, :]
        m_got = st_got[h : h + 1, :]
        m_all = jnp.maximum(m_own, m_got)
        w_own = jnp.exp(m_own - m_all)
        w_got = jnp.exp(m_got - m_all)
        denom = st_own[heads + h : heads + h + 1, :] * w_own + st_got[heads + h : heads + h + 1, :] * w_got
        mixed.append((o_ref[rows, :] * w_own + og_ref[rows, :] * w_got) / denom)
    attended = jnp.concatenate(mixed, axis=0).T.astype(jnp.bfloat16)
    out = hid_ref[...].astype(jnp.float32) + jnp.dot(
        attended, wo_ref[...], preferred_element_type=jnp.float32
    )
    out_ref[...] = out.astype(out_ref.dtype)


def finish(o_part, st_part, o_got, st_got, hidden, out_weight, heads, head_size):
    rows, width_out = hidden.shape
    width = heads * head_size
    whole = lambda i: (0, 0)
    return pl.pallas_call(
        functools.partial(finish_kernel, heads, head_size),
        grid=(1,),
        in_specs=[
            pl.BlockSpec((width, rows), whole),
            pl.BlockSpec((2 * heads, rows), whole),
            pl.BlockSpec((width, rows), whole),
            pl.BlockSpec((2 * heads, rows), whole),
            pl.BlockSpec((rows, width_out), whole),
            pl.BlockSpec((width, width_out), whole),
        ],
        out_specs=pl.BlockSpec((rows, width_out), whole),
        out_shape=jax.ShapeDtypeStruct((rows, width_out), jnp.bfloat16),
    )(o_part, st_part, o_got, st_got, hidden, out_weight)


def ring_gather_kernel(side, heads, head_size, x_ref, h_ref, wq_ref, wv_ref, scale_ref,
                       out_ref, qt_ref, wvt_ref, send_sem, recv_sem, local_sem):
    me = lax.axis_index("zx")
    z, x = me // side, me % side
    half = x_ref.shape[1]
    q = half // 2
    mesh_ids = pl.DeviceIdType.MESH

    def slot(stream, a, b):
        a = lax.rem(a + side, side)
        b = lax.rem(b + side, side)
        return b * side + a if stream == 0 else a * side + b

    own = [(x, z), (z, x)]
    barrier = pltpu.get_barrier_semaphore()
    for target in (slot(0, x + 1, z), slot(0, x - 1, z), slot(1, z + 1, x), slot(1, z - 1, x)):
        pl.semaphore_signal(barrier, inc=1, device_id={"zx": target}, device_id_type=mesh_ids)
    pl.semaphore_wait(barrier, 4)
    local = pltpu.make_async_copy(x_ref, out_ref.at[me], local_sem)
    local.start()

    sends = []
    index = {}

    def send(key, src, view, target):
        idx = len(index)
        index[key] = idx
        copy = pltpu.make_async_remote_copy(
            src_ref=src, dst_ref=view, send_sem=send_sem.at[idx], recv_sem=recv_sem.at[idx],
            device_id={"zx": target}, device_id_type=mesh_ids,
        )
        copy.start()
        sends.append(copy)

    def recv(key, view, source):
        idx = index[key]
        pltpu.make_async_remote_copy(
            src_ref=view, dst_ref=view, send_sem=send_sem.at[idx], recv_sem=recv_sem.at[idx],
            device_id={"zx": source}, device_id_type=mesh_ids,
        ).wait_recv()

    def part(stream, a, b, lo=None):
        view = out_ref.at[slot(stream, a, b), stream]
        return view if lo is None else view.at[pl.ds(lo, q)]

    for st in range(2):
        a0, b0 = own[st]
        send((st, 1, 1), x_ref.at[st], part(st, a0, b0), slot(st, a0 + 1, b0))
        send((st, 1, -1), x_ref.at[st], part(st, a0, b0), slot(st, a0 - 1, b0))
    proj = jnp.dot(h_ref[...], wq_ref[...], preferred_element_type=jnp.float32)
    scale = scale_ref[...]
    normed = []
    for h in range(heads):
        cols = slice(h * head_size, (h + 1) * head_size)
        part_q = proj[:, cols]
        mean_sq = jnp.mean(part_q * part_q, axis=1, keepdims=True)
        normed.append(part_q * lax.rsqrt(mean_sq + 1e-06) * scale[:, cols])
    qt_ref[...] = jnp.concatenate(normed, axis=1).T.astype(qt_ref.dtype)
    wvt_ref[...] = wv_ref[...].astype(jnp.float32).T.astype(wvt_ref.dtype)
    for st in range(2):
        a0, b0 = own[st]
        recv((st, 1, 1), part(st, a0 - 1, b0), slot(st, a0 - 1, b0))
        recv((st, 1, -1), part(st, a0 + 1, b0), slot(st, a0 + 1, b0))
        send((st, 2, 1), part(st, a0 - 1, b0, 0), part(st, a0 - 1, b0, 0), slot(st, a0 + 1, b0))
        send((st, 2, -1), part(st, a0 + 1, b0, q), part(st, a0 + 1, b0, q), slot(st, a0 - 1, b0))
    for st in range(2):
        a0, b0 = own[st]
        recv((st, 2, 1), part(st, a0 - 2, b0, 0), slot(st, a0 - 1, b0))
        recv((st, 2, -1), part(st, a0 + 2, b0, q), slot(st, a0 + 1, b0))
        for k in range(side):
            src = x_ref.at[st] if k == 0 else part(st, a0 + k, b0)
            send((st, 3, 1, k), src, part(st, a0 + k, b0), slot(st, a0, b0 + 1))
            send((st, 3, -1, k), src, part(st, a0 + k, b0), slot(st, a0, b0 - 1))
    for st in range(2):
        a0, b0 = own[st]
        for k in range(side):
            recv((st, 3, 1, k), part(st, a0 + k, b0 - 1), slot(st, a0, b0 - 1))
            recv((st, 3, -1, k), part(st, a0 + k, b0 + 1), slot(st, a0, b0 + 1))
            send((st, 4, 1, k), part(st, a0 + k, b0 - 1, 0), part(st, a0 + k, b0 - 1, 0), slot(st, a0, b0 + 1))
            send((st, 4, -1, k), part(st, a0 + k, b0 + 1, q), part(st, a0 + k, b0 + 1, q), slot(st, a0, b0 - 1))
    for st in range(2):
        a0, b0 = own[st]
        for k in range(side):
            recv((st, 4, 1, k), part(st, a0 + k, b0 - 2, 0), slot(st, a0, b0 - 1))
            recv((st, 4, -1, k), part(st, a0 + k, b0 + 2, q), slot(st, a0, b0 + 1))
    local.wait()
    for copy in sends:
        copy.wait_send()


def gather_rows(block, qkv_weight, scale_row, heads, head_size, axis):
    n = lax.axis_size(axis)
    side = math.isqrt(n)
    rows, width = block.shape
    channels, width_qkv = qkv_weight.shape
    width_all = width_qkv // 3
    copies = 2 * (2 + 2 + 4 * side)
    whole = lambda i: (0, 0)
    out, qt, wvt = pl.pallas_call(
        functools.partial(ring_gather_kernel, side, heads, head_size),
        grid=(1,),
        in_specs=[
            pl.BlockSpec(memory_space=pl.ANY),
            pl.BlockSpec((rows, width), whole),
            pl.BlockSpec((channels, width_all), lambda i: (0, 0)),
            pl.BlockSpec((channels, width_all), lambda i: (0, 2)),
            pl.BlockSpec((1, width_all), whole),
        ],
        out_specs=[
            pl.BlockSpec(memory_space=pl.ANY),
            pl.BlockSpec((width_all, rows), whole),
            pl.BlockSpec((width_all, channels), whole),
        ],
        out_shape=[
            jax.ShapeDtypeStruct((n, 2, rows // 2, width), block.dtype),
            jax.ShapeDtypeStruct((width_all, rows), jnp.bfloat16),
            jax.ShapeDtypeStruct((width_all, channels), jnp.bfloat16),
        ],
        scratch_shapes=[
            pltpu.SemaphoreType.DMA((copies,)),
            pltpu.SemaphoreType.DMA((copies,)),
            pltpu.SemaphoreType.DMA,
        ],
        compiler_params=pltpu.CompilerParams(collective_id=0, has_side_effects=True),
    )(block.reshape(2, rows // 2, width), block, qkv_weight, qkv_weight, scale_row)
    return out.reshape(n * rows, width), qt, wvt


def body(sequence_input, conv_first, conv_second, qkv_weight, out_weight, logit_scale):
    row_count = sequence_input.shape[0]
    padded_input = padded_2(sequence_input, 2)
    first_out = jax.nn.gelu(convolve(padded_input, conv_first, row_count)).astype(jnp.bfloat16)
    padded_first = padded_2(first_out, 2)
    second = convolve(padded_first, conv_second, row_count)
    hidden = (first_out.astype(jnp.float32) + second).astype(jnp.bfloat16)
    head_count = logit_scale.shape[0]
    width_all = qkv_weight.shape[1] // 3
    head_size = width_all // head_count
    scale_row = jnp.repeat(logit_scale / math.sqrt(head_size), head_size)[None, :]

    swap = [(0, 1), (1, 0)]
    hidden_all, qt_own, wvt = gather_rows(hidden, qkv_weight, scale_row, head_count, head_size, "zx")
    qt_other = lax.ppermute(qt_own, "core", swap)
    o_part, st_part = attend_partial(qt_own, qt_other, hidden_all, qkv_weight, wvt, head_count, head_size)
    o_got, st_got = lax.ppermute((o_part[:, row_count:], st_part[:, row_count:]), "core", swap)
    return finish(o_part, st_part, o_got, st_got, hidden, out_weight, head_count, head_size)


def solution(mesh):
    devices = np.asarray(mesh.devices)
    seq_size = mesh.shape["seq"]
    batch_size = mesh.shape["batch"]
    order = [mesh.axis_names.index("seq"), mesh.axis_names.index("batch")]
    devices = devices.transpose(order).reshape(seq_size // 2, 2, batch_size)
    split_mesh = Mesh(devices, ("zx", "core", "batch"))
    rows = P(("batch", "zx", "core"), None)
    in_specs = (rows, P(), P(), P(), P(), P())
    return jax.shard_map(body, mesh=split_mesh, in_specs=in_specs, out_specs=rows, check_vma=False)
```

```python
import functools
import math

import jax
import jax.numpy as jnp
import numpy as np
from jax import lax
from jax.experimental import pallas as pl
from jax.experimental.pallas import tpu as pltpu
from jax.sharding import Mesh
from jax.sharding import PartitionSpec as P

SEQ_AXES = ("zx", "core")


def padded_2(block, width):
    count = lax.axis_size(SEQ_AXES)
    forward = [(i, i + 1) for i in range(count - 1)]
    backward = [(target, source) for source, target in forward]
    low = lax.ppermute(lax.slice_in_dim(block, block.shape[0] - width, None, axis=0), SEQ_AXES, forward)
    high = lax.ppermute(lax.slice_in_dim(block, 0, width, axis=0), SEQ_AXES, backward)
    return jnp.concatenate([low, block, high], axis=0)


def convolve(padded, weight, row_count):
    conv_sum = jnp.dot(padded[0:row_count], weight[0], preferred_element_type=jnp.float32)
    for offset in range(1, weight.shape[0]):
        conv_sum = conv_sum + jnp.dot(
            padded[offset : offset + row_count], weight[offset], preferred_element_type=jnp.float32
        )
    return conv_sum


def head_rms(tensor):
    return tensor * lax.rsqrt(jnp.mean(tensor * tensor, axis=-1, keepdims=True) + 1e-06)


def head_norm(block, heads, head_size):
    parts = []
    for h in range(heads):
        part = block[:, h * head_size : (h + 1) * head_size]
        mean_sq = jnp.mean(part * part, axis=1, keepdims=True)
        parts.append(part * lax.rsqrt(mean_sq + 1e-06))
    return parts


def attend_kernel(heads, head_size, nk, qa_ref, qb_ref, hkv_ref, wk_ref, wvt_ref,
                  o_ref, st_ref, ob_ref, sb_ref, qt_sc, m_sc, l_sc, acc_sc):
    j = pl.program_id(0)
    contract_last = (((1,), (1,)), ((), ()))

    @pl.when(j == 0)
    def _():
        own = qa_ref.shape[1]
        qt_sc[:, :own] = qa_ref[...]
        qt_sc[:, own:] = qb_ref[...]
        m_sc[...] = jnp.full(m_sc.shape, -jnp.inf, jnp.float32)
        l_sc[...] = jnp.zeros(l_sc.shape, jnp.float32)
        acc_sc[...] = jnp.zeros(acc_sc.shape, jnp.float32)

    hkv = hkv_ref[...]
    k_all = jnp.dot(hkv, wk_ref[...], preferred_element_type=jnp.float32)
    v_t = lax.dot_general(wvt_ref[...], hkv, contract_last, preferred_element_type=jnp.float32)
    for h in range(heads):
        rows = slice(h * head_size, (h + 1) * head_size)
        k_h = k_all[:, rows]
        k_h = (k_h * lax.rsqrt(jnp.mean(k_h * k_h, axis=1, keepdims=True) + 1e-06)).astype(
            jnp.bfloat16
        )
        s_t = jnp.dot(k_h, qt_sc[rows, :], preferred_element_type=jnp.float32)
        m_prev = m_sc[h]
        m_next = jnp.maximum(m_prev, jnp.max(s_t, axis=0, keepdims=True))
        alpha = jnp.exp(m_prev - m_next)
        p_t = jnp.exp(s_t - m_next)
        l_sc[h] = alpha * l_sc[h] + jnp.sum(p_t, axis=0, keepdims=True)
        acc_sc[rows, :] = alpha * acc_sc[rows, :] + jnp.dot(
            v_t[rows, :].astype(jnp.bfloat16), p_t.astype(jnp.bfloat16),
            preferred_element_type=jnp.float32,
        )
        m_sc[h] = m_next

    @pl.when(j == nk - 1)
    def _():
        own = o_ref.shape[1]
        o_ref[...] = acc_sc[:, :own]
        ob_ref[...] = acc_sc[:, own:]
        for h in range(heads):
            st_ref[h : h + 1, :] = m_sc[h][:, :own]
            st_ref[heads + h : heads + h + 1, :] = l_sc[h][:, :own]
            sb_ref[h : h + 1, :] = m_sc[h][:, own:]
            sb_ref[heads + h : heads + h + 1, :] = l_sc[h][:, own:]


def attend_partial(qt_own, qt_other, hidden_kv, qkv_weight, wvt, heads, head_size, tk=512):
    width, own = qt_own.shape
    q_rows = 2 * own
    k_rows, channels = hidden_kv.shape
    nk = k_rows // tk
    whole = lambda j: (0, 0)
    return pl.pallas_call(
        functools.partial(attend_kernel, heads, head_size, nk),
        grid=(nk,),
        in_specs=[
            pl.BlockSpec((width, own), whole),
            pl.BlockSpec((width, own), whole),
            pl.BlockSpec((tk, channels), lambda j: (j, 0)),
            pl.BlockSpec((channels, width), lambda j: (0, 1)),
            pl.BlockSpec((width, channels), whole),
        ],
        out_specs=[
            pl.BlockSpec((width, own), whole),
            pl.BlockSpec((2 * heads, own), whole),
        ] * 2,
        out_shape=[
            jax.ShapeDtypeStruct((width, own), jnp.float32),
            jax.ShapeDtypeStruct((2 * heads, own), jnp.float32),
        ] * 2,
        scratch_shapes=[
            pltpu.VMEM((width, q_rows), jnp.bfloat16),
            pltpu.VMEM((heads, 1, q_rows), jnp.float32),
            pltpu.VMEM((heads, 1, q_rows), jnp.float32),
            pltpu.VMEM((width, q_rows), jnp.float32),
        ],
        compiler_params=pltpu.CompilerParams(dimension_semantics=("arbitrary",)),
        cost_estimate=pl.CostEstimate(
            flops=4 * q_rows * k_rows * width + 2 * k_rows * channels * 2 * width,
            transcendentals=q_rows * k_rows * heads,
            bytes_accessed=k_rows * channels * 2 + q_rows * width * 8,
        ),
    )(qt_own, qt_other, hidden_kv, qkv_weight, wvt)


def finish_kernel(heads, head_size, o_ref, st_ref, og_ref, sg_ref, hid_ref, wo_ref, out_ref):
    st_own = st_ref[...]
    st_got = sg_ref[...]
    mixed = []
    for h in range(heads):
        rows = slice(h * head_size, (h + 1) * head_size)
        m_own = st_own[h : h + 1, :]
        m_got = st_got[h : h + 1, :]
        m_all = jnp.maximum(m_own, m_got)
        w_own = jnp.exp(m_own - m_all)
        w_got = jnp.exp(m_got - m_all)
        denom = st_own[heads + h : heads + h + 1, :] * w_own + st_got[heads + h : heads + h + 1, :] * w_got
        mixed.append((o_ref[rows, :] * w_own + og_ref[rows, :] * w_got) / denom)
    attended = jnp.concatenate(mixed, axis=0).T.astype(jnp.bfloat16)
    out = hid_ref[...].astype(jnp.float32) + jnp.dot(
        attended, wo_ref[...], preferred_element_type=jnp.float32
    )
    out_ref[...] = out.astype(out_ref.dtype)


def finish(o_part, st_part, o_got, st_got, hidden, out_weight, heads, head_size):
    rows, width_out = hidden.shape
    width = heads * head_size
    whole = lambda i: (0, 0)
    return pl.pallas_call(
        functools.partial(finish_kernel, heads, head_size),
        grid=(1,),
        in_specs=[
            pl.BlockSpec((width, rows), whole),
            pl.BlockSpec((2 * heads, rows), whole),
            pl.BlockSpec((width, rows), whole),
            pl.BlockSpec((2 * heads, rows), whole),
            pl.BlockSpec((rows, width_out), whole),
            pl.BlockSpec((width, width_out), whole),
        ],
        out_specs=pl.BlockSpec((rows, width_out), whole),
        out_shape=jax.ShapeDtypeStruct((rows, width_out), jnp.bfloat16),
    )(o_part, st_part, o_got, st_got, hidden, out_weight)


def ring_gather_kernel(side, heads, head_size, x_ref, h_ref, wq_ref, wv_ref, scale_ref,
                       out_ref, qt_ref, wvt_ref, send_sem, recv_sem, local_sem):
    me = lax.axis_index("zx")
    z, x = me // side, me % side
    half = x_ref.shape[1]
    q = half // 2
    mesh_ids = pl.DeviceIdType.MESH

    def slot(stream, a, b):
        a = lax.rem(a + side, side)
        b = lax.rem(b + side, side)
        return b * side + a if stream == 0 else a * side + b

    own = [(x, z), (z, x)]
    barrier = pltpu.get_barrier_semaphore()
    for target in (slot(0, x + 1, z), slot(0, x - 1, z), slot(1, z + 1, x), slot(1, z - 1, x)):
        pl.semaphore_signal(barrier, inc=1, device_id={"zx": target}, device_id_type=mesh_ids)
    pl.semaphore_wait(barrier, 4)
    local = pltpu.make_async_copy(x_ref, out_ref.at[me], local_sem)
    local.start()

    sends = []
    index = {}

    def send(key, src, view, target):
        idx = len(index)
        index[key] = idx
        copy = pltpu.make_async_remote_copy(
            src_ref=src, dst_ref=view, send_sem=send_sem.at[idx], recv_sem=recv_sem.at[idx],
            device_id={"zx": target}, device_id_type=mesh_ids,
        )
        copy.start()
        sends.append(copy)

    def recv(key, view, source):
        idx = index[key]
        pltpu.make_async_remote_copy(
            src_ref=view, dst_ref=view, send_sem=send_sem.at[idx], recv_sem=recv_sem.at[idx],
            device_id={"zx": source}, device_id_type=mesh_ids,
        ).wait_recv()

    def part(stream, a, b, lo=None):
        view = out_ref.at[slot(stream, a, b), stream]
        return view if lo is None else view.at[pl.ds(lo, q)]

    for st in range(2):
        a0, b0 = own[st]
        send((st, 1, 1), x_ref.at[st], part(st, a0, b0), slot(st, a0 + 1, b0))
        send((st, 1, -1), x_ref.at[st], part(st, a0, b0), slot(st, a0 - 1, b0))
    for st in range(2):
        a0, b0 = own[st]
        recv((st, 1, 1), part(st, a0 - 1, b0), slot(st, a0 - 1, b0))
        recv((st, 1, -1), part(st, a0 + 1, b0), slot(st, a0 + 1, b0))
        send((st, 2, 1), part(st, a0 - 1, b0, 0), part(st, a0 - 1, b0, 0), slot(st, a0 + 1, b0))
        send((st, 2, -1), part(st, a0 + 1, b0, q), part(st, a0 + 1, b0, q), slot(st, a0 - 1, b0))
    for st in range(2):
        a0, b0 = own[st]
        recv((st, 2, 1), part(st, a0 - 2, b0, 0), slot(st, a0 - 1, b0))
        recv((st, 2, -1), part(st, a0 + 2, b0, q), slot(st, a0 + 1, b0))
        for k in range(side):
            src = x_ref.at[st] if k == 0 else part(st, a0 + k, b0)
            send((st, 3, 1, k), src, part(st, a0 + k, b0), slot(st, a0, b0 + 1))
            send((st, 3, -1, k), src, part(st, a0 + k, b0), slot(st, a0, b0 - 1))
    for st in range(2):
        a0, b0 = own[st]
        for k in range(side):
            recv((st, 3, 1, k), part(st, a0 + k, b0 - 1), slot(st, a0, b0 - 1))
            recv((st, 3, -1, k), part(st, a0 + k, b0 + 1), slot(st, a0, b0 + 1))
            send((st, 4, 1, k), part(st, a0 + k, b0 - 1, 0), part(st, a0 + k, b0 - 1, 0), slot(st, a0, b0 + 1))
            send((st, 4, -1, k), part(st, a0 + k, b0 + 1, q), part(st, a0 + k, b0 + 1, q), slot(st, a0, b0 - 1))
    proj = jnp.dot(h_ref[...], wq_ref[...], preferred_element_type=jnp.float32)
    scale = scale_ref[...]
    normed = []
    for h in range(heads):
        cols = slice(h * head_size, (h + 1) * head_size)
        part_q = proj[:, cols]
        mean_sq = jnp.mean(part_q * part_q, axis=1, keepdims=True)
        normed.append(part_q * lax.rsqrt(mean_sq + 1e-06) * scale[:, cols])
    qt_ref[...] = jnp.concatenate(normed, axis=1).T.astype(qt_ref.dtype)
    wvt_ref[...] = wv_ref[...].astype(jnp.float32).T.astype(wvt_ref.dtype)
    for st in range(2):
        a0, b0 = own[st]
        for k in range(side):
            recv((st, 4, 1, k), part(st, a0 + k, b0 - 2, 0), slot(st, a0, b0 - 1))
            recv((st, 4, -1, k), part(st, a0 + k, b0 + 2, q), slot(st, a0, b0 + 1))
    local.wait()
    for copy in sends:
        copy.wait_send()


def gather_rows(block, qkv_weight, scale_row, heads, head_size, axis):
    n = lax.axis_size(axis)
    side = math.isqrt(n)
    rows, width = block.shape
    channels, width_qkv = qkv_weight.shape
    width_all = width_qkv // 3
    copies = 2 * (2 + 2 + 4 * side)
    whole = lambda i: (0, 0)
    out, qt, wvt = pl.pallas_call(
        functools.partial(ring_gather_kernel, side, heads, head_size),
        grid=(1,),
        in_specs=[
            pl.BlockSpec(memory_space=pl.ANY),
            pl.BlockSpec((rows, width), whole),
            pl.BlockSpec((channels, width_all), lambda i: (0, 0)),
            pl.BlockSpec((channels, width_all), lambda i: (0, 2)),
            pl.BlockSpec((1, width_all), whole),
        ],
        out_specs=[
            pl.BlockSpec(memory_space=pl.ANY),
            pl.BlockSpec((width_all, rows), whole),
            pl.BlockSpec((width_all, channels), whole),
        ],
        out_shape=[
            jax.ShapeDtypeStruct((n, 2, rows // 2, width), block.dtype),
            jax.ShapeDtypeStruct((width_all, rows), jnp.bfloat16),
            jax.ShapeDtypeStruct((width_all, channels), jnp.bfloat16),
        ],
        scratch_shapes=[
            pltpu.SemaphoreType.DMA((copies,)),
            pltpu.SemaphoreType.DMA((copies,)),
            pltpu.SemaphoreType.DMA,
        ],
        compiler_params=pltpu.CompilerParams(collective_id=0, has_side_effects=True),
    )(block.reshape(2, rows // 2, width), block, qkv_weight, qkv_weight, scale_row)
    return out.reshape(n * rows, width), qt, wvt


def body(sequence_input, conv_first, conv_second, qkv_weight, out_weight, logit_scale):
    row_count = sequence_input.shape[0]
    padded_input = padded_2(sequence_input, 2)
    first_out = jax.nn.gelu(convolve(padded_input, conv_first, row_count)).astype(jnp.bfloat16)
    padded_first = padded_2(first_out, 2)
    second = convolve(padded_first, conv_second, row_count)
    hidden = (first_out.astype(jnp.float32) + second).astype(jnp.bfloat16)
    head_count = logit_scale.shape[0]
    width_all = qkv_weight.shape[1] // 3
    head_size = width_all // head_count
    scale_row = jnp.repeat(logit_scale / math.sqrt(head_size), head_size)[None, :]

    swap = [(0, 1), (1, 0)]
    hidden_all, qt_own, wvt = gather_rows(hidden, qkv_weight, scale_row, head_count, head_size, "zx")
    qt_other = lax.ppermute(qt_own, "core", swap)
    o_part, st_part, o_send, st_send = attend_partial(
        qt_own, qt_other, hidden_all, qkv_weight, wvt, head_count, head_size
    )
    o_got, st_got = lax.ppermute((o_send, st_send), "core", swap)
    return finish(o_part, st_part, o_got, st_got, hidden, out_weight, head_count, head_size)


def solution(mesh):
    devices = np.asarray(mesh.devices)
    seq_size = mesh.shape["seq"]
    batch_size = mesh.shape["batch"]
    order = [mesh.axis_names.index("seq"), mesh.axis_names.index("batch")]
    devices = devices.transpose(order).reshape(seq_size // 2, 2, batch_size)
    split_mesh = Mesh(devices, ("zx", "core", "batch"))
    rows = P(("batch", "zx", "core"), None)
    in_specs = (rows, P(), P(), P(), P(), P())
    return jax.shard_map(body, mesh=split_mesh, in_specs=in_specs, out_specs=rows, check_vma=False)
```

```python
import functools
import math

import jax
import jax.numpy as jnp
import numpy as np
from jax import lax
from jax.experimental import pallas as pl
from jax.experimental.pallas import tpu as pltpu
from jax.sharding import Mesh
from jax.sharding import PartitionSpec as P

SEQ_AXES = ("zx", "core")


def padded_2(block, width):
    count = lax.axis_size(SEQ_AXES)
    forward = [(i, i + 1) for i in range(count - 1)]
    backward = [(target, source) for source, target in forward]
    low = lax.ppermute(lax.slice_in_dim(block, block.shape[0] - width, None, axis=0), SEQ_AXES, forward)
    high = lax.ppermute(lax.slice_in_dim(block, 0, width, axis=0), SEQ_AXES, backward)
    return jnp.concatenate([low, block, high], axis=0)


def convolve(padded, weight, row_count):
    conv_sum = jnp.dot(padded[0:row_count], weight[0], preferred_element_type=jnp.float32)
    for offset in range(1, weight.shape[0]):
        conv_sum = conv_sum + jnp.dot(
            padded[offset : offset + row_count], weight[offset], preferred_element_type=jnp.float32
        )
    return conv_sum


def head_rms(tensor):
    return tensor * lax.rsqrt(jnp.mean(tensor * tensor, axis=-1, keepdims=True) + 1e-06)


def head_norm(block, heads, head_size):
    parts = []
    for h in range(heads):
        part = block[:, h * head_size : (h + 1) * head_size]
        mean_sq = jnp.mean(part * part, axis=1, keepdims=True)
        parts.append(part * lax.rsqrt(mean_sq + 1e-06))
    return parts


def attend_kernel(heads, head_size, nk, qa_ref, qb_ref, hkv_ref, wk_ref, wvt_ref,
                  o_ref, st_ref, ob_ref, sb_ref, qt_sc, m_sc, l_sc, acc_sc):
    j = pl.program_id(0)
    contract_last = (((1,), (1,)), ((), ()))

    @pl.when(j == 0)
    def _():
        own = qa_ref.shape[1]
        qt_sc[:, :own] = qa_ref[...]
        qt_sc[:, own:] = qb_ref[...]
        m_sc[...] = jnp.full(m_sc.shape, -jnp.inf, jnp.float32)
        l_sc[...] = jnp.zeros(l_sc.shape, jnp.float32)
        acc_sc[...] = jnp.zeros(acc_sc.shape, jnp.float32)

    hkv = hkv_ref[...]
    k_all = jnp.dot(hkv, wk_ref[...], preferred_element_type=jnp.float32)
    v_t = lax.dot_general(wvt_ref[...], hkv, contract_last, preferred_element_type=jnp.float32)
    for h in range(heads):
        rows = slice(h * head_size, (h + 1) * head_size)
        k_h = k_all[:, rows]
        k_h = (k_h * lax.rsqrt(jnp.mean(k_h * k_h, axis=1, keepdims=True) + 1e-06)).astype(
            jnp.bfloat16
        )
        s_t = jnp.dot(k_h, qt_sc[rows, :], preferred_element_type=jnp.float32)
        m_prev = m_sc[h]
        m_next = jnp.maximum(m_prev, jnp.max(s_t, axis=0, keepdims=True))
        alpha = jnp.exp(m_prev - m_next)
        p_t = jnp.exp(s_t - m_next)
        l_sc[h] = alpha * l_sc[h] + jnp.sum(p_t, axis=0, keepdims=True)
        acc_sc[rows, :] = alpha * acc_sc[rows, :] + jnp.dot(
            v_t[rows, :].astype(jnp.bfloat16), p_t.astype(jnp.bfloat16),
            preferred_element_type=jnp.float32,
        )
        m_sc[h] = m_next

    @pl.when(j == nk - 1)
    def _():
        own = o_ref.shape[1]
        o_ref[...] = acc_sc[:, :own]
        ob_ref[...] = acc_sc[:, own:]
        for h in range(heads):
            st_ref[h : h + 1, :] = m_sc[h][:, :own]
            st_ref[heads + h : heads + h + 1, :] = l_sc[h][:, :own]
            sb_ref[h : h + 1, :] = m_sc[h][:, own:]
            sb_ref[heads + h : heads + h + 1, :] = l_sc[h][:, own:]


def attend_partial(qt_own, qt_other, hidden_kv, qkv_weight, wvt, heads, head_size, tk=1024):
    width, own = qt_own.shape
    q_rows = 2 * own
    k_rows, channels = hidden_kv.shape
    nk = k_rows // tk
    whole = lambda j: (0, 0)
    return pl.pallas_call(
        functools.partial(attend_kernel, heads, head_size, nk),
        grid=(nk,),
        in_specs=[
            pl.BlockSpec((width, own), whole),
            pl.BlockSpec((width, own), whole),
            pl.BlockSpec((tk, channels), lambda j: (j, 0)),
            pl.BlockSpec((channels, width), lambda j: (0, 1)),
            pl.BlockSpec((width, channels), whole),
        ],
        out_specs=[
            pl.BlockSpec((width, own), whole),
            pl.BlockSpec((2 * heads, own), whole),
        ] * 2,
        out_shape=[
            jax.ShapeDtypeStruct((width, own), jnp.float32),
            jax.ShapeDtypeStruct((2 * heads, own), jnp.float32),
        ] * 2,
        scratch_shapes=[
            pltpu.VMEM((width, q_rows), jnp.bfloat16),
            pltpu.VMEM((heads, 1, q_rows), jnp.float32),
            pltpu.VMEM((heads, 1, q_rows), jnp.float32),
            pltpu.VMEM((width, q_rows), jnp.float32),
        ],
        compiler_params=pltpu.CompilerParams(dimension_semantics=("arbitrary",)),
        cost_estimate=pl.CostEstimate(
            flops=4 * q_rows * k_rows * width + 2 * k_rows * channels * 2 * width,
            transcendentals=q_rows * k_rows * heads,
            bytes_accessed=k_rows * channels * 2 + q_rows * width * 8,
        ),
    )(qt_own, qt_other, hidden_kv, qkv_weight, wvt)


def finish_kernel(heads, head_size, o_ref, st_ref, og_ref, sg_ref, hid_ref, wo_ref, out_ref):
    st_own = st_ref[...]
    st_got = sg_ref[...]
    mixed = []
    for h in range(heads):
        rows = slice(h * head_size, (h + 1) * head_size)
        m_own = st_own[h : h + 1, :]
        m_got = st_got[h : h + 1, :]
        m_all = jnp.maximum(m_own, m_got)
        w_own = jnp.exp(m_own - m_all)
        w_got = jnp.exp(m_got - m_all)
        denom = st_own[heads + h : heads + h + 1, :] * w_own + st_got[heads + h : heads + h + 1, :] * w_got
        mixed.append((o_ref[rows, :] * w_own + og_ref[rows, :] * w_got) / denom)
    attended = jnp.concatenate(mixed, axis=0).T.astype(jnp.bfloat16)
    out = hid_ref[...].astype(jnp.float32) + jnp.dot(
        attended, wo_ref[...], preferred_element_type=jnp.float32
    )
    out_ref[...] = out.astype(out_ref.dtype)


def finish(o_part, st_part, o_got, st_got, hidden, out_weight, heads, head_size):
    rows, width_out = hidden.shape
    width = heads * head_size
    whole = lambda i: (0, 0)
    return pl.pallas_call(
        functools.partial(finish_kernel, heads, head_size),
        grid=(1,),
        in_specs=[
            pl.BlockSpec((width, rows), whole),
            pl.BlockSpec((2 * heads, rows), whole),
            pl.BlockSpec((width, rows), whole),
            pl.BlockSpec((2 * heads, rows), whole),
            pl.BlockSpec((rows, width_out), whole),
            pl.BlockSpec((width, width_out), whole),
        ],
        out_specs=pl.BlockSpec((rows, width_out), whole),
        out_shape=jax.ShapeDtypeStruct((rows, width_out), jnp.bfloat16),
    )(o_part, st_part, o_got, st_got, hidden, out_weight)


def ring_gather_kernel(side, heads, head_size, x_ref, h_ref, wq_ref, wv_ref, scale_ref,
                       out_ref, qt_ref, wvt_ref, send_sem, recv_sem, local_sem):
    me = lax.axis_index("zx")
    z, x = me // side, me % side
    half = x_ref.shape[1]
    q = half // 2
    mesh_ids = pl.DeviceIdType.MESH

    def slot(stream, a, b):
        a = lax.rem(a + side, side)
        b = lax.rem(b + side, side)
        return b * side + a if stream == 0 else a * side + b

    own = [(x, z), (z, x)]
    barrier = pltpu.get_barrier_semaphore()
    for target in (slot(0, x + 1, z), slot(0, x - 1, z), slot(1, z + 1, x), slot(1, z - 1, x)):
        pl.semaphore_signal(barrier, inc=1, device_id={"zx": target}, device_id_type=mesh_ids)
    pl.semaphore_wait(barrier, 4)
    local = pltpu.make_async_copy(x_ref, out_ref.at[me], local_sem)
    local.start()

    sends = []
    index = {}

    def send(key, src, view, target):
        idx = len(index)
        index[key] = idx
        copy = pltpu.make_async_remote_copy(
            src_ref=src, dst_ref=view, send_sem=send_sem.at[idx], recv_sem=recv_sem.at[idx],
            device_id={"zx": target}, device_id_type=mesh_ids,
        )
        copy.start()
        sends.append(copy)

    def recv(key, view, source):
        idx = index[key]
        pltpu.make_async_remote_copy(
            src_ref=view, dst_ref=view, send_sem=send_sem.at[idx], recv_sem=recv_sem.at[idx],
            device_id={"zx": source}, device_id_type=mesh_ids,
        ).wait_recv()

    def part(stream, a, b, lo=None):
        view = out_ref.at[slot(stream, a, b), stream]
        return view if lo is None else view.at[pl.ds(lo, q)]

    for st in range(2):
        a0, b0 = own[st]
        send((st, 1, 1), x_ref.at[st], part(st, a0, b0), slot(st, a0 + 1, b0))
        send((st, 1, -1), x_ref.at[st], part(st, a0, b0), slot(st, a0 - 1, b0))
    for st in range(2):
        a0, b0 = own[st]
        recv((st, 1, 1), part(st, a0 - 1, b0), slot(st, a0 - 1, b0))
        recv((st, 1, -1), part(st, a0 + 1, b0), slot(st, a0 + 1, b0))
        send((st, 2, 1), part(st, a0 - 1, b0, 0), part(st, a0 - 1, b0, 0), slot(st, a0 + 1, b0))
        send((st, 2, -1), part(st, a0 + 1, b0, q), part(st, a0 + 1, b0, q), slot(st, a0 - 1, b0))
    for st in range(2):
        a0, b0 = own[st]
        recv((st, 2, 1), part(st, a0 - 2, b0, 0), slot(st, a0 - 1, b0))
        recv((st, 2, -1), part(st, a0 + 2, b0, q), slot(st, a0 + 1, b0))
        for k in range(side):
            src = x_ref.at[st] if k == 0 else part(st, a0 + k, b0)
            send((st, 3, 1, k), src, part(st, a0 + k, b0), slot(st, a0, b0 + 1))
            send((st, 3, -1, k), src, part(st, a0 + k, b0), slot(st, a0, b0 - 1))
    for st in range(2):
        a0, b0 = own[st]
        for k in range(side):
            recv((st, 3, 1, k), part(st, a0 + k, b0 - 1), slot(st, a0, b0 - 1))
            recv((st, 3, -1, k), part(st, a0 + k, b0 + 1), slot(st, a0, b0 + 1))
            send((st, 4, 1, k), part(st, a0 + k, b0 - 1, 0), part(st, a0 + k, b0 - 1, 0), slot(st, a0, b0 + 1))
            send((st, 4, -1, k), part(st, a0 + k, b0 + 1, q), part(st, a0 + k, b0 + 1, q), slot(st, a0, b0 - 1))
    proj = jnp.dot(h_ref[...], wq_ref[...], preferred_element_type=jnp.float32)
    scale = scale_ref[...]
    normed = []
    for h in range(heads):
        cols = slice(h * head_size, (h + 1) * head_size)
        part_q = proj[:, cols]
        mean_sq = jnp.mean(part_q * part_q, axis=1, keepdims=True)
        normed.append(part_q * lax.rsqrt(mean_sq + 1e-06) * scale[:, cols])
    qt_ref[...] = jnp.concatenate(normed, axis=1).T.astype(qt_ref.dtype)
    wvt_ref[...] = wv_ref[...].astype(jnp.float32).T.astype(wvt_ref.dtype)
    for st in range(2):
        a0, b0 = own[st]
        for k in range(side):
            recv((st, 4, 1, k), part(st, a0 + k, b0 - 2, 0), slot(st, a0, b0 - 1))
            recv((st, 4, -1, k), part(st, a0 + k, b0 + 2, q), slot(st, a0, b0 + 1))
    local.wait()
    for copy in sends:
        copy.wait_send()


def gather_rows(block, qkv_weight, scale_row, heads, head_size, axis):
    n = lax.axis_size(axis)
    side = math.isqrt(n)
    rows, width = block.shape
    channels, width_qkv = qkv_weight.shape
    width_all = width_qkv // 3
    copies = 2 * (2 + 2 + 4 * side)
    whole = lambda i: (0, 0)
    out, qt, wvt = pl.pallas_call(
        functools.partial(ring_gather_kernel, side, heads, head_size),
        grid=(1,),
        in_specs=[
            pl.BlockSpec(memory_space=pl.ANY),
            pl.BlockSpec((rows, width), whole),
            pl.BlockSpec((channels, width_all), lambda i: (0, 0)),
            pl.BlockSpec((channels, width_all), lambda i: (0, 2)),
            pl.BlockSpec((1, width_all), whole),
        ],
        out_specs=[
            pl.BlockSpec(memory_space=pl.ANY),
            pl.BlockSpec((width_all, rows), whole),
            pl.BlockSpec((width_all, channels), whole),
        ],
        out_shape=[
            jax.ShapeDtypeStruct((n, 2, rows // 2, width), block.dtype),
            jax.ShapeDtypeStruct((width_all, rows), jnp.bfloat16),
            jax.ShapeDtypeStruct((width_all, channels), jnp.bfloat16),
        ],
        scratch_shapes=[
            pltpu.SemaphoreType.DMA((copies,)),
            pltpu.SemaphoreType.DMA((copies,)),
            pltpu.SemaphoreType.DMA,
        ],
        compiler_params=pltpu.CompilerParams(collective_id=0, has_side_effects=True),
    )(block.reshape(2, rows // 2, width), block, qkv_weight, qkv_weight, scale_row)
    return out.reshape(n * rows, width), qt, wvt


def body(sequence_input, conv_first, conv_second, qkv_weight, out_weight, logit_scale):
    row_count = sequence_input.shape[0]
    padded_input = padded_2(sequence_input, 2)
    first_out = jax.nn.gelu(convolve(padded_input, conv_first, row_count)).astype(jnp.bfloat16)
    padded_first = padded_2(first_out, 2)
    second = convolve(padded_first, conv_second, row_count)
    hidden = (first_out.astype(jnp.float32) + second).astype(jnp.bfloat16)
    head_count = logit_scale.shape[0]
    width_all = qkv_weight.shape[1] // 3
    head_size = width_all // head_count
    scale_row = jnp.repeat(logit_scale / math.sqrt(head_size), head_size)[None, :]

    swap = [(0, 1), (1, 0)]
    hidden_all, qt_own, wvt = gather_rows(hidden, qkv_weight, scale_row, head_count, head_size, "zx")
    qt_other = lax.ppermute(qt_own, "core", swap)
    o_part, st_part, o_send, st_send = attend_partial(
        qt_own, qt_other, hidden_all, qkv_weight, wvt, head_count, head_size
    )
    o_got, st_got = lax.ppermute((o_send, st_send), "core", swap)
    return finish(o_part, st_part, o_got, st_got, hidden, out_weight, head_count, head_size)


def solution(mesh):
    devices = np.asarray(mesh.devices)
    seq_size = mesh.shape["seq"]
    batch_size = mesh.shape["batch"]
    order = [mesh.axis_names.index("seq"), mesh.axis_names.index("batch")]
    devices = devices.transpose(order).reshape(seq_size // 2, 2, batch_size)
    split_mesh = Mesh(devices, ("zx", "core", "batch"))
    rows = P(("batch", "zx", "core"), None)
    in_specs = (rows, P(), P(), P(), P(), P())
    return jax.shard_map(body, mesh=split_mesh, in_specs=in_specs, out_specs=rows, check_vma=False)
```

```python
import functools
import math

import jax
import jax.numpy as jnp
import numpy as np
from jax import lax
from jax.experimental import pallas as pl
from jax.experimental.pallas import tpu as pltpu
from jax.sharding import Mesh
from jax.sharding import PartitionSpec as P

SEQ_AXES = ("zx", "core")


def padded_2(block, width, align=1):
    count = lax.axis_size(SEQ_AXES)
    forward = [(i, i + 1) for i in range(count - 1)]
    backward = [(target, source) for source, target in forward]
    low = lax.ppermute(lax.slice_in_dim(block, block.shape[0] - width, None, axis=0), SEQ_AXES, forward)
    high = lax.ppermute(lax.slice_in_dim(block, 0, width, axis=0), SEQ_AXES, backward)
    extra = (-(block.shape[0] + 2 * width)) % align
    fill = jnp.zeros((extra, block.shape[1]), block.dtype)
    return jnp.concatenate([low, block, high, fill], axis=0)


def convolve(padded, weight, row_count):
    conv_sum = jnp.dot(padded[0:row_count], weight[0], preferred_element_type=jnp.float32)
    for offset in range(1, weight.shape[0]):
        conv_sum = conv_sum + jnp.dot(
            padded[offset : offset + row_count], weight[offset], preferred_element_type=jnp.float32
        )
    return conv_sum


def head_rms(tensor):
    return tensor * lax.rsqrt(jnp.mean(tensor * tensor, axis=-1, keepdims=True) + 1e-06)


def head_norm(block, heads, head_size):
    parts = []
    for h in range(heads):
        part = block[:, h * head_size : (h + 1) * head_size]
        mean_sq = jnp.mean(part * part, axis=1, keepdims=True)
        parts.append(part * lax.rsqrt(mean_sq + 1e-06))
    return parts


def attend_kernel(heads, head_size, nk, qa_ref, qb_ref, hkv_ref, wk_ref, wvt_ref,
                  o_ref, st_ref, ob_ref, sb_ref, qt_sc, m_sc, l_sc, acc_sc):
    j = pl.program_id(0)
    contract_last = (((1,), (1,)), ((), ()))

    @pl.when(j == 0)
    def _():
        own = qa_ref.shape[1]
        qt_sc[:, :own] = qa_ref[...]
        qt_sc[:, own:] = qb_ref[...]
        m_sc[...] = jnp.full(m_sc.shape, -jnp.inf, jnp.float32)
        l_sc[...] = jnp.zeros(l_sc.shape, jnp.float32)
        acc_sc[...] = jnp.zeros(acc_sc.shape, jnp.float32)

    hkv = hkv_ref[...]
    k_all = jnp.dot(hkv, wk_ref[...], preferred_element_type=jnp.float32)
    v_t = lax.dot_general(wvt_ref[...], hkv, contract_last, preferred_element_type=jnp.float32)
    for h in range(heads):
        rows = slice(h * head_size, (h + 1) * head_size)
        k_h = k_all[:, rows]
        k_h = (k_h * lax.rsqrt(jnp.mean(k_h * k_h, axis=1, keepdims=True) + 1e-06)).astype(
            jnp.bfloat16
        )
        s_t = jnp.dot(k_h, qt_sc[rows, :], preferred_element_type=jnp.float32)
        m_prev = m_sc[h]
        m_next = jnp.maximum(m_prev, jnp.max(s_t, axis=0, keepdims=True))
        alpha = jnp.exp(m_prev - m_next)
        p_t = jnp.exp(s_t - m_next)
        l_sc[h] = alpha * l_sc[h] + jnp.sum(p_t, axis=0, keepdims=True)
        acc_sc[rows, :] = alpha * acc_sc[rows, :] + jnp.dot(
            v_t[rows, :].astype(jnp.bfloat16), p_t.astype(jnp.bfloat16),
            preferred_element_type=jnp.float32,
        )
        m_sc[h] = m_next

    @pl.when(j == nk - 1)
    def _():
        own = o_ref.shape[1]
        o_ref[...] = acc_sc[:, :own]
        ob_ref[...] = acc_sc[:, own:]
        for h in range(heads):
            st_ref[h : h + 1, :] = m_sc[h][:, :own]
            st_ref[heads + h : heads + h + 1, :] = l_sc[h][:, :own]
            sb_ref[h : h + 1, :] = m_sc[h][:, own:]
            sb_ref[heads + h : heads + h + 1, :] = l_sc[h][:, own:]


def attend_partial(qt_own, qt_other, hidden_kv, qkv_weight, wvt, heads, head_size, tk=1024):
    width, own = qt_own.shape
    q_rows = 2 * own
    k_rows, channels = hidden_kv.shape
    nk = k_rows // tk
    whole = lambda j: (0, 0)
    return pl.pallas_call(
        functools.partial(attend_kernel, heads, head_size, nk),
        grid=(nk,),
        in_specs=[
            pl.BlockSpec((width, own), whole),
            pl.BlockSpec((width, own), whole),
            pl.BlockSpec((tk, channels), lambda j: (j, 0)),
            pl.BlockSpec((channels, width), lambda j: (0, 1)),
            pl.BlockSpec((width, channels), whole),
        ],
        out_specs=[
            pl.BlockSpec((width, own), whole),
            pl.BlockSpec((2 * heads, own), whole),
        ] * 2,
        out_shape=[
            jax.ShapeDtypeStruct((width, own), jnp.float32),
            jax.ShapeDtypeStruct((2 * heads, own), jnp.float32),
        ] * 2,
        scratch_shapes=[
            pltpu.VMEM((width, q_rows), jnp.bfloat16),
            pltpu.VMEM((heads, 1, q_rows), jnp.float32),
            pltpu.VMEM((heads, 1, q_rows), jnp.float32),
            pltpu.VMEM((width, q_rows), jnp.float32),
        ],
        compiler_params=pltpu.CompilerParams(dimension_semantics=("arbitrary",)),
        cost_estimate=pl.CostEstimate(
            flops=4 * q_rows * k_rows * width + 2 * k_rows * channels * 2 * width,
            transcendentals=q_rows * k_rows * heads,
            bytes_accessed=k_rows * channels * 2 + q_rows * width * 8,
        ),
    )(qt_own, qt_other, hidden_kv, qkv_weight, wvt)


def finish_kernel(heads, head_size, o_ref, st_ref, og_ref, sg_ref, hid_ref, wo_ref, out_ref):
    st_own = st_ref[...]
    st_got = sg_ref[...]
    mixed = []
    for h in range(heads):
        rows = slice(h * head_size, (h + 1) * head_size)
        m_own = st_own[h : h + 1, :]
        m_got = st_got[h : h + 1, :]
        m_all = jnp.maximum(m_own, m_got)
        w_own = jnp.exp(m_own - m_all)
        w_got = jnp.exp(m_got - m_all)
        denom = st_own[heads + h : heads + h + 1, :] * w_own + st_got[heads + h : heads + h + 1, :] * w_got
        mixed.append((o_ref[rows, :] * w_own + og_ref[rows, :] * w_got) / denom)
    attended = jnp.concatenate(mixed, axis=0).T.astype(jnp.bfloat16)
    out = hid_ref[...].astype(jnp.float32) + jnp.dot(
        attended, wo_ref[...], preferred_element_type=jnp.float32
    )
    out_ref[...] = out.astype(out_ref.dtype)


def finish(o_part, st_part, o_got, st_got, hidden, out_weight, heads, head_size):
    rows, width_out = hidden.shape
    width = heads * head_size
    whole = lambda i: (0, 0)
    return pl.pallas_call(
        functools.partial(finish_kernel, heads, head_size),
        grid=(1,),
        in_specs=[
            pl.BlockSpec((width, rows), whole),
            pl.BlockSpec((2 * heads, rows), whole),
            pl.BlockSpec((width, rows), whole),
            pl.BlockSpec((2 * heads, rows), whole),
            pl.BlockSpec((rows, width_out), whole),
            pl.BlockSpec((width, width_out), whole),
        ],
        out_specs=pl.BlockSpec((rows, width_out), whole),
        out_shape=jax.ShapeDtypeStruct((rows, width_out), jnp.bfloat16),
    )(o_part, st_part, o_got, st_got, hidden, out_weight)


def ring_gather_kernel(side, heads, head_size, x_ref, h_ref, wq_ref, wv_ref, scale_ref,
                       out_ref, qt_ref, wvt_ref, send_sem, recv_sem, local_sem):
    me = lax.axis_index("zx")
    z, x = me // side, me % side
    half = x_ref.shape[1]
    q = half // 2
    mesh_ids = pl.DeviceIdType.MESH

    def slot(stream, a, b):
        a = lax.rem(a + side, side)
        b = lax.rem(b + side, side)
        return b * side + a if stream == 0 else a * side + b

    own = [(x, z), (z, x)]
    barrier = pltpu.get_barrier_semaphore()
    for target in (slot(0, x + 1, z), slot(0, x - 1, z), slot(1, z + 1, x), slot(1, z - 1, x)):
        pl.semaphore_signal(barrier, inc=1, device_id={"zx": target}, device_id_type=mesh_ids)
    pl.semaphore_wait(barrier, 4)
    local = pltpu.make_async_copy(x_ref, out_ref.at[me], local_sem)
    local.start()

    sends = []
    index = {}

    def send(key, src, view, target):
        idx = len(index)
        index[key] = idx
        copy = pltpu.make_async_remote_copy(
            src_ref=src, dst_ref=view, send_sem=send_sem.at[idx], recv_sem=recv_sem.at[idx],
            device_id={"zx": target}, device_id_type=mesh_ids,
        )
        copy.start()
        sends.append(copy)

    def recv(key, view, source):
        idx = index[key]
        pltpu.make_async_remote_copy(
            src_ref=view, dst_ref=view, send_sem=send_sem.at[idx], recv_sem=recv_sem.at[idx],
            device_id={"zx": source}, device_id_type=mesh_ids,
        ).wait_recv()

    def part(stream, a, b, lo=None):
        view = out_ref.at[slot(stream, a, b), stream]
        return view if lo is None else view.at[pl.ds(lo, q)]

    for st in range(2):
        a0, b0 = own[st]
        send((st, 1, 1), x_ref.at[st], part(st, a0, b0), slot(st, a0 + 1, b0))
        send((st, 1, -1), x_ref.at[st], part(st, a0, b0), slot(st, a0 - 1, b0))
    for st in range(2):
        a0, b0 = own[st]
        recv((st, 1, 1), part(st, a0 - 1, b0), slot(st, a0 - 1, b0))
        recv((st, 1, -1), part(st, a0 + 1, b0), slot(st, a0 + 1, b0))
        send((st, 2, 1), part(st, a0 - 1, b0, 0), part(st, a0 - 1, b0, 0), slot(st, a0 + 1, b0))
        send((st, 2, -1), part(st, a0 + 1, b0, q), part(st, a0 + 1, b0, q), slot(st, a0 - 1, b0))
    for st in range(2):
        a0, b0 = own[st]
        recv((st, 2, 1), part(st, a0 - 2, b0, 0), slot(st, a0 - 1, b0))
        recv((st, 2, -1), part(st, a0 + 2, b0, q), slot(st, a0 + 1, b0))
        for k in range(side):
            src = x_ref.at[st] if k == 0 else part(st, a0 + k, b0)
            send((st, 3, 1, k), src, part(st, a0 + k, b0), slot(st, a0, b0 + 1))
            send((st, 3, -1, k), src, part(st, a0 + k, b0), slot(st, a0, b0 - 1))
    for st in range(2):
        a0, b0 = own[st]
        for k in range(side):
            recv((st, 3, 1, k), part(st, a0 + k, b0 - 1), slot(st, a0, b0 - 1))
            recv((st, 3, -1, k), part(st, a0 + k, b0 + 1), slot(st, a0, b0 + 1))
            send((st, 4, 1, k), part(st, a0 + k, b0 - 1, 0), part(st, a0 + k, b0 - 1, 0), slot(st, a0, b0 + 1))
            send((st, 4, -1, k), part(st, a0 + k, b0 + 1, q), part(st, a0 + k, b0 + 1, q), slot(st, a0, b0 - 1))
    proj = jnp.dot(h_ref[...], wq_ref[...], preferred_element_type=jnp.float32)
    scale = scale_ref[...]
    normed = []
    for h in range(heads):
        cols = slice(h * head_size, (h + 1) * head_size)
        part_q = proj[:, cols]
        mean_sq = jnp.mean(part_q * part_q, axis=1, keepdims=True)
        normed.append(part_q * lax.rsqrt(mean_sq + 1e-06) * scale[:, cols])
    qt_ref[...] = jnp.concatenate(normed, axis=1).T.astype(qt_ref.dtype)
    wvt_ref[...] = wv_ref[...].astype(jnp.float32).T.astype(wvt_ref.dtype)
    for st in range(2):
        a0, b0 = own[st]
        for k in range(side):
            recv((st, 4, 1, k), part(st, a0 + k, b0 - 2, 0), slot(st, a0, b0 - 1))
            recv((st, 4, -1, k), part(st, a0 + k, b0 + 2, q), slot(st, a0, b0 + 1))
    local.wait()
    for copy in sends:
        copy.wait_send()


def gather_rows(block, qkv_weight, scale_row, heads, head_size, axis):
    n = lax.axis_size(axis)
    side = math.isqrt(n)
    rows, width = block.shape
    channels, width_qkv = qkv_weight.shape
    width_all = width_qkv // 3
    copies = 2 * (2 + 2 + 4 * side)
    whole = lambda i: (0, 0)
    out, qt, wvt = pl.pallas_call(
        functools.partial(ring_gather_kernel, side, heads, head_size),
        grid=(1,),
        in_specs=[
            pl.BlockSpec(memory_space=pl.ANY),
            pl.BlockSpec((rows, width), whole),
            pl.BlockSpec((channels, width_all), lambda i: (0, 0)),
            pl.BlockSpec((channels, width_all), lambda i: (0, 2)),
            pl.BlockSpec((1, width_all), whole),
        ],
        out_specs=[
            pl.BlockSpec(memory_space=pl.ANY),
            pl.BlockSpec((width_all, rows), whole),
            pl.BlockSpec((width_all, channels), whole),
        ],
        out_shape=[
            jax.ShapeDtypeStruct((n, 2, rows // 2, width), block.dtype),
            jax.ShapeDtypeStruct((width_all, rows), jnp.bfloat16),
            jax.ShapeDtypeStruct((width_all, channels), jnp.bfloat16),
        ],
        scratch_shapes=[
            pltpu.SemaphoreType.DMA((copies,)),
            pltpu.SemaphoreType.DMA((copies,)),
            pltpu.SemaphoreType.DMA,
        ],
        compiler_params=pltpu.CompilerParams(collective_id=0, has_side_effects=True),
    )(block.reshape(2, rows // 2, width), block, qkv_weight, qkv_weight, scale_row)
    return out.reshape(n * rows, width), qt, wvt


def conv_gelu_kernel(taps, rows, x_ref, w_ref, o_ref, acc_sc):
    j = pl.program_id(0)
    product = jnp.dot(x_ref[...], w_ref[...], preferred_element_type=jnp.float32)
    for t in range(taps):

        @pl.when(j == t)
        def _():
            if t == 0:
                acc_sc[...] = product[t : t + rows]
            else:
                acc_sc[...] = acc_sc[...] + product[t : t + rows]

    @pl.when(j == taps - 1)
    def _():
        o_ref[...] = jax.nn.gelu(acc_sc[...]).astype(o_ref.dtype)


def conv_gelu(padded, weight, rows):
    taps, channels, width = weight.shape
    whole = lambda j: (0, 0)
    return pl.pallas_call(
        functools.partial(conv_gelu_kernel, taps, rows),
        grid=(taps,),
        in_specs=[
            pl.BlockSpec(padded.shape, whole),
            pl.BlockSpec((None, channels, width), lambda j: (j, 0, 0)),
        ],
        out_specs=pl.BlockSpec((rows, width), whole),
        out_shape=jax.ShapeDtypeStruct((rows, width), jnp.bfloat16),
        scratch_shapes=[pltpu.VMEM((rows, width), jnp.float32)],
        compiler_params=pltpu.CompilerParams(
            dimension_semantics=("arbitrary",), vmem_limit_bytes=24 * 1024 * 1024
        ),
        cost_estimate=pl.CostEstimate(
            flops=2 * taps * padded.shape[0] * channels * width,
            transcendentals=rows * width,
            bytes_accessed=taps * channels * width * 2 + padded.size * 2 + rows * width * 2,
        ),
    )(padded, weight)


def body(sequence_input, conv_first, conv_second, qkv_weight, out_weight, logit_scale):
    row_count = sequence_input.shape[0]
    padded_input = padded_2(sequence_input, 2, align=8)
    first_out = conv_gelu(padded_input, conv_first, row_count)
    padded_first = padded_2(first_out, 2)
    second = convolve(padded_first, conv_second, row_count)
    hidden = (first_out.astype(jnp.float32) + second).astype(jnp.bfloat16)
    head_count = logit_scale.shape[0]
    width_all = qkv_weight.shape[1] // 3
    head_size = width_all // head_count
    scale_row = jnp.repeat(logit_scale / math.sqrt(head_size), head_size)[None, :]

    swap = [(0, 1), (1, 0)]
    hidden_all, qt_own, wvt = gather_rows(hidden, qkv_weight, scale_row, head_count, head_size, "zx")
    qt_other = lax.ppermute(qt_own, "core", swap)
    o_part, st_part, o_send, st_send = attend_partial(
        qt_own, qt_other, hidden_all, qkv_weight, wvt, head_count, head_size
    )
    o_got, st_got = lax.ppermute((o_send, st_send), "core", swap)
    return finish(o_part, st_part, o_got, st_got, hidden, out_weight, head_count, head_size)


def solution(mesh):
    devices = np.asarray(mesh.devices)
    seq_size = mesh.shape["seq"]
    batch_size = mesh.shape["batch"]
    order = [mesh.axis_names.index("seq"), mesh.axis_names.index("batch")]
    devices = devices.transpose(order).reshape(seq_size // 2, 2, batch_size)
    split_mesh = Mesh(devices, ("zx", "core", "batch"))
    rows = P(("batch", "zx", "core"), None)
    in_specs = (rows, P(), P(), P(), P(), P())
    return jax.shard_map(body, mesh=split_mesh, in_specs=in_specs, out_specs=rows, check_vma=False)
```

```python
import functools
import math

import jax
import jax.numpy as jnp
import numpy as np
from jax import lax
from jax.experimental import pallas as pl
from jax.experimental.pallas import tpu as pltpu
from jax.sharding import Mesh
from jax.sharding import PartitionSpec as P

SEQ_AXES = ("zx", "core")


def padded_2(block, width, align=1):
    count = lax.axis_size(SEQ_AXES)
    forward = [(i, i + 1) for i in range(count - 1)]
    backward = [(target, source) for source, target in forward]
    low = lax.ppermute(lax.slice_in_dim(block, block.shape[0] - width, None, axis=0), SEQ_AXES, forward)
    high = lax.ppermute(lax.slice_in_dim(block, 0, width, axis=0), SEQ_AXES, backward)
    extra = (-(block.shape[0] + 2 * width)) % align
    fill = jnp.zeros((extra, block.shape[1]), block.dtype)
    return jnp.concatenate([low, block, high, fill], axis=0)


def convolve(padded, weight, row_count):
    conv_sum = jnp.dot(padded[0:row_count], weight[0], preferred_element_type=jnp.float32)
    for offset in range(1, weight.shape[0]):
        conv_sum = conv_sum + jnp.dot(
            padded[offset : offset + row_count], weight[offset], preferred_element_type=jnp.float32
        )
    return conv_sum


def head_rms(tensor):
    return tensor * lax.rsqrt(jnp.mean(tensor * tensor, axis=-1, keepdims=True) + 1e-06)


def head_norm(block, heads, head_size):
    parts = []
    for h in range(heads):
        part = block[:, h * head_size : (h + 1) * head_size]
        mean_sq = jnp.mean(part * part, axis=1, keepdims=True)
        parts.append(part * lax.rsqrt(mean_sq + 1e-06))
    return parts


def attend_kernel(heads, head_size, nk, qa_ref, qb_ref, hkv_ref, wk_ref, wvt_ref,
                  o_ref, st_ref, ob_ref, sb_ref, qt_sc, m_sc, l_sc, acc_sc):
    j = pl.program_id(0)
    contract_last = (((1,), (1,)), ((), ()))

    @pl.when(j == 0)
    def _():
        own = qa_ref.shape[1]
        qt_sc[:, :own] = qa_ref[...]
        qt_sc[:, own:] = qb_ref[...]
        m_sc[...] = jnp.full(m_sc.shape, -jnp.inf, jnp.float32)
        l_sc[...] = jnp.zeros(l_sc.shape, jnp.float32)
        acc_sc[...] = jnp.zeros(acc_sc.shape, jnp.float32)

    hkv = hkv_ref[...]
    k_all = jnp.dot(hkv, wk_ref[...], preferred_element_type=jnp.float32)
    v_t = lax.dot_general(wvt_ref[...], hkv, contract_last, preferred_element_type=jnp.float32)
    for h in range(heads):
        rows = slice(h * head_size, (h + 1) * head_size)
        k_h = k_all[:, rows]
        k_h = (k_h * lax.rsqrt(jnp.mean(k_h * k_h, axis=1, keepdims=True) + 1e-06)).astype(
            jnp.bfloat16
        )
        s_t = jnp.dot(k_h, qt_sc[rows, :], preferred_element_type=jnp.float32)
        m_prev = m_sc[h]
        m_next = jnp.maximum(m_prev, jnp.max(s_t, axis=0, keepdims=True))
        alpha = jnp.exp(m_prev - m_next)
        p_t = jnp.exp(s_t - m_next)
        l_sc[h] = alpha * l_sc[h] + jnp.sum(p_t, axis=0, keepdims=True)
        acc_sc[rows, :] = alpha * acc_sc[rows, :] + jnp.dot(
            v_t[rows, :].astype(jnp.bfloat16), p_t.astype(jnp.bfloat16),
            preferred_element_type=jnp.float32,
        )
        m_sc[h] = m_next

    @pl.when(j == nk - 1)
    def _():
        own = o_ref.shape[1]
        o_ref[...] = acc_sc[:, :own]
        ob_ref[...] = acc_sc[:, own:]
        for h in range(heads):
            st_ref[h : h + 1, :] = m_sc[h][:, :own]
            st_ref[heads + h : heads + h + 1, :] = l_sc[h][:, :own]
            sb_ref[h : h + 1, :] = m_sc[h][:, own:]
            sb_ref[heads + h : heads + h + 1, :] = l_sc[h][:, own:]


def attend_partial(qt_own, qt_other, hidden_kv, qkv_weight, wvt, heads, head_size, tk=1024):
    width, own = qt_own.shape
    q_rows = 2 * own
    k_rows, channels = hidden_kv.shape
    nk = k_rows // tk
    whole = lambda j: (0, 0)
    return pl.pallas_call(
        functools.partial(attend_kernel, heads, head_size, nk),
        grid=(nk,),
        in_specs=[
            pl.BlockSpec((width, own), whole),
            pl.BlockSpec((width, own), whole),
            pl.BlockSpec((tk, channels), lambda j: (j, 0)),
            pl.BlockSpec((channels, width), lambda j: (0, 1)),
            pl.BlockSpec((width, channels), whole),
        ],
        out_specs=[
            pl.BlockSpec((width, own), whole),
            pl.BlockSpec((2 * heads, own), whole),
        ] * 2,
        out_shape=[
            jax.ShapeDtypeStruct((width, own), jnp.float32),
            jax.ShapeDtypeStruct((2 * heads, own), jnp.float32),
        ] * 2,
        scratch_shapes=[
            pltpu.VMEM((width, q_rows), jnp.bfloat16),
            pltpu.VMEM((heads, 1, q_rows), jnp.float32),
            pltpu.VMEM((heads, 1, q_rows), jnp.float32),
            pltpu.VMEM((width, q_rows), jnp.float32),
        ],
        compiler_params=pltpu.CompilerParams(dimension_semantics=("arbitrary",)),
        cost_estimate=pl.CostEstimate(
            flops=4 * q_rows * k_rows * width + 2 * k_rows * channels * 2 * width,
            transcendentals=q_rows * k_rows * heads,
            bytes_accessed=k_rows * channels * 2 + q_rows * width * 8,
        ),
    )(qt_own, qt_other, hidden_kv, qkv_weight, wvt)


def finish_kernel(heads, head_size, o_ref, st_ref, og_ref, sg_ref, hid_ref, wo_ref, out_ref):
    st_own = st_ref[...]
    st_got = sg_ref[...]
    mixed = []
    for h in range(heads):
        rows = slice(h * head_size, (h + 1) * head_size)
        m_own = st_own[h : h + 1, :]
        m_got = st_got[h : h + 1, :]
        m_all = jnp.maximum(m_own, m_got)
        w_own = jnp.exp(m_own - m_all)
        w_got = jnp.exp(m_got - m_all)
        denom = st_own[heads + h : heads + h + 1, :] * w_own + st_got[heads + h : heads + h + 1, :] * w_got
        mixed.append((o_ref[rows, :] * w_own + og_ref[rows, :] * w_got) / denom)
    attended = jnp.concatenate(mixed, axis=0).T.astype(jnp.bfloat16)
    out = hid_ref[...].astype(jnp.float32) + jnp.dot(
        attended, wo_ref[...], preferred_element_type=jnp.float32
    )
    out_ref[...] = out.astype(out_ref.dtype)


def finish(o_part, st_part, o_got, st_got, hidden, out_weight, heads, head_size):
    rows, width_out = hidden.shape
    width = heads * head_size
    whole = lambda i: (0, 0)
    return pl.pallas_call(
        functools.partial(finish_kernel, heads, head_size),
        grid=(1,),
        in_specs=[
            pl.BlockSpec((width, rows), whole),
            pl.BlockSpec((2 * heads, rows), whole),
            pl.BlockSpec((width, rows), whole),
            pl.BlockSpec((2 * heads, rows), whole),
            pl.BlockSpec((rows, width_out), whole),
            pl.BlockSpec((width, width_out), whole),
        ],
        out_specs=pl.BlockSpec((rows, width_out), whole),
        out_shape=jax.ShapeDtypeStruct((rows, width_out), jnp.bfloat16),
    )(o_part, st_part, o_got, st_got, hidden, out_weight)


def ring_gather_kernel(side, heads, head_size, x_ref, h_ref, wq_ref, wv_ref, scale_ref,
                       out_ref, qt_ref, wvt_ref, send_sem, recv_sem, local_sem):
    me = lax.axis_index("zx")
    z, x = me // side, me % side
    half = x_ref.shape[1]
    q = half // 2
    mesh_ids = pl.DeviceIdType.MESH

    def slot(stream, a, b):
        a = lax.rem(a + side, side)
        b = lax.rem(b + side, side)
        return b * side + a if stream == 0 else a * side + b

    own = [(x, z), (z, x)]
    barrier = pltpu.get_barrier_semaphore()
    for target in (slot(0, x + 1, z), slot(0, x - 1, z), slot(1, z + 1, x), slot(1, z - 1, x)):
        pl.semaphore_signal(barrier, inc=1, device_id={"zx": target}, device_id_type=mesh_ids)
    pl.semaphore_wait(barrier, 4)
    local = pltpu.make_async_copy(x_ref, out_ref.at[me], local_sem)
    local.start()

    sends = []
    index = {}

    def send(key, src, view, target):
        idx = len(index)
        index[key] = idx
        copy = pltpu.make_async_remote_copy(
            src_ref=src, dst_ref=view, send_sem=send_sem.at[idx], recv_sem=recv_sem.at[idx],
            device_id={"zx": target}, device_id_type=mesh_ids,
        )
        copy.start()
        sends.append(copy)

    def recv(key, view, source):
        idx = index[key]
        pltpu.make_async_remote_copy(
            src_ref=view, dst_ref=view, send_sem=send_sem.at[idx], recv_sem=recv_sem.at[idx],
            device_id={"zx": source}, device_id_type=mesh_ids,
        ).wait_recv()

    def part(stream, a, b, lo=None):
        view = out_ref.at[slot(stream, a, b), stream]
        return view if lo is None else view.at[pl.ds(lo, q)]

    for st in range(2):
        a0, b0 = own[st]
        send((st, 1, 1), x_ref.at[st], part(st, a0, b0), slot(st, a0 + 1, b0))
        send((st, 1, -1), x_ref.at[st], part(st, a0, b0), slot(st, a0 - 1, b0))
    for st in range(2):
        a0, b0 = own[st]
        recv((st, 1, 1), part(st, a0 - 1, b0), slot(st, a0 - 1, b0))
        recv((st, 1, -1), part(st, a0 + 1, b0), slot(st, a0 + 1, b0))
        send((st, 2, 1), part(st, a0 - 1, b0, 0), part(st, a0 - 1, b0, 0), slot(st, a0 + 1, b0))
        send((st, 2, -1), part(st, a0 + 1, b0, q), part(st, a0 + 1, b0, q), slot(st, a0 - 1, b0))
    for st in range(2):
        a0, b0 = own[st]
        recv((st, 2, 1), part(st, a0 - 2, b0, 0), slot(st, a0 - 1, b0))
        recv((st, 2, -1), part(st, a0 + 2, b0, q), slot(st, a0 + 1, b0))
        for k in range(side):
            src = x_ref.at[st] if k == 0 else part(st, a0 + k, b0)
            send((st, 3, 1, k), src, part(st, a0 + k, b0), slot(st, a0, b0 + 1))
            send((st, 3, -1, k), src, part(st, a0 + k, b0), slot(st, a0, b0 - 1))
    for st in range(2):
        a0, b0 = own[st]
        for k in range(side):
            recv((st, 3, 1, k), part(st, a0 + k, b0 - 1), slot(st, a0, b0 - 1))
            recv((st, 3, -1, k), part(st, a0 + k, b0 + 1), slot(st, a0, b0 + 1))
            send((st, 4, 1, k), part(st, a0 + k, b0 - 1, 0), part(st, a0 + k, b0 - 1, 0), slot(st, a0, b0 + 1))
            send((st, 4, -1, k), part(st, a0 + k, b0 + 1, q), part(st, a0 + k, b0 + 1, q), slot(st, a0, b0 - 1))
    proj = jnp.dot(h_ref[...], wq_ref[...], preferred_element_type=jnp.float32)
    scale = scale_ref[...]
    normed = []
    for h in range(heads):
        cols = slice(h * head_size, (h + 1) * head_size)
        part_q = proj[:, cols]
        mean_sq = jnp.mean(part_q * part_q, axis=1, keepdims=True)
        normed.append(part_q * lax.rsqrt(mean_sq + 1e-06) * scale[:, cols])
    qt_ref[...] = jnp.concatenate(normed, axis=1).T.astype(qt_ref.dtype)
    wvt_ref[...] = wv_ref[...].astype(jnp.float32).T.astype(wvt_ref.dtype)
    for st in range(2):
        a0, b0 = own[st]
        for k in range(side):
            recv((st, 4, 1, k), part(st, a0 + k, b0 - 2, 0), slot(st, a0, b0 - 1))
            recv((st, 4, -1, k), part(st, a0 + k, b0 + 2, q), slot(st, a0, b0 + 1))
    local.wait()
    for copy in sends:
        copy.wait_send()


def gather_rows(block, qkv_weight, scale_row, heads, head_size, axis):
    n = lax.axis_size(axis)
    side = math.isqrt(n)
    rows, width = block.shape
    channels, width_qkv = qkv_weight.shape
    width_all = width_qkv // 3
    copies = 2 * (2 + 2 + 4 * side)
    whole = lambda i: (0, 0)
    out, qt, wvt = pl.pallas_call(
        functools.partial(ring_gather_kernel, side, heads, head_size),
        grid=(1,),
        in_specs=[
            pl.BlockSpec(memory_space=pl.ANY),
            pl.BlockSpec((rows, width), whole),
            pl.BlockSpec((channels, width_all), lambda i: (0, 0)),
            pl.BlockSpec((channels, width_all), lambda i: (0, 2)),
            pl.BlockSpec((1, width_all), whole),
        ],
        out_specs=[
            pl.BlockSpec(memory_space=pl.ANY),
            pl.BlockSpec((width_all, rows), whole),
            pl.BlockSpec((width_all, channels), whole),
        ],
        out_shape=[
            jax.ShapeDtypeStruct((n, 2, rows // 2, width), block.dtype),
            jax.ShapeDtypeStruct((width_all, rows), jnp.bfloat16),
            jax.ShapeDtypeStruct((width_all, channels), jnp.bfloat16),
        ],
        scratch_shapes=[
            pltpu.SemaphoreType.DMA((copies,)),
            pltpu.SemaphoreType.DMA((copies,)),
            pltpu.SemaphoreType.DMA,
        ],
        compiler_params=pltpu.CompilerParams(collective_id=0, has_side_effects=True),
    )(block.reshape(2, rows // 2, width), block, qkv_weight, qkv_weight, scale_row)
    return out.reshape(n * rows, width), qt, wvt


def conv_gelu_kernel(taps, rows, halo, x_ref, w_ref, o_ref, acc_sc):
    j = pl.program_id(0)
    product = jnp.dot(x_ref[...], w_ref[...], preferred_element_type=jnp.float32)
    for t in range(taps):

        @pl.when(j == t)
        def _():
            if t == 0:
                acc_sc[...] = product[t : t + rows]
            else:
                acc_sc[...] = acc_sc[...] + product[t : t + rows]

    @pl.when(j == taps - 1)
    def _():
        place = lax.axis_index(SEQ_AXES)
        last = lax.axis_size(SEQ_AXES) - 1
        row = lax.broadcasted_iota(jnp.int32, acc_sc.shape, 0)
        outside = jnp.logical_or(
            jnp.logical_and(place == 0, row < halo),
            jnp.logical_and(place == last, row >= rows - halo),
        )
        value = jax.nn.gelu(acc_sc[...])
        o_ref[...] = jnp.where(outside, 0.0, value).astype(o_ref.dtype)


def conv_gelu(padded, weight, halo):
    taps, channels, width = weight.shape
    rows = padded.shape[0] - taps + 1
    whole = lambda j: (0, 0)
    return pl.pallas_call(
        functools.partial(conv_gelu_kernel, taps, rows, halo),
        grid=(taps,),
        in_specs=[
            pl.BlockSpec(padded.shape, whole),
            pl.BlockSpec((None, channels, width), lambda j: (j, 0, 0)),
        ],
        out_specs=pl.BlockSpec((rows, width), whole),
        out_shape=jax.ShapeDtypeStruct((rows, width), jnp.bfloat16),
        scratch_shapes=[pltpu.VMEM((rows, width), jnp.float32)],
        compiler_params=pltpu.CompilerParams(
            dimension_semantics=("arbitrary",), vmem_limit_bytes=24 * 1024 * 1024
        ),
        cost_estimate=pl.CostEstimate(
            flops=2 * taps * padded.shape[0] * channels * width,
            transcendentals=rows * width,
            bytes_accessed=taps * channels * width * 2 + padded.size * 2 + rows * width * 2,
        ),
    )(padded, weight)


def body(sequence_input, conv_first, conv_second, qkv_weight, out_weight, logit_scale):
    row_count = sequence_input.shape[0]
    padded_input = padded_2(sequence_input, 4)
    padded_first = conv_gelu(padded_input, conv_first, 2)
    first_out = padded_first[2 : 2 + row_count]
    second = convolve(padded_first, conv_second, row_count)
    hidden = (first_out.astype(jnp.float32) + second).astype(jnp.bfloat16)
    head_count = logit_scale.shape[0]
    width_all = qkv_weight.shape[1] // 3
    head_size = width_all // head_count
    scale_row = jnp.repeat(logit_scale / math.sqrt(head_size), head_size)[None, :]

    swap = [(0, 1), (1, 0)]
    hidden_all, qt_own, wvt = gather_rows(hidden, qkv_weight, scale_row, head_count, head_size, "zx")
    qt_other = lax.ppermute(qt_own, "core", swap)
    o_part, st_part, o_send, st_send = attend_partial(
        qt_own, qt_other, hidden_all, qkv_weight, wvt, head_count, head_size
    )
    o_got, st_got = lax.ppermute((o_send, st_send), "core", swap)
    return finish(o_part, st_part, o_got, st_got, hidden, out_weight, head_count, head_size)


def solution(mesh):
    devices = np.asarray(mesh.devices)
    seq_size = mesh.shape["seq"]
    batch_size = mesh.shape["batch"]
    order = [mesh.axis_names.index("seq"), mesh.axis_names.index("batch")]
    devices = devices.transpose(order).reshape(seq_size // 2, 2, batch_size)
    split_mesh = Mesh(devices, ("zx", "core", "batch"))
    rows = P(("batch", "zx", "core"), None)
    in_specs = (rows, P(), P(), P(), P(), P())
    return jax.shard_map(body, mesh=split_mesh, in_specs=in_specs, out_specs=rows, check_vma=False)
```

```python
import functools
import math

import jax
import jax.numpy as jnp
import numpy as np
from jax import lax
from jax.experimental import pallas as pl
from jax.experimental.pallas import tpu as pltpu
from jax.sharding import Mesh
from jax.sharding import PartitionSpec as P

SEQ_AXES = ("zx", "core")


def padded_2(block, width, align=1):
    count = lax.axis_size(SEQ_AXES)
    forward = [(i, i + 1) for i in range(count - 1)]
    backward = [(target, source) for source, target in forward]
    low = lax.ppermute(lax.slice_in_dim(block, block.shape[0] - width, None, axis=0), SEQ_AXES, forward)
    high = lax.ppermute(lax.slice_in_dim(block, 0, width, axis=0), SEQ_AXES, backward)
    extra = (-(block.shape[0] + 2 * width)) % align
    fill = jnp.zeros((extra, block.shape[1]), block.dtype)
    return jnp.concatenate([low, block, high, fill], axis=0)


def convolve(padded, weight, row_count):
    conv_sum = jnp.dot(padded[0:row_count], weight[0], preferred_element_type=jnp.float32)
    for offset in range(1, weight.shape[0]):
        conv_sum = conv_sum + jnp.dot(
            padded[offset : offset + row_count], weight[offset], preferred_element_type=jnp.float32
        )
    return conv_sum


def head_rms(tensor):
    return tensor * lax.rsqrt(jnp.mean(tensor * tensor, axis=-1, keepdims=True) + 1e-06)


def head_norm(block, heads, head_size):
    parts = []
    for h in range(heads):
        part = block[:, h * head_size : (h + 1) * head_size]
        mean_sq = jnp.mean(part * part, axis=1, keepdims=True)
        parts.append(part * lax.rsqrt(mean_sq + 1e-06))
    return parts


def attend_kernel(heads, head_size, nk, qa_ref, qb_ref, hkv_ref, wk_ref, wvt_ref,
                  o_ref, st_ref, ob_ref, sb_ref, qt_sc, m_sc, l_sc, acc_sc):
    j = pl.program_id(0)
    contract_last = (((1,), (1,)), ((), ()))

    @pl.when(j == 0)
    def _():
        own = qa_ref.shape[1]
        qt_sc[:, :own] = qa_ref[...]
        qt_sc[:, own:] = qb_ref[...]
        m_sc[...] = jnp.full(m_sc.shape, -jnp.inf, jnp.float32)
        l_sc[...] = jnp.zeros(l_sc.shape, jnp.float32)
        acc_sc[...] = jnp.zeros(acc_sc.shape, jnp.float32)

    hkv = hkv_ref[...]
    k_all = jnp.dot(hkv, wk_ref[...], preferred_element_type=jnp.float32)
    v_t = lax.dot_general(wvt_ref[...], hkv, contract_last, preferred_element_type=jnp.float32)
    for h in range(heads):
        rows = slice(h * head_size, (h + 1) * head_size)
        k_h = k_all[:, rows]
        k_h = (k_h * lax.rsqrt(jnp.mean(k_h * k_h, axis=1, keepdims=True) + 1e-06)).astype(
            jnp.bfloat16
        )
        s_t = jnp.dot(k_h, qt_sc[rows, :], preferred_element_type=jnp.float32)
        m_prev = m_sc[h]
        m_next = jnp.maximum(m_prev, jnp.max(s_t, axis=0, keepdims=True))
        alpha = jnp.exp(m_prev - m_next)
        p_t = jnp.exp(s_t - m_next)
        l_sc[h] = alpha * l_sc[h] + jnp.sum(p_t, axis=0, keepdims=True)
        acc_sc[rows, :] = alpha * acc_sc[rows, :] + jnp.dot(
            v_t[rows, :].astype(jnp.bfloat16), p_t.astype(jnp.bfloat16),
            preferred_element_type=jnp.float32,
        )
        m_sc[h] = m_next

    @pl.when(j == nk - 1)
    def _():
        own = o_ref.shape[1]
        o_ref[...] = acc_sc[:, :own]
        ob_ref[...] = acc_sc[:, own:]
        for h in range(heads):
            st_ref[h : h + 1, :] = m_sc[h][:, :own]
            st_ref[heads + h : heads + h + 1, :] = l_sc[h][:, :own]
            sb_ref[h : h + 1, :] = m_sc[h][:, own:]
            sb_ref[heads + h : heads + h + 1, :] = l_sc[h][:, own:]


def attend_partial(qt_own, qt_other, hidden_kv, qkv_weight, wvt, heads, head_size, tk=1024):
    width, own = qt_own.shape
    q_rows = 2 * own
    k_rows, channels = hidden_kv.shape
    nk = k_rows // tk
    whole = lambda j: (0, 0)
    return pl.pallas_call(
        functools.partial(attend_kernel, heads, head_size, nk),
        grid=(nk,),
        in_specs=[
            pl.BlockSpec((width, own), whole),
            pl.BlockSpec((width, own), whole),
            pl.BlockSpec((tk, channels), lambda j: (j, 0)),
            pl.BlockSpec((channels, width), lambda j: (0, 1)),
            pl.BlockSpec((width, channels), whole),
        ],
        out_specs=[
            pl.BlockSpec((width, own), whole),
            pl.BlockSpec((2 * heads, own), whole),
        ] * 2,
        out_shape=[
            jax.ShapeDtypeStruct((width, own), jnp.float32),
            jax.ShapeDtypeStruct((2 * heads, own), jnp.float32),
        ] * 2,
        scratch_shapes=[
            pltpu.VMEM((width, q_rows), jnp.bfloat16),
            pltpu.VMEM((heads, 1, q_rows), jnp.float32),
            pltpu.VMEM((heads, 1, q_rows), jnp.float32),
            pltpu.VMEM((width, q_rows), jnp.float32),
        ],
        compiler_params=pltpu.CompilerParams(dimension_semantics=("arbitrary",)),
        cost_estimate=pl.CostEstimate(
            flops=4 * q_rows * k_rows * width + 2 * k_rows * channels * 2 * width,
            transcendentals=q_rows * k_rows * heads,
            bytes_accessed=k_rows * channels * 2 + q_rows * width * 8,
        ),
    )(qt_own, qt_other, hidden_kv, qkv_weight, wvt)


def finish_kernel(heads, head_size, o_ref, st_ref, og_ref, sg_ref, hid_ref, wo_ref, out_ref):
    st_own = st_ref[...]
    st_got = sg_ref[...]
    mixed = []
    for h in range(heads):
        rows = slice(h * head_size, (h + 1) * head_size)
        m_own = st_own[h : h + 1, :]
        m_got = st_got[h : h + 1, :]
        m_all = jnp.maximum(m_own, m_got)
        w_own = jnp.exp(m_own - m_all)
        w_got = jnp.exp(m_got - m_all)
        denom = st_own[heads + h : heads + h + 1, :] * w_own + st_got[heads + h : heads + h + 1, :] * w_got
        mixed.append((o_ref[rows, :] * w_own + og_ref[rows, :] * w_got) / denom)
    attended = jnp.concatenate(mixed, axis=0).T.astype(jnp.bfloat16)
    out = hid_ref[...].astype(jnp.float32) + jnp.dot(
        attended, wo_ref[...], preferred_element_type=jnp.float32
    )
    out_ref[...] = out.astype(out_ref.dtype)


def finish(o_part, st_part, o_got, st_got, hidden, out_weight, heads, head_size):
    rows, width_out = hidden.shape
    width = heads * head_size
    whole = lambda i: (0, 0)
    return pl.pallas_call(
        functools.partial(finish_kernel, heads, head_size),
        grid=(1,),
        in_specs=[
            pl.BlockSpec((width, rows), whole),
            pl.BlockSpec((2 * heads, rows), whole),
            pl.BlockSpec((width, rows), whole),
            pl.BlockSpec((2 * heads, rows), whole),
            pl.BlockSpec((rows, width_out), whole),
            pl.BlockSpec((width, width_out), whole),
        ],
        out_specs=pl.BlockSpec((rows, width_out), whole),
        out_shape=jax.ShapeDtypeStruct((rows, width_out), jnp.bfloat16),
    )(o_part, st_part, o_got, st_got, hidden, out_weight)


def ring_gather_kernel(side, heads, head_size, x_ref, h_ref, wq_ref, wv_ref, scale_ref,
                       out_ref, qt_ref, wvt_ref, send_sem, recv_sem, local_sem):
    me = lax.axis_index("zx")
    z, x = me // side, me % side
    half = x_ref.shape[1]
    q = half // 2
    mesh_ids = pl.DeviceIdType.MESH

    def slot(stream, a, b):
        a = lax.rem(a + side, side)
        b = lax.rem(b + side, side)
        return b * side + a if stream == 0 else a * side + b

    own = [(x, z), (z, x)]
    barrier = pltpu.get_barrier_semaphore()
    for target in (slot(0, x + 1, z), slot(0, x - 1, z), slot(1, z + 1, x), slot(1, z - 1, x)):
        pl.semaphore_signal(barrier, inc=1, device_id={"zx": target}, device_id_type=mesh_ids)
    pl.semaphore_wait(barrier, 4)
    local = pltpu.make_async_copy(x_ref, out_ref.at[me], local_sem)
    local.start()

    sends = []
    index = {}

    def send(key, src, view, target):
        idx = len(index)
        index[key] = idx
        copy = pltpu.make_async_remote_copy(
            src_ref=src, dst_ref=view, send_sem=send_sem.at[idx], recv_sem=recv_sem.at[idx],
            device_id={"zx": target}, device_id_type=mesh_ids,
        )
        copy.start()
        sends.append(copy)

    def recv(key, view, source):
        idx = index[key]
        pltpu.make_async_remote_copy(
            src_ref=view, dst_ref=view, send_sem=send_sem.at[idx], recv_sem=recv_sem.at[idx],
            device_id={"zx": source}, device_id_type=mesh_ids,
        ).wait_recv()

    def part(stream, a, b, lo=None):
        view = out_ref.at[slot(stream, a, b), stream]
        return view if lo is None else view.at[pl.ds(lo, q)]

    def send_row(st, k):
        a0, b0 = own[st]
        src = x_ref.at[st] if k == 0 else part(st, a0 + k, b0)
        send((st, 3, 1, k), src, part(st, a0 + k, b0), slot(st, a0, b0 + 1))
        send((st, 3, -1, k), src, part(st, a0 + k, b0), slot(st, a0, b0 - 1))

    for st in range(2):
        a0, b0 = own[st]
        send((st, 1, 1), x_ref.at[st], part(st, a0, b0), slot(st, a0 + 1, b0))
        send((st, 1, -1), x_ref.at[st], part(st, a0, b0), slot(st, a0 - 1, b0))
        send_row(st, 0)
    for st in range(2):
        a0, b0 = own[st]
        recv((st, 1, 1), part(st, a0 - 1, b0), slot(st, a0 - 1, b0))
        recv((st, 1, -1), part(st, a0 + 1, b0), slot(st, a0 + 1, b0))
        send((st, 2, 1), part(st, a0 - 1, b0, 0), part(st, a0 - 1, b0, 0), slot(st, a0 + 1, b0))
        send((st, 2, -1), part(st, a0 + 1, b0, q), part(st, a0 + 1, b0, q), slot(st, a0 - 1, b0))
        send_row(st, 1)
        send_row(st, side - 1)
    for st in range(2):
        a0, b0 = own[st]
        recv((st, 2, 1), part(st, a0 - 2, b0, 0), slot(st, a0 - 1, b0))
        recv((st, 2, -1), part(st, a0 + 2, b0, q), slot(st, a0 + 1, b0))
        for k in range(2, side - 1):
            send_row(st, k)
    for st in range(2):
        a0, b0 = own[st]
        for k in range(side):
            recv((st, 3, 1, k), part(st, a0 + k, b0 - 1), slot(st, a0, b0 - 1))
            recv((st, 3, -1, k), part(st, a0 + k, b0 + 1), slot(st, a0, b0 + 1))
            send((st, 4, 1, k), part(st, a0 + k, b0 - 1, 0), part(st, a0 + k, b0 - 1, 0), slot(st, a0, b0 + 1))
            send((st, 4, -1, k), part(st, a0 + k, b0 + 1, q), part(st, a0 + k, b0 + 1, q), slot(st, a0, b0 - 1))
    proj = jnp.dot(h_ref[...], wq_ref[...], preferred_element_type=jnp.float32)
    scale = scale_ref[...]
    normed = []
    for h in range(heads):
        cols = slice(h * head_size, (h + 1) * head_size)
        part_q = proj[:, cols]
        mean_sq = jnp.mean(part_q * part_q, axis=1, keepdims=True)
        normed.append(part_q * lax.rsqrt(mean_sq + 1e-06) * scale[:, cols])
    qt_ref[...] = jnp.concatenate(normed, axis=1).T.astype(qt_ref.dtype)
    wvt_ref[...] = wv_ref[...].astype(jnp.float32).T.astype(wvt_ref.dtype)
    for st in range(2):
        a0, b0 = own[st]
        for k in range(side):
            recv((st, 4, 1, k), part(st, a0 + k, b0 - 2, 0), slot(st, a0, b0 - 1))
            recv((st, 4, -1, k), part(st, a0 + k, b0 + 2, q), slot(st, a0, b0 + 1))
    local.wait()
    for copy in sends:
        copy.wait_send()


def gather_rows(block, qkv_weight, scale_row, heads, head_size, axis):
    n = lax.axis_size(axis)
    side = math.isqrt(n)
    rows, width = block.shape
    channels, width_qkv = qkv_weight.shape
    width_all = width_qkv // 3
    copies = 2 * (2 + 2 + 4 * side)
    whole = lambda i: (0, 0)
    out, qt, wvt = pl.pallas_call(
        functools.partial(ring_gather_kernel, side, heads, head_size),
        grid=(1,),
        in_specs=[
            pl.BlockSpec(memory_space=pl.ANY),
            pl.BlockSpec((rows, width), whole),
            pl.BlockSpec((channels, width_all), lambda i: (0, 0)),
            pl.BlockSpec((channels, width_all), lambda i: (0, 2)),
            pl.BlockSpec((1, width_all), whole),
        ],
        out_specs=[
            pl.BlockSpec(memory_space=pl.ANY),
            pl.BlockSpec((width_all, rows), whole),
            pl.BlockSpec((width_all, channels), whole),
        ],
        out_shape=[
            jax.ShapeDtypeStruct((n, 2, rows // 2, width), block.dtype),
            jax.ShapeDtypeStruct((width_all, rows), jnp.bfloat16),
            jax.ShapeDtypeStruct((width_all, channels), jnp.bfloat16),
        ],
        scratch_shapes=[
            pltpu.SemaphoreType.DMA((copies,)),
            pltpu.SemaphoreType.DMA((copies,)),
            pltpu.SemaphoreType.DMA,
        ],
        compiler_params=pltpu.CompilerParams(collective_id=0, has_side_effects=True),
    )(block.reshape(2, rows // 2, width), block, qkv_weight, qkv_weight, scale_row)
    return out.reshape(n * rows, width), qt, wvt


def conv_gelu_kernel(taps, rows, halo, x_ref, w_ref, o_ref, acc_sc):
    j = pl.program_id(0)
    product = jnp.dot(x_ref[...], w_ref[...], preferred_element_type=jnp.float32)
    for t in range(taps):

        @pl.when(j == t)
        def _():
            if t == 0:
                acc_sc[...] = product[t : t + rows]
            else:
                acc_sc[...] = acc_sc[...] + product[t : t + rows]

    @pl.when(j == taps - 1)
    def _():
        place = lax.axis_index(SEQ_AXES)
        last = lax.axis_size(SEQ_AXES) - 1
        row = lax.broadcasted_iota(jnp.int32, acc_sc.shape, 0)
        outside = jnp.logical_or(
            jnp.logical_and(place == 0, row < halo),
            jnp.logical_and(place == last, row >= rows - halo),
        )
        value = jax.nn.gelu(acc_sc[...])
        o_ref[...] = jnp.where(outside, 0.0, value).astype(o_ref.dtype)


def conv_gelu(padded, weight, halo):
    taps, channels, width = weight.shape
    rows = padded.shape[0] - taps + 1
    whole = lambda j: (0, 0)
    return pl.pallas_call(
        functools.partial(conv_gelu_kernel, taps, rows, halo),
        grid=(taps,),
        in_specs=[
            pl.BlockSpec(padded.shape, whole),
            pl.BlockSpec((None, channels, width), lambda j: (j, 0, 0)),
        ],
        out_specs=pl.BlockSpec((rows, width), whole),
        out_shape=jax.ShapeDtypeStruct((rows, width), jnp.bfloat16),
        scratch_shapes=[pltpu.VMEM((rows, width), jnp.float32)],
        compiler_params=pltpu.CompilerParams(
            dimension_semantics=("arbitrary",), vmem_limit_bytes=24 * 1024 * 1024
        ),
        cost_estimate=pl.CostEstimate(
            flops=2 * taps * padded.shape[0] * channels * width,
            transcendentals=rows * width,
            bytes_accessed=taps * channels * width * 2 + padded.size * 2 + rows * width * 2,
        ),
    )(padded, weight)


def body(sequence_input, conv_first, conv_second, qkv_weight, out_weight, logit_scale):
    row_count = sequence_input.shape[0]
    padded_input = padded_2(sequence_input, 4)
    padded_first = conv_gelu(padded_input, conv_first, 2)
    first_out = padded_first[2 : 2 + row_count]
    second = convolve(padded_first, conv_second, row_count)
    hidden = (first_out.astype(jnp.float32) + second).astype(jnp.bfloat16)
    head_count = logit_scale.shape[0]
    width_all = qkv_weight.shape[1] // 3
    head_size = width_all // head_count
    scale_row = jnp.repeat(logit_scale / math.sqrt(head_size), head_size)[None, :]

    swap = [(0, 1), (1, 0)]
    hidden_all, qt_own, wvt = gather_rows(hidden, qkv_weight, scale_row, head_count, head_size, "zx")
    qt_other = lax.ppermute(qt_own, "core", swap)
    o_part, st_part, o_send, st_send = attend_partial(
        qt_own, qt_other, hidden_all, qkv_weight, wvt, head_count, head_size
    )
    o_got, st_got = lax.ppermute((o_send, st_send), "core", swap)
    return finish(o_part, st_part, o_got, st_got, hidden, out_weight, head_count, head_size)


def solution(mesh):
    devices = np.asarray(mesh.devices)
    seq_size = mesh.shape["seq"]
    batch_size = mesh.shape["batch"]
    order = [mesh.axis_names.index("seq"), mesh.axis_names.index("batch")]
    devices = devices.transpose(order).reshape(seq_size // 2, 2, batch_size)
    split_mesh = Mesh(devices, ("zx", "core", "batch"))
    rows = P(("batch", "zx", "core"), None)
    in_specs = (rows, P(), P(), P(), P(), P())
    return jax.shard_map(body, mesh=split_mesh, in_specs=in_specs, out_specs=rows, check_vma=False)
```

```python
import functools
import math

import jax
import jax.numpy as jnp
import numpy as np
from jax import lax
from jax.experimental import pallas as pl
from jax.experimental.pallas import tpu as pltpu
from jax.sharding import Mesh
from jax.sharding import PartitionSpec as P

SEQ_AXES = ("zx", "core")


def padded_2(block, width, align=1):
    count = lax.axis_size(SEQ_AXES)
    forward = [(i, i + 1) for i in range(count - 1)]
    backward = [(target, source) for source, target in forward]
    low = lax.ppermute(lax.slice_in_dim(block, block.shape[0] - width, None, axis=0), SEQ_AXES, forward)
    high = lax.ppermute(lax.slice_in_dim(block, 0, width, axis=0), SEQ_AXES, backward)
    extra = (-(block.shape[0] + 2 * width)) % align
    fill = jnp.zeros((extra, block.shape[1]), block.dtype)
    return jnp.concatenate([low, block, high, fill], axis=0)


def convolve(padded, weight, row_count):
    conv_sum = jnp.dot(padded[0:row_count], weight[0], preferred_element_type=jnp.float32)
    for offset in range(1, weight.shape[0]):
        conv_sum = conv_sum + jnp.dot(
            padded[offset : offset + row_count], weight[offset], preferred_element_type=jnp.float32
        )
    return conv_sum


def head_rms(tensor):
    return tensor * lax.rsqrt(jnp.mean(tensor * tensor, axis=-1, keepdims=True) + 1e-06)


def head_norm(block, heads, head_size):
    parts = []
    for h in range(heads):
        part = block[:, h * head_size : (h + 1) * head_size]
        mean_sq = jnp.mean(part * part, axis=1, keepdims=True)
        parts.append(part * lax.rsqrt(mean_sq + 1e-06))
    return parts


def attend_kernel(heads, head_size, nk, qa_ref, qb_ref, hkv_ref, wk_ref, wvt_ref,
                  o_ref, st_ref, ob_ref, sb_ref, qt_sc, m_sc, l_sc, acc_sc):
    j = pl.program_id(0)
    contract_last = (((1,), (1,)), ((), ()))

    @pl.when(j == 0)
    def _():
        own = qa_ref.shape[1]
        qt_sc[:, :own] = qa_ref[...]
        qt_sc[:, own:] = qb_ref[...]
        m_sc[...] = jnp.full(m_sc.shape, -jnp.inf, jnp.float32)
        l_sc[...] = jnp.zeros(l_sc.shape, jnp.float32)
        acc_sc[...] = jnp.zeros(acc_sc.shape, jnp.float32)

    hkv = hkv_ref[...]
    k_all = jnp.dot(hkv, wk_ref[...], preferred_element_type=jnp.float32)
    v_t = lax.dot_general(wvt_ref[...], hkv, contract_last, preferred_element_type=jnp.float32)
    for h in range(heads):
        rows = slice(h * head_size, (h + 1) * head_size)
        k_h = k_all[:, rows]
        k_h = (k_h * lax.rsqrt(jnp.mean(k_h * k_h, axis=1, keepdims=True) + 1e-06)).astype(
            jnp.bfloat16
        )
        s_t = jnp.dot(k_h, qt_sc[rows, :], preferred_element_type=jnp.float32)
        m_prev = m_sc[h]
        m_next = jnp.maximum(m_prev, jnp.max(s_t, axis=0, keepdims=True))
        alpha = jnp.exp(m_prev - m_next)
        p_t = jnp.exp(s_t - m_next)
        l_sc[h] = alpha * l_sc[h] + jnp.sum(p_t, axis=0, keepdims=True)
        acc_sc[rows, :] = alpha * acc_sc[rows, :] + jnp.dot(
            v_t[rows, :].astype(jnp.bfloat16), p_t.astype(jnp.bfloat16),
            preferred_element_type=jnp.float32,
        )
        m_sc[h] = m_next

    @pl.when(j == nk - 1)
    def _():
        own = o_ref.shape[1]
        o_ref[...] = acc_sc[:, :own]
        ob_ref[...] = acc_sc[:, own:]
        for h in range(heads):
            st_ref[h : h + 1, :] = m_sc[h][:, :own]
            st_ref[heads + h : heads + h + 1, :] = l_sc[h][:, :own]
            sb_ref[h : h + 1, :] = m_sc[h][:, own:]
            sb_ref[heads + h : heads + h + 1, :] = l_sc[h][:, own:]


def attend_partial(qt_own, qt_other, hidden_kv, qkv_weight, wvt, heads, head_size, tk=1024):
    width, own = qt_own.shape
    q_rows = 2 * own
    k_rows, channels = hidden_kv.shape
    nk = k_rows // tk
    whole = lambda j: (0, 0)
    return pl.pallas_call(
        functools.partial(attend_kernel, heads, head_size, nk),
        grid=(nk,),
        in_specs=[
            pl.BlockSpec((width, own), whole),
            pl.BlockSpec((width, own), whole),
            pl.BlockSpec((tk, channels), lambda j: (j, 0)),
            pl.BlockSpec((channels, width), lambda j: (0, 1)),
            pl.BlockSpec((width, channels), whole),
        ],
        out_specs=[
            pl.BlockSpec((width, own), whole),
            pl.BlockSpec((2 * heads, own), whole),
        ] * 2,
        out_shape=[
            jax.ShapeDtypeStruct((width, own), jnp.float32),
            jax.ShapeDtypeStruct((2 * heads, own), jnp.float32),
        ] * 2,
        scratch_shapes=[
            pltpu.VMEM((width, q_rows), jnp.bfloat16),
            pltpu.VMEM((heads, 1, q_rows), jnp.float32),
            pltpu.VMEM((heads, 1, q_rows), jnp.float32),
            pltpu.VMEM((width, q_rows), jnp.float32),
        ],
        compiler_params=pltpu.CompilerParams(dimension_semantics=("arbitrary",)),
        cost_estimate=pl.CostEstimate(
            flops=4 * q_rows * k_rows * width + 2 * k_rows * channels * 2 * width,
            transcendentals=q_rows * k_rows * heads,
            bytes_accessed=k_rows * channels * 2 + q_rows * width * 8,
        ),
    )(qt_own, qt_other, hidden_kv, qkv_weight, wvt)


def finish_kernel(heads, head_size, o_ref, st_ref, og_ref, sg_ref, hid_ref, wo_ref, out_ref):
    st_own = st_ref[...]
    st_got = sg_ref[...]
    mixed = []
    for h in range(heads):
        rows = slice(h * head_size, (h + 1) * head_size)
        m_own = st_own[h : h + 1, :]
        m_got = st_got[h : h + 1, :]
        m_all = jnp.maximum(m_own, m_got)
        w_own = jnp.exp(m_own - m_all)
        w_got = jnp.exp(m_got - m_all)
        denom = st_own[heads + h : heads + h + 1, :] * w_own + st_got[heads + h : heads + h + 1, :] * w_got
        mixed.append((o_ref[rows, :] * w_own + og_ref[rows, :] * w_got) / denom)
    attended = jnp.concatenate(mixed, axis=0).T.astype(jnp.bfloat16)
    out = hid_ref[...].astype(jnp.float32) + jnp.dot(
        attended, wo_ref[...], preferred_element_type=jnp.float32
    )
    out_ref[...] = out.astype(out_ref.dtype)


def finish(o_part, st_part, o_got, st_got, hidden, out_weight, heads, head_size):
    rows, width_out = hidden.shape
    width = heads * head_size
    whole = lambda i: (0, 0)
    return pl.pallas_call(
        functools.partial(finish_kernel, heads, head_size),
        grid=(1,),
        in_specs=[
            pl.BlockSpec((width, rows), whole),
            pl.BlockSpec((2 * heads, rows), whole),
            pl.BlockSpec((width, rows), whole),
            pl.BlockSpec((2 * heads, rows), whole),
            pl.BlockSpec((rows, width_out), whole),
            pl.BlockSpec((width, width_out), whole),
        ],
        out_specs=pl.BlockSpec((rows, width_out), whole),
        out_shape=jax.ShapeDtypeStruct((rows, width_out), jnp.bfloat16),
    )(o_part, st_part, o_got, st_got, hidden, out_weight)


def ring_gather_kernel(side, heads, head_size, x_ref, h_ref, wq_ref, wv_ref, scale_ref,
                       out_ref, qt_ref, wvt_ref, send_sem, recv_sem, local_sem):
    me = lax.axis_index("zx")
    z, x = me // side, me % side
    half = x_ref.shape[1]
    q = half // 2
    mesh_ids = pl.DeviceIdType.MESH

    def slot(stream, a, b):
        a = lax.rem(a + side, side)
        b = lax.rem(b + side, side)
        return b * side + a if stream == 0 else a * side + b

    own = [(x, z), (z, x)]
    barrier = pltpu.get_barrier_semaphore()
    for target in (slot(0, x + 1, z), slot(0, x - 1, z), slot(1, z + 1, x), slot(1, z - 1, x)):
        pl.semaphore_signal(barrier, inc=1, device_id={"zx": target}, device_id_type=mesh_ids)
    pl.semaphore_wait(barrier, 4)
    local = pltpu.make_async_copy(x_ref, out_ref.at[me], local_sem)
    local.start()

    sends = []
    index = {}

    def send(key, src, view, target):
        idx = len(index)
        index[key] = idx
        copy = pltpu.make_async_remote_copy(
            src_ref=src, dst_ref=view, send_sem=send_sem.at[idx], recv_sem=recv_sem.at[idx],
            device_id={"zx": target}, device_id_type=mesh_ids,
        )
        copy.start()
        sends.append(copy)

    def recv(key, view, source):
        idx = index[key]
        pltpu.make_async_remote_copy(
            src_ref=view, dst_ref=view, send_sem=send_sem.at[idx], recv_sem=recv_sem.at[idx],
            device_id={"zx": source}, device_id_type=mesh_ids,
        ).wait_recv()

    def part(stream, a, b, lo=None):
        view = out_ref.at[slot(stream, a, b), stream]
        return view if lo is None else view.at[pl.ds(lo, q)]

    def send_row(st, k):
        a0, b0 = own[st]
        src = x_ref.at[st] if k == 0 else part(st, a0 + k, b0)
        send((st, 3, 1, k), src, part(st, a0 + k, b0), slot(st, a0, b0 + 1))
        send((st, 3, -1, k), src, part(st, a0 + k, b0), slot(st, a0, b0 - 1))

    for st in range(2):
        a0, b0 = own[st]
        send((st, 1, 1), x_ref.at[st], part(st, a0, b0), slot(st, a0 + 1, b0))
        send((st, 1, -1), x_ref.at[st], part(st, a0, b0), slot(st, a0 - 1, b0))
        send_row(st, 0)
    for st in range(2):
        a0, b0 = own[st]
        recv((st, 1, 1), part(st, a0 - 1, b0), slot(st, a0 - 1, b0))
        recv((st, 1, -1), part(st, a0 + 1, b0), slot(st, a0 + 1, b0))
        send((st, 2, 1), part(st, a0 - 1, b0, 0), part(st, a0 - 1, b0, 0), slot(st, a0 + 1, b0))
        send((st, 2, -1), part(st, a0 + 1, b0, q), part(st, a0 + 1, b0, q), slot(st, a0 - 1, b0))
        send_row(st, 1)
        send_row(st, side - 1)
    proj = jnp.dot(h_ref[...], wq_ref[...], preferred_element_type=jnp.float32)
    scale = scale_ref[...]
    normed = []
    for h in range(heads):
        cols = slice(h * head_size, (h + 1) * head_size)
        part_q = proj[:, cols]
        mean_sq = jnp.mean(part_q * part_q, axis=1, keepdims=True)
        normed.append(part_q * lax.rsqrt(mean_sq + 1e-06) * scale[:, cols])
    qt_ref[...] = jnp.concatenate(normed, axis=1).T.astype(qt_ref.dtype)
    wvt_ref[...] = wv_ref[...].astype(jnp.float32).T.astype(wvt_ref.dtype)
    for st in range(2):
        a0, b0 = own[st]
        recv((st, 2, 1), part(st, a0 - 2, b0, 0), slot(st, a0 - 1, b0))
        recv((st, 2, -1), part(st, a0 + 2, b0, q), slot(st, a0 + 1, b0))
        for k in range(2, side - 1):
            send_row(st, k)
    for st in range(2):
        a0, b0 = own[st]
        for k in range(side):
            recv((st, 3, 1, k), part(st, a0 + k, b0 - 1), slot(st, a0, b0 - 1))
            recv((st, 3, -1, k), part(st, a0 + k, b0 + 1), slot(st, a0, b0 + 1))
            send((st, 4, 1, k), part(st, a0 + k, b0 - 1, 0), part(st, a0 + k, b0 - 1, 0), slot(st, a0, b0 + 1))
            send((st, 4, -1, k), part(st, a0 + k, b0 + 1, q), part(st, a0 + k, b0 + 1, q), slot(st, a0, b0 - 1))
    for st in range(2):
        a0, b0 = own[st]
        for k in range(side):
            recv((st, 4, 1, k), part(st, a0 + k, b0 - 2, 0), slot(st, a0, b0 - 1))
            recv((st, 4, -1, k), part(st, a0 + k, b0 + 2, q), slot(st, a0, b0 + 1))
    local.wait()
    for copy in sends:
        copy.wait_send()


def gather_rows(block, qkv_weight, scale_row, heads, head_size, axis):
    n = lax.axis_size(axis)
    side = math.isqrt(n)
    rows, width = block.shape
    channels, width_qkv = qkv_weight.shape
    width_all = width_qkv // 3
    copies = 2 * (2 + 2 + 4 * side)
    whole = lambda i: (0, 0)
    out, qt, wvt = pl.pallas_call(
        functools.partial(ring_gather_kernel, side, heads, head_size),
        grid=(1,),
        in_specs=[
            pl.BlockSpec(memory_space=pl.ANY),
            pl.BlockSpec((rows, width), whole),
            pl.BlockSpec((channels, width_all), lambda i: (0, 0)),
            pl.BlockSpec((channels, width_all), lambda i: (0, 2)),
            pl.BlockSpec((1, width_all), whole),
        ],
        out_specs=[
            pl.BlockSpec(memory_space=pl.ANY),
            pl.BlockSpec((width_all, rows), whole),
            pl.BlockSpec((width_all, channels), whole),
        ],
        out_shape=[
            jax.ShapeDtypeStruct((n, 2, rows // 2, width), block.dtype),
            jax.ShapeDtypeStruct((width_all, rows), jnp.bfloat16),
            jax.ShapeDtypeStruct((width_all, channels), jnp.bfloat16),
        ],
        scratch_shapes=[
            pltpu.SemaphoreType.DMA((copies,)),
            pltpu.SemaphoreType.DMA((copies,)),
            pltpu.SemaphoreType.DMA,
        ],
        compiler_params=pltpu.CompilerParams(collective_id=0, has_side_effects=True),
    )(block.reshape(2, rows // 2, width), block, qkv_weight, qkv_weight, scale_row)
    return out.reshape(n * rows, width), qt, wvt


def conv_gelu_kernel(taps, rows, halo, x_ref, w_ref, o_ref, acc_sc):
    j = pl.program_id(0)
    product = jnp.dot(x_ref[...], w_ref[...], preferred_element_type=jnp.float32)
    for t in range(taps):

        @pl.when(j == t)
        def _():
            if t == 0:
                acc_sc[...] = product[t : t + rows]
            else:
                acc_sc[...] = acc_sc[...] + product[t : t + rows]

    @pl.when(j == taps - 1)
    def _():
        place = lax.axis_index(SEQ_AXES)
        last = lax.axis_size(SEQ_AXES) - 1
        row = lax.broadcasted_iota(jnp.int32, acc_sc.shape, 0)
        outside = jnp.logical_or(
            jnp.logical_and(place == 0, row < halo),
            jnp.logical_and(place == last, row >= rows - halo),
        )
        value = jax.nn.gelu(acc_sc[...])
        o_ref[...] = jnp.where(outside, 0.0, value).astype(o_ref.dtype)


def conv_gelu(padded, weight, halo):
    taps, channels, width = weight.shape
    rows = padded.shape[0] - taps + 1
    whole = lambda j: (0, 0)
    return pl.pallas_call(
        functools.partial(conv_gelu_kernel, taps, rows, halo),
        grid=(taps,),
        in_specs=[
            pl.BlockSpec(padded.shape, whole),
            pl.BlockSpec((None, channels, width), lambda j: (j, 0, 0)),
        ],
        out_specs=pl.BlockSpec((rows, width), whole),
        out_shape=jax.ShapeDtypeStruct((rows, width), jnp.bfloat16),
        scratch_shapes=[pltpu.VMEM((rows, width), jnp.float32)],
        compiler_params=pltpu.CompilerParams(
            dimension_semantics=("arbitrary",), vmem_limit_bytes=24 * 1024 * 1024
        ),
        cost_estimate=pl.CostEstimate(
            flops=2 * taps * padded.shape[0] * channels * width,
            transcendentals=rows * width,
            bytes_accessed=taps * channels * width * 2 + padded.size * 2 + rows * width * 2,
        ),
    )(padded, weight)


def body(sequence_input, conv_first, conv_second, qkv_weight, out_weight, logit_scale):
    row_count = sequence_input.shape[0]
    padded_input = padded_2(sequence_input, 4)
    padded_first = conv_gelu(padded_input, conv_first, 2)
    first_out = padded_first[2 : 2 + row_count]
    second = convolve(padded_first, conv_second, row_count)
    hidden = (first_out.astype(jnp.float32) + second).astype(jnp.bfloat16)
    head_count = logit_scale.shape[0]
    width_all = qkv_weight.shape[1] // 3
    head_size = width_all // head_count
    scale_row = jnp.repeat(logit_scale / math.sqrt(head_size), head_size)[None, :]

    swap = [(0, 1), (1, 0)]
    hidden_all, qt_own, wvt = gather_rows(hidden, qkv_weight, scale_row, head_count, head_size, "zx")
    qt_other = lax.ppermute(qt_own, "core", swap)
    o_part, st_part, o_send, st_send = attend_partial(
        qt_own, qt_other, hidden_all, qkv_weight, wvt, head_count, head_size
    )
    o_got, st_got = lax.ppermute((o_send, st_send), "core", swap)
    return finish(o_part, st_part, o_got, st_got, hidden, out_weight, head_count, head_size)


def solution(mesh):
    devices = np.asarray(mesh.devices)
    seq_size = mesh.shape["seq"]
    batch_size = mesh.shape["batch"]
    order = [mesh.axis_names.index("seq"), mesh.axis_names.index("batch")]
    devices = devices.transpose(order).reshape(seq_size // 2, 2, batch_size)
    split_mesh = Mesh(devices, ("zx", "core", "batch"))
    rows = P(("batch", "zx", "core"), None)
    in_specs = (rows, P(), P(), P(), P(), P())
    return jax.shard_map(body, mesh=split_mesh, in_specs=in_specs, out_specs=rows, check_vma=False)
```

```python
import functools
import math

import jax
import jax.numpy as jnp
import numpy as np
from jax import lax
from jax.experimental import pallas as pl
from jax.experimental.pallas import tpu as pltpu
from jax.sharding import Mesh
from jax.sharding import PartitionSpec as P

SEQ_AXES = ("zx", "core")


def padded_2(block, width, align=1):
    count = lax.axis_size(SEQ_AXES)
    forward = [(i, i + 1) for i in range(count - 1)]
    backward = [(target, source) for source, target in forward]
    low = lax.ppermute(lax.slice_in_dim(block, block.shape[0] - width, None, axis=0), SEQ_AXES, forward)
    high = lax.ppermute(lax.slice_in_dim(block, 0, width, axis=0), SEQ_AXES, backward)
    extra = (-(block.shape[0] + 2 * width)) % align
    fill = jnp.zeros((extra, block.shape[1]), block.dtype)
    return jnp.concatenate([low, block, high, fill], axis=0)


def convolve(padded, weight, row_count):
    conv_sum = jnp.dot(padded[0:row_count], weight[0], preferred_element_type=jnp.float32)
    for offset in range(1, weight.shape[0]):
        conv_sum = conv_sum + jnp.dot(
            padded[offset : offset + row_count], weight[offset], preferred_element_type=jnp.float32
        )
    return conv_sum


def head_rms(tensor):
    return tensor * lax.rsqrt(jnp.mean(tensor * tensor, axis=-1, keepdims=True) + 1e-06)


def head_norm(block, heads, head_size):
    parts = []
    for h in range(heads):
        part = block[:, h * head_size : (h + 1) * head_size]
        mean_sq = jnp.mean(part * part, axis=1, keepdims=True)
        parts.append(part * lax.rsqrt(mean_sq + 1e-06))
    return parts


def attend_kernel(heads, head_size, nk, qa_ref, qb_ref, hkv_ref, wk_ref, wvt_ref,
                  o_ref, st_ref, ob_ref, sb_ref, qt_sc, m_sc, l_sc, acc_sc):
    j = pl.program_id(0)
    contract_last = (((1,), (1,)), ((), ()))

    @pl.when(j == 0)
    def _():
        own = qa_ref.shape[1]
        qt_sc[:, :own] = qa_ref[...]
        qt_sc[:, own:] = qb_ref[...]
        m_sc[...] = jnp.full(m_sc.shape, -jnp.inf, jnp.float32)
        l_sc[...] = jnp.zeros(l_sc.shape, jnp.float32)
        acc_sc[...] = jnp.zeros(acc_sc.shape, jnp.float32)

    hkv = hkv_ref[...]
    k_all = jnp.dot(hkv, wk_ref[...], preferred_element_type=jnp.float32)
    v_t = lax.dot_general(wvt_ref[...], hkv, contract_last, preferred_element_type=jnp.float32)
    for h in range(heads):
        rows = slice(h * head_size, (h + 1) * head_size)
        k_h = k_all[:, rows]
        k_h = (k_h * lax.rsqrt(jnp.mean(k_h * k_h, axis=1, keepdims=True) + 1e-06)).astype(
            jnp.bfloat16
        )
        s_t = jnp.dot(k_h, qt_sc[rows, :], preferred_element_type=jnp.float32)
        m_prev = m_sc[h]
        m_next = jnp.maximum(m_prev, jnp.max(s_t, axis=0, keepdims=True))
        alpha = jnp.exp(m_prev - m_next)
        p_t = jnp.exp(s_t - m_next)
        l_sc[h] = alpha * l_sc[h] + jnp.sum(p_t, axis=0, keepdims=True)
        acc_sc[rows, :] = alpha * acc_sc[rows, :] + jnp.dot(
            v_t[rows, :].astype(jnp.bfloat16), p_t.astype(jnp.bfloat16),
            preferred_element_type=jnp.float32,
        )
        m_sc[h] = m_next

    @pl.when(j == nk - 1)
    def _():
        own = o_ref.shape[1]
        o_ref[...] = acc_sc[:, :own]
        ob_ref[...] = acc_sc[:, own:]
        for h in range(heads):
            st_ref[h : h + 1, :] = m_sc[h][:, :own]
            st_ref[heads + h : heads + h + 1, :] = l_sc[h][:, :own]
            sb_ref[h : h + 1, :] = m_sc[h][:, own:]
            sb_ref[heads + h : heads + h + 1, :] = l_sc[h][:, own:]


def attend_partial(qt_own, qt_other, hidden_kv, qkv_weight, wvt, heads, head_size, tk=2048):
    width, own = qt_own.shape
    q_rows = 2 * own
    k_rows, channels = hidden_kv.shape
    nk = k_rows // tk
    whole = lambda j: (0, 0)
    return pl.pallas_call(
        functools.partial(attend_kernel, heads, head_size, nk),
        grid=(nk,),
        in_specs=[
            pl.BlockSpec((width, own), whole),
            pl.BlockSpec((width, own), whole),
            pl.BlockSpec((tk, channels), lambda j: (j, 0)),
            pl.BlockSpec((channels, width), lambda j: (0, 1)),
            pl.BlockSpec((width, channels), whole),
        ],
        out_specs=[
            pl.BlockSpec((width, own), whole),
            pl.BlockSpec((2 * heads, own), whole),
        ] * 2,
        out_shape=[
            jax.ShapeDtypeStruct((width, own), jnp.float32),
            jax.ShapeDtypeStruct((2 * heads, own), jnp.float32),
        ] * 2,
        scratch_shapes=[
            pltpu.VMEM((width, q_rows), jnp.bfloat16),
            pltpu.VMEM((heads, 1, q_rows), jnp.float32),
            pltpu.VMEM((heads, 1, q_rows), jnp.float32),
            pltpu.VMEM((width, q_rows), jnp.float32),
        ],
        compiler_params=pltpu.CompilerParams(dimension_semantics=("arbitrary",)),
        cost_estimate=pl.CostEstimate(
            flops=4 * q_rows * k_rows * width + 2 * k_rows * channels * 2 * width,
            transcendentals=q_rows * k_rows * heads,
            bytes_accessed=k_rows * channels * 2 + q_rows * width * 8,
        ),
    )(qt_own, qt_other, hidden_kv, qkv_weight, wvt)


def finish_kernel(heads, head_size, o_ref, st_ref, og_ref, sg_ref, hid_ref, wo_ref, out_ref):
    st_own = st_ref[...]
    st_got = sg_ref[...]
    mixed = []
    for h in range(heads):
        rows = slice(h * head_size, (h + 1) * head_size)
        m_own = st_own[h : h + 1, :]
        m_got = st_got[h : h + 1, :]
        m_all = jnp.maximum(m_own, m_got)
        w_own = jnp.exp(m_own - m_all)
        w_got = jnp.exp(m_got - m_all)
        denom = st_own[heads + h : heads + h + 1, :] * w_own + st_got[heads + h : heads + h + 1, :] * w_got
        mixed.append((o_ref[rows, :] * w_own + og_ref[rows, :] * w_got) / denom)
    attended = jnp.concatenate(mixed, axis=0).T.astype(jnp.bfloat16)
    out = hid_ref[...].astype(jnp.float32) + jnp.dot(
        attended, wo_ref[...], preferred_element_type=jnp.float32
    )
    out_ref[...] = out.astype(out_ref.dtype)


def finish(o_part, st_part, o_got, st_got, hidden, out_weight, heads, head_size):
    rows, width_out = hidden.shape
    width = heads * head_size
    whole = lambda i: (0, 0)
    return pl.pallas_call(
        functools.partial(finish_kernel, heads, head_size),
        grid=(1,),
        in_specs=[
            pl.BlockSpec((width, rows), whole),
            pl.BlockSpec((2 * heads, rows), whole),
            pl.BlockSpec((width, rows), whole),
            pl.BlockSpec((2 * heads, rows), whole),
            pl.BlockSpec((rows, width_out), whole),
            pl.BlockSpec((width, width_out), whole),
        ],
        out_specs=pl.BlockSpec((rows, width_out), whole),
        out_shape=jax.ShapeDtypeStruct((rows, width_out), jnp.bfloat16),
    )(o_part, st_part, o_got, st_got, hidden, out_weight)


def ring_gather_kernel(side, heads, head_size, x_ref, h_ref, wq_ref, wv_ref, scale_ref,
                       out_ref, qt_ref, wvt_ref, send_sem, recv_sem, local_sem):
    me = lax.axis_index("zx")
    z, x = me // side, me % side
    half = x_ref.shape[1]
    q = half // 2
    mesh_ids = pl.DeviceIdType.MESH

    def slot(stream, a, b):
        a = lax.rem(a + side, side)
        b = lax.rem(b + side, side)
        return b * side + a if stream == 0 else a * side + b

    own = [(x, z), (z, x)]
    barrier = pltpu.get_barrier_semaphore()
    for target in (slot(0, x + 1, z), slot(0, x - 1, z), slot(1, z + 1, x), slot(1, z - 1, x)):
        pl.semaphore_signal(barrier, inc=1, device_id={"zx": target}, device_id_type=mesh_ids)
    pl.semaphore_wait(barrier, 4)
    local = pltpu.make_async_copy(x_ref, out_ref.at[me], local_sem)
    local.start()

    sends = []
    index = {}

    def send(key, src, view, target):
        idx = len(index)
        index[key] = idx
        copy = pltpu.make_async_remote_copy(
            src_ref=src, dst_ref=view, send_sem=send_sem.at[idx], recv_sem=recv_sem.at[idx],
            device_id={"zx": target}, device_id_type=mesh_ids,
        )
        copy.start()
        sends.append(copy)

    def recv(key, view, source):
        idx = index[key]
        pltpu.make_async_remote_copy(
            src_ref=view, dst_ref=view, send_sem=send_sem.at[idx], recv_sem=recv_sem.at[idx],
            device_id={"zx": source}, device_id_type=mesh_ids,
        ).wait_recv()

    def part(stream, a, b, lo=None):
        view = out_ref.at[slot(stream, a, b), stream]
        return view if lo is None else view.at[pl.ds(lo, q)]

    def send_row(st, k):
        a0, b0 = own[st]
        src = x_ref.at[st] if k == 0 else part(st, a0 + k, b0)
        send((st, 3, 1, k), src, part(st, a0 + k, b0), slot(st, a0, b0 + 1))
        send((st, 3, -1, k), src, part(st, a0 + k, b0), slot(st, a0, b0 - 1))

    for st in range(2):
        a0, b0 = own[st]
        send((st, 1, 1), x_ref.at[st], part(st, a0, b0), slot(st, a0 + 1, b0))
        send((st, 1, -1), x_ref.at[st], part(st, a0, b0), slot(st, a0 - 1, b0))
        send_row(st, 0)
    for st in range(2):
        a0, b0 = own[st]
        recv((st, 1, 1), part(st, a0 - 1, b0), slot(st, a0 - 1, b0))
        recv((st, 1, -1), part(st, a0 + 1, b0), slot(st, a0 + 1, b0))
        send((st, 2, 1), part(st, a0 - 1, b0, 0), part(st, a0 - 1, b0, 0), slot(st, a0 + 1, b0))
        send((st, 2, -1), part(st, a0 + 1, b0, q), part(st, a0 + 1, b0, q), slot(st, a0 - 1, b0))
        send_row(st, 1)
        send_row(st, side - 1)
    for st in range(2):
        a0, b0 = own[st]
        recv((st, 2, 1), part(st, a0 - 2, b0, 0), slot(st, a0 - 1, b0))
        recv((st, 2, -1), part(st, a0 + 2, b0, q), slot(st, a0 + 1, b0))
        for k in range(2, side - 1):
            send_row(st, k)
    for st in range(2):
        a0, b0 = own[st]
        for k in range(side):
            recv((st, 3, 1, k), part(st, a0 + k, b0 - 1), slot(st, a0, b0 - 1))
            recv((st, 3, -1, k), part(st, a0 + k, b0 + 1), slot(st, a0, b0 + 1))
            send((st, 4, 1, k), part(st, a0 + k, b0 - 1, 0), part(st, a0 + k, b0 - 1, 0), slot(st, a0, b0 + 1))
            send((st, 4, -1, k), part(st, a0 + k, b0 + 1, q), part(st, a0 + k, b0 + 1, q), slot(st, a0, b0 - 1))
    proj = jnp.dot(h_ref[...], wq_ref[...], preferred_element_type=jnp.float32)
    scale = scale_ref[...]
    normed = []
    for h in range(heads):
        cols = slice(h * head_size, (h + 1) * head_size)
        part_q = proj[:, cols]
        mean_sq = jnp.mean(part_q * part_q, axis=1, keepdims=True)
        normed.append(part_q * lax.rsqrt(mean_sq + 1e-06) * scale[:, cols])
    qt_ref[...] = jnp.concatenate(normed, axis=1).T.astype(qt_ref.dtype)
    wvt_ref[...] = wv_ref[...].astype(jnp.float32).T.astype(wvt_ref.dtype)
    for st in range(2):
        a0, b0 = own[st]
        for k in range(side):
            recv((st, 4, 1, k), part(st, a0 + k, b0 - 2, 0), slot(st, a0, b0 - 1))
            recv((st, 4, -1, k), part(st, a0 + k, b0 + 2, q), slot(st, a0, b0 + 1))
    local.wait()
    for copy in sends:
        copy.wait_send()


def gather_rows(block, qkv_weight, scale_row, heads, head_size, axis):
    n = lax.axis_size(axis)
    side = math.isqrt(n)
    rows, width = block.shape
    channels, width_qkv = qkv_weight.shape
    width_all = width_qkv // 3
    copies = 2 * (2 + 2 + 4 * side)
    whole = lambda i: (0, 0)
    out, qt, wvt = pl.pallas_call(
        functools.partial(ring_gather_kernel, side, heads, head_size),
        grid=(1,),
        in_specs=[
            pl.BlockSpec(memory_space=pl.ANY),
            pl.BlockSpec((rows, width), whole),
            pl.BlockSpec((channels, width_all), lambda i: (0, 0)),
            pl.BlockSpec((channels, width_all), lambda i: (0, 2)),
            pl.BlockSpec((1, width_all), whole),
        ],
        out_specs=[
            pl.BlockSpec(memory_space=pl.ANY),
            pl.BlockSpec((width_all, rows), whole),
            pl.BlockSpec((width_all, channels), whole),
        ],
        out_shape=[
            jax.ShapeDtypeStruct((n, 2, rows // 2, width), block.dtype),
            jax.ShapeDtypeStruct((width_all, rows), jnp.bfloat16),
            jax.ShapeDtypeStruct((width_all, channels), jnp.bfloat16),
        ],
        scratch_shapes=[
            pltpu.SemaphoreType.DMA((copies,)),
            pltpu.SemaphoreType.DMA((copies,)),
            pltpu.SemaphoreType.DMA,
        ],
        compiler_params=pltpu.CompilerParams(collective_id=0, has_side_effects=True),
    )(block.reshape(2, rows // 2, width), block, qkv_weight, qkv_weight, scale_row)
    return out.reshape(n * rows, width), qt, wvt


def conv_gelu_kernel(taps, rows, halo, x_ref, w_ref, o_ref, acc_sc):
    j = pl.program_id(0)
    product = jnp.dot(x_ref[...], w_ref[...], preferred_element_type=jnp.float32)
    for t in range(taps):

        @pl.when(j == t)
        def _():
            if t == 0:
                acc_sc[...] = product[t : t + rows]
            else:
                acc_sc[...] = acc_sc[...] + product[t : t + rows]

    @pl.when(j == taps - 1)
    def _():
        place = lax.axis_index(SEQ_AXES)
        last = lax.axis_size(SEQ_AXES) - 1
        row = lax.broadcasted_iota(jnp.int32, acc_sc.shape, 0)
        outside = jnp.logical_or(
            jnp.logical_and(place == 0, row < halo),
            jnp.logical_and(place == last, row >= rows - halo),
        )
        value = jax.nn.gelu(acc_sc[...])
        o_ref[...] = jnp.where(outside, 0.0, value).astype(o_ref.dtype)


def conv_gelu(padded, weight, halo):
    taps, channels, width = weight.shape
    rows = padded.shape[0] - taps + 1
    whole = lambda j: (0, 0)
    return pl.pallas_call(
        functools.partial(conv_gelu_kernel, taps, rows, halo),
        grid=(taps,),
        in_specs=[
            pl.BlockSpec(padded.shape, whole),
            pl.BlockSpec((None, channels, width), lambda j: (j, 0, 0)),
        ],
        out_specs=pl.BlockSpec((rows, width), whole),
        out_shape=jax.ShapeDtypeStruct((rows, width), jnp.bfloat16),
        scratch_shapes=[pltpu.VMEM((rows, width), jnp.float32)],
        compiler_params=pltpu.CompilerParams(
            dimension_semantics=("arbitrary",), vmem_limit_bytes=24 * 1024 * 1024
        ),
        cost_estimate=pl.CostEstimate(
            flops=2 * taps * padded.shape[0] * channels * width,
            transcendentals=rows * width,
            bytes_accessed=taps * channels * width * 2 + padded.size * 2 + rows * width * 2,
        ),
    )(padded, weight)


def body(sequence_input, conv_first, conv_second, qkv_weight, out_weight, logit_scale):
    row_count = sequence_input.shape[0]
    padded_input = padded_2(sequence_input, 4)
    padded_first = conv_gelu(padded_input, conv_first, 2)
    first_out = padded_first[2 : 2 + row_count]
    second = convolve(padded_first, conv_second, row_count)
    hidden = (first_out.astype(jnp.float32) + second).astype(jnp.bfloat16)
    head_count = logit_scale.shape[0]
    width_all = qkv_weight.shape[1] // 3
    head_size = width_all // head_count
    scale_row = jnp.repeat(logit_scale / math.sqrt(head_size), head_size)[None, :]

    swap = [(0, 1), (1, 0)]
    hidden_all, qt_own, wvt = gather_rows(hidden, qkv_weight, scale_row, head_count, head_size, "zx")
    qt_other = lax.ppermute(qt_own, "core", swap)
    o_part, st_part, o_send, st_send = attend_partial(
        qt_own, qt_other, hidden_all, qkv_weight, wvt, head_count, head_size
    )
    o_got, st_got = lax.ppermute((o_send, st_send), "core", swap)
    return finish(o_part, st_part, o_got, st_got, hidden, out_weight, head_count, head_size)


def solution(mesh):
    devices = np.asarray(mesh.devices)
    seq_size = mesh.shape["seq"]
    batch_size = mesh.shape["batch"]
    order = [mesh.axis_names.index("seq"), mesh.axis_names.index("batch")]
    devices = devices.transpose(order).reshape(seq_size // 2, 2, batch_size)
    split_mesh = Mesh(devices, ("zx", "core", "batch"))
    rows = P(("batch", "zx", "core"), None)
    in_specs = (rows, P(), P(), P(), P(), P())
    return jax.shard_map(body, mesh=split_mesh, in_specs=in_specs, out_specs=rows, check_vma=False)
```

```python
import functools
import math

import jax
import jax.numpy as jnp
import numpy as np
from jax import lax
from jax.experimental import pallas as pl
from jax.experimental.pallas import tpu as pltpu
from jax.sharding import Mesh
from jax.sharding import PartitionSpec as P

SEQ_AXES = ("zx", "core")


def padded_2(block, width, align=1):
    count = lax.axis_size(SEQ_AXES)
    forward = [(i, i + 1) for i in range(count - 1)]
    backward = [(target, source) for source, target in forward]
    low = lax.ppermute(lax.slice_in_dim(block, block.shape[0] - width, None, axis=0), SEQ_AXES, forward)
    high = lax.ppermute(lax.slice_in_dim(block, 0, width, axis=0), SEQ_AXES, backward)
    extra = (-(block.shape[0] + 2 * width)) % align
    fill = jnp.zeros((extra, block.shape[1]), block.dtype)
    return jnp.concatenate([low, block, high, fill], axis=0)


def convolve(padded, weight, row_count):
    conv_sum = jnp.dot(padded[0:row_count], weight[0], preferred_element_type=jnp.float32)
    for offset in range(1, weight.shape[0]):
        conv_sum = conv_sum + jnp.dot(
            padded[offset : offset + row_count], weight[offset], preferred_element_type=jnp.float32
        )
    return conv_sum


def head_rms(tensor):
    return tensor * lax.rsqrt(jnp.mean(tensor * tensor, axis=-1, keepdims=True) + 1e-06)


def head_norm(block, heads, head_size):
    parts = []
    for h in range(heads):
        part = block[:, h * head_size : (h + 1) * head_size]
        mean_sq = jnp.mean(part * part, axis=1, keepdims=True)
        parts.append(part * lax.rsqrt(mean_sq + 1e-06))
    return parts


def attend_kernel(heads, head_size, nk, qa_ref, qb_ref, hkv_ref, wk_ref, wvt_ref,
                  o_ref, st_ref, ob_ref, sb_ref, qt_sc, m_sc, l_sc, acc_sc):
    j = pl.program_id(0)
    contract_last = (((1,), (1,)), ((), ()))

    @pl.when(j == 0)
    def _():
        own = qa_ref.shape[1]
        qt_sc[:, :own] = qa_ref[...]
        qt_sc[:, own:] = qb_ref[...]
        m_sc[...] = jnp.full(m_sc.shape, -jnp.inf, jnp.float32)
        l_sc[...] = jnp.zeros(l_sc.shape, jnp.float32)
        acc_sc[...] = jnp.zeros(acc_sc.shape, jnp.float32)

    hkv = hkv_ref[...]
    k_all = jnp.dot(hkv, wk_ref[...], preferred_element_type=jnp.float32)
    v_t = lax.dot_general(wvt_ref[...], hkv, contract_last, preferred_element_type=jnp.float32)
    for h in range(heads):
        rows = slice(h * head_size, (h + 1) * head_size)
        k_h = k_all[:, rows]
        k_h = (k_h * lax.rsqrt(jnp.mean(k_h * k_h, axis=1, keepdims=True) + 1e-06)).astype(
            jnp.bfloat16
        )
        s_t = jnp.dot(k_h, qt_sc[rows, :], preferred_element_type=jnp.float32)
        m_prev = m_sc[h]
        m_next = jnp.maximum(m_prev, jnp.max(s_t, axis=0, keepdims=True))
        alpha = jnp.exp(m_prev - m_next)
        p_t = jnp.exp(s_t - m_next)
        l_sc[h] = alpha * l_sc[h] + jnp.sum(p_t, axis=0, keepdims=True)
        acc_sc[rows, :] = alpha * acc_sc[rows, :] + jnp.dot(
            v_t[rows, :].astype(jnp.bfloat16), p_t.astype(jnp.bfloat16),
            preferred_element_type=jnp.float32,
        )
        m_sc[h] = m_next

    @pl.when(j == nk - 1)
    def _():
        own = o_ref.shape[1]
        o_ref[...] = acc_sc[:, :own]
        ob_ref[...] = acc_sc[:, own:]
        for h in range(heads):
            st_ref[h : h + 1, :] = m_sc[h][:, :own]
            st_ref[heads + h : heads + h + 1, :] = l_sc[h][:, :own]
            sb_ref[h : h + 1, :] = m_sc[h][:, own:]
            sb_ref[heads + h : heads + h + 1, :] = l_sc[h][:, own:]


def attend_partial(qt_own, qt_other, hidden_kv, qkv_weight, wvt, heads, head_size, tk=2048):
    width, own = qt_own.shape
    q_rows = 2 * own
    k_rows, channels = hidden_kv.shape
    nk = k_rows // tk
    whole = lambda j: (0, 0)
    return pl.pallas_call(
        functools.partial(attend_kernel, heads, head_size, nk),
        grid=(nk,),
        in_specs=[
            pl.BlockSpec((width, own), whole),
            pl.BlockSpec((width, own), whole),
            pl.BlockSpec((tk, channels), lambda j: (j, 0)),
            pl.BlockSpec((channels, width), lambda j: (0, 1)),
            pl.BlockSpec((width, channels), whole),
        ],
        out_specs=[
            pl.BlockSpec((width, own), whole),
            pl.BlockSpec((2 * heads, own), whole),
        ] * 2,
        out_shape=[
            jax.ShapeDtypeStruct((width, own), jnp.float32),
            jax.ShapeDtypeStruct((2 * heads, own), jnp.float32),
        ] * 2,
        scratch_shapes=[
            pltpu.VMEM((width, q_rows), jnp.bfloat16),
            pltpu.VMEM((heads, 1, q_rows), jnp.float32),
            pltpu.VMEM((heads, 1, q_rows), jnp.float32),
            pltpu.VMEM((width, q_rows), jnp.float32),
        ],
        compiler_params=pltpu.CompilerParams(dimension_semantics=("arbitrary",)),
        cost_estimate=pl.CostEstimate(
            flops=4 * q_rows * k_rows * width + 2 * k_rows * channels * 2 * width,
            transcendentals=q_rows * k_rows * heads,
            bytes_accessed=k_rows * channels * 2 + q_rows * width * 8,
        ),
    )(qt_own, qt_other, hidden_kv, qkv_weight, wvt)


def finish_kernel(heads, head_size, o_ref, st_ref, og_ref, sg_ref, hid_ref, wo_ref, out_ref):
    st_own = st_ref[...]
    st_got = sg_ref[...]
    mixed = []
    for h in range(heads):
        rows = slice(h * head_size, (h + 1) * head_size)
        m_own = st_own[h : h + 1, :]
        m_got = st_got[h : h + 1, :]
        m_all = jnp.maximum(m_own, m_got)
        w_own = jnp.exp(m_own - m_all)
        w_got = jnp.exp(m_got - m_all)
        denom = st_own[heads + h : heads + h + 1, :] * w_own + st_got[heads + h : heads + h + 1, :] * w_got
        mixed.append((o_ref[rows, :] * w_own + og_ref[rows, :] * w_got) / denom)
    attended = jnp.concatenate(mixed, axis=0).T.astype(jnp.bfloat16)
    out = hid_ref[...].astype(jnp.float32) + jnp.dot(
        attended, wo_ref[...], preferred_element_type=jnp.float32
    )
    out_ref[...] = out.astype(out_ref.dtype)


def finish(o_part, st_part, o_got, st_got, hidden, out_weight, heads, head_size):
    rows, width_out = hidden.shape
    width = heads * head_size
    whole = lambda i: (0, 0)
    return pl.pallas_call(
        functools.partial(finish_kernel, heads, head_size),
        grid=(1,),
        in_specs=[
            pl.BlockSpec((width, rows), whole),
            pl.BlockSpec((2 * heads, rows), whole),
            pl.BlockSpec((width, rows), whole),
            pl.BlockSpec((2 * heads, rows), whole),
            pl.BlockSpec((rows, width_out), whole),
            pl.BlockSpec((width, width_out), whole),
        ],
        out_specs=pl.BlockSpec((rows, width_out), whole),
        out_shape=jax.ShapeDtypeStruct((rows, width_out), jnp.bfloat16),
    )(o_part, st_part, o_got, st_got, hidden, out_weight)


def ring_gather_kernel(side, heads, head_size, x_ref, h_ref, wq_ref, wv_ref, scale_ref,
                       out_ref, qt_ref, wvt_ref, send_sem, recv_sem, local_sem):
    me = lax.axis_index("zx")
    z, x = me // side, me % side
    half = x_ref.shape[1]
    q = half // 2
    mesh_ids = pl.DeviceIdType.MESH

    def slot(stream, a, b):
        a = lax.rem(a + side, side)
        b = lax.rem(b + side, side)
        return b * side + a if stream == 0 else a * side + b

    own = [(x, z), (z, x)]
    barrier = pltpu.get_barrier_semaphore()
    for target in (slot(0, x + 1, z), slot(0, x - 1, z), slot(1, z + 1, x), slot(1, z - 1, x)):
        pl.semaphore_signal(barrier, inc=1, device_id={"zx": target}, device_id_type=mesh_ids)
    pl.semaphore_wait(barrier, 4)
    local = pltpu.make_async_copy(x_ref, out_ref.at[me], local_sem)
    local.start()

    sends = []
    index = {}

    def send(key, src, view, target):
        idx = len(index)
        index[key] = idx
        copy = pltpu.make_async_remote_copy(
            src_ref=src, dst_ref=view, send_sem=send_sem.at[idx], recv_sem=recv_sem.at[idx],
            device_id={"zx": target}, device_id_type=mesh_ids,
        )
        copy.start()
        sends.append(copy)

    def recv(key, view, source):
        idx = index[key]
        pltpu.make_async_remote_copy(
            src_ref=view, dst_ref=view, send_sem=send_sem.at[idx], recv_sem=recv_sem.at[idx],
            device_id={"zx": source}, device_id_type=mesh_ids,
        ).wait_recv()

    def part(stream, a, b, lo=None):
        view = out_ref.at[slot(stream, a, b), stream]
        return view if lo is None else view.at[pl.ds(lo, q)]

    def send_row(st, k):
        a0, b0 = own[st]
        src = x_ref.at[st] if k == 0 else part(st, a0 + k, b0)
        send((st, 3, 1, k), src, part(st, a0 + k, b0), slot(st, a0, b0 + 1))
        send((st, 3, -1, k), src, part(st, a0 + k, b0), slot(st, a0, b0 - 1))

    for st in range(2):
        a0, b0 = own[st]
        send((st, 1, 1), x_ref.at[st], part(st, a0, b0), slot(st, a0 + 1, b0))
        send((st, 1, -1), x_ref.at[st], part(st, a0, b0), slot(st, a0 - 1, b0))
        send_row(st, 0)
    for st in range(2):
        a0, b0 = own[st]
        recv((st, 1, 1), part(st, a0 - 1, b0), slot(st, a0 - 1, b0))
        recv((st, 1, -1), part(st, a0 + 1, b0), slot(st, a0 + 1, b0))
        send((st, 2, 1), part(st, a0 - 1, b0, 0), part(st, a0 - 1, b0, 0), slot(st, a0 + 1, b0))
        send((st, 2, -1), part(st, a0 + 1, b0, q), part(st, a0 + 1, b0, q), slot(st, a0 - 1, b0))
        send_row(st, 1)
        send_row(st, side - 1)
    for st in range(2):
        a0, b0 = own[st]
        recv((st, 2, 1), part(st, a0 - 2, b0, 0), slot(st, a0 - 1, b0))
        recv((st, 2, -1), part(st, a0 + 2, b0, q), slot(st, a0 + 1, b0))
        for k in range(2, side - 1):
            send_row(st, k)
    arrival = [0, 1, side - 1] + list(range(2, side - 1))
    for k in arrival:
        for st in range(2):
            a0, b0 = own[st]
            recv((st, 3, 1, k), part(st, a0 + k, b0 - 1), slot(st, a0, b0 - 1))
            recv((st, 3, -1, k), part(st, a0 + k, b0 + 1), slot(st, a0, b0 + 1))
            send((st, 4, 1, k), part(st, a0 + k, b0 - 1, 0), part(st, a0 + k, b0 - 1, 0), slot(st, a0, b0 + 1))
            send((st, 4, -1, k), part(st, a0 + k, b0 + 1, q), part(st, a0 + k, b0 + 1, q), slot(st, a0, b0 - 1))
    proj = jnp.dot(h_ref[...], wq_ref[...], preferred_element_type=jnp.float32)
    scale = scale_ref[...]
    normed = []
    for h in range(heads):
        cols = slice(h * head_size, (h + 1) * head_size)
        part_q = proj[:, cols]
        mean_sq = jnp.mean(part_q * part_q, axis=1, keepdims=True)
        normed.append(part_q * lax.rsqrt(mean_sq + 1e-06) * scale[:, cols])
    qt_ref[...] = jnp.concatenate(normed, axis=1).T.astype(qt_ref.dtype)
    wvt_ref[...] = wv_ref[...].astype(jnp.float32).T.astype(wvt_ref.dtype)
    for st in range(2):
        a0, b0 = own[st]
        for k in range(side):
            recv((st, 4, 1, k), part(st, a0 + k, b0 - 2, 0), slot(st, a0, b0 - 1))
            recv((st, 4, -1, k), part(st, a0 + k, b0 + 2, q), slot(st, a0, b0 + 1))
    local.wait()
    for copy in sends:
        copy.wait_send()


def gather_rows(block, qkv_weight, scale_row, heads, head_size, axis):
    n = lax.axis_size(axis)
    side = math.isqrt(n)
    rows, width = block.shape
    channels, width_qkv = qkv_weight.shape
    width_all = width_qkv // 3
    copies = 2 * (2 + 2 + 4 * side)
    whole = lambda i: (0, 0)
    out, qt, wvt = pl.pallas_call(
        functools.partial(ring_gather_kernel, side, heads, head_size),
        grid=(1,),
        in_specs=[
            pl.BlockSpec(memory_space=pl.ANY),
            pl.BlockSpec((rows, width), whole),
            pl.BlockSpec((channels, width_all), lambda i: (0, 0)),
            pl.BlockSpec((channels, width_all), lambda i: (0, 2)),
            pl.BlockSpec((1, width_all), whole),
        ],
        out_specs=[
            pl.BlockSpec(memory_space=pl.ANY),
            pl.BlockSpec((width_all, rows), whole),
            pl.BlockSpec((width_all, channels), whole),
        ],
        out_shape=[
            jax.ShapeDtypeStruct((n, 2, rows // 2, width), block.dtype),
            jax.ShapeDtypeStruct((width_all, rows), jnp.bfloat16),
            jax.ShapeDtypeStruct((width_all, channels), jnp.bfloat16),
        ],
        scratch_shapes=[
            pltpu.SemaphoreType.DMA((copies,)),
            pltpu.SemaphoreType.DMA((copies,)),
            pltpu.SemaphoreType.DMA,
        ],
        compiler_params=pltpu.CompilerParams(collective_id=0, has_side_effects=True),
    )(block.reshape(2, rows // 2, width), block, qkv_weight, qkv_weight, scale_row)
    return out.reshape(n * rows, width), qt, wvt


def conv_gelu_kernel(taps, rows, halo, x_ref, w_ref, o_ref, acc_sc):
    j = pl.program_id(0)
    product = jnp.dot(x_ref[...], w_ref[...], preferred_element_type=jnp.float32)
    for t in range(taps):

        @pl.when(j == t)
        def _():
            if t == 0:
                acc_sc[...] = product[t : t + rows]
            else:
                acc_sc[...] = acc_sc[...] + product[t : t + rows]

    @pl.when(j == taps - 1)
    def _():
        place = lax.axis_index(SEQ_AXES)
        last = lax.axis_size(SEQ_AXES) - 1
        row = lax.broadcasted_iota(jnp.int32, acc_sc.shape, 0)
        outside = jnp.logical_or(
            jnp.logical_and(place == 0, row < halo),
            jnp.logical_and(place == last, row >= rows - halo),
        )
        value = jax.nn.gelu(acc_sc[...])
        o_ref[...] = jnp.where(outside, 0.0, value).astype(o_ref.dtype)


def conv_gelu(padded, weight, halo):
    taps, channels, width = weight.shape
    rows = padded.shape[0] - taps + 1
    whole = lambda j: (0, 0)
    return pl.pallas_call(
        functools.partial(conv_gelu_kernel, taps, rows, halo),
        grid=(taps,),
        in_specs=[
            pl.BlockSpec(padded.shape, whole),
            pl.BlockSpec((None, channels, width), lambda j: (j, 0, 0)),
        ],
        out_specs=pl.BlockSpec((rows, width), whole),
        out_shape=jax.ShapeDtypeStruct((rows, width), jnp.bfloat16),
        scratch_shapes=[pltpu.VMEM((rows, width), jnp.float32)],
        compiler_params=pltpu.CompilerParams(
            dimension_semantics=("arbitrary",), vmem_limit_bytes=24 * 1024 * 1024
        ),
        cost_estimate=pl.CostEstimate(
            flops=2 * taps * padded.shape[0] * channels * width,
            transcendentals=rows * width,
            bytes_accessed=taps * channels * width * 2 + padded.size * 2 + rows * width * 2,
        ),
    )(padded, weight)


def body(sequence_input, conv_first, conv_second, qkv_weight, out_weight, logit_scale):
    row_count = sequence_input.shape[0]
    padded_input = padded_2(sequence_input, 4)
    padded_first = conv_gelu(padded_input, conv_first, 2)
    first_out = padded_first[2 : 2 + row_count]
    second = convolve(padded_first, conv_second, row_count)
    hidden = (first_out.astype(jnp.float32) + second).astype(jnp.bfloat16)
    head_count = logit_scale.shape[0]
    width_all = qkv_weight.shape[1] // 3
    head_size = width_all // head_count
    scale_row = jnp.repeat(logit_scale / math.sqrt(head_size), head_size)[None, :]

    swap = [(0, 1), (1, 0)]
    hidden_all, qt_own, wvt = gather_rows(hidden, qkv_weight, scale_row, head_count, head_size, "zx")
    qt_other = lax.ppermute(qt_own, "core", swap)
    o_part, st_part, o_send, st_send = attend_partial(
        qt_own, qt_other, hidden_all, qkv_weight, wvt, head_count, head_size
    )
    o_got, st_got = lax.ppermute((o_send, st_send), "core", swap)
    return finish(o_part, st_part, o_got, st_got, hidden, out_weight, head_count, head_size)


def solution(mesh):
    devices = np.asarray(mesh.devices)
    seq_size = mesh.shape["seq"]
    batch_size = mesh.shape["batch"]
    order = [mesh.axis_names.index("seq"), mesh.axis_names.index("batch")]
    devices = devices.transpose(order).reshape(seq_size // 2, 2, batch_size)
    split_mesh = Mesh(devices, ("zx", "core", "batch"))
    rows = P(("batch", "zx", "core"), None)
    in_specs = (rows, P(), P(), P(), P(), P())
    return jax.shard_map(body, mesh=split_mesh, in_specs=in_specs, out_specs=rows, check_vma=False)
```

```python
import functools
import math

import jax
import jax.numpy as jnp
import numpy as np
from jax import lax
from jax.experimental import pallas as pl
from jax.experimental.pallas import tpu as pltpu
from jax.sharding import Mesh
from jax.sharding import PartitionSpec as P

SEQ_AXES = ("zx", "core")


def padded_2(block, width, align=1):
    count = lax.axis_size(SEQ_AXES)
    forward = [(i, i + 1) for i in range(count - 1)]
    backward = [(target, source) for source, target in forward]
    low = lax.ppermute(lax.slice_in_dim(block, block.shape[0] - width, None, axis=0), SEQ_AXES, forward)
    high = lax.ppermute(lax.slice_in_dim(block, 0, width, axis=0), SEQ_AXES, backward)
    extra = (-(block.shape[0] + 2 * width)) % align
    fill = jnp.zeros((extra, block.shape[1]), block.dtype)
    return jnp.concatenate([low, block, high, fill], axis=0)


def convolve(padded, weight, row_count):
    conv_sum = jnp.dot(padded[0:row_count], weight[0], preferred_element_type=jnp.float32)
    for offset in range(1, weight.shape[0]):
        conv_sum = conv_sum + jnp.dot(
            padded[offset : offset + row_count], weight[offset], preferred_element_type=jnp.float32
        )
    return conv_sum


def head_rms(tensor):
    return tensor * lax.rsqrt(jnp.mean(tensor * tensor, axis=-1, keepdims=True) + 1e-06)


def head_norm(block, heads, head_size):
    parts = []
    for h in range(heads):
        part = block[:, h * head_size : (h + 1) * head_size]
        mean_sq = jnp.mean(part * part, axis=1, keepdims=True)
        parts.append(part * lax.rsqrt(mean_sq + 1e-06))
    return parts


def attend_kernel(heads, head_size, nk, qa_ref, qb_ref, hkv_ref, wk_ref, wvt_ref,
                  o_ref, st_ref, ob_ref, sb_ref, qt_sc, m_sc, l_sc, acc_sc):
    j = pl.program_id(0)
    contract_last = (((1,), (1,)), ((), ()))

    @pl.when(j == 0)
    def _():
        own = qa_ref.shape[1]
        qt_sc[:, :own] = qa_ref[...]
        qt_sc[:, own:] = qb_ref[...]
        m_sc[...] = jnp.full(m_sc.shape, -jnp.inf, jnp.float32)
        l_sc[...] = jnp.zeros(l_sc.shape, jnp.float32)
        acc_sc[...] = jnp.zeros(acc_sc.shape, jnp.float32)

    hkv = hkv_ref[...]
    k_all = jnp.dot(hkv, wk_ref[...], preferred_element_type=jnp.float32)
    v_t = lax.dot_general(wvt_ref[...], hkv, contract_last, preferred_element_type=jnp.float32)
    for h in range(heads):
        rows = slice(h * head_size, (h + 1) * head_size)
        k_h = k_all[:, rows]
        k_h = (k_h * lax.rsqrt(jnp.mean(k_h * k_h, axis=1, keepdims=True) + 1e-06)).astype(
            jnp.bfloat16
        )
        s_t = jnp.dot(k_h, qt_sc[rows, :], preferred_element_type=jnp.float32)
        m_prev = m_sc[h]
        m_next = jnp.maximum(m_prev, jnp.max(s_t, axis=0, keepdims=True))
        alpha = jnp.exp(m_prev - m_next)
        p_t = jnp.exp(s_t - m_next)
        l_sc[h] = alpha * l_sc[h] + jnp.sum(p_t, axis=0, keepdims=True)
        acc_sc[rows, :] = alpha * acc_sc[rows, :] + jnp.dot(
            v_t[rows, :].astype(jnp.bfloat16), p_t.astype(jnp.bfloat16),
            preferred_element_type=jnp.float32,
        )
        m_sc[h] = m_next

    @pl.when(j == nk - 1)
    def _():
        own = o_ref.shape[1]
        o_ref[...] = acc_sc[:, :own]
        ob_ref[...] = acc_sc[:, own:]
        for h in range(heads):
            st_ref[h : h + 1, :] = m_sc[h][:, :own]
            st_ref[heads + h : heads + h + 1, :] = l_sc[h][:, :own]
            sb_ref[h : h + 1, :] = m_sc[h][:, own:]
            sb_ref[heads + h : heads + h + 1, :] = l_sc[h][:, own:]


def attend_partial(qt_own, qt_other, hidden_kv, qkv_weight, wvt, heads, head_size, tk=2048):
    width, own = qt_own.shape
    q_rows = 2 * own
    k_rows, channels = hidden_kv.shape
    nk = k_rows // tk
    whole = lambda j: (0, 0)
    return pl.pallas_call(
        functools.partial(attend_kernel, heads, head_size, nk),
        grid=(nk,),
        in_specs=[
            pl.BlockSpec((width, own), whole),
            pl.BlockSpec((width, own), whole),
            pl.BlockSpec((tk, channels), lambda j: (j, 0)),
            pl.BlockSpec((channels, width), lambda j: (0, 1)),
            pl.BlockSpec((width, channels), whole),
        ],
        out_specs=[
            pl.BlockSpec((width, own), whole),
            pl.BlockSpec((2 * heads, own), whole),
        ] * 2,
        out_shape=[
            jax.ShapeDtypeStruct((width, own), jnp.float32),
            jax.ShapeDtypeStruct((2 * heads, own), jnp.float32),
        ] * 2,
        scratch_shapes=[
            pltpu.VMEM((width, q_rows), jnp.bfloat16),
            pltpu.VMEM((heads, 1, q_rows), jnp.float32),
            pltpu.VMEM((heads, 1, q_rows), jnp.float32),
            pltpu.VMEM((width, q_rows), jnp.float32),
        ],
        compiler_params=pltpu.CompilerParams(dimension_semantics=("arbitrary",)),
        cost_estimate=pl.CostEstimate(
            flops=4 * q_rows * k_rows * width + 2 * k_rows * channels * 2 * width,
            transcendentals=q_rows * k_rows * heads,
            bytes_accessed=k_rows * channels * 2 + q_rows * width * 8,
        ),
    )(qt_own, qt_other, hidden_kv, qkv_weight, wvt)


def finish_kernel(heads, head_size, o_ref, st_ref, og_ref, sg_ref, hid_ref, wo_ref, out_ref):
    st_own = st_ref[...]
    st_got = sg_ref[...]
    mixed = []
    for h in range(heads):
        rows = slice(h * head_size, (h + 1) * head_size)
        m_own = st_own[h : h + 1, :]
        m_got = st_got[h : h + 1, :]
        m_all = jnp.maximum(m_own, m_got)
        w_own = jnp.exp(m_own - m_all)
        w_got = jnp.exp(m_got - m_all)
        denom = st_own[heads + h : heads + h + 1, :] * w_own + st_got[heads + h : heads + h + 1, :] * w_got
        mixed.append((o_ref[rows, :] * w_own + og_ref[rows, :] * w_got) / denom)
    attended = jnp.concatenate(mixed, axis=0).T.astype(jnp.bfloat16)
    out = hid_ref[...].astype(jnp.float32) + jnp.dot(
        attended, wo_ref[...], preferred_element_type=jnp.float32
    )
    out_ref[...] = out.astype(out_ref.dtype)


def finish(o_part, st_part, o_got, st_got, hidden, out_weight, heads, head_size):
    rows, width_out = hidden.shape
    width = heads * head_size
    whole = lambda i: (0, 0)
    return pl.pallas_call(
        functools.partial(finish_kernel, heads, head_size),
        grid=(1,),
        in_specs=[
            pl.BlockSpec((width, rows), whole),
            pl.BlockSpec((2 * heads, rows), whole),
            pl.BlockSpec((width, rows), whole),
            pl.BlockSpec((2 * heads, rows), whole),
            pl.BlockSpec((rows, width_out), whole),
            pl.BlockSpec((width, width_out), whole),
        ],
        out_specs=pl.BlockSpec((rows, width_out), whole),
        out_shape=jax.ShapeDtypeStruct((rows, width_out), jnp.bfloat16),
    )(o_part, st_part, o_got, st_got, hidden, out_weight)


def ring_gather_kernel(side, heads, head_size, x_ref, h_ref, wq_ref, wv_ref, scale_ref,
                       out_ref, qt_ref, wvt_ref, send_sem, recv_sem, local_sem):
    me = lax.axis_index("zx")
    z, x = me // side, me % side
    half = x_ref.shape[1]
    q = half // 2
    mesh_ids = pl.DeviceIdType.MESH

    def slot(stream, a, b):
        a = lax.rem(a + side, side)
        b = lax.rem(b + side, side)
        return b * side + a if stream == 0 else a * side + b

    own = [(x, z), (z, x)]
    barrier = pltpu.get_barrier_semaphore()
    for target in (slot(0, x + 1, z), slot(0, x - 1, z), slot(1, z + 1, x), slot(1, z - 1, x)):
        pl.semaphore_signal(barrier, inc=1, device_id={"zx": target}, device_id_type=mesh_ids)
    proj = jnp.dot(h_ref[...], wq_ref[...], preferred_element_type=jnp.float32)
    scale = scale_ref[...]
    normed = []
    for h in range(heads):
        cols = slice(h * head_size, (h + 1) * head_size)
        part_q = proj[:, cols]
        mean_sq = jnp.mean(part_q * part_q, axis=1, keepdims=True)
        normed.append(part_q * lax.rsqrt(mean_sq + 1e-06) * scale[:, cols])
    qt_ref[...] = jnp.concatenate(normed, axis=1).T.astype(qt_ref.dtype)
    wvt_ref[...] = wv_ref[...].astype(jnp.float32).T.astype(wvt_ref.dtype)
    pl.semaphore_wait(barrier, 4)
    local = pltpu.make_async_copy(x_ref, out_ref.at[me], local_sem)
    local.start()

    sends = []
    index = {}

    def send(key, src, view, target):
        idx = len(index)
        index[key] = idx
        copy = pltpu.make_async_remote_copy(
            src_ref=src, dst_ref=view, send_sem=send_sem.at[idx], recv_sem=recv_sem.at[idx],
            device_id={"zx": target}, device_id_type=mesh_ids,
        )
        copy.start()
        sends.append(copy)

    def recv(key, view, source):
        idx = index[key]
        pltpu.make_async_remote_copy(
            src_ref=view, dst_ref=view, send_sem=send_sem.at[idx], recv_sem=recv_sem.at[idx],
            device_id={"zx": source}, device_id_type=mesh_ids,
        ).wait_recv()

    def part(stream, a, b, lo=None):
        view = out_ref.at[slot(stream, a, b), stream]
        return view if lo is None else view.at[pl.ds(lo, q)]

    def send_row(st, k):
        a0, b0 = own[st]
        src = x_ref.at[st] if k == 0 else part(st, a0 + k, b0)
        send((st, 3, 1, k), src, part(st, a0 + k, b0), slot(st, a0, b0 + 1))
        send((st, 3, -1, k), src, part(st, a0 + k, b0), slot(st, a0, b0 - 1))

    for st in range(2):
        a0, b0 = own[st]
        send((st, 1, 1), x_ref.at[st], part(st, a0, b0), slot(st, a0 + 1, b0))
        send((st, 1, -1), x_ref.at[st], part(st, a0, b0), slot(st, a0 - 1, b0))
        send_row(st, 0)
    for st in range(2):
        a0, b0 = own[st]
        recv((st, 1, 1), part(st, a0 - 1, b0), slot(st, a0 - 1, b0))
        recv((st, 1, -1), part(st, a0 + 1, b0), slot(st, a0 + 1, b0))
        send((st, 2, 1), part(st, a0 - 1, b0, 0), part(st, a0 - 1, b0, 0), slot(st, a0 + 1, b0))
        send((st, 2, -1), part(st, a0 + 1, b0, q), part(st, a0 + 1, b0, q), slot(st, a0 - 1, b0))
        send_row(st, 1)
        send_row(st, side - 1)
    for st in range(2):
        a0, b0 = own[st]
        recv((st, 2, 1), part(st, a0 - 2, b0, 0), slot(st, a0 - 1, b0))
        recv((st, 2, -1), part(st, a0 + 2, b0, q), slot(st, a0 + 1, b0))
        for k in range(2, side - 1):
            send_row(st, k)
    for st in range(2):
        a0, b0 = own[st]
        for k in range(side):
            recv((st, 3, 1, k), part(st, a0 + k, b0 - 1), slot(st, a0, b0 - 1))
            recv((st, 3, -1, k), part(st, a0 + k, b0 + 1), slot(st, a0, b0 + 1))
            send((st, 4, 1, k), part(st, a0 + k, b0 - 1, 0), part(st, a0 + k, b0 - 1, 0), slot(st, a0, b0 + 1))
            send((st, 4, -1, k), part(st, a0 + k, b0 + 1, q), part(st, a0 + k, b0 + 1, q), slot(st, a0, b0 - 1))
    for st in range(2):
        a0, b0 = own[st]
        for k in range(side):
            recv((st, 4, 1, k), part(st, a0 + k, b0 - 2, 0), slot(st, a0, b0 - 1))
            recv((st, 4, -1, k), part(st, a0 + k, b0 + 2, q), slot(st, a0, b0 + 1))
    local.wait()
    for copy in sends:
        copy.wait_send()


def gather_rows(block, qkv_weight, scale_row, heads, head_size, axis):
    n = lax.axis_size(axis)
    side = math.isqrt(n)
    rows, width = block.shape
    channels, width_qkv = qkv_weight.shape
    width_all = width_qkv // 3
    copies = 2 * (2 + 2 + 4 * side)
    whole = lambda i: (0, 0)
    out, qt, wvt = pl.pallas_call(
        functools.partial(ring_gather_kernel, side, heads, head_size),
        grid=(1,),
        in_specs=[
            pl.BlockSpec(memory_space=pl.ANY),
            pl.BlockSpec((rows, width), whole),
            pl.BlockSpec((channels, width_all), lambda i: (0, 0)),
            pl.BlockSpec((channels, width_all), lambda i: (0, 2)),
            pl.BlockSpec((1, width_all), whole),
        ],
        out_specs=[
            pl.BlockSpec(memory_space=pl.ANY),
            pl.BlockSpec((width_all, rows), whole),
            pl.BlockSpec((width_all, channels), whole),
        ],
        out_shape=[
            jax.ShapeDtypeStruct((n, 2, rows // 2, width), block.dtype),
            jax.ShapeDtypeStruct((width_all, rows), jnp.bfloat16),
            jax.ShapeDtypeStruct((width_all, channels), jnp.bfloat16),
        ],
        scratch_shapes=[
            pltpu.SemaphoreType.DMA((copies,)),
            pltpu.SemaphoreType.DMA((copies,)),
            pltpu.SemaphoreType.DMA,
        ],
        compiler_params=pltpu.CompilerParams(collective_id=0, has_side_effects=True),
    )(block.reshape(2, rows // 2, width), block, qkv_weight, qkv_weight, scale_row)
    return out.reshape(n * rows, width), qt, wvt


def conv_gelu_kernel(taps, rows, halo, x_ref, w_ref, o_ref, acc_sc):
    j = pl.program_id(0)
    product = jnp.dot(x_ref[...], w_ref[...], preferred_element_type=jnp.float32)
    for t in range(taps):

        @pl.when(j == t)
        def _():
            if t == 0:
                acc_sc[...] = product[t : t + rows]
            else:
                acc_sc[...] = acc_sc[...] + product[t : t + rows]

    @pl.when(j == taps - 1)
    def _():
        place = lax.axis_index(SEQ_AXES)
        last = lax.axis_size(SEQ_AXES) - 1
        row = lax.broadcasted_iota(jnp.int32, acc_sc.shape, 0)
        outside = jnp.logical_or(
            jnp.logical_and(place == 0, row < halo),
            jnp.logical_and(place == last, row >= rows - halo),
        )
        value = jax.nn.gelu(acc_sc[...])
        o_ref[...] = jnp.where(outside, 0.0, value).astype(o_ref.dtype)


def conv_gelu(padded, weight, halo):
    taps, channels, width = weight.shape
    rows = padded.shape[0] - taps + 1
    whole = lambda j: (0, 0)
    return pl.pallas_call(
        functools.partial(conv_gelu_kernel, taps, rows, halo),
        grid=(taps,),
        in_specs=[
            pl.BlockSpec(padded.shape, whole),
            pl.BlockSpec((None, channels, width), lambda j: (j, 0, 0)),
        ],
        out_specs=pl.BlockSpec((rows, width), whole),
        out_shape=jax.ShapeDtypeStruct((rows, width), jnp.bfloat16),
        scratch_shapes=[pltpu.VMEM((rows, width), jnp.float32)],
        compiler_params=pltpu.CompilerParams(
            dimension_semantics=("arbitrary",), vmem_limit_bytes=24 * 1024 * 1024
        ),
        cost_estimate=pl.CostEstimate(
            flops=2 * taps * padded.shape[0] * channels * width,
            transcendentals=rows * width,
            bytes_accessed=taps * channels * width * 2 + padded.size * 2 + rows * width * 2,
        ),
    )(padded, weight)


def body(sequence_input, conv_first, conv_second, qkv_weight, out_weight, logit_scale):
    row_count = sequence_input.shape[0]
    padded_input = padded_2(sequence_input, 4)
    padded_first = conv_gelu(padded_input, conv_first, 2)
    first_out = padded_first[2 : 2 + row_count]
    second = convolve(padded_first, conv_second, row_count)
    hidden = (first_out.astype(jnp.float32) + second).astype(jnp.bfloat16)
    head_count = logit_scale.shape[0]
    width_all = qkv_weight.shape[1] // 3
    head_size = width_all // head_count
    scale_row = jnp.repeat(logit_scale / math.sqrt(head_size), head_size)[None, :]

    swap = [(0, 1), (1, 0)]
    hidden_all, qt_own, wvt = gather_rows(hidden, qkv_weight, scale_row, head_count, head_size, "zx")
    qt_other = lax.ppermute(qt_own, "core", swap)
    o_part, st_part, o_send, st_send = attend_partial(
        qt_own, qt_other, hidden_all, qkv_weight, wvt, head_count, head_size
    )
    o_got, st_got = lax.ppermute((o_send, st_send), "core", swap)
    return finish(o_part, st_part, o_got, st_got, hidden, out_weight, head_count, head_size)


def solution(mesh):
    devices = np.asarray(mesh.devices)
    seq_size = mesh.shape["seq"]
    batch_size = mesh.shape["batch"]
    order = [mesh.axis_names.index("seq"), mesh.axis_names.index("batch")]
    devices = devices.transpose(order).reshape(seq_size // 2, 2, batch_size)
    split_mesh = Mesh(devices, ("zx", "core", "batch"))
    rows = P(("batch", "zx", "core"), None)
    in_specs = (rows, P(), P(), P(), P(), P())
    return jax.shard_map(body, mesh=split_mesh, in_specs=in_specs, out_specs=rows, check_vma=False)
```

```python
import functools
import math

import jax
import jax.numpy as jnp
import numpy as np
from jax import lax
from jax.experimental import pallas as pl
from jax.experimental.pallas import tpu as pltpu
from jax.sharding import Mesh
from jax.sharding import PartitionSpec as P

SEQ_AXES = ("zx", "core")


def padded_2(block, width, align=1):
    count = lax.axis_size(SEQ_AXES)
    forward = [(i, i + 1) for i in range(count - 1)]
    backward = [(target, source) for source, target in forward]
    low = lax.ppermute(lax.slice_in_dim(block, block.shape[0] - width, None, axis=0), SEQ_AXES, forward)
    high = lax.ppermute(lax.slice_in_dim(block, 0, width, axis=0), SEQ_AXES, backward)
    extra = (-(block.shape[0] + 2 * width)) % align
    fill = jnp.zeros((extra, block.shape[1]), block.dtype)
    return jnp.concatenate([low, block, high, fill], axis=0)


def convolve(padded, weight, row_count):
    conv_sum = jnp.dot(padded[0:row_count], weight[0], preferred_element_type=jnp.float32)
    for offset in range(1, weight.shape[0]):
        conv_sum = conv_sum + jnp.dot(
            padded[offset : offset + row_count], weight[offset], preferred_element_type=jnp.float32
        )
    return conv_sum


def head_rms(tensor):
    return tensor * lax.rsqrt(jnp.mean(tensor * tensor, axis=-1, keepdims=True) + 1e-06)


def head_norm(block, heads, head_size):
    parts = []
    for h in range(heads):
        part = block[:, h * head_size : (h + 1) * head_size]
        mean_sq = jnp.mean(part * part, axis=1, keepdims=True)
        parts.append(part * lax.rsqrt(mean_sq + 1e-06))
    return parts


def attend_kernel(heads, head_size, nk, qa_ref, qb_ref, hkv_ref, wk_ref, wvt_ref,
                  o_ref, st_ref, ob_ref, sb_ref, qt_sc, m_sc, l_sc, acc_sc):
    j = pl.program_id(0)
    contract_last = (((1,), (1,)), ((), ()))

    @pl.when(j == 0)
    def _():
        own = qa_ref.shape[1]
        qt_sc[:, :own] = qa_ref[...]
        qt_sc[:, own:] = qb_ref[...]
        m_sc[...] = jnp.full(m_sc.shape, -jnp.inf, jnp.float32)
        l_sc[...] = jnp.zeros(l_sc.shape, jnp.float32)
        acc_sc[...] = jnp.zeros(acc_sc.shape, jnp.float32)

    hkv = hkv_ref[...]
    k_all = jnp.dot(hkv, wk_ref[...], preferred_element_type=jnp.float32)
    v_t = lax.dot_general(wvt_ref[...], hkv, contract_last, preferred_element_type=jnp.float32)
    for h in range(heads):
        rows = slice(h * head_size, (h + 1) * head_size)
        k_h = k_all[:, rows]
        k_h = (k_h * lax.rsqrt(jnp.mean(k_h * k_h, axis=1, keepdims=True) + 1e-06)).astype(
            jnp.bfloat16
        )
        s_t = jnp.dot(k_h, qt_sc[rows, :], preferred_element_type=jnp.float32)
        m_prev = m_sc[h]
        m_next = jnp.maximum(m_prev, jnp.max(s_t, axis=0, keepdims=True))
        alpha = jnp.exp(m_prev - m_next)
        p_t = jnp.exp(s_t - m_next)
        l_sc[h] = alpha * l_sc[h] + jnp.sum(p_t, axis=0, keepdims=True)
        acc_sc[rows, :] = alpha * acc_sc[rows, :] + jnp.dot(
            v_t[rows, :].astype(jnp.bfloat16), p_t.astype(jnp.bfloat16),
            preferred_element_type=jnp.float32,
        )
        m_sc[h] = m_next

    @pl.when(j == nk - 1)
    def _():
        own = o_ref.shape[1]
        o_ref[...] = acc_sc[:, :own]
        ob_ref[...] = acc_sc[:, own:]
        for h in range(heads):
            st_ref[h : h + 1, :] = m_sc[h][:, :own]
            st_ref[heads + h : heads + h + 1, :] = l_sc[h][:, :own]
            sb_ref[h : h + 1, :] = m_sc[h][:, own:]
            sb_ref[heads + h : heads + h + 1, :] = l_sc[h][:, own:]


def attend_partial(qt_own, qt_other, hidden_kv, qkv_weight, wvt, heads, head_size, tk=2048):
    width, own = qt_own.shape
    q_rows = 2 * own
    k_rows, channels = hidden_kv.shape
    nk = k_rows // tk
    whole = lambda j: (0, 0)
    return pl.pallas_call(
        functools.partial(attend_kernel, heads, head_size, nk),
        grid=(nk,),
        in_specs=[
            pl.BlockSpec((width, own), whole),
            pl.BlockSpec((width, own), whole),
            pl.BlockSpec((tk, channels), lambda j: (j, 0)),
            pl.BlockSpec((channels, width), lambda j: (0, 1)),
            pl.BlockSpec((width, channels), whole),
        ],
        out_specs=[
            pl.BlockSpec((width, own), whole),
            pl.BlockSpec((2 * heads, own), whole),
        ] * 2,
        out_shape=[
            jax.ShapeDtypeStruct((width, own), jnp.float32),
            jax.ShapeDtypeStruct((2 * heads, own), jnp.float32),
        ] * 2,
        scratch_shapes=[
            pltpu.VMEM((width, q_rows), jnp.bfloat16),
            pltpu.VMEM((heads, 1, q_rows), jnp.float32),
            pltpu.VMEM((heads, 1, q_rows), jnp.float32),
            pltpu.VMEM((width, q_rows), jnp.float32),
        ],
        compiler_params=pltpu.CompilerParams(dimension_semantics=("arbitrary",)),
        cost_estimate=pl.CostEstimate(
            flops=4 * q_rows * k_rows * width + 2 * k_rows * channels * 2 * width,
            transcendentals=q_rows * k_rows * heads,
            bytes_accessed=k_rows * channels * 2 + q_rows * width * 8,
        ),
    )(qt_own, qt_other, hidden_kv, qkv_weight, wvt)


def finish_kernel(heads, head_size, o_ref, st_ref, og_ref, sg_ref, hid_ref, wo_ref, out_ref):
    st_own = st_ref[...]
    st_got = sg_ref[...]
    mixed = []
    for h in range(heads):
        rows = slice(h * head_size, (h + 1) * head_size)
        m_own = st_own[h : h + 1, :]
        m_got = st_got[h : h + 1, :]
        m_all = jnp.maximum(m_own, m_got)
        w_own = jnp.exp(m_own - m_all)
        w_got = jnp.exp(m_got - m_all)
        denom = st_own[heads + h : heads + h + 1, :] * w_own + st_got[heads + h : heads + h + 1, :] * w_got
        mixed.append((o_ref[rows, :] * w_own + og_ref[rows, :] * w_got) / denom)
    attended = jnp.concatenate(mixed, axis=0).T.astype(jnp.bfloat16)
    out = hid_ref[...].astype(jnp.float32) + jnp.dot(
        attended, wo_ref[...], preferred_element_type=jnp.float32
    )
    out_ref[...] = out.astype(out_ref.dtype)


def finish(o_part, st_part, o_got, st_got, hidden, out_weight, heads, head_size):
    rows, width_out = hidden.shape
    width = heads * head_size
    whole = lambda i: (0, 0)
    return pl.pallas_call(
        functools.partial(finish_kernel, heads, head_size),
        grid=(1,),
        in_specs=[
            pl.BlockSpec((width, rows), whole),
            pl.BlockSpec((2 * heads, rows), whole),
            pl.BlockSpec((width, rows), whole),
            pl.BlockSpec((2 * heads, rows), whole),
            pl.BlockSpec((rows, width_out), whole),
            pl.BlockSpec((width, width_out), whole),
        ],
        out_specs=pl.BlockSpec((rows, width_out), whole),
        out_shape=jax.ShapeDtypeStruct((rows, width_out), jnp.bfloat16),
    )(o_part, st_part, o_got, st_got, hidden, out_weight)


def ring_gather_kernel(side, heads, head_size, x_ref, h_ref, wq_ref, wv_ref, scale_ref,
                       out_ref, qt_ref, wvt_ref, qo_ref, send_sem, recv_sem, local_sem, pair_sem):
    me = lax.axis_index("zx")
    z, x = me // side, me % side
    half = x_ref.shape[1]
    q = half // 2
    mesh_ids = pl.DeviceIdType.MESH

    def slot(stream, a, b):
        a = lax.rem(a + side, side)
        b = lax.rem(b + side, side)
        return b * side + a if stream == 0 else a * side + b

    own = [(x, z), (z, x)]
    barrier = pltpu.get_barrier_semaphore()
    for target in (slot(0, x + 1, z), slot(0, x - 1, z), slot(1, z + 1, x), slot(1, z - 1, x)):
        pl.semaphore_signal(barrier, inc=1, device_id={"zx": target}, device_id_type=mesh_ids)
    sibling = 1 - lax.axis_index("core")
    pl.semaphore_signal(barrier, inc=1, device_id={"core": sibling}, device_id_type=mesh_ids)
    pl.semaphore_wait(barrier, 5)
    local = pltpu.make_async_copy(x_ref, out_ref.at[me], local_sem)
    local.start()

    sends = []
    index = {}

    def send(key, src, view, target):
        idx = len(index)
        index[key] = idx
        copy = pltpu.make_async_remote_copy(
            src_ref=src, dst_ref=view, send_sem=send_sem.at[idx], recv_sem=recv_sem.at[idx],
            device_id={"zx": target}, device_id_type=mesh_ids,
        )
        copy.start()
        sends.append(copy)

    def recv(key, view, source):
        idx = index[key]
        pltpu.make_async_remote_copy(
            src_ref=view, dst_ref=view, send_sem=send_sem.at[idx], recv_sem=recv_sem.at[idx],
            device_id={"zx": source}, device_id_type=mesh_ids,
        ).wait_recv()

    def part(stream, a, b, lo=None):
        view = out_ref.at[slot(stream, a, b), stream]
        return view if lo is None else view.at[pl.ds(lo, q)]

    def send_row(st, k):
        a0, b0 = own[st]
        src = x_ref.at[st] if k == 0 else part(st, a0 + k, b0)
        send((st, 3, 1, k), src, part(st, a0 + k, b0), slot(st, a0, b0 + 1))
        send((st, 3, -1, k), src, part(st, a0 + k, b0), slot(st, a0, b0 - 1))

    for st in range(2):
        a0, b0 = own[st]
        send((st, 1, 1), x_ref.at[st], part(st, a0, b0), slot(st, a0 + 1, b0))
        send((st, 1, -1), x_ref.at[st], part(st, a0, b0), slot(st, a0 - 1, b0))
        send_row(st, 0)
    for st in range(2):
        a0, b0 = own[st]
        recv((st, 1, 1), part(st, a0 - 1, b0), slot(st, a0 - 1, b0))
        recv((st, 1, -1), part(st, a0 + 1, b0), slot(st, a0 + 1, b0))
        send((st, 2, 1), part(st, a0 - 1, b0, 0), part(st, a0 - 1, b0, 0), slot(st, a0 + 1, b0))
        send((st, 2, -1), part(st, a0 + 1, b0, q), part(st, a0 + 1, b0, q), slot(st, a0 - 1, b0))
        send_row(st, 1)
        send_row(st, side - 1)
    for st in range(2):
        a0, b0 = own[st]
        recv((st, 2, 1), part(st, a0 - 2, b0, 0), slot(st, a0 - 1, b0))
        recv((st, 2, -1), part(st, a0 + 2, b0, q), slot(st, a0 + 1, b0))
        for k in range(2, side - 1):
            send_row(st, k)
    for st in range(2):
        a0, b0 = own[st]
        for k in range(side):
            recv((st, 3, 1, k), part(st, a0 + k, b0 - 1), slot(st, a0, b0 - 1))
            recv((st, 3, -1, k), part(st, a0 + k, b0 + 1), slot(st, a0, b0 + 1))
            send((st, 4, 1, k), part(st, a0 + k, b0 - 1, 0), part(st, a0 + k, b0 - 1, 0), slot(st, a0, b0 + 1))
            send((st, 4, -1, k), part(st, a0 + k, b0 + 1, q), part(st, a0 + k, b0 + 1, q), slot(st, a0, b0 - 1))
    proj = jnp.dot(h_ref[...], wq_ref[...], preferred_element_type=jnp.float32)
    scale = scale_ref[...]
    normed = []
    for h in range(heads):
        cols = slice(h * head_size, (h + 1) * head_size)
        part_q = proj[:, cols]
        mean_sq = jnp.mean(part_q * part_q, axis=1, keepdims=True)
        normed.append(part_q * lax.rsqrt(mean_sq + 1e-06) * scale[:, cols])
    qt_ref[...] = jnp.concatenate(normed, axis=1).T.astype(qt_ref.dtype)
    wvt_ref[...] = wv_ref[...].astype(jnp.float32).T.astype(wvt_ref.dtype)
    pair = pltpu.make_async_remote_copy(
        src_ref=qt_ref, dst_ref=qo_ref, send_sem=pair_sem.at[0], recv_sem=pair_sem.at[1],
        device_id={"core": sibling}, device_id_type=mesh_ids,
    )
    pair.start()
    for st in range(2):
        a0, b0 = own[st]
        for k in range(side):
            recv((st, 4, 1, k), part(st, a0 + k, b0 - 2, 0), slot(st, a0, b0 - 1))
            recv((st, 4, -1, k), part(st, a0 + k, b0 + 2, q), slot(st, a0, b0 + 1))
    pair.wait_send()
    pair.wait_recv()
    local.wait()
    for copy in sends:
        copy.wait_send()


def gather_rows(block, qkv_weight, scale_row, heads, head_size, axis):
    n = lax.axis_size(axis)
    side = math.isqrt(n)
    rows, width = block.shape
    channels, width_qkv = qkv_weight.shape
    width_all = width_qkv // 3
    copies = 2 * (2 + 2 + 4 * side)
    whole = lambda i: (0, 0)
    out, qt, wvt, qo = pl.pallas_call(
        functools.partial(ring_gather_kernel, side, heads, head_size),
        grid=(1,),
        in_specs=[
            pl.BlockSpec(memory_space=pl.ANY),
            pl.BlockSpec((rows, width), whole),
            pl.BlockSpec((channels, width_all), lambda i: (0, 0)),
            pl.BlockSpec((channels, width_all), lambda i: (0, 2)),
            pl.BlockSpec((1, width_all), whole),
        ],
        out_specs=[
            pl.BlockSpec(memory_space=pl.ANY),
            pl.BlockSpec((width_all, rows), whole),
            pl.BlockSpec((width_all, channels), whole),
            pl.BlockSpec(memory_space=pl.ANY),
        ],
        out_shape=[
            jax.ShapeDtypeStruct((n, 2, rows // 2, width), block.dtype),
            jax.ShapeDtypeStruct((width_all, rows), jnp.bfloat16),
            jax.ShapeDtypeStruct((width_all, channels), jnp.bfloat16),
            jax.ShapeDtypeStruct((width_all, rows), jnp.bfloat16),
        ],
        scratch_shapes=[
            pltpu.SemaphoreType.DMA((copies,)),
            pltpu.SemaphoreType.DMA((copies,)),
            pltpu.SemaphoreType.DMA,
            pltpu.SemaphoreType.DMA((2,)),
        ],
        compiler_params=pltpu.CompilerParams(collective_id=0, has_side_effects=True),
    )(block.reshape(2, rows // 2, width), block, qkv_weight, qkv_weight, scale_row)
    return out.reshape(n * rows, width), qt, wvt, qo


def conv_gelu_kernel(taps, rows, halo, x_ref, w_ref, o_ref, acc_sc):
    j = pl.program_id(0)
    product = jnp.dot(x_ref[...], w_ref[...], preferred_element_type=jnp.float32)
    for t in range(taps):

        @pl.when(j == t)
        def _():
            if t == 0:
                acc_sc[...] = product[t : t + rows]
            else:
                acc_sc[...] = acc_sc[...] + product[t : t + rows]

    @pl.when(j == taps - 1)
    def _():
        place = lax.axis_index(SEQ_AXES)
        last = lax.axis_size(SEQ_AXES) - 1
        row = lax.broadcasted_iota(jnp.int32, acc_sc.shape, 0)
        outside = jnp.logical_or(
            jnp.logical_and(place == 0, row < halo),
            jnp.logical_and(place == last, row >= rows - halo),
        )
        value = jax.nn.gelu(acc_sc[...])
        o_ref[...] = jnp.where(outside, 0.0, value).astype(o_ref.dtype)


def conv_gelu(padded, weight, halo):
    taps, channels, width = weight.shape
    rows = padded.shape[0] - taps + 1
    whole = lambda j: (0, 0)
    return pl.pallas_call(
        functools.partial(conv_gelu_kernel, taps, rows, halo),
        grid=(taps,),
        in_specs=[
            pl.BlockSpec(padded.shape, whole),
            pl.BlockSpec((None, channels, width), lambda j: (j, 0, 0)),
        ],
        out_specs=pl.BlockSpec((rows, width), whole),
        out_shape=jax.ShapeDtypeStruct((rows, width), jnp.bfloat16),
        scratch_shapes=[pltpu.VMEM((rows, width), jnp.float32)],
        compiler_params=pltpu.CompilerParams(
            dimension_semantics=("arbitrary",), vmem_limit_bytes=24 * 1024 * 1024
        ),
        cost_estimate=pl.CostEstimate(
            flops=2 * taps * padded.shape[0] * channels * width,
            transcendentals=rows * width,
            bytes_accessed=taps * channels * width * 2 + padded.size * 2 + rows * width * 2,
        ),
    )(padded, weight)


def body(sequence_input, conv_first, conv_second, qkv_weight, out_weight, logit_scale):
    row_count = sequence_input.shape[0]
    padded_input = padded_2(sequence_input, 4)
    padded_first = conv_gelu(padded_input, conv_first, 2)
    first_out = padded_first[2 : 2 + row_count]
    second = convolve(padded_first, conv_second, row_count)
    hidden = (first_out.astype(jnp.float32) + second).astype(jnp.bfloat16)
    head_count = logit_scale.shape[0]
    width_all = qkv_weight.shape[1] // 3
    head_size = width_all // head_count
    scale_row = jnp.repeat(logit_scale / math.sqrt(head_size), head_size)[None, :]

    swap = [(0, 1), (1, 0)]
    hidden_all, qt_own, wvt, qt_other = gather_rows(hidden, qkv_weight, scale_row, head_count, head_size, "zx")
    o_part, st_part, o_send, st_send = attend_partial(
        qt_own, qt_other, hidden_all, qkv_weight, wvt, head_count, head_size
    )
    o_got, st_got = lax.ppermute((o_send, st_send), "core", swap)
    return finish(o_part, st_part, o_got, st_got, hidden, out_weight, head_count, head_size)


def solution(mesh):
    devices = np.asarray(mesh.devices)
    seq_size = mesh.shape["seq"]
    batch_size = mesh.shape["batch"]
    order = [mesh.axis_names.index("seq"), mesh.axis_names.index("batch")]
    devices = devices.transpose(order).reshape(seq_size // 2, 2, batch_size)
    split_mesh = Mesh(devices, ("zx", "core", "batch"))
    rows = P(("batch", "zx", "core"), None)
    in_specs = (rows, P(), P(), P(), P(), P())
    return jax.shard_map(body, mesh=split_mesh, in_specs=in_specs, out_specs=rows, check_vma=False)
```

```python
import functools
import math

import jax
import jax.numpy as jnp
import numpy as np
from jax import lax
from jax.experimental import pallas as pl
from jax.experimental.pallas import tpu as pltpu
from jax.sharding import Mesh
from jax.sharding import PartitionSpec as P

SEQ_AXES = ("zx", "core")


def padded_2(block, width, align=1):
    count = lax.axis_size(SEQ_AXES)
    forward = [(i, i + 1) for i in range(count - 1)]
    backward = [(target, source) for source, target in forward]
    low = lax.ppermute(lax.slice_in_dim(block, block.shape[0] - width, None, axis=0), SEQ_AXES, forward)
    high = lax.ppermute(lax.slice_in_dim(block, 0, width, axis=0), SEQ_AXES, backward)
    extra = (-(block.shape[0] + 2 * width)) % align
    fill = jnp.zeros((extra, block.shape[1]), block.dtype)
    return jnp.concatenate([low, block, high, fill], axis=0)


def convolve(padded, weight, row_count):
    conv_sum = jnp.dot(padded[0:row_count], weight[0], preferred_element_type=jnp.float32)
    for offset in range(1, weight.shape[0]):
        conv_sum = conv_sum + jnp.dot(
            padded[offset : offset + row_count], weight[offset], preferred_element_type=jnp.float32
        )
    return conv_sum


def head_rms(tensor):
    return tensor * lax.rsqrt(jnp.mean(tensor * tensor, axis=-1, keepdims=True) + 1e-06)


def head_norm(block, heads, head_size):
    parts = []
    for h in range(heads):
        part = block[:, h * head_size : (h + 1) * head_size]
        mean_sq = jnp.mean(part * part, axis=1, keepdims=True)
        parts.append(part * lax.rsqrt(mean_sq + 1e-06))
    return parts


def attend_kernel(heads, head_size, nk, qa_ref, qb_ref, hkv_ref, wk_ref, wvt_ref,
                  o_ref, st_ref, og_ref, sg_ref, qt_sc, m_sc, l_sc, acc_sc, st_send, pair_sem):
    j = pl.program_id(0)
    contract_last = (((1,), (1,)), ((), ()))

    mesh_ids = pl.DeviceIdType.MESH
    sibling = 1 - lax.axis_index("core")

    @pl.when(j == 0)
    def _():
        barrier = pltpu.get_barrier_semaphore()
        pl.semaphore_signal(barrier, inc=1, device_id={"core": sibling}, device_id_type=mesh_ids)
        pl.semaphore_wait(barrier, 1)
        own = qa_ref.shape[1]
        qt_sc[:, :own] = qa_ref[...]
        qt_sc[:, own:] = qb_ref[...]
        m_sc[...] = jnp.full(m_sc.shape, -jnp.inf, jnp.float32)
        l_sc[...] = jnp.zeros(l_sc.shape, jnp.float32)
        acc_sc[...] = jnp.zeros(acc_sc.shape, jnp.float32)

    hkv = hkv_ref[...]
    k_all = jnp.dot(hkv, wk_ref[...], preferred_element_type=jnp.float32)
    v_t = lax.dot_general(wvt_ref[...], hkv, contract_last, preferred_element_type=jnp.float32)
    for h in range(heads):
        rows = slice(h * head_size, (h + 1) * head_size)
        k_h = k_all[:, rows]
        k_h = (k_h * lax.rsqrt(jnp.mean(k_h * k_h, axis=1, keepdims=True) + 1e-06)).astype(
            jnp.bfloat16
        )
        s_t = jnp.dot(k_h, qt_sc[rows, :], preferred_element_type=jnp.float32)
        m_prev = m_sc[h]
        m_next = jnp.maximum(m_prev, jnp.max(s_t, axis=0, keepdims=True))
        alpha = jnp.exp(m_prev - m_next)
        p_t = jnp.exp(s_t - m_next)
        l_sc[h] = alpha * l_sc[h] + jnp.sum(p_t, axis=0, keepdims=True)
        acc_sc[rows, :] = alpha * acc_sc[rows, :] + jnp.dot(
            v_t[rows, :].astype(jnp.bfloat16), p_t.astype(jnp.bfloat16),
            preferred_element_type=jnp.float32,
        )
        m_sc[h] = m_next

    @pl.when(j == nk - 1)
    def _():
        own = o_ref.shape[1]
        for h in range(heads):
            st_send[h : h + 1, :] = m_sc[h][:, own:]
            st_send[heads + h : heads + h + 1, :] = l_sc[h][:, own:]
        copies = [
            pltpu.make_async_remote_copy(
                src_ref=src, dst_ref=dst, send_sem=pair_sem.at[0, i], recv_sem=pair_sem.at[1, i],
                device_id={"core": sibling}, device_id_type=mesh_ids,
            )
            for i, (src, dst) in enumerate(((acc_sc.at[:, pl.ds(own, own)], og_ref), (st_send, sg_ref)))
        ]
        for copy in copies:
            copy.start()
        o_ref[...] = acc_sc[:, :own]
        for h in range(heads):
            st_ref[h : h + 1, :] = m_sc[h][:, :own]
            st_ref[heads + h : heads + h + 1, :] = l_sc[h][:, :own]
        for copy in copies:
            copy.wait_send()
            copy.wait_recv()


def attend_partial(qt_own, qt_other, hidden_kv, qkv_weight, wvt, heads, head_size, tk=2048):
    width, own = qt_own.shape
    q_rows = 2 * own
    k_rows, channels = hidden_kv.shape
    nk = k_rows // tk
    whole = lambda j: (0, 0)
    return pl.pallas_call(
        functools.partial(attend_kernel, heads, head_size, nk),
        grid=(nk,),
        in_specs=[
            pl.BlockSpec((width, own), whole),
            pl.BlockSpec((width, own), whole),
            pl.BlockSpec((tk, channels), lambda j: (j, 0)),
            pl.BlockSpec((channels, width), lambda j: (0, 1)),
            pl.BlockSpec((width, channels), whole),
        ],
        out_specs=[
            pl.BlockSpec((width, own), whole),
            pl.BlockSpec((2 * heads, own), whole),
            pl.BlockSpec(memory_space=pl.ANY),
            pl.BlockSpec(memory_space=pl.ANY),
        ],
        out_shape=[
            jax.ShapeDtypeStruct((width, own), jnp.float32),
            jax.ShapeDtypeStruct((2 * heads, own), jnp.float32),
        ] * 2,
        scratch_shapes=[
            pltpu.VMEM((width, q_rows), jnp.bfloat16),
            pltpu.VMEM((heads, 1, q_rows), jnp.float32),
            pltpu.VMEM((heads, 1, q_rows), jnp.float32),
            pltpu.VMEM((width, q_rows), jnp.float32),
            pltpu.VMEM((2 * heads, own), jnp.float32),
            pltpu.SemaphoreType.DMA((2, 2)),
        ],
        compiler_params=pltpu.CompilerParams(
            dimension_semantics=("arbitrary",), collective_id=1, has_side_effects=True
        ),
        cost_estimate=pl.CostEstimate(
            flops=4 * q_rows * k_rows * width + 2 * k_rows * channels * 2 * width,
            transcendentals=q_rows * k_rows * heads,
            bytes_accessed=k_rows * channels * 2 + q_rows * width * 8,
        ),
    )(qt_own, qt_other, hidden_kv, qkv_weight, wvt)


def finish_kernel(heads, head_size, o_ref, st_ref, og_ref, sg_ref, hid_ref, wo_ref, out_ref):
    st_own = st_ref[...]
    st_got = sg_ref[...]
    mixed = []
    for h in range(heads):
        rows = slice(h * head_size, (h + 1) * head_size)
        m_own = st_own[h : h + 1, :]
        m_got = st_got[h : h + 1, :]
        m_all = jnp.maximum(m_own, m_got)
        w_own = jnp.exp(m_own - m_all)
        w_got = jnp.exp(m_got - m_all)
        denom = st_own[heads + h : heads + h + 1, :] * w_own + st_got[heads + h : heads + h + 1, :] * w_got
        mixed.append((o_ref[rows, :] * w_own + og_ref[rows, :] * w_got) / denom)
    attended = jnp.concatenate(mixed, axis=0).T.astype(jnp.bfloat16)
    out = hid_ref[...].astype(jnp.float32) + jnp.dot(
        attended, wo_ref[...], preferred_element_type=jnp.float32
    )
    out_ref[...] = out.astype(out_ref.dtype)


def finish(o_part, st_part, o_got, st_got, hidden, out_weight, heads, head_size):
    rows, width_out = hidden.shape
    width = heads * head_size
    whole = lambda i: (0, 0)
    return pl.pallas_call(
        functools.partial(finish_kernel, heads, head_size),
        grid=(1,),
        in_specs=[
            pl.BlockSpec((width, rows), whole),
            pl.BlockSpec((2 * heads, rows), whole),
            pl.BlockSpec((width, rows), whole),
            pl.BlockSpec((2 * heads, rows), whole),
            pl.BlockSpec((rows, width_out), whole),
            pl.BlockSpec((width, width_out), whole),
        ],
        out_specs=pl.BlockSpec((rows, width_out), whole),
        out_shape=jax.ShapeDtypeStruct((rows, width_out), jnp.bfloat16),
    )(o_part, st_part, o_got, st_got, hidden, out_weight)


def ring_gather_kernel(side, heads, head_size, x_ref, h_ref, wq_ref, wv_ref, scale_ref,
                       out_ref, qt_ref, wvt_ref, qo_ref, send_sem, recv_sem, local_sem, pair_sem):
    me = lax.axis_index("zx")
    z, x = me // side, me % side
    half = x_ref.shape[1]
    q = half // 2
    mesh_ids = pl.DeviceIdType.MESH

    def slot(stream, a, b):
        a = lax.rem(a + side, side)
        b = lax.rem(b + side, side)
        return b * side + a if stream == 0 else a * side + b

    own = [(x, z), (z, x)]
    barrier = pltpu.get_barrier_semaphore()
    for target in (slot(0, x + 1, z), slot(0, x - 1, z), slot(1, z + 1, x), slot(1, z - 1, x)):
        pl.semaphore_signal(barrier, inc=1, device_id={"zx": target}, device_id_type=mesh_ids)
    sibling = 1 - lax.axis_index("core")
    pl.semaphore_signal(barrier, inc=1, device_id={"core": sibling}, device_id_type=mesh_ids)
    pl.semaphore_wait(barrier, 5)
    local = pltpu.make_async_copy(x_ref, out_ref.at[me], local_sem)
    local.start()

    sends = []
    index = {}

    def send(key, src, view, target):
        idx = len(index)
        index[key] = idx
        copy = pltpu.make_async_remote_copy(
            src_ref=src, dst_ref=view, send_sem=send_sem.at[idx], recv_sem=recv_sem.at[idx],
            device_id={"zx": target}, device_id_type=mesh_ids,
        )
        copy.start()
        sends.append(copy)

    def recv(key, view, source):
        idx = index[key]
        pltpu.make_async_remote_copy(
            src_ref=view, dst_ref=view, send_sem=send_sem.at[idx], recv_sem=recv_sem.at[idx],
            device_id={"zx": source}, device_id_type=mesh_ids,
        ).wait_recv()

    def part(stream, a, b, lo=None):
        view = out_ref.at[slot(stream, a, b), stream]
        return view if lo is None else view.at[pl.ds(lo, q)]

    def send_row(st, k):
        a0, b0 = own[st]
        src = x_ref.at[st] if k == 0 else part(st, a0 + k, b0)
        send((st, 3, 1, k), src, part(st, a0 + k, b0), slot(st, a0, b0 + 1))
        send((st, 3, -1, k), src, part(st, a0 + k, b0), slot(st, a0, b0 - 1))

    for st in range(2):
        a0, b0 = own[st]
        send((st, 1, 1), x_ref.at[st], part(st, a0, b0), slot(st, a0 + 1, b0))
        send((st, 1, -1), x_ref.at[st], part(st, a0, b0), slot(st, a0 - 1, b0))
        send_row(st, 0)
    for st in range(2):
        a0, b0 = own[st]
        recv((st, 1, 1), part(st, a0 - 1, b0), slot(st, a0 - 1, b0))
        recv((st, 1, -1), part(st, a0 + 1, b0), slot(st, a0 + 1, b0))
        send((st, 2, 1), part(st, a0 - 1, b0, 0), part(st, a0 - 1, b0, 0), slot(st, a0 + 1, b0))
        send((st, 2, -1), part(st, a0 + 1, b0, q), part(st, a0 + 1, b0, q), slot(st, a0 - 1, b0))
        send_row(st, 1)
        send_row(st, side - 1)
    for st in range(2):
        a0, b0 = own[st]
        recv((st, 2, 1), part(st, a0 - 2, b0, 0), slot(st, a0 - 1, b0))
        recv((st, 2, -1), part(st, a0 + 2, b0, q), slot(st, a0 + 1, b0))
        for k in range(2, side - 1):
            send_row(st, k)
    for st in range(2):
        a0, b0 = own[st]
        for k in range(side):
            recv((st, 3, 1, k), part(st, a0 + k, b0 - 1), slot(st, a0, b0 - 1))
            recv((st, 3, -1, k), part(st, a0 + k, b0 + 1), slot(st, a0, b0 + 1))
            send((st, 4, 1, k), part(st, a0 + k, b0 - 1, 0), part(st, a0 + k, b0 - 1, 0), slot(st, a0, b0 + 1))
            send((st, 4, -1, k), part(st, a0 + k, b0 + 1, q), part(st, a0 + k, b0 + 1, q), slot(st, a0, b0 - 1))
    proj = jnp.dot(h_ref[...], wq_ref[...], preferred_element_type=jnp.float32)
    scale = scale_ref[...]
    normed = []
    for h in range(heads):
        cols = slice(h * head_size, (h + 1) * head_size)
        part_q = proj[:, cols]
        mean_sq = jnp.mean(part_q * part_q, axis=1, keepdims=True)
        normed.append(part_q * lax.rsqrt(mean_sq + 1e-06) * scale[:, cols])
    qt_ref[...] = jnp.concatenate(normed, axis=1).T.astype(qt_ref.dtype)
    wvt_ref[...] = wv_ref[...].astype(jnp.float32).T.astype(wvt_ref.dtype)
    pair = pltpu.make_async_remote_copy(
        src_ref=qt_ref, dst_ref=qo_ref, send_sem=pair_sem.at[0], recv_sem=pair_sem.at[1],
        device_id={"core": sibling}, device_id_type=mesh_ids,
    )
    pair.start()
    for st in range(2):
        a0, b0 = own[st]
        for k in range(side):
            recv((st, 4, 1, k), part(st, a0 + k, b0 - 2, 0), slot(st, a0, b0 - 1))
            recv((st, 4, -1, k), part(st, a0 + k, b0 + 2, q), slot(st, a0, b0 + 1))
    pair.wait_send()
    pair.wait_recv()
    local.wait()
    for copy in sends:
        copy.wait_send()


def gather_rows(block, qkv_weight, scale_row, heads, head_size, axis):
    n = lax.axis_size(axis)
    side = math.isqrt(n)
    rows, width = block.shape
    channels, width_qkv = qkv_weight.shape
    width_all = width_qkv // 3
    copies = 2 * (2 + 2 + 4 * side)
    whole = lambda i: (0, 0)
    out, qt, wvt, qo = pl.pallas_call(
        functools.partial(ring_gather_kernel, side, heads, head_size),
        grid=(1,),
        in_specs=[
            pl.BlockSpec(memory_space=pl.ANY),
            pl.BlockSpec((rows, width), whole),
            pl.BlockSpec((channels, width_all), lambda i: (0, 0)),
            pl.BlockSpec((channels, width_all), lambda i: (0, 2)),
            pl.BlockSpec((1, width_all), whole),
        ],
        out_specs=[
            pl.BlockSpec(memory_space=pl.ANY),
            pl.BlockSpec((width_all, rows), whole),
            pl.BlockSpec((width_all, channels), whole),
            pl.BlockSpec(memory_space=pl.ANY),
        ],
        out_shape=[
            jax.ShapeDtypeStruct((n, 2, rows // 2, width), block.dtype),
            jax.ShapeDtypeStruct((width_all, rows), jnp.bfloat16),
            jax.ShapeDtypeStruct((width_all, channels), jnp.bfloat16),
            jax.ShapeDtypeStruct((width_all, rows), jnp.bfloat16),
        ],
        scratch_shapes=[
            pltpu.SemaphoreType.DMA((copies,)),
            pltpu.SemaphoreType.DMA((copies,)),
            pltpu.SemaphoreType.DMA,
            pltpu.SemaphoreType.DMA((2,)),
        ],
        compiler_params=pltpu.CompilerParams(collective_id=0, has_side_effects=True),
    )(block.reshape(2, rows // 2, width), block, qkv_weight, qkv_weight, scale_row)
    return out.reshape(n * rows, width), qt, wvt, qo


def conv_gelu_kernel(taps, rows, halo, x_ref, w_ref, o_ref, acc_sc):
    j = pl.program_id(0)
    product = jnp.dot(x_ref[...], w_ref[...], preferred_element_type=jnp.float32)
    for t in range(taps):

        @pl.when(j == t)
        def _():
            if t == 0:
                acc_sc[...] = product[t : t + rows]
            else:
                acc_sc[...] = acc_sc[...] + product[t : t + rows]

    @pl.when(j == taps - 1)
    def _():
        place = lax.axis_index(SEQ_AXES)
        last = lax.axis_size(SEQ_AXES) - 1
        row = lax.broadcasted_iota(jnp.int32, acc_sc.shape, 0)
        outside = jnp.logical_or(
            jnp.logical_and(place == 0, row < halo),
            jnp.logical_and(place == last, row >= rows - halo),
        )
        value = jax.nn.gelu(acc_sc[...])
        o_ref[...] = jnp.where(outside, 0.0, value).astype(o_ref.dtype)


def conv_gelu(padded, weight, halo):
    taps, channels, width = weight.shape
    rows = padded.shape[0] - taps + 1
    whole = lambda j: (0, 0)
    return pl.pallas_call(
        functools.partial(conv_gelu_kernel, taps, rows, halo),
        grid=(taps,),
        in_specs=[
            pl.BlockSpec(padded.shape, whole),
            pl.BlockSpec((None, channels, width), lambda j: (j, 0, 0)),
        ],
        out_specs=pl.BlockSpec((rows, width), whole),
        out_shape=jax.ShapeDtypeStruct((rows, width), jnp.bfloat16),
        scratch_shapes=[pltpu.VMEM((rows, width), jnp.float32)],
        compiler_params=pltpu.CompilerParams(
            dimension_semantics=("arbitrary",), vmem_limit_bytes=24 * 1024 * 1024
        ),
        cost_estimate=pl.CostEstimate(
            flops=2 * taps * padded.shape[0] * channels * width,
            transcendentals=rows * width,
            bytes_accessed=taps * channels * width * 2 + padded.size * 2 + rows * width * 2,
        ),
    )(padded, weight)


def body(sequence_input, conv_first, conv_second, qkv_weight, out_weight, logit_scale):
    row_count = sequence_input.shape[0]
    padded_input = padded_2(sequence_input, 4)
    padded_first = conv_gelu(padded_input, conv_first, 2)
    first_out = padded_first[2 : 2 + row_count]
    second = convolve(padded_first, conv_second, row_count)
    hidden = (first_out.astype(jnp.float32) + second).astype(jnp.bfloat16)
    head_count = logit_scale.shape[0]
    width_all = qkv_weight.shape[1] // 3
    head_size = width_all // head_count
    scale_row = jnp.repeat(logit_scale / math.sqrt(head_size), head_size)[None, :]

    swap = [(0, 1), (1, 0)]
    hidden_all, qt_own, wvt, qt_other = gather_rows(hidden, qkv_weight, scale_row, head_count, head_size, "zx")
    o_part, st_part, o_got, st_got = attend_partial(
        qt_own, qt_other, hidden_all, qkv_weight, wvt, head_count, head_size
    )
    return finish(o_part, st_part, o_got, st_got, hidden, out_weight, head_count, head_size)


def solution(mesh):
    devices = np.asarray(mesh.devices)
    seq_size = mesh.shape["seq"]
    batch_size = mesh.shape["batch"]
    order = [mesh.axis_names.index("seq"), mesh.axis_names.index("batch")]
    devices = devices.transpose(order).reshape(seq_size // 2, 2, batch_size)
    split_mesh = Mesh(devices, ("zx", "core", "batch"))
    rows = P(("batch", "zx", "core"), None)
    in_specs = (rows, P(), P(), P(), P(), P())
    return jax.shard_map(body, mesh=split_mesh, in_specs=in_specs, out_specs=rows, check_vma=False)
```

```python
import functools
import math

import jax
import jax.numpy as jnp
import numpy as np
from jax import lax
from jax.experimental import pallas as pl
from jax.experimental.pallas import tpu as pltpu
from jax.sharding import Mesh
from jax.sharding import PartitionSpec as P

SEQ_AXES = ("zx", "core")


def padded_2(block, width, align=1):
    count = lax.axis_size(SEQ_AXES)
    forward = [(i, i + 1) for i in range(count - 1)]
    backward = [(target, source) for source, target in forward]
    low = lax.ppermute(lax.slice_in_dim(block, block.shape[0] - width, None, axis=0), SEQ_AXES, forward)
    high = lax.ppermute(lax.slice_in_dim(block, 0, width, axis=0), SEQ_AXES, backward)
    extra = (-(block.shape[0] + 2 * width)) % align
    fill = jnp.zeros((extra, block.shape[1]), block.dtype)
    return jnp.concatenate([low, block, high, fill], axis=0)


def convolve(padded, weight, row_count):
    conv_sum = jnp.dot(padded[0:row_count], weight[0], preferred_element_type=jnp.float32)
    for offset in range(1, weight.shape[0]):
        conv_sum = conv_sum + jnp.dot(
            padded[offset : offset + row_count], weight[offset], preferred_element_type=jnp.float32
        )
    return conv_sum


def head_rms(tensor):
    return tensor * lax.rsqrt(jnp.mean(tensor * tensor, axis=-1, keepdims=True) + 1e-06)


def head_norm(block, heads, head_size):
    parts = []
    for h in range(heads):
        part = block[:, h * head_size : (h + 1) * head_size]
        mean_sq = jnp.mean(part * part, axis=1, keepdims=True)
        parts.append(part * lax.rsqrt(mean_sq + 1e-06))
    return parts


def attend_kernel(heads, head_size, nk, qa_ref, qb_ref, hkv_ref, wk_ref, wvt_ref, hid_ref, wo_ref,
                  out_ref, qt_sc, m_sc, l_sc, acc_sc, st_send, og_sc, sg_sc, pair_sem):
    j = pl.program_id(0)
    contract_last = (((1,), (1,)), ((), ()))

    mesh_ids = pl.DeviceIdType.MESH
    sibling = 1 - lax.axis_index("core")

    @pl.when(j == 0)
    def _():
        barrier = pltpu.get_barrier_semaphore()
        pl.semaphore_signal(barrier, inc=1, device_id={"core": sibling}, device_id_type=mesh_ids)
        pl.semaphore_wait(barrier, 1)
        own = qa_ref.shape[1]
        qt_sc[:, :own] = qa_ref[...]
        qt_sc[:, own:] = qb_ref[...]
        m_sc[...] = jnp.full(m_sc.shape, -jnp.inf, jnp.float32)
        l_sc[...] = jnp.zeros(l_sc.shape, jnp.float32)
        acc_sc[...] = jnp.zeros(acc_sc.shape, jnp.float32)

    hkv = hkv_ref[...]
    k_all = jnp.dot(hkv, wk_ref[...], preferred_element_type=jnp.float32)
    v_t = lax.dot_general(wvt_ref[...], hkv, contract_last, preferred_element_type=jnp.float32)
    for h in range(heads):
        rows = slice(h * head_size, (h + 1) * head_size)
        k_h = k_all[:, rows]
        k_h = (k_h * lax.rsqrt(jnp.mean(k_h * k_h, axis=1, keepdims=True) + 1e-06)).astype(
            jnp.bfloat16
        )
        s_t = jnp.dot(k_h, qt_sc[rows, :], preferred_element_type=jnp.float32)
        m_prev = m_sc[h]
        m_next = jnp.maximum(m_prev, jnp.max(s_t, axis=0, keepdims=True))
        alpha = jnp.exp(m_prev - m_next)
        p_t = jnp.exp(s_t - m_next)
        l_sc[h] = alpha * l_sc[h] + jnp.sum(p_t, axis=0, keepdims=True)
        acc_sc[rows, :] = alpha * acc_sc[rows, :] + jnp.dot(
            v_t[rows, :].astype(jnp.bfloat16), p_t.astype(jnp.bfloat16),
            preferred_element_type=jnp.float32,
        )
        m_sc[h] = m_next

    @pl.when(j == nk - 1)
    def _():
        own = qa_ref.shape[1]
        for h in range(heads):
            st_send[h : h + 1, :] = m_sc[h][:, own:]
            st_send[heads + h : heads + h + 1, :] = l_sc[h][:, own:]
        copies = [
            pltpu.make_async_remote_copy(
                src_ref=src, dst_ref=dst, send_sem=pair_sem.at[0, i], recv_sem=pair_sem.at[1, i],
                device_id={"core": sibling}, device_id_type=mesh_ids,
            )
            for i, (src, dst) in enumerate(((acc_sc.at[:, pl.ds(own, own)], og_sc), (st_send, sg_sc)))
        ]
        for copy in copies:
            copy.start()
        for copy in copies:
            copy.wait_send()
            copy.wait_recv()
        st_got = sg_sc[...]
        mixed = []
        for h in range(heads):
            rows = slice(h * head_size, (h + 1) * head_size)
            m_own = m_sc[h][:, :own]
            m_got = st_got[h : h + 1, :]
            m_all = jnp.maximum(m_own, m_got)
            w_own = jnp.exp(m_own - m_all)
            w_got = jnp.exp(m_got - m_all)
            denom = l_sc[h][:, :own] * w_own + st_got[heads + h : heads + h + 1, :] * w_got
            mixed.append((acc_sc[rows, :own] * w_own + og_sc[rows, :] * w_got) / denom)
        attended = jnp.concatenate(mixed, axis=0).T.astype(jnp.bfloat16)
        out = hid_ref[...].astype(jnp.float32) + jnp.dot(
            attended, wo_ref[...], preferred_element_type=jnp.float32
        )
        out_ref[...] = out.astype(out_ref.dtype)


def attend_partial(qt_own, qt_other, hidden_kv, qkv_weight, wvt, hidden, out_weight, heads, head_size, tk=2048):
    width, own = qt_own.shape
    q_rows = 2 * own
    k_rows, channels = hidden_kv.shape
    nk = k_rows // tk
    whole = lambda j: (0, 0)
    return pl.pallas_call(
        functools.partial(attend_kernel, heads, head_size, nk),
        grid=(nk,),
        in_specs=[
            pl.BlockSpec((width, own), whole),
            pl.BlockSpec((width, own), whole),
            pl.BlockSpec((tk, channels), lambda j: (j, 0)),
            pl.BlockSpec((channels, width), lambda j: (0, 1)),
            pl.BlockSpec((width, channels), whole),
            pl.BlockSpec(hidden.shape, whole),
            pl.BlockSpec(out_weight.shape, whole),
        ],
        out_specs=pl.BlockSpec(hidden.shape, whole),
        out_shape=jax.ShapeDtypeStruct(hidden.shape, jnp.bfloat16),
        scratch_shapes=[
            pltpu.VMEM((width, q_rows), jnp.bfloat16),
            pltpu.VMEM((heads, 1, q_rows), jnp.float32),
            pltpu.VMEM((heads, 1, q_rows), jnp.float32),
            pltpu.VMEM((width, q_rows), jnp.float32),
            pltpu.VMEM((2 * heads, own), jnp.float32),
            pltpu.VMEM((width, own), jnp.float32),
            pltpu.VMEM((2 * heads, own), jnp.float32),
            pltpu.SemaphoreType.DMA((2, 2)),
        ],
        compiler_params=pltpu.CompilerParams(
            dimension_semantics=("arbitrary",), collective_id=1, has_side_effects=True
        ),
        cost_estimate=pl.CostEstimate(
            flops=4 * q_rows * k_rows * width + 2 * k_rows * channels * 2 * width,
            transcendentals=q_rows * k_rows * heads,
            bytes_accessed=k_rows * channels * 2 + q_rows * width * 8,
        ),
    )(qt_own, qt_other, hidden_kv, qkv_weight, wvt, hidden, out_weight)


def finish_kernel(heads, head_size, o_ref, st_ref, og_ref, sg_ref, hid_ref, wo_ref, out_ref):
    st_own = st_ref[...]
    st_got = sg_ref[...]
    mixed = []
    for h in range(heads):
        rows = slice(h * head_size, (h + 1) * head_size)
        m_own = st_own[h : h + 1, :]
        m_got = st_got[h : h + 1, :]
        m_all = jnp.maximum(m_own, m_got)
        w_own = jnp.exp(m_own - m_all)
        w_got = jnp.exp(m_got - m_all)
        denom = st_own[heads + h : heads + h + 1, :] * w_own + st_got[heads + h : heads + h + 1, :] * w_got
        mixed.append((o_ref[rows, :] * w_own + og_ref[rows, :] * w_got) / denom)
    attended = jnp.concatenate(mixed, axis=0).T.astype(jnp.bfloat16)
    out = hid_ref[...].astype(jnp.float32) + jnp.dot(
        attended, wo_ref[...], preferred_element_type=jnp.float32
    )
    out_ref[...] = out.astype(out_ref.dtype)


def finish(o_part, st_part, o_got, st_got, hidden, out_weight, heads, head_size):
    rows, width_out = hidden.shape
    width = heads * head_size
    whole = lambda i: (0, 0)
    return pl.pallas_call(
        functools.partial(finish_kernel, heads, head_size),
        grid=(1,),
        in_specs=[
            pl.BlockSpec((width, rows), whole),
            pl.BlockSpec((2 * heads, rows), whole),
            pl.BlockSpec((width, rows), whole),
            pl.BlockSpec((2 * heads, rows), whole),
            pl.BlockSpec((rows, width_out), whole),
            pl.BlockSpec((width, width_out), whole),
        ],
        out_specs=pl.BlockSpec((rows, width_out), whole),
        out_shape=jax.ShapeDtypeStruct((rows, width_out), jnp.bfloat16),
    )(o_part, st_part, o_got, st_got, hidden, out_weight)


def ring_gather_kernel(side, heads, head_size, x_ref, h_ref, wq_ref, wv_ref, scale_ref,
                       out_ref, qt_ref, wvt_ref, qo_ref, send_sem, recv_sem, local_sem, pair_sem):
    me = lax.axis_index("zx")
    z, x = me // side, me % side
    half = x_ref.shape[1]
    q = half // 2
    mesh_ids = pl.DeviceIdType.MESH

    def slot(stream, a, b):
        a = lax.rem(a + side, side)
        b = lax.rem(b + side, side)
        return b * side + a if stream == 0 else a * side + b

    own = [(x, z), (z, x)]
    barrier = pltpu.get_barrier_semaphore()
    for target in (slot(0, x + 1, z), slot(0, x - 1, z), slot(1, z + 1, x), slot(1, z - 1, x)):
        pl.semaphore_signal(barrier, inc=1, device_id={"zx": target}, device_id_type=mesh_ids)
    sibling = 1 - lax.axis_index("core")
    pl.semaphore_signal(barrier, inc=1, device_id={"core": sibling}, device_id_type=mesh_ids)
    pl.semaphore_wait(barrier, 5)
    local = pltpu.make_async_copy(x_ref, out_ref.at[me], local_sem)
    local.start()

    sends = []
    index = {}

    def send(key, src, view, target):
        idx = len(index)
        index[key] = idx
        copy = pltpu.make_async_remote_copy(
            src_ref=src, dst_ref=view, send_sem=send_sem.at[idx], recv_sem=recv_sem.at[idx],
            device_id={"zx": target}, device_id_type=mesh_ids,
        )
        copy.start()
        sends.append(copy)

    def recv(key, view, source):
        idx = index[key]
        pltpu.make_async_remote_copy(
            src_ref=view, dst_ref=view, send_sem=send_sem.at[idx], recv_sem=recv_sem.at[idx],
            device_id={"zx": source}, device_id_type=mesh_ids,
        ).wait_recv()

    def part(stream, a, b, lo=None):
        view = out_ref.at[slot(stream, a, b), stream]
        return view if lo is None else view.at[pl.ds(lo, q)]

    def send_row(st, k):
        a0, b0 = own[st]
        src = x_ref.at[st] if k == 0 else part(st, a0 + k, b0)
        send((st, 3, 1, k), src, part(st, a0 + k, b0), slot(st, a0, b0 + 1))
        send((st, 3, -1, k), src, part(st, a0 + k, b0), slot(st, a0, b0 - 1))

    for st in range(2):
        a0, b0 = own[st]
        send((st, 1, 1), x_ref.at[st], part(st, a0, b0), slot(st, a0 + 1, b0))
        send((st, 1, -1), x_ref.at[st], part(st, a0, b0), slot(st, a0 - 1, b0))
        send_row(st, 0)
    for st in range(2):
        a0, b0 = own[st]
        recv((st, 1, 1), part(st, a0 - 1, b0), slot(st, a0 - 1, b0))
        recv((st, 1, -1), part(st, a0 + 1, b0), slot(st, a0 + 1, b0))
        send((st, 2, 1), part(st, a0 - 1, b0, 0), part(st, a0 - 1, b0, 0), slot(st, a0 + 1, b0))
        send((st, 2, -1), part(st, a0 + 1, b0, q), part(st, a0 + 1, b0, q), slot(st, a0 - 1, b0))
        send_row(st, 1)
        send_row(st, side - 1)
    for st in range(2):
        a0, b0 = own[st]
        recv((st, 2, 1), part(st, a0 - 2, b0, 0), slot(st, a0 - 1, b0))
        recv((st, 2, -1), part(st, a0 + 2, b0, q), slot(st, a0 + 1, b0))
        for k in range(2, side - 1):
            send_row(st, k)
    for st in range(2):
        a0, b0 = own[st]
        for k in range(side):
            recv((st, 3, 1, k), part(st, a0 + k, b0 - 1), slot(st, a0, b0 - 1))
            recv((st, 3, -1, k), part(st, a0 + k, b0 + 1), slot(st, a0, b0 + 1))
            send((st, 4, 1, k), part(st, a0 + k, b0 - 1, 0), part(st, a0 + k, b0 - 1, 0), slot(st, a0, b0 + 1))
            send((st, 4, -1, k), part(st, a0 + k, b0 + 1, q), part(st, a0 + k, b0 + 1, q), slot(st, a0, b0 - 1))
    proj = jnp.dot(h_ref[...], wq_ref[...], preferred_element_type=jnp.float32)
    scale = scale_ref[...]
    normed = []
    for h in range(heads):
        cols = slice(h * head_size, (h + 1) * head_size)
        part_q = proj[:, cols]
        mean_sq = jnp.mean(part_q * part_q, axis=1, keepdims=True)
        normed.append(part_q * lax.rsqrt(mean_sq + 1e-06) * scale[:, cols])
    qt_ref[...] = jnp.concatenate(normed, axis=1).T.astype(qt_ref.dtype)
    wvt_ref[...] = wv_ref[...].astype(jnp.float32).T.astype(wvt_ref.dtype)
    pair = pltpu.make_async_remote_copy(
        src_ref=qt_ref, dst_ref=qo_ref, send_sem=pair_sem.at[0], recv_sem=pair_sem.at[1],
        device_id={"core": sibling}, device_id_type=mesh_ids,
    )
    pair.start()
    for st in range(2):
        a0, b0 = own[st]
        for k in range(side):
            recv((st, 4, 1, k), part(st, a0 + k, b0 - 2, 0), slot(st, a0, b0 - 1))
            recv((st, 4, -1, k), part(st, a0 + k, b0 + 2, q), slot(st, a0, b0 + 1))
    pair.wait_send()
    pair.wait_recv()
    local.wait()
    for copy in sends:
        copy.wait_send()


def gather_rows(block, qkv_weight, scale_row, heads, head_size, axis):
    n = lax.axis_size(axis)
    side = math.isqrt(n)
    rows, width = block.shape
    channels, width_qkv = qkv_weight.shape
    width_all = width_qkv // 3
    copies = 2 * (2 + 2 + 4 * side)
    whole = lambda i: (0, 0)
    out, qt, wvt, qo = pl.pallas_call(
        functools.partial(ring_gather_kernel, side, heads, head_size),
        grid=(1,),
        in_specs=[
            pl.BlockSpec(memory_space=pl.ANY),
            pl.BlockSpec((rows, width), whole),
            pl.BlockSpec((channels, width_all), lambda i: (0, 0)),
            pl.BlockSpec((channels, width_all), lambda i: (0, 2)),
            pl.BlockSpec((1, width_all), whole),
        ],
        out_specs=[
            pl.BlockSpec(memory_space=pl.ANY),
            pl.BlockSpec((width_all, rows), whole),
            pl.BlockSpec((width_all, channels), whole),
            pl.BlockSpec(memory_space=pl.ANY),
        ],
        out_shape=[
            jax.ShapeDtypeStruct((n, 2, rows // 2, width), block.dtype),
            jax.ShapeDtypeStruct((width_all, rows), jnp.bfloat16),
            jax.ShapeDtypeStruct((width_all, channels), jnp.bfloat16),
            jax.ShapeDtypeStruct((width_all, rows), jnp.bfloat16),
        ],
        scratch_shapes=[
            pltpu.SemaphoreType.DMA((copies,)),
            pltpu.SemaphoreType.DMA((copies,)),
            pltpu.SemaphoreType.DMA,
            pltpu.SemaphoreType.DMA((2,)),
        ],
        compiler_params=pltpu.CompilerParams(collective_id=0, has_side_effects=True),
    )(block.reshape(2, rows // 2, width), block, qkv_weight, qkv_weight, scale_row)
    return out.reshape(n * rows, width), qt, wvt, qo


def conv_gelu_kernel(taps, rows, halo, x_ref, w_ref, o_ref, acc_sc):
    j = pl.program_id(0)
    product = jnp.dot(x_ref[...], w_ref[...], preferred_element_type=jnp.float32)
    for t in range(taps):

        @pl.when(j == t)
        def _():
            if t == 0:
                acc_sc[...] = product[t : t + rows]
            else:
                acc_sc[...] = acc_sc[...] + product[t : t + rows]

    @pl.when(j == taps - 1)
    def _():
        place = lax.axis_index(SEQ_AXES)
        last = lax.axis_size(SEQ_AXES) - 1
        row = lax.broadcasted_iota(jnp.int32, acc_sc.shape, 0)
        outside = jnp.logical_or(
            jnp.logical_and(place == 0, row < halo),
            jnp.logical_and(place == last, row >= rows - halo),
        )
        value = jax.nn.gelu(acc_sc[...])
        o_ref[...] = jnp.where(outside, 0.0, value).astype(o_ref.dtype)


def conv_gelu(padded, weight, halo):
    taps, channels, width = weight.shape
    rows = padded.shape[0] - taps + 1
    whole = lambda j: (0, 0)
    return pl.pallas_call(
        functools.partial(conv_gelu_kernel, taps, rows, halo),
        grid=(taps,),
        in_specs=[
            pl.BlockSpec(padded.shape, whole),
            pl.BlockSpec((None, channels, width), lambda j: (j, 0, 0)),
        ],
        out_specs=pl.BlockSpec((rows, width), whole),
        out_shape=jax.ShapeDtypeStruct((rows, width), jnp.bfloat16),
        scratch_shapes=[pltpu.VMEM((rows, width), jnp.float32)],
        compiler_params=pltpu.CompilerParams(
            dimension_semantics=("arbitrary",), vmem_limit_bytes=24 * 1024 * 1024
        ),
        cost_estimate=pl.CostEstimate(
            flops=2 * taps * padded.shape[0] * channels * width,
            transcendentals=rows * width,
            bytes_accessed=taps * channels * width * 2 + padded.size * 2 + rows * width * 2,
        ),
    )(padded, weight)


def body(sequence_input, conv_first, conv_second, qkv_weight, out_weight, logit_scale):
    row_count = sequence_input.shape[0]
    padded_input = padded_2(sequence_input, 4)
    padded_first = conv_gelu(padded_input, conv_first, 2)
    first_out = padded_first[2 : 2 + row_count]
    second = convolve(padded_first, conv_second, row_count)
    hidden = (first_out.astype(jnp.float32) + second).astype(jnp.bfloat16)
    head_count = logit_scale.shape[0]
    width_all = qkv_weight.shape[1] // 3
    head_size = width_all // head_count
    scale_row = jnp.repeat(logit_scale / math.sqrt(head_size), head_size)[None, :]

    hidden_all, qt_own, wvt, qt_other = gather_rows(hidden, qkv_weight, scale_row, head_count, head_size, "zx")
    return attend_partial(
        qt_own, qt_other, hidden_all, qkv_weight, wvt, hidden, out_weight, head_count, head_size
    )


def solution(mesh):
    devices = np.asarray(mesh.devices)
    seq_size = mesh.shape["seq"]
    batch_size = mesh.shape["batch"]
    order = [mesh.axis_names.index("seq"), mesh.axis_names.index("batch")]
    devices = devices.transpose(order).reshape(seq_size // 2, 2, batch_size)
    split_mesh = Mesh(devices, ("zx", "core", "batch"))
    rows = P(("batch", "zx", "core"), None)
    in_specs = (rows, P(), P(), P(), P(), P())
    return jax.shard_map(body, mesh=split_mesh, in_specs=in_specs, out_specs=rows, check_vma=False)
```

```python
import functools
import math

import jax
import jax.numpy as jnp
import numpy as np
from jax import lax
from jax.experimental import pallas as pl
from jax.experimental.pallas import tpu as pltpu
from jax.sharding import Mesh
from jax.sharding import PartitionSpec as P

SEQ_AXES = ("zx", "core")


def padded_2(block, width, align=1):
    count = lax.axis_size(SEQ_AXES)
    forward = [(i, i + 1) for i in range(count - 1)]
    backward = [(target, source) for source, target in forward]
    low = lax.ppermute(lax.slice_in_dim(block, block.shape[0] - width, None, axis=0), SEQ_AXES, forward)
    high = lax.ppermute(lax.slice_in_dim(block, 0, width, axis=0), SEQ_AXES, backward)
    extra = (-(block.shape[0] + 2 * width)) % align
    fill = jnp.zeros((extra, block.shape[1]), block.dtype)
    return jnp.concatenate([low, block, high, fill], axis=0)


def convolve(padded, weight, row_count):
    conv_sum = jnp.dot(padded[0:row_count], weight[0], preferred_element_type=jnp.float32)
    for offset in range(1, weight.shape[0]):
        conv_sum = conv_sum + jnp.dot(
            padded[offset : offset + row_count], weight[offset], preferred_element_type=jnp.float32
        )
    return conv_sum


def head_rms(tensor):
    return tensor * lax.rsqrt(jnp.mean(tensor * tensor, axis=-1, keepdims=True) + 1e-06)


def head_norm(block, heads, head_size):
    parts = []
    for h in range(heads):
        part = block[:, h * head_size : (h + 1) * head_size]
        mean_sq = jnp.mean(part * part, axis=1, keepdims=True)
        parts.append(part * lax.rsqrt(mean_sq + 1e-06))
    return parts


def attend_kernel(heads, head_size, nk, qa_ref, qb_ref, hkv_ref, wk_ref, wvt_ref,
                  out_ref, qt_sc, m_sc, l_sc, acc_sc, st_send, og_sc, sg_sc, pair_sem):
    j = pl.program_id(0)
    contract_last = (((1,), (1,)), ((), ()))

    mesh_ids = pl.DeviceIdType.MESH
    sibling = 1 - lax.axis_index("core")

    @pl.when(j == 0)
    def _():
        barrier = pltpu.get_barrier_semaphore()
        pl.semaphore_signal(barrier, inc=1, device_id={"core": sibling}, device_id_type=mesh_ids)
        pl.semaphore_wait(barrier, 1)
        own = qa_ref.shape[1]
        qt_sc[:, :own] = qa_ref[...]
        qt_sc[:, own:] = qb_ref[...]
        m_sc[...] = jnp.full(m_sc.shape, -jnp.inf, jnp.float32)
        l_sc[...] = jnp.zeros(l_sc.shape, jnp.float32)
        acc_sc[...] = jnp.zeros(acc_sc.shape, jnp.float32)

    hkv = hkv_ref[...]
    k_all = jnp.dot(hkv, wk_ref[...], preferred_element_type=jnp.float32)
    v_t = lax.dot_general(wvt_ref[...], hkv, contract_last, preferred_element_type=jnp.float32)
    for h in range(heads):
        rows = slice(h * head_size, (h + 1) * head_size)
        k_h = k_all[:, rows]
        k_h = (k_h * lax.rsqrt(jnp.mean(k_h * k_h, axis=1, keepdims=True) + 1e-06)).astype(
            jnp.bfloat16
        )
        s_t = jnp.dot(k_h, qt_sc[rows, :], preferred_element_type=jnp.float32)
        m_prev = m_sc[h]
        m_next = jnp.maximum(m_prev, jnp.max(s_t, axis=0, keepdims=True))
        alpha = jnp.exp(m_prev - m_next)
        p_t = jnp.exp(s_t - m_next)
        l_sc[h] = alpha * l_sc[h] + jnp.sum(p_t, axis=0, keepdims=True)
        acc_sc[rows, :] = alpha * acc_sc[rows, :] + jnp.dot(
            v_t[rows, :].astype(jnp.bfloat16), p_t.astype(jnp.bfloat16),
            preferred_element_type=jnp.float32,
        )
        m_sc[h] = m_next

    @pl.when(j == nk - 1)
    def _():
        own = qa_ref.shape[1]
        for h in range(heads):
            st_send[h : h + 1, :] = m_sc[h][:, own:]
            st_send[heads + h : heads + h + 1, :] = l_sc[h][:, own:]
        copies = [
            pltpu.make_async_remote_copy(
                src_ref=src, dst_ref=dst, send_sem=pair_sem.at[0, i], recv_sem=pair_sem.at[1, i],
                device_id={"core": sibling}, device_id_type=mesh_ids,
            )
            for i, (src, dst) in enumerate(((acc_sc.at[:, pl.ds(own, own)], og_sc), (st_send, sg_sc)))
        ]
        for copy in copies:
            copy.start()
        for copy in copies:
            copy.wait_send()
            copy.wait_recv()
        st_got = sg_sc[...]
        mixed = []
        for h in range(heads):
            rows = slice(h * head_size, (h + 1) * head_size)
            m_own = m_sc[h][:, :own]
            m_got = st_got[h : h + 1, :]
            m_all = jnp.maximum(m_own, m_got)
            w_own = jnp.exp(m_own - m_all)
            w_got = jnp.exp(m_got - m_all)
            denom = l_sc[h][:, :own] * w_own + st_got[heads + h : heads + h + 1, :] * w_got
            mixed.append((acc_sc[rows, :own] * w_own + og_sc[rows, :] * w_got) / denom)
        out_ref[...] = jnp.concatenate(mixed, axis=0).T.astype(out_ref.dtype)


def attend_partial(qt_own, qt_other, hidden_kv, qkv_weight, wvt, heads, head_size, tk=2048):
    width, own = qt_own.shape
    q_rows = 2 * own
    k_rows, channels = hidden_kv.shape
    nk = k_rows // tk
    whole = lambda j: (0, 0)
    return pl.pallas_call(
        functools.partial(attend_kernel, heads, head_size, nk),
        grid=(nk,),
        in_specs=[
            pl.BlockSpec((width, own), whole),
            pl.BlockSpec((width, own), whole),
            pl.BlockSpec((tk, channels), lambda j: (j, 0)),
            pl.BlockSpec((channels, width), lambda j: (0, 1)),
            pl.BlockSpec((width, channels), whole),
        ],
        out_specs=pl.BlockSpec((own, width), whole),
        out_shape=jax.ShapeDtypeStruct((own, width), jnp.bfloat16),
        scratch_shapes=[
            pltpu.VMEM((width, q_rows), jnp.bfloat16),
            pltpu.VMEM((heads, 1, q_rows), jnp.float32),
            pltpu.VMEM((heads, 1, q_rows), jnp.float32),
            pltpu.VMEM((width, q_rows), jnp.float32),
            pltpu.VMEM((2 * heads, own), jnp.float32),
            pltpu.VMEM((width, own), jnp.float32),
            pltpu.VMEM((2 * heads, own), jnp.float32),
            pltpu.SemaphoreType.DMA((2, 2)),
        ],
        compiler_params=pltpu.CompilerParams(
            dimension_semantics=("arbitrary",), collective_id=1, has_side_effects=True
        ),
        cost_estimate=pl.CostEstimate(
            flops=4 * q_rows * k_rows * width + 2 * k_rows * channels * 2 * width,
            transcendentals=q_rows * k_rows * heads,
            bytes_accessed=k_rows * channels * 2 + q_rows * width * 8,
        ),
    )(qt_own, qt_other, hidden_kv, qkv_weight, wvt)


def finish_kernel(heads, head_size, o_ref, st_ref, og_ref, sg_ref, hid_ref, wo_ref, out_ref):
    st_own = st_ref[...]
    st_got = sg_ref[...]
    mixed = []
    for h in range(heads):
        rows = slice(h * head_size, (h + 1) * head_size)
        m_own = st_own[h : h + 1, :]
        m_got = st_got[h : h + 1, :]
        m_all = jnp.maximum(m_own, m_got)
        w_own = jnp.exp(m_own - m_all)
        w_got = jnp.exp(m_got - m_all)
        denom = st_own[heads + h : heads + h + 1, :] * w_own + st_got[heads + h : heads + h + 1, :] * w_got
        mixed.append((o_ref[rows, :] * w_own + og_ref[rows, :] * w_got) / denom)
    attended = jnp.concatenate(mixed, axis=0).T.astype(jnp.bfloat16)
    out = hid_ref[...].astype(jnp.float32) + jnp.dot(
        attended, wo_ref[...], preferred_element_type=jnp.float32
    )
    out_ref[...] = out.astype(out_ref.dtype)


def finish(o_part, st_part, o_got, st_got, hidden, out_weight, heads, head_size):
    rows, width_out = hidden.shape
    width = heads * head_size
    whole = lambda i: (0, 0)
    return pl.pallas_call(
        functools.partial(finish_kernel, heads, head_size),
        grid=(1,),
        in_specs=[
            pl.BlockSpec((width, rows), whole),
            pl.BlockSpec((2 * heads, rows), whole),
            pl.BlockSpec((width, rows), whole),
            pl.BlockSpec((2 * heads, rows), whole),
            pl.BlockSpec((rows, width_out), whole),
            pl.BlockSpec((width, width_out), whole),
        ],
        out_specs=pl.BlockSpec((rows, width_out), whole),
        out_shape=jax.ShapeDtypeStruct((rows, width_out), jnp.bfloat16),
    )(o_part, st_part, o_got, st_got, hidden, out_weight)


def ring_gather_kernel(side, heads, head_size, x_ref, h_ref, wq_ref, wv_ref, scale_ref,
                       out_ref, qt_ref, wvt_ref, qo_ref, send_sem, recv_sem, local_sem, pair_sem):
    me = lax.axis_index("zx")
    z, x = me // side, me % side
    half = x_ref.shape[1]
    q = half // 2
    mesh_ids = pl.DeviceIdType.MESH

    def slot(stream, a, b):
        a = lax.rem(a + side, side)
        b = lax.rem(b + side, side)
        return b * side + a if stream == 0 else a * side + b

    own = [(x, z), (z, x)]
    barrier = pltpu.get_barrier_semaphore()
    for target in (slot(0, x + 1, z), slot(0, x - 1, z), slot(1, z + 1, x), slot(1, z - 1, x)):
        pl.semaphore_signal(barrier, inc=1, device_id={"zx": target}, device_id_type=mesh_ids)
    sibling = 1 - lax.axis_index("core")
    pl.semaphore_signal(barrier, inc=1, device_id={"core": sibling}, device_id_type=mesh_ids)
    pl.semaphore_wait(barrier, 5)
    local = pltpu.make_async_copy(x_ref, out_ref.at[me], local_sem)
    local.start()

    sends = []
    index = {}

    def send(key, src, view, target):
        idx = len(index)
        index[key] = idx
        copy = pltpu.make_async_remote_copy(
            src_ref=src, dst_ref=view, send_sem=send_sem.at[idx], recv_sem=recv_sem.at[idx],
            device_id={"zx": target}, device_id_type=mesh_ids,
        )
        copy.start()
        sends.append(copy)

    def recv(key, view, source):
        idx = index[key]
        pltpu.make_async_remote_copy(
            src_ref=view, dst_ref=view, send_sem=send_sem.at[idx], recv_sem=recv_sem.at[idx],
            device_id={"zx": source}, device_id_type=mesh_ids,
        ).wait_recv()

    def part(stream, a, b, lo=None):
        view = out_ref.at[slot(stream, a, b), stream]
        return view if lo is None else view.at[pl.ds(lo, q)]

    def send_row(st, k):
        a0, b0 = own[st]
        src = x_ref.at[st] if k == 0 else part(st, a0 + k, b0)
        send((st, 3, 1, k), src, part(st, a0 + k, b0), slot(st, a0, b0 + 1))
        send((st, 3, -1, k), src, part(st, a0 + k, b0), slot(st, a0, b0 - 1))

    for st in range(2):
        a0, b0 = own[st]
        send((st, 1, 1), x_ref.at[st], part(st, a0, b0), slot(st, a0 + 1, b0))
        send((st, 1, -1), x_ref.at[st], part(st, a0, b0), slot(st, a0 - 1, b0))
        send_row(st, 0)
    for st in range(2):
        a0, b0 = own[st]
        recv((st, 1, 1), part(st, a0 - 1, b0), slot(st, a0 - 1, b0))
        recv((st, 1, -1), part(st, a0 + 1, b0), slot(st, a0 + 1, b0))
        send((st, 2, 1), part(st, a0 - 1, b0, 0), part(st, a0 - 1, b0, 0), slot(st, a0 + 1, b0))
        send((st, 2, -1), part(st, a0 + 1, b0, q), part(st, a0 + 1, b0, q), slot(st, a0 - 1, b0))
        send_row(st, 1)
        send_row(st, side - 1)
    for st in range(2):
        a0, b0 = own[st]
        recv((st, 2, 1), part(st, a0 - 2, b0, 0), slot(st, a0 - 1, b0))
        recv((st, 2, -1), part(st, a0 + 2, b0, q), slot(st, a0 + 1, b0))
        for k in range(2, side - 1):
            send_row(st, k)
    for st in range(2):
        a0, b0 = own[st]
        for k in range(side):
            recv((st, 3, 1, k), part(st, a0 + k, b0 - 1), slot(st, a0, b0 - 1))
            recv((st, 3, -1, k), part(st, a0 + k, b0 + 1), slot(st, a0, b0 + 1))
            send((st, 4, 1, k), part(st, a0 + k, b0 - 1, 0), part(st, a0 + k, b0 - 1, 0), slot(st, a0, b0 + 1))
            send((st, 4, -1, k), part(st, a0 + k, b0 + 1, q), part(st, a0 + k, b0 + 1, q), slot(st, a0, b0 - 1))
    proj = jnp.dot(h_ref[...], wq_ref[...], preferred_element_type=jnp.float32)
    scale = scale_ref[...]
    normed = []
    for h in range(heads):
        cols = slice(h * head_size, (h + 1) * head_size)
        part_q = proj[:, cols]
        mean_sq = jnp.mean(part_q * part_q, axis=1, keepdims=True)
        normed.append(part_q * lax.rsqrt(mean_sq + 1e-06) * scale[:, cols])
    qt_ref[...] = jnp.concatenate(normed, axis=1).T.astype(qt_ref.dtype)
    wvt_ref[...] = wv_ref[...].astype(jnp.float32).T.astype(wvt_ref.dtype)
    pair = pltpu.make_async_remote_copy(
        src_ref=qt_ref, dst_ref=qo_ref, send_sem=pair_sem.at[0], recv_sem=pair_sem.at[1],
        device_id={"core": sibling}, device_id_type=mesh_ids,
    )
    pair.start()
    for st in range(2):
        a0, b0 = own[st]
        for k in range(side):
            recv((st, 4, 1, k), part(st, a0 + k, b0 - 2, 0), slot(st, a0, b0 - 1))
            recv((st, 4, -1, k), part(st, a0 + k, b0 + 2, q), slot(st, a0, b0 + 1))
    pair.wait_send()
    pair.wait_recv()
    local.wait()
    for copy in sends:
        copy.wait_send()


def gather_rows(block, qkv_weight, scale_row, heads, head_size, axis):
    n = lax.axis_size(axis)
    side = math.isqrt(n)
    rows, width = block.shape
    channels, width_qkv = qkv_weight.shape
    width_all = width_qkv // 3
    copies = 2 * (2 + 2 + 4 * side)
    whole = lambda i: (0, 0)
    out, qt, wvt, qo = pl.pallas_call(
        functools.partial(ring_gather_kernel, side, heads, head_size),
        grid=(1,),
        in_specs=[
            pl.BlockSpec(memory_space=pl.ANY),
            pl.BlockSpec((rows, width), whole),
            pl.BlockSpec((channels, width_all), lambda i: (0, 0)),
            pl.BlockSpec((channels, width_all), lambda i: (0, 2)),
            pl.BlockSpec((1, width_all), whole),
        ],
        out_specs=[
            pl.BlockSpec(memory_space=pl.ANY),
            pl.BlockSpec((width_all, rows), whole),
            pl.BlockSpec((width_all, channels), whole),
            pl.BlockSpec(memory_space=pl.ANY),
        ],
        out_shape=[
            jax.ShapeDtypeStruct((n, 2, rows // 2, width), block.dtype),
            jax.ShapeDtypeStruct((width_all, rows), jnp.bfloat16),
            jax.ShapeDtypeStruct((width_all, channels), jnp.bfloat16),
            jax.ShapeDtypeStruct((width_all, rows), jnp.bfloat16),
        ],
        scratch_shapes=[
            pltpu.SemaphoreType.DMA((copies,)),
            pltpu.SemaphoreType.DMA((copies,)),
            pltpu.SemaphoreType.DMA,
            pltpu.SemaphoreType.DMA((2,)),
        ],
        compiler_params=pltpu.CompilerParams(collective_id=0, has_side_effects=True),
    )(block.reshape(2, rows // 2, width), block, qkv_weight, qkv_weight, scale_row)
    return out.reshape(n * rows, width), qt, wvt, qo


def conv_gelu_kernel(taps, rows, halo, x_ref, w_ref, o_ref, acc_sc):
    j = pl.program_id(0)
    product = jnp.dot(x_ref[...], w_ref[...], preferred_element_type=jnp.float32)
    for t in range(taps):

        @pl.when(j == t)
        def _():
            if t == 0:
                acc_sc[...] = product[t : t + rows]
            else:
                acc_sc[...] = acc_sc[...] + product[t : t + rows]

    @pl.when(j == taps - 1)
    def _():
        place = lax.axis_index(SEQ_AXES)
        last = lax.axis_size(SEQ_AXES) - 1
        row = lax.broadcasted_iota(jnp.int32, acc_sc.shape, 0)
        outside = jnp.logical_or(
            jnp.logical_and(place == 0, row < halo),
            jnp.logical_and(place == last, row >= rows - halo),
        )
        value = jax.nn.gelu(acc_sc[...])
        o_ref[...] = jnp.where(outside, 0.0, value).astype(o_ref.dtype)


def conv_gelu(padded, weight, halo):
    taps, channels, width = weight.shape
    rows = padded.shape[0] - taps + 1
    whole = lambda j: (0, 0)
    return pl.pallas_call(
        functools.partial(conv_gelu_kernel, taps, rows, halo),
        grid=(taps,),
        in_specs=[
            pl.BlockSpec(padded.shape, whole),
            pl.BlockSpec((None, channels, width), lambda j: (j, 0, 0)),
        ],
        out_specs=pl.BlockSpec((rows, width), whole),
        out_shape=jax.ShapeDtypeStruct((rows, width), jnp.bfloat16),
        scratch_shapes=[pltpu.VMEM((rows, width), jnp.float32)],
        compiler_params=pltpu.CompilerParams(
            dimension_semantics=("arbitrary",), vmem_limit_bytes=24 * 1024 * 1024
        ),
        cost_estimate=pl.CostEstimate(
            flops=2 * taps * padded.shape[0] * channels * width,
            transcendentals=rows * width,
            bytes_accessed=taps * channels * width * 2 + padded.size * 2 + rows * width * 2,
        ),
    )(padded, weight)


def body(sequence_input, conv_first, conv_second, qkv_weight, out_weight, logit_scale):
    row_count = sequence_input.shape[0]
    padded_input = padded_2(sequence_input, 4)
    padded_first = conv_gelu(padded_input, conv_first, 2)
    first_out = padded_first[2 : 2 + row_count]
    second = convolve(padded_first, conv_second, row_count)
    hidden = (first_out.astype(jnp.float32) + second).astype(jnp.bfloat16)
    head_count = logit_scale.shape[0]
    width_all = qkv_weight.shape[1] // 3
    head_size = width_all // head_count
    scale_row = jnp.repeat(logit_scale / math.sqrt(head_size), head_size)[None, :]

    hidden_all, qt_own, wvt, qt_other = gather_rows(hidden, qkv_weight, scale_row, head_count, head_size, "zx")
    attended = attend_partial(qt_own, qt_other, hidden_all, qkv_weight, wvt, head_count, head_size)
    return (
        hidden.astype(jnp.float32)
        + jnp.dot(attended, out_weight, preferred_element_type=jnp.float32)
    ).astype(jnp.bfloat16)


def solution(mesh):
    devices = np.asarray(mesh.devices)
    seq_size = mesh.shape["seq"]
    batch_size = mesh.shape["batch"]
    order = [mesh.axis_names.index("seq"), mesh.axis_names.index("batch")]
    devices = devices.transpose(order).reshape(seq_size // 2, 2, batch_size)
    split_mesh = Mesh(devices, ("zx", "core", "batch"))
    rows = P(("batch", "zx", "core"), None)
    in_specs = (rows, P(), P(), P(), P(), P())
    return jax.shard_map(body, mesh=split_mesh, in_specs=in_specs, out_specs=rows, check_vma=False)
```

```python
import functools
import math

import jax
import jax.numpy as jnp
import numpy as np
from jax import lax
from jax.experimental import pallas as pl
from jax.experimental.pallas import tpu as pltpu
from jax.sharding import Mesh
from jax.sharding import PartitionSpec as P

SEQ_AXES = ("zx", "core")


def padded_2(block, width, align=1):
    count = lax.axis_size(SEQ_AXES)
    forward = [(i, i + 1) for i in range(count - 1)]
    backward = [(target, source) for source, target in forward]
    low = lax.ppermute(lax.slice_in_dim(block, block.shape[0] - width, None, axis=0), SEQ_AXES, forward)
    high = lax.ppermute(lax.slice_in_dim(block, 0, width, axis=0), SEQ_AXES, backward)
    extra = (-(block.shape[0] + 2 * width)) % align
    fill = jnp.zeros((extra, block.shape[1]), block.dtype)
    return jnp.concatenate([low, block, high, fill], axis=0)


def convolve(padded, weight, row_count):
    conv_sum = jnp.dot(padded[0:row_count], weight[0], preferred_element_type=jnp.float32)
    for offset in range(1, weight.shape[0]):
        conv_sum = conv_sum + jnp.dot(
            padded[offset : offset + row_count], weight[offset], preferred_element_type=jnp.float32
        )
    return conv_sum


def head_rms(tensor):
    return tensor * lax.rsqrt(jnp.mean(tensor * tensor, axis=-1, keepdims=True) + 1e-06)


def head_norm(block, heads, head_size):
    parts = []
    for h in range(heads):
        part = block[:, h * head_size : (h + 1) * head_size]
        mean_sq = jnp.mean(part * part, axis=1, keepdims=True)
        parts.append(part * lax.rsqrt(mean_sq + 1e-06))
    return parts


def attend_kernel(heads, head_size, nk, qa_ref, qb_ref, hkv_ref, wk_ref, wvt_ref,
                  out_ref, qt_sc, m_sc, l_sc, acc_sc, st_send, og_sc, sg_sc, pair_sem):
    j = pl.program_id(0)
    contract_last = (((1,), (1,)), ((), ()))

    mesh_ids = pl.DeviceIdType.MESH
    sibling = 1 - lax.axis_index("core")

    @pl.when(j == 0)
    def _():
        barrier = pltpu.get_barrier_semaphore()
        pl.semaphore_signal(barrier, inc=1, device_id={"core": sibling}, device_id_type=mesh_ids)
        pl.semaphore_wait(barrier, 1)
        own = qa_ref.shape[1]
        qt_sc[:, :own] = qa_ref[...]
        qt_sc[:, own:] = qb_ref[...]
        m_sc[...] = jnp.full(m_sc.shape, -jnp.inf, jnp.float32)
        l_sc[...] = jnp.zeros(l_sc.shape, jnp.float32)
        acc_sc[...] = jnp.zeros(acc_sc.shape, jnp.float32)

    hkv = hkv_ref[...]
    k_all = jnp.dot(hkv, wk_ref[...], preferred_element_type=jnp.float32)
    v_t = lax.dot_general(wvt_ref[...], hkv, contract_last, preferred_element_type=jnp.float32)
    for h in range(heads):
        rows = slice(h * head_size, (h + 1) * head_size)
        k_h = k_all[:, rows]
        k_h = (k_h * lax.rsqrt(jnp.mean(k_h * k_h, axis=1, keepdims=True) + 1e-06)).astype(
            jnp.bfloat16
        )
        s_t = jnp.dot(k_h, qt_sc[rows, :], preferred_element_type=jnp.float32)
        m_prev = m_sc[h]
        m_next = jnp.maximum(m_prev, jnp.max(s_t, axis=0, keepdims=True))
        alpha = jnp.exp(m_prev - m_next)
        p_t = jnp.exp(s_t - m_next)
        l_sc[h] = alpha * l_sc[h] + jnp.sum(p_t, axis=0, keepdims=True)
        acc_sc[rows, :] = alpha * acc_sc[rows, :] + jnp.dot(
            v_t[rows, :].astype(jnp.bfloat16), p_t.astype(jnp.bfloat16),
            preferred_element_type=jnp.float32,
        )
        m_sc[h] = m_next

    @pl.when(j == nk - 1)
    def _():
        own = qa_ref.shape[1]
        for h in range(heads):
            st_send[h : h + 1, :] = m_sc[h][:, own:]
            st_send[heads + h : heads + h + 1, :] = l_sc[h][:, own:]
        copies = [
            pltpu.make_async_remote_copy(
                src_ref=src, dst_ref=dst, send_sem=pair_sem.at[0, i], recv_sem=pair_sem.at[1, i],
                device_id={"core": sibling}, device_id_type=mesh_ids,
            )
            for i, (src, dst) in enumerate(((acc_sc.at[:, pl.ds(own, own)], og_sc), (st_send, sg_sc)))
        ]
        for copy in copies:
            copy.start()
        for copy in copies:
            copy.wait_send()
            copy.wait_recv()
        st_got = sg_sc[...]
        mixed = []
        for h in range(heads):
            rows = slice(h * head_size, (h + 1) * head_size)
            m_own = m_sc[h][:, :own]
            m_got = st_got[h : h + 1, :]
            m_all = jnp.maximum(m_own, m_got)
            w_own = jnp.exp(m_own - m_all)
            w_got = jnp.exp(m_got - m_all)
            denom = l_sc[h][:, :own] * w_own + st_got[heads + h : heads + h + 1, :] * w_got
            mixed.append((acc_sc[rows, :own] * w_own + og_sc[rows, :] * w_got) / denom)
        out_ref[...] = jnp.concatenate(mixed, axis=0).T.astype(out_ref.dtype)


def attend_partial(qt_own, qt_other, hidden_kv, qkv_weight, wvt, heads, head_size, tk=2048):
    width, own = qt_own.shape
    q_rows = 2 * own
    k_rows, channels = hidden_kv.shape
    nk = k_rows // tk
    whole = lambda j: (0, 0)
    return pl.pallas_call(
        functools.partial(attend_kernel, heads, head_size, nk),
        grid=(nk,),
        in_specs=[
            pl.BlockSpec((width, own), whole),
            pl.BlockSpec((width, own), whole),
            pl.BlockSpec((tk, channels), lambda j: (j, 0)),
            pl.BlockSpec((channels, width), lambda j: (0, 1)),
            pl.BlockSpec((width, channels), whole),
        ],
        out_specs=pl.BlockSpec((own, width), whole),
        out_shape=jax.ShapeDtypeStruct((own, width), jnp.bfloat16),
        scratch_shapes=[
            pltpu.VMEM((width, q_rows), jnp.bfloat16),
            pltpu.VMEM((heads, 1, q_rows), jnp.float32),
            pltpu.VMEM((heads, 1, q_rows), jnp.float32),
            pltpu.VMEM((width, q_rows), jnp.float32),
            pltpu.VMEM((2 * heads, own), jnp.float32),
            pltpu.VMEM((width, own), jnp.float32),
            pltpu.VMEM((2 * heads, own), jnp.float32),
            pltpu.SemaphoreType.DMA((2, 2)),
        ],
        compiler_params=pltpu.CompilerParams(
            dimension_semantics=("arbitrary",), collective_id=1, has_side_effects=True
        ),
        cost_estimate=pl.CostEstimate(
            flops=4 * q_rows * k_rows * width + 2 * k_rows * channels * 2 * width,
            transcendentals=q_rows * k_rows * heads,
            bytes_accessed=k_rows * channels * 2 + q_rows * width * 8,
        ),
    )(qt_own, qt_other, hidden_kv, qkv_weight, wvt)


def finish_kernel(heads, head_size, o_ref, st_ref, og_ref, sg_ref, hid_ref, wo_ref, out_ref):
    st_own = st_ref[...]
    st_got = sg_ref[...]
    mixed = []
    for h in range(heads):
        rows = slice(h * head_size, (h + 1) * head_size)
        m_own = st_own[h : h + 1, :]
        m_got = st_got[h : h + 1, :]
        m_all = jnp.maximum(m_own, m_got)
        w_own = jnp.exp(m_own - m_all)
        w_got = jnp.exp(m_got - m_all)
        denom = st_own[heads + h : heads + h + 1, :] * w_own + st_got[heads + h : heads + h + 1, :] * w_got
        mixed.append((o_ref[rows, :] * w_own + og_ref[rows, :] * w_got) / denom)
    attended = jnp.concatenate(mixed, axis=0).T.astype(jnp.bfloat16)
    out = hid_ref[...].astype(jnp.float32) + jnp.dot(
        attended, wo_ref[...], preferred_element_type=jnp.float32
    )
    out_ref[...] = out.astype(out_ref.dtype)


def finish(o_part, st_part, o_got, st_got, hidden, out_weight, heads, head_size):
    rows, width_out = hidden.shape
    width = heads * head_size
    whole = lambda i: (0, 0)
    return pl.pallas_call(
        functools.partial(finish_kernel, heads, head_size),
        grid=(1,),
        in_specs=[
            pl.BlockSpec((width, rows), whole),
            pl.BlockSpec((2 * heads, rows), whole),
            pl.BlockSpec((width, rows), whole),
            pl.BlockSpec((2 * heads, rows), whole),
            pl.BlockSpec((rows, width_out), whole),
            pl.BlockSpec((width, width_out), whole),
        ],
        out_specs=pl.BlockSpec((rows, width_out), whole),
        out_shape=jax.ShapeDtypeStruct((rows, width_out), jnp.bfloat16),
    )(o_part, st_part, o_got, st_got, hidden, out_weight)


def ring_gather_kernel(side, heads, head_size, x_ref, h_ref, wq_ref, wv_ref, scale_ref,
                       out_ref, qt_ref, wvt_ref, qo_ref, send_sem, recv_sem, local_sem, pair_sem):
    me = lax.axis_index("zx")
    z, x = me // side, me % side
    half = x_ref.shape[1]
    q = half // 2
    mesh_ids = pl.DeviceIdType.MESH

    def slot(stream, a, b):
        a = lax.rem(a + side, side)
        b = lax.rem(b + side, side)
        return b * side + a if stream == 0 else a * side + b

    own = [(x, z), (z, x)]
    barrier = pltpu.get_barrier_semaphore()
    for target in (slot(0, x + 1, z), slot(0, x - 1, z), slot(1, z + 1, x), slot(1, z - 1, x)):
        pl.semaphore_signal(barrier, inc=1, device_id={"zx": target}, device_id_type=mesh_ids)
    sibling = 1 - lax.axis_index("core")
    pl.semaphore_signal(barrier, inc=1, device_id={"core": sibling}, device_id_type=mesh_ids)
    pl.semaphore_wait(barrier, 5)
    local = pltpu.make_async_copy(x_ref, out_ref.at[me], local_sem)
    local.start()

    sends = []
    index = {}

    def send(key, src, view, target):
        idx = len(index)
        index[key] = idx
        copy = pltpu.make_async_remote_copy(
            src_ref=src, dst_ref=view, send_sem=send_sem.at[idx], recv_sem=recv_sem.at[idx],
            device_id={"zx": target}, device_id_type=mesh_ids,
        )
        copy.start()
        sends.append(copy)

    def recv(key, view, source):
        idx = index[key]
        pltpu.make_async_remote_copy(
            src_ref=view, dst_ref=view, send_sem=send_sem.at[idx], recv_sem=recv_sem.at[idx],
            device_id={"zx": source}, device_id_type=mesh_ids,
        ).wait_recv()

    def part(stream, a, b, lo=None):
        view = out_ref.at[slot(stream, a, b), stream]
        return view if lo is None else view.at[pl.ds(lo, q)]

    def send_row(st, k):
        a0, b0 = own[st]
        src = x_ref.at[st] if k == 0 else part(st, a0 + k, b0)
        send((st, 3, 1, k), src, part(st, a0 + k, b0), slot(st, a0, b0 + 1))
        send((st, 3, -1, k), src, part(st, a0 + k, b0), slot(st, a0, b0 - 1))

    for st in range(2):
        a0, b0 = own[st]
        send((st, 1, 1), x_ref.at[st], part(st, a0, b0), slot(st, a0 + 1, b0))
        send((st, 1, -1), x_ref.at[st], part(st, a0, b0), slot(st, a0 - 1, b0))
        send_row(st, 0)
    for st in range(2):
        a0, b0 = own[st]
        recv((st, 1, 1), part(st, a0 - 1, b0), slot(st, a0 - 1, b0))
        recv((st, 1, -1), part(st, a0 + 1, b0), slot(st, a0 + 1, b0))
        send((st, 2, 1), part(st, a0 - 1, b0, 0), part(st, a0 - 1, b0, 0), slot(st, a0 + 1, b0))
        send((st, 2, -1), part(st, a0 + 1, b0, q), part(st, a0 + 1, b0, q), slot(st, a0 - 1, b0))
        send_row(st, 1)
        send_row(st, side - 1)
    for st in range(2):
        a0, b0 = own[st]
        recv((st, 2, 1), part(st, a0 - 2, b0, 0), slot(st, a0 - 1, b0))
        recv((st, 2, -1), part(st, a0 + 2, b0, q), slot(st, a0 + 1, b0))
        for k in range(2, side - 1):
            send_row(st, k)
    for st in range(2):
        a0, b0 = own[st]
        for k in range(side):
            recv((st, 3, 1, k), part(st, a0 + k, b0 - 1), slot(st, a0, b0 - 1))
            recv((st, 3, -1, k), part(st, a0 + k, b0 + 1), slot(st, a0, b0 + 1))
            send((st, 4, 1, k), part(st, a0 + k, b0 - 1, 0), part(st, a0 + k, b0 - 1, 0), slot(st, a0, b0 + 1))
            send((st, 4, -1, k), part(st, a0 + k, b0 + 1, q), part(st, a0 + k, b0 + 1, q), slot(st, a0, b0 - 1))
    proj = jnp.dot(h_ref[...], wq_ref[...], preferred_element_type=jnp.float32)
    normed = []
    for h in range(heads):
        cols = slice(h * head_size, (h + 1) * head_size)
        part_q = proj[:, cols]
        mean_sq = jnp.mean(part_q * part_q, axis=1, keepdims=True)
        scale = jnp.full((1, head_size), scale_ref[h], jnp.float32) / math.sqrt(head_size)
        normed.append(part_q * lax.rsqrt(mean_sq + 1e-06) * scale)
    qt_ref[...] = jnp.concatenate(normed, axis=1).T.astype(qt_ref.dtype)
    wvt_ref[...] = wv_ref[...].astype(jnp.float32).T.astype(wvt_ref.dtype)
    pair = pltpu.make_async_remote_copy(
        src_ref=qt_ref, dst_ref=qo_ref, send_sem=pair_sem.at[0], recv_sem=pair_sem.at[1],
        device_id={"core": sibling}, device_id_type=mesh_ids,
    )
    pair.start()
    for st in range(2):
        a0, b0 = own[st]
        for k in range(side):
            recv((st, 4, 1, k), part(st, a0 + k, b0 - 2, 0), slot(st, a0, b0 - 1))
            recv((st, 4, -1, k), part(st, a0 + k, b0 + 2, q), slot(st, a0, b0 + 1))
    pair.wait_send()
    pair.wait_recv()
    local.wait()
    for copy in sends:
        copy.wait_send()


def gather_rows(block, qkv_weight, logit_scale, heads, head_size, axis):
    n = lax.axis_size(axis)
    side = math.isqrt(n)
    rows, width = block.shape
    channels, width_qkv = qkv_weight.shape
    width_all = width_qkv // 3
    copies = 2 * (2 + 2 + 4 * side)
    whole = lambda i: (0, 0)
    out, qt, wvt, qo = pl.pallas_call(
        functools.partial(ring_gather_kernel, side, heads, head_size),
        grid=(1,),
        in_specs=[
            pl.BlockSpec(memory_space=pl.ANY),
            pl.BlockSpec((rows, width), whole),
            pl.BlockSpec((channels, width_all), lambda i: (0, 0)),
            pl.BlockSpec((channels, width_all), lambda i: (0, 2)),
            pl.BlockSpec(memory_space=pltpu.SMEM),
        ],
        out_specs=[
            pl.BlockSpec(memory_space=pl.ANY),
            pl.BlockSpec((width_all, rows), whole),
            pl.BlockSpec((width_all, channels), whole),
            pl.BlockSpec(memory_space=pl.ANY),
        ],
        out_shape=[
            jax.ShapeDtypeStruct((n, 2, rows // 2, width), block.dtype),
            jax.ShapeDtypeStruct((width_all, rows), jnp.bfloat16),
            jax.ShapeDtypeStruct((width_all, channels), jnp.bfloat16),
            jax.ShapeDtypeStruct((width_all, rows), jnp.bfloat16),
        ],
        scratch_shapes=[
            pltpu.SemaphoreType.DMA((copies,)),
            pltpu.SemaphoreType.DMA((copies,)),
            pltpu.SemaphoreType.DMA,
            pltpu.SemaphoreType.DMA((2,)),
        ],
        compiler_params=pltpu.CompilerParams(collective_id=0, has_side_effects=True),
    )(block.reshape(2, rows // 2, width), block, qkv_weight, qkv_weight, logit_scale)
    return out.reshape(n * rows, width), qt, wvt, qo


def conv_gelu_kernel(taps, rows, halo, x_ref, w_ref, o_ref, acc_sc):
    j = pl.program_id(0)
    product = jnp.dot(x_ref[...], w_ref[...], preferred_element_type=jnp.float32)
    for t in range(taps):

        @pl.when(j == t)
        def _():
            if t == 0:
                acc_sc[...] = product[t : t + rows]
            else:
                acc_sc[...] = acc_sc[...] + product[t : t + rows]

    @pl.when(j == taps - 1)
    def _():
        place = lax.axis_index(SEQ_AXES)
        last = lax.axis_size(SEQ_AXES) - 1
        row = lax.broadcasted_iota(jnp.int32, acc_sc.shape, 0)
        outside = jnp.logical_or(
            jnp.logical_and(place == 0, row < halo),
            jnp.logical_and(place == last, row >= rows - halo),
        )
        value = jax.nn.gelu(acc_sc[...])
        o_ref[...] = jnp.where(outside, 0.0, value).astype(o_ref.dtype)


def conv_gelu(padded, weight, halo):
    taps, channels, width = weight.shape
    rows = padded.shape[0] - taps + 1
    whole = lambda j: (0, 0)
    return pl.pallas_call(
        functools.partial(conv_gelu_kernel, taps, rows, halo),
        grid=(taps,),
        in_specs=[
            pl.BlockSpec(padded.shape, whole),
            pl.BlockSpec((None, channels, width), lambda j: (j, 0, 0)),
        ],
        out_specs=pl.BlockSpec((rows, width), whole),
        out_shape=jax.ShapeDtypeStruct((rows, width), jnp.bfloat16),
        scratch_shapes=[pltpu.VMEM((rows, width), jnp.float32)],
        compiler_params=pltpu.CompilerParams(
            dimension_semantics=("arbitrary",), vmem_limit_bytes=24 * 1024 * 1024
        ),
        cost_estimate=pl.CostEstimate(
            flops=2 * taps * padded.shape[0] * channels * width,
            transcendentals=rows * width,
            bytes_accessed=taps * channels * width * 2 + padded.size * 2 + rows * width * 2,
        ),
    )(padded, weight)


def body(sequence_input, conv_first, conv_second, qkv_weight, out_weight, logit_scale):
    row_count = sequence_input.shape[0]
    padded_input = padded_2(sequence_input, 4)
    padded_first = conv_gelu(padded_input, conv_first, 2)
    first_out = padded_first[2 : 2 + row_count]
    second = convolve(padded_first, conv_second, row_count)
    hidden = (first_out.astype(jnp.float32) + second).astype(jnp.bfloat16)
    head_count = logit_scale.shape[0]
    width_all = qkv_weight.shape[1] // 3
    head_size = width_all // head_count

    hidden_all, qt_own, wvt, qt_other = gather_rows(hidden, qkv_weight, logit_scale, head_count, head_size, "zx")
    attended = attend_partial(qt_own, qt_other, hidden_all, qkv_weight, wvt, head_count, head_size)
    return (
        hidden.astype(jnp.float32)
        + jnp.dot(attended, out_weight, preferred_element_type=jnp.float32)
    ).astype(jnp.bfloat16)


def solution(mesh):
    devices = np.asarray(mesh.devices)
    seq_size = mesh.shape["seq"]
    batch_size = mesh.shape["batch"]
    order = [mesh.axis_names.index("seq"), mesh.axis_names.index("batch")]
    devices = devices.transpose(order).reshape(seq_size // 2, 2, batch_size)
    split_mesh = Mesh(devices, ("zx", "core", "batch"))
    rows = P(("batch", "zx", "core"), None)
    in_specs = (rows, P(), P(), P(), P(), P())
    return jax.shard_map(body, mesh=split_mesh, in_specs=in_specs, out_specs=rows, check_vma=False)
```

```python
import functools
import math

import jax
import jax.numpy as jnp
import numpy as np
from jax import lax
from jax.experimental import pallas as pl
from jax.experimental.pallas import tpu as pltpu
from jax.sharding import Mesh
from jax.sharding import PartitionSpec as P

SEQ_AXES = ("zx", "core")


def padded_2(block, width, align=1):
    count = lax.axis_size(SEQ_AXES)
    forward = [(i, i + 1) for i in range(count - 1)]
    backward = [(target, source) for source, target in forward]
    low = lax.ppermute(lax.slice_in_dim(block, block.shape[0] - width, None, axis=0), SEQ_AXES, forward)
    high = lax.ppermute(lax.slice_in_dim(block, 0, width, axis=0), SEQ_AXES, backward)
    extra = (-(block.shape[0] + 2 * width)) % align
    fill = jnp.zeros((extra, block.shape[1]), block.dtype)
    return jnp.concatenate([low, block, high, fill], axis=0)


def halo_rows(block, width):
    count = lax.axis_size(SEQ_AXES)
    forward = [(i, i + 1) for i in range(count - 1)]
    backward = [(target, source) for source, target in forward]
    low = lax.ppermute(lax.slice_in_dim(block, block.shape[0] - width, None, axis=0), SEQ_AXES, forward)
    high = lax.ppermute(lax.slice_in_dim(block, 0, width, axis=0), SEQ_AXES, backward)
    return low, high


def convolve(padded, weight, row_count):
    conv_sum = jnp.dot(padded[0:row_count], weight[0], preferred_element_type=jnp.float32)
    for offset in range(1, weight.shape[0]):
        conv_sum = conv_sum + jnp.dot(
            padded[offset : offset + row_count], weight[offset], preferred_element_type=jnp.float32
        )
    return conv_sum


def head_rms(tensor):
    return tensor * lax.rsqrt(jnp.mean(tensor * tensor, axis=-1, keepdims=True) + 1e-06)


def head_norm(block, heads, head_size):
    parts = []
    for h in range(heads):
        part = block[:, h * head_size : (h + 1) * head_size]
        mean_sq = jnp.mean(part * part, axis=1, keepdims=True)
        parts.append(part * lax.rsqrt(mean_sq + 1e-06))
    return parts


def attend_kernel(heads, head_size, nk, qa_ref, qb_ref, hkv_ref, wk_ref, wvt_ref,
                  out_ref, qt_sc, m_sc, l_sc, acc_sc, st_send, og_sc, sg_sc, pair_sem):
    j = pl.program_id(0)
    contract_last = (((1,), (1,)), ((), ()))

    mesh_ids = pl.DeviceIdType.MESH
    sibling = 1 - lax.axis_index("core")

    @pl.when(j == 0)
    def _():
        barrier = pltpu.get_barrier_semaphore()
        pl.semaphore_signal(barrier, inc=1, device_id={"core": sibling}, device_id_type=mesh_ids)
        pl.semaphore_wait(barrier, 1)
        own = qa_ref.shape[1]
        qt_sc[:, :own] = qa_ref[...]
        qt_sc[:, own:] = qb_ref[...]
        m_sc[...] = jnp.full(m_sc.shape, -jnp.inf, jnp.float32)
        l_sc[...] = jnp.zeros(l_sc.shape, jnp.float32)
        acc_sc[...] = jnp.zeros(acc_sc.shape, jnp.float32)

    hkv = hkv_ref[...]
    k_all = jnp.dot(hkv, wk_ref[...], preferred_element_type=jnp.float32)
    v_t = lax.dot_general(wvt_ref[...], hkv, contract_last, preferred_element_type=jnp.float32)
    for h in range(heads):
        rows = slice(h * head_size, (h + 1) * head_size)
        k_h = k_all[:, rows]
        k_h = (k_h * lax.rsqrt(jnp.mean(k_h * k_h, axis=1, keepdims=True) + 1e-06)).astype(
            jnp.bfloat16
        )
        s_t = jnp.dot(k_h, qt_sc[rows, :], preferred_element_type=jnp.float32)
        m_prev = m_sc[h]
        m_next = jnp.maximum(m_prev, jnp.max(s_t, axis=0, keepdims=True))
        alpha = jnp.exp(m_prev - m_next)
        p_t = jnp.exp(s_t - m_next)
        l_sc[h] = alpha * l_sc[h] + jnp.sum(p_t, axis=0, keepdims=True)
        acc_sc[rows, :] = alpha * acc_sc[rows, :] + jnp.dot(
            v_t[rows, :].astype(jnp.bfloat16), p_t.astype(jnp.bfloat16),
            preferred_element_type=jnp.float32,
        )
        m_sc[h] = m_next

    @pl.when(j == nk - 1)
    def _():
        own = qa_ref.shape[1]
        for h in range(heads):
            st_send[h : h + 1, :] = m_sc[h][:, own:]
            st_send[heads + h : heads + h + 1, :] = l_sc[h][:, own:]
        copies = [
            pltpu.make_async_remote_copy(
                src_ref=src, dst_ref=dst, send_sem=pair_sem.at[0, i], recv_sem=pair_sem.at[1, i],
                device_id={"core": sibling}, device_id_type=mesh_ids,
            )
            for i, (src, dst) in enumerate(((acc_sc.at[:, pl.ds(own, own)], og_sc), (st_send, sg_sc)))
        ]
        for copy in copies:
            copy.start()
        for copy in copies:
            copy.wait_send()
            copy.wait_recv()
        st_got = sg_sc[...]
        mixed = []
        for h in range(heads):
            rows = slice(h * head_size, (h + 1) * head_size)
            m_own = m_sc[h][:, :own]
            m_got = st_got[h : h + 1, :]
            m_all = jnp.maximum(m_own, m_got)
            w_own = jnp.exp(m_own - m_all)
            w_got = jnp.exp(m_got - m_all)
            denom = l_sc[h][:, :own] * w_own + st_got[heads + h : heads + h + 1, :] * w_got
            mixed.append((acc_sc[rows, :own] * w_own + og_sc[rows, :] * w_got) / denom)
        out_ref[...] = jnp.concatenate(mixed, axis=0).T.astype(out_ref.dtype)


def attend_partial(qt_own, qt_other, hidden_kv, qkv_weight, wvt, heads, head_size, tk=2048):
    width, own = qt_own.shape
    q_rows = 2 * own
    k_rows, channels = hidden_kv.shape
    nk = k_rows // tk
    whole = lambda j: (0, 0)
    return pl.pallas_call(
        functools.partial(attend_kernel, heads, head_size, nk),
        grid=(nk,),
        in_specs=[
            pl.BlockSpec((width, own), whole),
            pl.BlockSpec((width, own), whole),
            pl.BlockSpec((tk, channels), lambda j: (j, 0)),
            pl.BlockSpec((channels, width), lambda j: (0, 1)),
            pl.BlockSpec((width, channels), whole),
        ],
        out_specs=pl.BlockSpec((own, width), whole),
        out_shape=jax.ShapeDtypeStruct((own, width), jnp.bfloat16),
        scratch_shapes=[
            pltpu.VMEM((width, q_rows), jnp.bfloat16),
            pltpu.VMEM((heads, 1, q_rows), jnp.float32),
            pltpu.VMEM((heads, 1, q_rows), jnp.float32),
            pltpu.VMEM((width, q_rows), jnp.float32),
            pltpu.VMEM((2 * heads, own), jnp.float32),
            pltpu.VMEM((width, own), jnp.float32),
            pltpu.VMEM((2 * heads, own), jnp.float32),
            pltpu.SemaphoreType.DMA((2, 2)),
        ],
        compiler_params=pltpu.CompilerParams(
            dimension_semantics=("arbitrary",), collective_id=1, has_side_effects=True
        ),
        cost_estimate=pl.CostEstimate(
            flops=4 * q_rows * k_rows * width + 2 * k_rows * channels * 2 * width,
            transcendentals=q_rows * k_rows * heads,
            bytes_accessed=k_rows * channels * 2 + q_rows * width * 8,
        ),
    )(qt_own, qt_other, hidden_kv, qkv_weight, wvt)


def finish_kernel(heads, head_size, o_ref, st_ref, og_ref, sg_ref, hid_ref, wo_ref, out_ref):
    st_own = st_ref[...]
    st_got = sg_ref[...]
    mixed = []
    for h in range(heads):
        rows = slice(h * head_size, (h + 1) * head_size)
        m_own = st_own[h : h + 1, :]
        m_got = st_got[h : h + 1, :]
        m_all = jnp.maximum(m_own, m_got)
        w_own = jnp.exp(m_own - m_all)
        w_got = jnp.exp(m_got - m_all)
        denom = st_own[heads + h : heads + h + 1, :] * w_own + st_got[heads + h : heads + h + 1, :] * w_got
        mixed.append((o_ref[rows, :] * w_own + og_ref[rows, :] * w_got) / denom)
    attended = jnp.concatenate(mixed, axis=0).T.astype(jnp.bfloat16)
    out = hid_ref[...].astype(jnp.float32) + jnp.dot(
        attended, wo_ref[...], preferred_element_type=jnp.float32
    )
    out_ref[...] = out.astype(out_ref.dtype)


def finish(o_part, st_part, o_got, st_got, hidden, out_weight, heads, head_size):
    rows, width_out = hidden.shape
    width = heads * head_size
    whole = lambda i: (0, 0)
    return pl.pallas_call(
        functools.partial(finish_kernel, heads, head_size),
        grid=(1,),
        in_specs=[
            pl.BlockSpec((width, rows), whole),
            pl.BlockSpec((2 * heads, rows), whole),
            pl.BlockSpec((width, rows), whole),
            pl.BlockSpec((2 * heads, rows), whole),
            pl.BlockSpec((rows, width_out), whole),
            pl.BlockSpec((width, width_out), whole),
        ],
        out_specs=pl.BlockSpec((rows, width_out), whole),
        out_shape=jax.ShapeDtypeStruct((rows, width_out), jnp.bfloat16),
    )(o_part, st_part, o_got, st_got, hidden, out_weight)


def ring_gather_kernel(side, heads, head_size, x_ref, h_ref, wq_ref, wv_ref, scale_ref,
                       out_ref, qt_ref, wvt_ref, qo_ref, send_sem, recv_sem, local_sem, pair_sem):
    me = lax.axis_index("zx")
    z, x = me // side, me % side
    half = x_ref.shape[1]
    q = half // 2
    mesh_ids = pl.DeviceIdType.MESH

    def slot(stream, a, b):
        a = lax.rem(a + side, side)
        b = lax.rem(b + side, side)
        return b * side + a if stream == 0 else a * side + b

    own = [(x, z), (z, x)]
    barrier = pltpu.get_barrier_semaphore()
    for target in (slot(0, x + 1, z), slot(0, x - 1, z), slot(1, z + 1, x), slot(1, z - 1, x)):
        pl.semaphore_signal(barrier, inc=1, device_id={"zx": target}, device_id_type=mesh_ids)
    sibling = 1 - lax.axis_index("core")
    pl.semaphore_signal(barrier, inc=1, device_id={"core": sibling}, device_id_type=mesh_ids)
    pl.semaphore_wait(barrier, 5)
    local = pltpu.make_async_copy(x_ref, out_ref.at[me], local_sem)
    local.start()

    sends = []
    index = {}

    def send(key, src, view, target):
        idx = len(index)
        index[key] = idx
        copy = pltpu.make_async_remote_copy(
            src_ref=src, dst_ref=view, send_sem=send_sem.at[idx], recv_sem=recv_sem.at[idx],
            device_id={"zx": target}, device_id_type=mesh_ids,
        )
        copy.start()
        sends.append(copy)

    def recv(key, view, source):
        idx = index[key]
        pltpu.make_async_remote_copy(
            src_ref=view, dst_ref=view, send_sem=send_sem.at[idx], recv_sem=recv_sem.at[idx],
            device_id={"zx": source}, device_id_type=mesh_ids,
        ).wait_recv()

    def part(stream, a, b, lo=None):
        view = out_ref.at[slot(stream, a, b), stream]
        return view if lo is None else view.at[pl.ds(lo, q)]

    def send_row(st, k):
        a0, b0 = own[st]
        src = x_ref.at[st] if k == 0 else part(st, a0 + k, b0)
        send((st, 3, 1, k), src, part(st, a0 + k, b0), slot(st, a0, b0 + 1))
        send((st, 3, -1, k), src, part(st, a0 + k, b0), slot(st, a0, b0 - 1))

    for st in range(2):
        a0, b0 = own[st]
        send((st, 1, 1), x_ref.at[st], part(st, a0, b0), slot(st, a0 + 1, b0))
        send((st, 1, -1), x_ref.at[st], part(st, a0, b0), slot(st, a0 - 1, b0))
        send_row(st, 0)
    for st in range(2):
        a0, b0 = own[st]
        recv((st, 1, 1), part(st, a0 - 1, b0), slot(st, a0 - 1, b0))
        recv((st, 1, -1), part(st, a0 + 1, b0), slot(st, a0 + 1, b0))
        send((st, 2, 1), part(st, a0 - 1, b0, 0), part(st, a0 - 1, b0, 0), slot(st, a0 + 1, b0))
        send((st, 2, -1), part(st, a0 + 1, b0, q), part(st, a0 + 1, b0, q), slot(st, a0 - 1, b0))
        send_row(st, 1)
        send_row(st, side - 1)
    for st in range(2):
        a0, b0 = own[st]
        recv((st, 2, 1), part(st, a0 - 2, b0, 0), slot(st, a0 - 1, b0))
        recv((st, 2, -1), part(st, a0 + 2, b0, q), slot(st, a0 + 1, b0))
        for k in range(2, side - 1):
            send_row(st, k)
    for st in range(2):
        a0, b0 = own[st]
        for k in range(side):
            recv((st, 3, 1, k), part(st, a0 + k, b0 - 1), slot(st, a0, b0 - 1))
            recv((st, 3, -1, k), part(st, a0 + k, b0 + 1), slot(st, a0, b0 + 1))
            send((st, 4, 1, k), part(st, a0 + k, b0 - 1, 0), part(st, a0 + k, b0 - 1, 0), slot(st, a0, b0 + 1))
            send((st, 4, -1, k), part(st, a0 + k, b0 + 1, q), part(st, a0 + k, b0 + 1, q), slot(st, a0, b0 - 1))
    proj = jnp.dot(h_ref[...], wq_ref[...], preferred_element_type=jnp.float32)
    normed = []
    for h in range(heads):
        cols = slice(h * head_size, (h + 1) * head_size)
        part_q = proj[:, cols]
        mean_sq = jnp.mean(part_q * part_q, axis=1, keepdims=True)
        scale = jnp.full((1, head_size), scale_ref[h], jnp.float32) / math.sqrt(head_size)
        normed.append(part_q * lax.rsqrt(mean_sq + 1e-06) * scale)
    qt_ref[...] = jnp.concatenate(normed, axis=1).T.astype(qt_ref.dtype)
    wvt_ref[...] = wv_ref[...].astype(jnp.float32).T.astype(wvt_ref.dtype)
    pair = pltpu.make_async_remote_copy(
        src_ref=qt_ref, dst_ref=qo_ref, send_sem=pair_sem.at[0], recv_sem=pair_sem.at[1],
        device_id={"core": sibling}, device_id_type=mesh_ids,
    )
    pair.start()
    for st in range(2):
        a0, b0 = own[st]
        for k in range(side):
            recv((st, 4, 1, k), part(st, a0 + k, b0 - 2, 0), slot(st, a0, b0 - 1))
            recv((st, 4, -1, k), part(st, a0 + k, b0 + 2, q), slot(st, a0, b0 + 1))
    pair.wait_send()
    pair.wait_recv()
    local.wait()
    for copy in sends:
        copy.wait_send()


def gather_rows(block, qkv_weight, logit_scale, heads, head_size, axis):
    n = lax.axis_size(axis)
    side = math.isqrt(n)
    rows, width = block.shape
    channels, width_qkv = qkv_weight.shape
    width_all = width_qkv // 3
    copies = 2 * (2 + 2 + 4 * side)
    whole = lambda i: (0, 0)
    out, qt, wvt, qo = pl.pallas_call(
        functools.partial(ring_gather_kernel, side, heads, head_size),
        grid=(1,),
        in_specs=[
            pl.BlockSpec(memory_space=pl.ANY),
            pl.BlockSpec((rows, width), whole),
            pl.BlockSpec((channels, width_all), lambda i: (0, 0)),
            pl.BlockSpec((channels, width_all), lambda i: (0, 2)),
            pl.BlockSpec(memory_space=pltpu.SMEM),
        ],
        out_specs=[
            pl.BlockSpec(memory_space=pl.ANY),
            pl.BlockSpec((width_all, rows), whole),
            pl.BlockSpec((width_all, channels), whole),
            pl.BlockSpec(memory_space=pl.ANY),
        ],
        out_shape=[
            jax.ShapeDtypeStruct((n, 2, rows // 2, width), block.dtype),
            jax.ShapeDtypeStruct((width_all, rows), jnp.bfloat16),
            jax.ShapeDtypeStruct((width_all, channels), jnp.bfloat16),
            jax.ShapeDtypeStruct((width_all, rows), jnp.bfloat16),
        ],
        scratch_shapes=[
            pltpu.SemaphoreType.DMA((copies,)),
            pltpu.SemaphoreType.DMA((copies,)),
            pltpu.SemaphoreType.DMA,
            pltpu.SemaphoreType.DMA((2,)),
        ],
        compiler_params=pltpu.CompilerParams(collective_id=0, has_side_effects=True),
    )(block.reshape(2, rows // 2, width), block, qkv_weight, qkv_weight, logit_scale)
    return out.reshape(n * rows, width), qt, wvt, qo


def conv_gelu_kernel(taps, rows, halo, lo_ref, mid_ref, hi_ref, w_ref, o_ref, x_ref, acc_sc):
    j = pl.program_id(0)
    edge = lo_ref.shape[0]

    @pl.when(j == 0)
    def _():
        x_ref[:edge, :] = lo_ref[...]
        x_ref[edge : edge + mid_ref.shape[0], :] = mid_ref[...]
        x_ref[edge + mid_ref.shape[0] :, :] = hi_ref[...]

    product = jnp.dot(x_ref[...], w_ref[...], preferred_element_type=jnp.float32)
    for t in range(taps):

        @pl.when(j == t)
        def _():
            if t == 0:
                acc_sc[...] = product[t : t + rows]
            else:
                acc_sc[...] = acc_sc[...] + product[t : t + rows]

    @pl.when(j == taps - 1)
    def _():
        place = lax.axis_index(SEQ_AXES)
        last = lax.axis_size(SEQ_AXES) - 1
        row = lax.broadcasted_iota(jnp.int32, acc_sc.shape, 0)
        outside = jnp.logical_or(
            jnp.logical_and(place == 0, row < halo),
            jnp.logical_and(place == last, row >= rows - halo),
        )
        value = jax.nn.gelu(acc_sc[...])
        o_ref[...] = jnp.where(outside, 0.0, value).astype(o_ref.dtype)


def conv_gelu(low, block, high, weight, halo):
    taps, channels, width = weight.shape
    total = low.shape[0] + block.shape[0] + high.shape[0]
    rows = total - taps + 1
    whole = lambda j: (0, 0)
    return pl.pallas_call(
        functools.partial(conv_gelu_kernel, taps, rows, halo),
        grid=(taps,),
        in_specs=[
            pl.BlockSpec(low.shape, whole),
            pl.BlockSpec(block.shape, whole),
            pl.BlockSpec(high.shape, whole),
            pl.BlockSpec((None, channels, width), lambda j: (j, 0, 0)),
        ],
        out_specs=pl.BlockSpec((rows, width), whole),
        out_shape=jax.ShapeDtypeStruct((rows, width), jnp.bfloat16),
        scratch_shapes=[pltpu.VMEM((total, channels), block.dtype), pltpu.VMEM((rows, width), jnp.float32)],
        compiler_params=pltpu.CompilerParams(
            dimension_semantics=("arbitrary",), vmem_limit_bytes=24 * 1024 * 1024
        ),
        cost_estimate=pl.CostEstimate(
            flops=2 * taps * total * channels * width,
            transcendentals=rows * width,
            bytes_accessed=taps * channels * width * 2 + total * channels * 2 + rows * width * 2,
        ),
    )(low, block, high, weight)


def body(sequence_input, conv_first, conv_second, qkv_weight, out_weight, logit_scale):
    row_count = sequence_input.shape[0]
    low, high = halo_rows(sequence_input, 4)
    padded_first = conv_gelu(low, sequence_input, high, conv_first, 2)
    first_out = padded_first[2 : 2 + row_count]
    second = convolve(padded_first, conv_second, row_count)
    hidden = (first_out.astype(jnp.float32) + second).astype(jnp.bfloat16)
    head_count = logit_scale.shape[0]
    width_all = qkv_weight.shape[1] // 3
    head_size = width_all // head_count

    hidden_all, qt_own, wvt, qt_other = gather_rows(hidden, qkv_weight, logit_scale, head_count, head_size, "zx")
    attended = attend_partial(qt_own, qt_other, hidden_all, qkv_weight, wvt, head_count, head_size)
    return (
        hidden.astype(jnp.float32)
        + jnp.dot(attended, out_weight, preferred_element_type=jnp.float32)
    ).astype(jnp.bfloat16)


def solution(mesh):
    devices = np.asarray(mesh.devices)
    seq_size = mesh.shape["seq"]
    batch_size = mesh.shape["batch"]
    order = [mesh.axis_names.index("seq"), mesh.axis_names.index("batch")]
    devices = devices.transpose(order).reshape(seq_size // 2, 2, batch_size)
    split_mesh = Mesh(devices, ("zx", "core", "batch"))
    rows = P(("batch", "zx", "core"), None)
    in_specs = (rows, P(), P(), P(), P(), P())
    return jax.shard_map(body, mesh=split_mesh, in_specs=in_specs, out_specs=rows, check_vma=False)
```

```python
import functools
import math

import jax
import jax.numpy as jnp
import numpy as np
from jax import lax
from jax.experimental import pallas as pl
from jax.experimental.pallas import tpu as pltpu
from jax.sharding import Mesh
from jax.sharding import PartitionSpec as P

SEQ_AXES = ("zx", "core")


def padded_2(block, width, align=1):
    count = lax.axis_size(SEQ_AXES)
    forward = [(i, i + 1) for i in range(count - 1)]
    backward = [(target, source) for source, target in forward]
    low = lax.ppermute(lax.slice_in_dim(block, block.shape[0] - width, None, axis=0), SEQ_AXES, forward)
    high = lax.ppermute(lax.slice_in_dim(block, 0, width, axis=0), SEQ_AXES, backward)
    extra = (-(block.shape[0] + 2 * width)) % align
    fill = jnp.zeros((extra, block.shape[1]), block.dtype)
    return jnp.concatenate([low, block, high, fill], axis=0)


def halo_rows(block, width):
    count = lax.axis_size(SEQ_AXES)
    forward = [(i, i + 1) for i in range(count - 1)]
    backward = [(target, source) for source, target in forward]
    low = lax.ppermute(lax.slice_in_dim(block, block.shape[0] - width, None, axis=0), SEQ_AXES, forward)
    high = lax.ppermute(lax.slice_in_dim(block, 0, width, axis=0), SEQ_AXES, backward)
    return low, high


def convolve(padded, weight, row_count):
    conv_sum = jnp.dot(padded[0:row_count], weight[0], preferred_element_type=jnp.float32)
    for offset in range(1, weight.shape[0]):
        conv_sum = conv_sum + jnp.dot(
            padded[offset : offset + row_count], weight[offset], preferred_element_type=jnp.float32
        )
    return conv_sum


def head_rms(tensor):
    return tensor * lax.rsqrt(jnp.mean(tensor * tensor, axis=-1, keepdims=True) + 1e-06)


def head_norm(block, heads, head_size):
    parts = []
    for h in range(heads):
        part = block[:, h * head_size : (h + 1) * head_size]
        mean_sq = jnp.mean(part * part, axis=1, keepdims=True)
        parts.append(part * lax.rsqrt(mean_sq + 1e-06))
    return parts


def attend_kernel(heads, head_size, nk, qa_ref, qb_ref, hkv_ref, wk_ref, wvt_ref,
                  out_ref, qt_sc, m_sc, l_sc, acc_sc, st_send, og_sc, sg_sc, pair_sem):
    j = pl.program_id(0)
    contract_last = (((1,), (1,)), ((), ()))

    mesh_ids = pl.DeviceIdType.MESH
    sibling = 1 - lax.axis_index("core")

    @pl.when(j == 0)
    def _():
        barrier = pltpu.get_barrier_semaphore()
        pl.semaphore_signal(barrier, inc=1, device_id={"core": sibling}, device_id_type=mesh_ids)
        pl.semaphore_wait(barrier, 1)
        own = qa_ref.shape[1]
        qt_sc[:, :own] = qa_ref[...]
        qt_sc[:, own:] = qb_ref[...]
        m_sc[...] = jnp.full(m_sc.shape, -jnp.inf, jnp.float32)
        l_sc[...] = jnp.zeros(l_sc.shape, jnp.float32)
        acc_sc[...] = jnp.zeros(acc_sc.shape, jnp.float32)

    hkv = hkv_ref[...]
    k_all = jnp.dot(hkv, wk_ref[...], preferred_element_type=jnp.float32)
    v_t = lax.dot_general(wvt_ref[...], hkv, contract_last, preferred_element_type=jnp.float32)
    for h in range(heads):
        rows = slice(h * head_size, (h + 1) * head_size)
        k_h = k_all[:, rows]
        k_h = (k_h * lax.rsqrt(jnp.mean(k_h * k_h, axis=1, keepdims=True) + 1e-06)).astype(
            jnp.bfloat16
        )
        s_t = jnp.dot(k_h, qt_sc[rows, :], preferred_element_type=jnp.float32)
        m_prev = m_sc[h]
        m_next = jnp.maximum(m_prev, jnp.max(s_t, axis=0, keepdims=True))
        alpha = jnp.exp(m_prev - m_next)
        p_t = jnp.exp(s_t - m_next)
        l_sc[h] = alpha * l_sc[h] + jnp.sum(p_t, axis=0, keepdims=True)
        acc_sc[rows, :] = alpha * acc_sc[rows, :] + jnp.dot(
            v_t[rows, :].astype(jnp.bfloat16), p_t.astype(jnp.bfloat16),
            preferred_element_type=jnp.float32,
        )
        m_sc[h] = m_next

    @pl.when(j == nk - 1)
    def _():
        own = qa_ref.shape[1]
        for h in range(heads):
            st_send[h : h + 1, :] = m_sc[h][:, own:]
            st_send[heads + h : heads + h + 1, :] = l_sc[h][:, own:]
        copies = [
            pltpu.make_async_remote_copy(
                src_ref=src, dst_ref=dst, send_sem=pair_sem.at[0, i], recv_sem=pair_sem.at[1, i],
                device_id={"core": sibling}, device_id_type=mesh_ids,
            )
            for i, (src, dst) in enumerate(((acc_sc.at[:, pl.ds(own, own)], og_sc), (st_send, sg_sc)))
        ]
        for copy in copies:
            copy.start()
        for copy in copies:
            copy.wait_send()
            copy.wait_recv()
        st_got = sg_sc[...]
        mixed = []
        for h in range(heads):
            rows = slice(h * head_size, (h + 1) * head_size)
            m_own = m_sc[h][:, :own]
            m_got = st_got[h : h + 1, :]
            m_all = jnp.maximum(m_own, m_got)
            w_own = jnp.exp(m_own - m_all)
            w_got = jnp.exp(m_got - m_all)
            denom = l_sc[h][:, :own] * w_own + st_got[heads + h : heads + h + 1, :] * w_got
            mixed.append((acc_sc[rows, :own] * w_own + og_sc[rows, :] * w_got) / denom)
        out_ref[...] = jnp.concatenate(mixed, axis=0).T.astype(out_ref.dtype)


def attend_partial(qt_own, qt_other, hidden_kv, qkv_weight, wvt, heads, head_size, tk=2048):
    width, own = qt_own.shape
    q_rows = 2 * own
    k_rows, channels = hidden_kv.shape
    nk = k_rows // tk
    whole = lambda j: (0, 0)
    return pl.pallas_call(
        functools.partial(attend_kernel, heads, head_size, nk),
        grid=(nk,),
        in_specs=[
            pl.BlockSpec((width, own), whole),
            pl.BlockSpec((width, own), whole),
            pl.BlockSpec((tk, channels), lambda j: (j, 0)),
            pl.BlockSpec((channels, width), lambda j: (0, 1)),
            pl.BlockSpec((width, channels), whole),
        ],
        out_specs=pl.BlockSpec((own, width), whole),
        out_shape=jax.ShapeDtypeStruct((own, width), jnp.bfloat16),
        scratch_shapes=[
            pltpu.VMEM((width, q_rows), jnp.bfloat16),
            pltpu.VMEM((heads, 1, q_rows), jnp.float32),
            pltpu.VMEM((heads, 1, q_rows), jnp.float32),
            pltpu.VMEM((width, q_rows), jnp.float32),
            pltpu.VMEM((2 * heads, own), jnp.float32),
            pltpu.VMEM((width, own), jnp.float32),
            pltpu.VMEM((2 * heads, own), jnp.float32),
            pltpu.SemaphoreType.DMA((2, 2)),
        ],
        compiler_params=pltpu.CompilerParams(
            dimension_semantics=("arbitrary",), collective_id=1, has_side_effects=True
        ),
        cost_estimate=pl.CostEstimate(
            flops=4 * q_rows * k_rows * width + 2 * k_rows * channels * 2 * width,
            transcendentals=q_rows * k_rows * heads,
            bytes_accessed=k_rows * channels * 2 + q_rows * width * 8,
        ),
    )(qt_own, qt_other, hidden_kv, qkv_weight, wvt)


def finish_kernel(heads, head_size, o_ref, st_ref, og_ref, sg_ref, hid_ref, wo_ref, out_ref):
    st_own = st_ref[...]
    st_got = sg_ref[...]
    mixed = []
    for h in range(heads):
        rows = slice(h * head_size, (h + 1) * head_size)
        m_own = st_own[h : h + 1, :]
        m_got = st_got[h : h + 1, :]
        m_all = jnp.maximum(m_own, m_got)
        w_own = jnp.exp(m_own - m_all)
        w_got = jnp.exp(m_got - m_all)
        denom = st_own[heads + h : heads + h + 1, :] * w_own + st_got[heads + h : heads + h + 1, :] * w_got
        mixed.append((o_ref[rows, :] * w_own + og_ref[rows, :] * w_got) / denom)
    attended = jnp.concatenate(mixed, axis=0).T.astype(jnp.bfloat16)
    out = hid_ref[...].astype(jnp.float32) + jnp.dot(
        attended, wo_ref[...], preferred_element_type=jnp.float32
    )
    out_ref[...] = out.astype(out_ref.dtype)


def finish(o_part, st_part, o_got, st_got, hidden, out_weight, heads, head_size):
    rows, width_out = hidden.shape
    width = heads * head_size
    whole = lambda i: (0, 0)
    return pl.pallas_call(
        functools.partial(finish_kernel, heads, head_size),
        grid=(1,),
        in_specs=[
            pl.BlockSpec((width, rows), whole),
            pl.BlockSpec((2 * heads, rows), whole),
            pl.BlockSpec((width, rows), whole),
            pl.BlockSpec((2 * heads, rows), whole),
            pl.BlockSpec((rows, width_out), whole),
            pl.BlockSpec((width, width_out), whole),
        ],
        out_specs=pl.BlockSpec((rows, width_out), whole),
        out_shape=jax.ShapeDtypeStruct((rows, width_out), jnp.bfloat16),
    )(o_part, st_part, o_got, st_got, hidden, out_weight)


def ring_gather_kernel(side, heads, head_size, x_ref, h_ref, wq_ref, wv_ref, scale_ref,
                       out_ref, qt_ref, wvt_ref, qo_ref, send_sem, recv_sem, local_sem, pair_sem):
    me = lax.axis_index("zx")
    z, x = me // side, me % side
    half = x_ref.shape[1]
    q = half // 2
    mesh_ids = pl.DeviceIdType.MESH

    def slot(stream, a, b):
        a = lax.rem(a + side, side)
        b = lax.rem(b + side, side)
        return b * side + a if stream == 0 else a * side + b

    own = [(x, z), (z, x)]
    barrier = pltpu.get_barrier_semaphore()
    for target in (slot(0, x + 1, z), slot(0, x - 1, z), slot(1, z + 1, x), slot(1, z - 1, x)):
        pl.semaphore_signal(barrier, inc=1, device_id={"zx": target}, device_id_type=mesh_ids)
    sibling = 1 - lax.axis_index("core")
    pl.semaphore_signal(barrier, inc=1, device_id={"core": sibling}, device_id_type=mesh_ids)
    pl.semaphore_wait(barrier, 5)
    local = pltpu.make_async_copy(x_ref, out_ref.at[me], local_sem)
    local.start()

    sends = []
    index = {}

    def send(key, src, view, target):
        idx = len(index)
        index[key] = idx
        copy = pltpu.make_async_remote_copy(
            src_ref=src, dst_ref=view, send_sem=send_sem.at[idx], recv_sem=recv_sem.at[idx],
            device_id={"zx": target}, device_id_type=mesh_ids,
        )
        copy.start()
        sends.append(copy)

    def recv(key, view, source):
        idx = index[key]
        pltpu.make_async_remote_copy(
            src_ref=view, dst_ref=view, send_sem=send_sem.at[idx], recv_sem=recv_sem.at[idx],
            device_id={"zx": source}, device_id_type=mesh_ids,
        ).wait_recv()

    def part(stream, a, b, lo=None):
        view = out_ref.at[slot(stream, a, b), stream]
        return view if lo is None else view.at[pl.ds(lo, q)]

    def send_row(st, k):
        a0, b0 = own[st]
        src = x_ref.at[st] if k == 0 else part(st, a0 + k, b0)
        send((st, 3, 1, k), src, part(st, a0 + k, b0), slot(st, a0, b0 + 1))
        send((st, 3, -1, k), src, part(st, a0 + k, b0), slot(st, a0, b0 - 1))

    for st in range(2):
        a0, b0 = own[st]
        send((st, 1, 1), x_ref.at[st], part(st, a0, b0), slot(st, a0 + 1, b0))
        send((st, 1, -1), x_ref.at[st], part(st, a0, b0), slot(st, a0 - 1, b0))
        send_row(st, 0)
    for st in range(2):
        a0, b0 = own[st]
        recv((st, 1, 1), part(st, a0 - 1, b0), slot(st, a0 - 1, b0))
        recv((st, 1, -1), part(st, a0 + 1, b0), slot(st, a0 + 1, b0))
        send((st, 2, 1), part(st, a0 - 1, b0, 0), part(st, a0 - 1, b0, 0), slot(st, a0 + 1, b0))
        send((st, 2, -1), part(st, a0 + 1, b0, q), part(st, a0 + 1, b0, q), slot(st, a0 - 1, b0))
        send_row(st, 1)
        send_row(st, side - 1)
    for st in range(2):
        a0, b0 = own[st]
        recv((st, 2, 1), part(st, a0 - 2, b0, 0), slot(st, a0 - 1, b0))
        recv((st, 2, -1), part(st, a0 + 2, b0, q), slot(st, a0 + 1, b0))
        for k in range(2, side - 1):
            send_row(st, k)
    for st in range(2):
        a0, b0 = own[st]
        for k in range(side):
            recv((st, 3, 1, k), part(st, a0 + k, b0 - 1), slot(st, a0, b0 - 1))
            recv((st, 3, -1, k), part(st, a0 + k, b0 + 1), slot(st, a0, b0 + 1))
            send((st, 4, 1, k), part(st, a0 + k, b0 - 1, 0), part(st, a0 + k, b0 - 1, 0), slot(st, a0, b0 + 1))
            send((st, 4, -1, k), part(st, a0 + k, b0 + 1, q), part(st, a0 + k, b0 + 1, q), slot(st, a0, b0 - 1))
    proj = jnp.dot(h_ref[...], wq_ref[...], preferred_element_type=jnp.float32)
    normed = []
    for h in range(heads):
        cols = slice(h * head_size, (h + 1) * head_size)
        part_q = proj[:, cols]
        mean_sq = jnp.mean(part_q * part_q, axis=1, keepdims=True)
        scale = jnp.full((1, head_size), scale_ref[h], jnp.float32) / math.sqrt(head_size)
        normed.append(part_q * lax.rsqrt(mean_sq + 1e-06) * scale)
    qt_ref[...] = jnp.concatenate(normed, axis=1).T.astype(qt_ref.dtype)
    wvt_ref[...] = wv_ref[...].astype(jnp.float32).T.astype(wvt_ref.dtype)
    pair = pltpu.make_async_remote_copy(
        src_ref=qt_ref, dst_ref=qo_ref, send_sem=pair_sem.at[0], recv_sem=pair_sem.at[1],
        device_id={"core": sibling}, device_id_type=mesh_ids,
    )
    pair.start()
    for st in range(2):
        a0, b0 = own[st]
        for k in range(side):
            recv((st, 4, 1, k), part(st, a0 + k, b0 - 2, 0), slot(st, a0, b0 - 1))
            recv((st, 4, -1, k), part(st, a0 + k, b0 + 2, q), slot(st, a0, b0 + 1))
    pair.wait_send()
    pair.wait_recv()
    local.wait()
    for copy in sends:
        copy.wait_send()


def gather_rows(block, qkv_weight, logit_scale, heads, head_size, axis):
    n = lax.axis_size(axis)
    side = math.isqrt(n)
    rows, width = block.shape
    channels, width_qkv = qkv_weight.shape
    width_all = width_qkv // 3
    copies = 2 * (2 + 2 + 4 * side)
    whole = lambda i: (0, 0)
    out, qt, wvt, qo = pl.pallas_call(
        functools.partial(ring_gather_kernel, side, heads, head_size),
        grid=(1,),
        in_specs=[
            pl.BlockSpec(memory_space=pl.ANY),
            pl.BlockSpec((rows, width), whole),
            pl.BlockSpec((channels, width_all), lambda i: (0, 0)),
            pl.BlockSpec((channels, width_all), lambda i: (0, 2)),
            pl.BlockSpec(memory_space=pltpu.SMEM),
        ],
        out_specs=[
            pl.BlockSpec(memory_space=pl.ANY),
            pl.BlockSpec((width_all, rows), whole),
            pl.BlockSpec((width_all, channels), whole),
            pl.BlockSpec(memory_space=pl.ANY),
        ],
        out_shape=[
            jax.ShapeDtypeStruct((n, 2, rows // 2, width), block.dtype),
            jax.ShapeDtypeStruct((width_all, rows), jnp.bfloat16),
            jax.ShapeDtypeStruct((width_all, channels), jnp.bfloat16),
            jax.ShapeDtypeStruct((width_all, rows), jnp.bfloat16),
        ],
        scratch_shapes=[
            pltpu.SemaphoreType.DMA((copies,)),
            pltpu.SemaphoreType.DMA((copies,)),
            pltpu.SemaphoreType.DMA,
            pltpu.SemaphoreType.DMA((2,)),
        ],
        compiler_params=pltpu.CompilerParams(collective_id=0, has_side_effects=True),
    )(block.reshape(2, rows // 2, width), block, qkv_weight, qkv_weight, logit_scale)
    return out.reshape(n * rows, width), qt, wvt, qo


def conv_gelu_kernel(taps, rows, halo, lo_ref, mid_ref, hi_ref, w_ref, w2_ref, o_ref, x_ref, acc_sc):
    j = pl.program_id(0)
    edge = lo_ref.shape[0]

    @pl.when(j == 0)
    def _():
        x_ref[:edge, :] = lo_ref[...]
        x_ref[edge : edge + mid_ref.shape[0], :] = mid_ref[...]
        x_ref[edge + mid_ref.shape[0] :, :] = hi_ref[...]

    product = jnp.dot(x_ref[...], w_ref[...], preferred_element_type=jnp.float32)
    for t in range(taps):

        @pl.when(j == t)
        def _():
            if t == 0:
                acc_sc[...] = product[t : t + rows]
            else:
                acc_sc[...] = acc_sc[...] + product[t : t + rows]

    @pl.when(j == taps - 1)
    def _():
        place = lax.axis_index(SEQ_AXES)
        last = lax.axis_size(SEQ_AXES) - 1
        row = lax.broadcasted_iota(jnp.int32, acc_sc.shape, 0)
        outside = jnp.logical_or(
            jnp.logical_and(place == 0, row < halo),
            jnp.logical_and(place == last, row >= rows - halo),
        )
        value = jax.nn.gelu(acc_sc[...])
        first = jnp.where(outside, 0.0, value).astype(jnp.bfloat16)
        out_rows = o_ref.shape[0]
        second = None
        for t in range(taps):
            product2 = jnp.dot(first, w2_ref[t], preferred_element_type=jnp.float32)
            term = product2[t : t + out_rows]
            second = term if second is None else second + term
        residual = first.astype(jnp.float32)[halo : halo + out_rows]
        o_ref[...] = (residual + second).astype(o_ref.dtype)


def conv_block(low, block, high, weight, weight2, halo):
    taps, channels, width = weight.shape
    total = low.shape[0] + block.shape[0] + high.shape[0]
    rows = total - taps + 1
    whole = lambda j: (0, 0)
    return pl.pallas_call(
        functools.partial(conv_gelu_kernel, taps, rows, halo),
        grid=(taps,),
        in_specs=[
            pl.BlockSpec(low.shape, whole),
            pl.BlockSpec(block.shape, whole),
            pl.BlockSpec(high.shape, whole),
            pl.BlockSpec((None, channels, width), lambda j: (j, 0, 0)),
            pl.BlockSpec(weight2.shape, lambda j: (0, 0, 0)),
        ],
        out_specs=pl.BlockSpec(block.shape[:1] + (width,), whole),
        out_shape=jax.ShapeDtypeStruct(block.shape[:1] + (width,), jnp.bfloat16),
        scratch_shapes=[pltpu.VMEM((total, channels), block.dtype), pltpu.VMEM((rows, width), jnp.float32)],
        compiler_params=pltpu.CompilerParams(
            dimension_semantics=("arbitrary",), vmem_limit_bytes=48 * 1024 * 1024
        ),
        cost_estimate=pl.CostEstimate(
            flops=2 * taps * total * channels * width,
            transcendentals=rows * width,
            bytes_accessed=taps * channels * width * 2 + total * channels * 2 + rows * width * 2,
        ),
    )(low, block, high, weight, weight2)


def body(sequence_input, conv_first, conv_second, qkv_weight, out_weight, logit_scale):
    row_count = sequence_input.shape[0]
    low, high = halo_rows(sequence_input, 4)
    hidden = conv_block(low, sequence_input, high, conv_first, conv_second, 2)
    head_count = logit_scale.shape[0]
    width_all = qkv_weight.shape[1] // 3
    head_size = width_all // head_count

    hidden_all, qt_own, wvt, qt_other = gather_rows(hidden, qkv_weight, logit_scale, head_count, head_size, "zx")
    attended = attend_partial(qt_own, qt_other, hidden_all, qkv_weight, wvt, head_count, head_size)
    return (
        hidden.astype(jnp.float32)
        + jnp.dot(attended, out_weight, preferred_element_type=jnp.float32)
    ).astype(jnp.bfloat16)


def solution(mesh):
    devices = np.asarray(mesh.devices)
    seq_size = mesh.shape["seq"]
    batch_size = mesh.shape["batch"]
    order = [mesh.axis_names.index("seq"), mesh.axis_names.index("batch")]
    devices = devices.transpose(order).reshape(seq_size // 2, 2, batch_size)
    split_mesh = Mesh(devices, ("zx", "core", "batch"))
    rows = P(("batch", "zx", "core"), None)
    in_specs = (rows, P(), P(), P(), P(), P())
    return jax.shard_map(body, mesh=split_mesh, in_specs=in_specs, out_specs=rows, check_vma=False)
```

```python
import functools
import math

import jax
import jax.numpy as jnp
import numpy as np
from jax import lax
from jax.experimental import pallas as pl
from jax.experimental.pallas import tpu as pltpu
from jax.sharding import Mesh
from jax.sharding import PartitionSpec as P

SEQ_AXES = ("zx", "core")


def padded_2(block, width, align=1):
    count = lax.axis_size(SEQ_AXES)
    forward = [(i, i + 1) for i in range(count - 1)]
    backward = [(target, source) for source, target in forward]
    low = lax.ppermute(lax.slice_in_dim(block, block.shape[0] - width, None, axis=0), SEQ_AXES, forward)
    high = lax.ppermute(lax.slice_in_dim(block, 0, width, axis=0), SEQ_AXES, backward)
    extra = (-(block.shape[0] + 2 * width)) % align
    fill = jnp.zeros((extra, block.shape[1]), block.dtype)
    return jnp.concatenate([low, block, high, fill], axis=0)


def halo_rows(block, width):
    count = lax.axis_size(SEQ_AXES)
    forward = [(i, i + 1) for i in range(count - 1)]
    backward = [(target, source) for source, target in forward]
    low = lax.ppermute(lax.slice_in_dim(block, block.shape[0] - width, None, axis=0), SEQ_AXES, forward)
    high = lax.ppermute(lax.slice_in_dim(block, 0, width, axis=0), SEQ_AXES, backward)
    return low, high


def convolve(padded, weight, row_count):
    conv_sum = jnp.dot(padded[0:row_count], weight[0], preferred_element_type=jnp.float32)
    for offset in range(1, weight.shape[0]):
        conv_sum = conv_sum + jnp.dot(
            padded[offset : offset + row_count], weight[offset], preferred_element_type=jnp.float32
        )
    return conv_sum


def head_rms(tensor):
    return tensor * lax.rsqrt(jnp.mean(tensor * tensor, axis=-1, keepdims=True) + 1e-06)


def head_norm(block, heads, head_size):
    parts = []
    for h in range(heads):
        part = block[:, h * head_size : (h + 1) * head_size]
        mean_sq = jnp.mean(part * part, axis=1, keepdims=True)
        parts.append(part * lax.rsqrt(mean_sq + 1e-06))
    return parts


def attend_kernel(heads, head_size, nk, qa_ref, qb_ref, hkv_ref, wk_ref, wvt_ref,
                  out_ref, qt_sc, m_sc, l_sc, acc_sc, st_send, og_sc, sg_sc, pair_sem):
    j = pl.program_id(0)
    contract_last = (((1,), (1,)), ((), ()))

    mesh_ids = pl.DeviceIdType.MESH
    sibling = 1 - lax.axis_index("core")

    @pl.when(j == 0)
    def _():
        barrier = pltpu.get_barrier_semaphore()
        pl.semaphore_signal(barrier, inc=1, device_id={"core": sibling}, device_id_type=mesh_ids)
        pl.semaphore_wait(barrier, 1)
        own = qa_ref.shape[1]
        qt_sc[:, :own] = qa_ref[...]
        qt_sc[:, own:] = qb_ref[...]
        m_sc[...] = jnp.full(m_sc.shape, -jnp.inf, jnp.float32)
        l_sc[...] = jnp.zeros(l_sc.shape, jnp.float32)
        acc_sc[...] = jnp.zeros(acc_sc.shape, jnp.float32)

    hkv = hkv_ref[...]
    k_all = jnp.dot(hkv, wk_ref[...], preferred_element_type=jnp.float32)
    v_t = lax.dot_general(wvt_ref[...], hkv, contract_last, preferred_element_type=jnp.float32)
    for h in range(heads):
        rows = slice(h * head_size, (h + 1) * head_size)
        k_h = k_all[:, rows]
        k_h = (k_h * lax.rsqrt(jnp.mean(k_h * k_h, axis=1, keepdims=True) + 1e-06)).astype(
            jnp.bfloat16
        )
        s_t = jnp.dot(k_h, qt_sc[rows, :], preferred_element_type=jnp.float32)
        m_prev = m_sc[h]
        m_next = jnp.maximum(m_prev, jnp.max(s_t, axis=0, keepdims=True))
        alpha = jnp.exp(m_prev - m_next)
        p_t = jnp.exp(s_t - m_next)
        l_sc[h] = alpha * l_sc[h] + jnp.sum(p_t, axis=0, keepdims=True)
        acc_sc[rows, :] = alpha * acc_sc[rows, :] + jnp.dot(
            v_t[rows, :].astype(jnp.bfloat16), p_t.astype(jnp.bfloat16),
            preferred_element_type=jnp.float32,
        )
        m_sc[h] = m_next

    @pl.when(j == nk - 1)
    def _():
        own = qa_ref.shape[1]
        for h in range(heads):
            st_send[h : h + 1, :] = m_sc[h][:, own:]
            st_send[heads + h : heads + h + 1, :] = l_sc[h][:, own:]
        copies = [
            pltpu.make_async_remote_copy(
                src_ref=src, dst_ref=dst, send_sem=pair_sem.at[0, i], recv_sem=pair_sem.at[1, i],
                device_id={"core": sibling}, device_id_type=mesh_ids,
            )
            for i, (src, dst) in enumerate(((acc_sc.at[:, pl.ds(own, own)], og_sc), (st_send, sg_sc)))
        ]
        for copy in copies:
            copy.start()
        for copy in copies:
            copy.wait_send()
            copy.wait_recv()
        st_got = sg_sc[...]
        mixed = []
        for h in range(heads):
            rows = slice(h * head_size, (h + 1) * head_size)
            m_own = m_sc[h][:, :own]
            m_got = st_got[h : h + 1, :]
            m_all = jnp.maximum(m_own, m_got)
            w_own = jnp.exp(m_own - m_all)
            w_got = jnp.exp(m_got - m_all)
            denom = l_sc[h][:, :own] * w_own + st_got[heads + h : heads + h + 1, :] * w_got
            mixed.append((acc_sc[rows, :own] * w_own + og_sc[rows, :] * w_got) / denom)
        out_ref[...] = jnp.concatenate(mixed, axis=0).T.astype(out_ref.dtype)


def attend_partial(qt_own, qt_other, hidden_kv, qkv_weight, wvt, heads, head_size, tk=4096):
    width, own = qt_own.shape
    q_rows = 2 * own
    k_rows, channels = hidden_kv.shape
    nk = k_rows // tk
    whole = lambda j: (0, 0)
    return pl.pallas_call(
        functools.partial(attend_kernel, heads, head_size, nk),
        grid=(nk,),
        in_specs=[
            pl.BlockSpec((width, own), whole),
            pl.BlockSpec((width, own), whole),
            pl.BlockSpec((tk, channels), lambda j: (j, 0)),
            pl.BlockSpec((channels, width), lambda j: (0, 1)),
            pl.BlockSpec((width, channels), whole),
        ],
        out_specs=pl.BlockSpec((own, width), whole),
        out_shape=jax.ShapeDtypeStruct((own, width), jnp.bfloat16),
        scratch_shapes=[
            pltpu.VMEM((width, q_rows), jnp.bfloat16),
            pltpu.VMEM((heads, 1, q_rows), jnp.float32),
            pltpu.VMEM((heads, 1, q_rows), jnp.float32),
            pltpu.VMEM((width, q_rows), jnp.float32),
            pltpu.VMEM((2 * heads, own), jnp.float32),
            pltpu.VMEM((width, own), jnp.float32),
            pltpu.VMEM((2 * heads, own), jnp.float32),
            pltpu.SemaphoreType.DMA((2, 2)),
        ],
        compiler_params=pltpu.CompilerParams(
            dimension_semantics=("arbitrary",), collective_id=1, has_side_effects=True
        ),
        cost_estimate=pl.CostEstimate(
            flops=4 * q_rows * k_rows * width + 2 * k_rows * channels * 2 * width,
            transcendentals=q_rows * k_rows * heads,
            bytes_accessed=k_rows * channels * 2 + q_rows * width * 8,
        ),
    )(qt_own, qt_other, hidden_kv, qkv_weight, wvt)


def finish_kernel(heads, head_size, o_ref, st_ref, og_ref, sg_ref, hid_ref, wo_ref, out_ref):
    st_own = st_ref[...]
    st_got = sg_ref[...]
    mixed = []
    for h in range(heads):
        rows = slice(h * head_size, (h + 1) * head_size)
        m_own = st_own[h : h + 1, :]
        m_got = st_got[h : h + 1, :]
        m_all = jnp.maximum(m_own, m_got)
        w_own = jnp.exp(m_own - m_all)
        w_got = jnp.exp(m_got - m_all)
        denom = st_own[heads + h : heads + h + 1, :] * w_own + st_got[heads + h : heads + h + 1, :] * w_got
        mixed.append((o_ref[rows, :] * w_own + og_ref[rows, :] * w_got) / denom)
    attended = jnp.concatenate(mixed, axis=0).T.astype(jnp.bfloat16)
    out = hid_ref[...].astype(jnp.float32) + jnp.dot(
        attended, wo_ref[...], preferred_element_type=jnp.float32
    )
    out_ref[...] = out.astype(out_ref.dtype)


def finish(o_part, st_part, o_got, st_got, hidden, out_weight, heads, head_size):
    rows, width_out = hidden.shape
    width = heads * head_size
    whole = lambda i: (0, 0)
    return pl.pallas_call(
        functools.partial(finish_kernel, heads, head_size),
        grid=(1,),
        in_specs=[
            pl.BlockSpec((width, rows), whole),
            pl.BlockSpec((2 * heads, rows), whole),
            pl.BlockSpec((width, rows), whole),
            pl.BlockSpec((2 * heads, rows), whole),
            pl.BlockSpec((rows, width_out), whole),
            pl.BlockSpec((width, width_out), whole),
        ],
        out_specs=pl.BlockSpec((rows, width_out), whole),
        out_shape=jax.ShapeDtypeStruct((rows, width_out), jnp.bfloat16),
    )(o_part, st_part, o_got, st_got, hidden, out_weight)


def ring_gather_kernel(side, heads, head_size, x_ref, h_ref, wq_ref, wv_ref, scale_ref,
                       out_ref, qt_ref, wvt_ref, qo_ref, send_sem, recv_sem, local_sem, pair_sem):
    me = lax.axis_index("zx")
    z, x = me // side, me % side
    half = x_ref.shape[1]
    q = half // 2
    mesh_ids = pl.DeviceIdType.MESH

    def slot(stream, a, b):
        a = lax.rem(a + side, side)
        b = lax.rem(b + side, side)
        return b * side + a if stream == 0 else a * side + b

    own = [(x, z), (z, x)]
    barrier = pltpu.get_barrier_semaphore()
    for target in (slot(0, x + 1, z), slot(0, x - 1, z), slot(1, z + 1, x), slot(1, z - 1, x)):
        pl.semaphore_signal(barrier, inc=1, device_id={"zx": target}, device_id_type=mesh_ids)
    sibling = 1 - lax.axis_index("core")
    pl.semaphore_signal(barrier, inc=1, device_id={"core": sibling}, device_id_type=mesh_ids)
    pl.semaphore_wait(barrier, 5)
    local = pltpu.make_async_copy(x_ref, out_ref.at[me], local_sem)
    local.start()

    sends = []
    index = {}

    def send(key, src, view, target):
        idx = len(index)
        index[key] = idx
        copy = pltpu.make_async_remote_copy(
            src_ref=src, dst_ref=view, send_sem=send_sem.at[idx], recv_sem=recv_sem.at[idx],
            device_id={"zx": target}, device_id_type=mesh_ids,
        )
        copy.start()
        sends.append(copy)

    def recv(key, view, source):
        idx = index[key]
        pltpu.make_async_remote_copy(
            src_ref=view, dst_ref=view, send_sem=send_sem.at[idx], recv_sem=recv_sem.at[idx],
            device_id={"zx": source}, device_id_type=mesh_ids,
        ).wait_recv()

    def part(stream, a, b, lo=None):
        view = out_ref.at[slot(stream, a, b), stream]
        return view if lo is None else view.at[pl.ds(lo, q)]

    def send_row(st, k):
        a0, b0 = own[st]
        src = x_ref.at[st] if k == 0 else part(st, a0 + k, b0)
        send((st, 3, 1, k), src, part(st, a0 + k, b0), slot(st, a0, b0 + 1))
        send((st, 3, -1, k), src, part(st, a0 + k, b0), slot(st, a0, b0 - 1))

    for st in range(2):
        a0, b0 = own[st]
        send((st, 1, 1), x_ref.at[st], part(st, a0, b0), slot(st, a0 + 1, b0))
        send((st, 1, -1), x_ref.at[st], part(st, a0, b0), slot(st, a0 - 1, b0))
        send_row(st, 0)
    for st in range(2):
        a0, b0 = own[st]
        recv((st, 1, 1), part(st, a0 - 1, b0), slot(st, a0 - 1, b0))
        recv((st, 1, -1), part(st, a0 + 1, b0), slot(st, a0 + 1, b0))
        send((st, 2, 1), part(st, a0 - 1, b0, 0), part(st, a0 - 1, b0, 0), slot(st, a0 + 1, b0))
        send((st, 2, -1), part(st, a0 + 1, b0, q), part(st, a0 + 1, b0, q), slot(st, a0 - 1, b0))
        send_row(st, 1)
        send_row(st, side - 1)
    for st in range(2):
        a0, b0 = own[st]
        recv((st, 2, 1), part(st, a0 - 2, b0, 0), slot(st, a0 - 1, b0))
        recv((st, 2, -1), part(st, a0 + 2, b0, q), slot(st, a0 + 1, b0))
        for k in range(2, side - 1):
            send_row(st, k)
    for st in range(2):
        a0, b0 = own[st]
        for k in range(side):
            recv((st, 3, 1, k), part(st, a0 + k, b0 - 1), slot(st, a0, b0 - 1))
            recv((st, 3, -1, k), part(st, a0 + k, b0 + 1), slot(st, a0, b0 + 1))
            send((st, 4, 1, k), part(st, a0 + k, b0 - 1, 0), part(st, a0 + k, b0 - 1, 0), slot(st, a0, b0 + 1))
            send((st, 4, -1, k), part(st, a0 + k, b0 + 1, q), part(st, a0 + k, b0 + 1, q), slot(st, a0, b0 - 1))
    proj = jnp.dot(h_ref[...], wq_ref[...], preferred_element_type=jnp.float32)
    normed = []
    for h in range(heads):
        cols = slice(h * head_size, (h + 1) * head_size)
        part_q = proj[:, cols]
        mean_sq = jnp.mean(part_q * part_q, axis=1, keepdims=True)
        scale = jnp.full((1, head_size), scale_ref[h], jnp.float32) / math.sqrt(head_size)
        normed.append(part_q * lax.rsqrt(mean_sq + 1e-06) * scale)
    qt_ref[...] = jnp.concatenate(normed, axis=1).T.astype(qt_ref.dtype)
    wvt_ref[...] = wv_ref[...].astype(jnp.float32).T.astype(wvt_ref.dtype)
    pair = pltpu.make_async_remote_copy(
        src_ref=qt_ref, dst_ref=qo_ref, send_sem=pair_sem.at[0], recv_sem=pair_sem.at[1],
        device_id={"core": sibling}, device_id_type=mesh_ids,
    )
    pair.start()
    for st in range(2):
        a0, b0 = own[st]
        for k in range(side):
            recv((st, 4, 1, k), part(st, a0 + k, b0 - 2, 0), slot(st, a0, b0 - 1))
            recv((st, 4, -1, k), part(st, a0 + k, b0 + 2, q), slot(st, a0, b0 + 1))
    pair.wait_send()
    pair.wait_recv()
    local.wait()
    for copy in sends:
        copy.wait_send()


def gather_rows(block, qkv_weight, logit_scale, heads, head_size, axis):
    n = lax.axis_size(axis)
    side = math.isqrt(n)
    rows, width = block.shape
    channels, width_qkv = qkv_weight.shape
    width_all = width_qkv // 3
    copies = 2 * (2 + 2 + 4 * side)
    whole = lambda i: (0, 0)
    out, qt, wvt, qo = pl.pallas_call(
        functools.partial(ring_gather_kernel, side, heads, head_size),
        grid=(1,),
        in_specs=[
            pl.BlockSpec(memory_space=pl.ANY),
            pl.BlockSpec((rows, width), whole),
            pl.BlockSpec((channels, width_all), lambda i: (0, 0)),
            pl.BlockSpec((channels, width_all), lambda i: (0, 2)),
            pl.BlockSpec(memory_space=pltpu.SMEM),
        ],
        out_specs=[
            pl.BlockSpec(memory_space=pl.ANY),
            pl.BlockSpec((width_all, rows), whole),
            pl.BlockSpec((width_all, channels), whole),
            pl.BlockSpec(memory_space=pl.ANY),
        ],
        out_shape=[
            jax.ShapeDtypeStruct((n, 2, rows // 2, width), block.dtype),
            jax.ShapeDtypeStruct((width_all, rows), jnp.bfloat16),
            jax.ShapeDtypeStruct((width_all, channels), jnp.bfloat16),
            jax.ShapeDtypeStruct((width_all, rows), jnp.bfloat16),
        ],
        scratch_shapes=[
            pltpu.SemaphoreType.DMA((copies,)),
            pltpu.SemaphoreType.DMA((copies,)),
            pltpu.SemaphoreType.DMA,
            pltpu.SemaphoreType.DMA((2,)),
        ],
        compiler_params=pltpu.CompilerParams(collective_id=0, has_side_effects=True),
    )(block.reshape(2, rows // 2, width), block, qkv_weight, qkv_weight, logit_scale)
    return out.reshape(n * rows, width), qt, wvt, qo


def conv_gelu_kernel(taps, rows, halo, lo_ref, mid_ref, hi_ref, w_ref, o_ref, x_ref, acc_sc):
    j = pl.program_id(0)
    edge = lo_ref.shape[0]

    @pl.when(j == 0)
    def _():
        x_ref[:edge, :] = lo_ref[...]
        x_ref[edge : edge + mid_ref.shape[0], :] = mid_ref[...]
        x_ref[edge + mid_ref.shape[0] :, :] = hi_ref[...]

    product = jnp.dot(x_ref[...], w_ref[...], preferred_element_type=jnp.float32)
    for t in range(taps):

        @pl.when(j == t)
        def _():
            if t == 0:
                acc_sc[...] = product[t : t + rows]
            else:
                acc_sc[...] = acc_sc[...] + product[t : t + rows]

    @pl.when(j == taps - 1)
    def _():
        place = lax.axis_index(SEQ_AXES)
        last = lax.axis_size(SEQ_AXES) - 1
        row = lax.broadcasted_iota(jnp.int32, acc_sc.shape, 0)
        outside = jnp.logical_or(
            jnp.logical_and(place == 0, row < halo),
            jnp.logical_and(place == last, row >= rows - halo),
        )
        value = jax.nn.gelu(acc_sc[...])
        o_ref[...] = jnp.where(outside, 0.0, value).astype(o_ref.dtype)


def conv_gelu(low, block, high, weight, halo):
    taps, channels, width = weight.shape
    total = low.shape[0] + block.shape[0] + high.shape[0]
    rows = total - taps + 1
    whole = lambda j: (0, 0)
    return pl.pallas_call(
        functools.partial(conv_gelu_kernel, taps, rows, halo),
        grid=(taps,),
        in_specs=[
            pl.BlockSpec(low.shape, whole),
            pl.BlockSpec(block.shape, whole),
            pl.BlockSpec(high.shape, whole),
            pl.BlockSpec((None, channels, width), lambda j: (j, 0, 0)),
        ],
        out_specs=pl.BlockSpec((rows, width), whole),
        out_shape=jax.ShapeDtypeStruct((rows, width), jnp.bfloat16),
        scratch_shapes=[pltpu.VMEM((total, channels), block.dtype), pltpu.VMEM((rows, width), jnp.float32)],
        compiler_params=pltpu.CompilerParams(
            dimension_semantics=("arbitrary",), vmem_limit_bytes=24 * 1024 * 1024
        ),
        cost_estimate=pl.CostEstimate(
            flops=2 * taps * total * channels * width,
            transcendentals=rows * width,
            bytes_accessed=taps * channels * width * 2 + total * channels * 2 + rows * width * 2,
        ),
    )(low, block, high, weight)


def body(sequence_input, conv_first, conv_second, qkv_weight, out_weight, logit_scale):
    row_count = sequence_input.shape[0]
    low, high = halo_rows(sequence_input, 4)
    padded_first = conv_gelu(low, sequence_input, high, conv_first, 2)
    first_out = padded_first[2 : 2 + row_count]
    second = convolve(padded_first, conv_second, row_count)
    hidden = (first_out.astype(jnp.float32) + second).astype(jnp.bfloat16)
    head_count = logit_scale.shape[0]
    width_all = qkv_weight.shape[1] // 3
    head_size = width_all // head_count

    hidden_all, qt_own, wvt, qt_other = gather_rows(hidden, qkv_weight, logit_scale, head_count, head_size, "zx")
    attended = attend_partial(qt_own, qt_other, hidden_all, qkv_weight, wvt, head_count, head_size)
    return (
        hidden.astype(jnp.float32)
        + jnp.dot(attended, out_weight, preferred_element_type=jnp.float32)
    ).astype(jnp.bfloat16)


def solution(mesh):
    devices = np.asarray(mesh.devices)
    seq_size = mesh.shape["seq"]
    batch_size = mesh.shape["batch"]
    order = [mesh.axis_names.index("seq"), mesh.axis_names.index("batch")]
    devices = devices.transpose(order).reshape(seq_size // 2, 2, batch_size)
    split_mesh = Mesh(devices, ("zx", "core", "batch"))
    rows = P(("batch", "zx", "core"), None)
    in_specs = (rows, P(), P(), P(), P(), P())
    return jax.shard_map(body, mesh=split_mesh, in_specs=in_specs, out_specs=rows, check_vma=False)
```

```python
import functools
import math

import jax
import jax.numpy as jnp
import numpy as np
from jax import lax
from jax.experimental import pallas as pl
from jax.experimental.pallas import tpu as pltpu
from jax.sharding import Mesh
from jax.sharding import PartitionSpec as P

SEQ_AXES = ("zx", "core")


def padded_2(block, width, align=1):
    count = lax.axis_size(SEQ_AXES)
    forward = [(i, i + 1) for i in range(count - 1)]
    backward = [(target, source) for source, target in forward]
    low = lax.ppermute(lax.slice_in_dim(block, block.shape[0] - width, None, axis=0), SEQ_AXES, forward)
    high = lax.ppermute(lax.slice_in_dim(block, 0, width, axis=0), SEQ_AXES, backward)
    extra = (-(block.shape[0] + 2 * width)) % align
    fill = jnp.zeros((extra, block.shape[1]), block.dtype)
    return jnp.concatenate([low, block, high, fill], axis=0)


def halo_rows(block, width):
    count = lax.axis_size(SEQ_AXES)
    forward = [(i, i + 1) for i in range(count - 1)]
    backward = [(target, source) for source, target in forward]
    low = lax.ppermute(lax.slice_in_dim(block, block.shape[0] - width, None, axis=0), SEQ_AXES, forward)
    high = lax.ppermute(lax.slice_in_dim(block, 0, width, axis=0), SEQ_AXES, backward)
    return low, high


def convolve(padded, weight, row_count):
    conv_sum = jnp.dot(padded[0:row_count], weight[0], preferred_element_type=jnp.float32)
    for offset in range(1, weight.shape[0]):
        conv_sum = conv_sum + jnp.dot(
            padded[offset : offset + row_count], weight[offset], preferred_element_type=jnp.float32
        )
    return conv_sum


def head_rms(tensor):
    return tensor * lax.rsqrt(jnp.mean(tensor * tensor, axis=-1, keepdims=True) + 1e-06)


def head_norm(block, heads, head_size):
    parts = []
    for h in range(heads):
        part = block[:, h * head_size : (h + 1) * head_size]
        mean_sq = jnp.mean(part * part, axis=1, keepdims=True)
        parts.append(part * lax.rsqrt(mean_sq + 1e-06))
    return parts


def attend_kernel(heads, head_size, nk, qa_ref, qb_ref, hkv_ref, wk_ref, wvt_ref,
                  out_ref, qt_sc, m_sc, l_sc, acc_sc, st_send, og_sc, sg_sc, pair_sem):
    j = pl.program_id(0)
    contract_last = (((1,), (1,)), ((), ()))

    mesh_ids = pl.DeviceIdType.MESH
    sibling = 1 - lax.axis_index("core")

    @pl.when(j == 0)
    def _():
        barrier = pltpu.get_barrier_semaphore()
        pl.semaphore_signal(barrier, inc=1, device_id={"core": sibling}, device_id_type=mesh_ids)
        pl.semaphore_wait(barrier, 1)
        own = qa_ref.shape[1]
        qt_sc[:, :own] = qa_ref[...]
        qt_sc[:, own:] = qb_ref[...]
        m_sc[...] = jnp.full(m_sc.shape, -jnp.inf, jnp.float32)
        l_sc[...] = jnp.zeros(l_sc.shape, jnp.float32)
        acc_sc[...] = jnp.zeros(acc_sc.shape, jnp.float32)

    hkv = hkv_ref[...]
    k_all = jnp.dot(hkv, wk_ref[...], preferred_element_type=jnp.float32)
    v_t = lax.dot_general(wvt_ref[...], hkv, contract_last, preferred_element_type=jnp.float32)
    for h in range(heads):
        rows = slice(h * head_size, (h + 1) * head_size)
        k_h = k_all[:, rows]
        k_h = (k_h * lax.rsqrt(jnp.mean(k_h * k_h, axis=1, keepdims=True) + 1e-06)).astype(
            jnp.bfloat16
        )
        s_t = jnp.dot(k_h, qt_sc[rows, :], preferred_element_type=jnp.float32)
        m_prev = m_sc[h]
        m_next = jnp.maximum(m_prev, jnp.max(s_t, axis=0, keepdims=True))
        alpha = jnp.exp(m_prev - m_next)
        p_t = jnp.exp(s_t - m_next)
        l_sc[h] = alpha * l_sc[h] + jnp.sum(p_t, axis=0, keepdims=True)
        acc_sc[rows, :] = alpha * acc_sc[rows, :] + jnp.dot(
            v_t[rows, :].astype(jnp.bfloat16), p_t.astype(jnp.bfloat16),
            preferred_element_type=jnp.float32,
        )
        m_sc[h] = m_next

    @pl.when(j == nk - 1)
    def _():
        own = qa_ref.shape[1]
        for h in range(heads):
            st_send[h : h + 1, :] = m_sc[h][:, own:]
            st_send[heads + h : heads + h + 1, :] = l_sc[h][:, own:]
        copies = [
            pltpu.make_async_remote_copy(
                src_ref=src, dst_ref=dst, send_sem=pair_sem.at[0, i], recv_sem=pair_sem.at[1, i],
                device_id={"core": sibling}, device_id_type=mesh_ids,
            )
            for i, (src, dst) in enumerate(((acc_sc.at[:, pl.ds(own, own)], og_sc), (st_send, sg_sc)))
        ]
        for copy in copies:
            copy.start()
        for copy in copies:
            copy.wait_send()
            copy.wait_recv()
        st_got = sg_sc[...]
        mixed = []
        for h in range(heads):
            rows = slice(h * head_size, (h + 1) * head_size)
            m_own = m_sc[h][:, :own]
            m_got = st_got[h : h + 1, :]
            m_all = jnp.maximum(m_own, m_got)
            w_own = jnp.exp(m_own - m_all)
            w_got = jnp.exp(m_got - m_all)
            denom = l_sc[h][:, :own] * w_own + st_got[heads + h : heads + h + 1, :] * w_got
            mixed.append((acc_sc[rows, :own] * w_own + og_sc[rows, :] * w_got) / denom)
        out_ref[...] = jnp.concatenate(mixed, axis=0).T.astype(out_ref.dtype)


def attend_partial(qt_own, qt_other, hidden_kv, qkv_weight, wvt, heads, head_size, tk=2048):
    width, own = qt_own.shape
    q_rows = 2 * own
    k_rows, channels = hidden_kv.shape
    nk = k_rows // tk
    whole = lambda j: (0, 0)
    return pl.pallas_call(
        functools.partial(attend_kernel, heads, head_size, nk),
        grid=(nk,),
        in_specs=[
            pl.BlockSpec((width, own), whole),
            pl.BlockSpec((width, own), whole),
            pl.BlockSpec((tk, channels), lambda j: (j, 0)),
            pl.BlockSpec((channels, width), lambda j: (0, 1)),
            pl.BlockSpec((width, channels), whole),
        ],
        out_specs=pl.BlockSpec((own, width), whole),
        out_shape=jax.ShapeDtypeStruct((own, width), jnp.bfloat16),
        scratch_shapes=[
            pltpu.VMEM((width, q_rows), jnp.bfloat16),
            pltpu.VMEM((heads, 1, q_rows), jnp.float32),
            pltpu.VMEM((heads, 1, q_rows), jnp.float32),
            pltpu.VMEM((width, q_rows), jnp.float32),
            pltpu.VMEM((2 * heads, own), jnp.float32),
            pltpu.VMEM((width, own), jnp.float32),
            pltpu.VMEM((2 * heads, own), jnp.float32),
            pltpu.SemaphoreType.DMA((2, 2)),
        ],
        compiler_params=pltpu.CompilerParams(
            dimension_semantics=("arbitrary",), collective_id=1, has_side_effects=True
        ),
        cost_estimate=pl.CostEstimate(
            flops=4 * q_rows * k_rows * width + 2 * k_rows * channels * 2 * width,
            transcendentals=q_rows * k_rows * heads,
            bytes_accessed=k_rows * channels * 2 + q_rows * width * 8,
        ),
    )(qt_own, qt_other, hidden_kv, qkv_weight, wvt)


def finish_kernel(heads, head_size, o_ref, st_ref, og_ref, sg_ref, hid_ref, wo_ref, out_ref):
    st_own = st_ref[...]
    st_got = sg_ref[...]
    mixed = []
    for h in range(heads):
        rows = slice(h * head_size, (h + 1) * head_size)
        m_own = st_own[h : h + 1, :]
        m_got = st_got[h : h + 1, :]
        m_all = jnp.maximum(m_own, m_got)
        w_own = jnp.exp(m_own - m_all)
        w_got = jnp.exp(m_got - m_all)
        denom = st_own[heads + h : heads + h + 1, :] * w_own + st_got[heads + h : heads + h + 1, :] * w_got
        mixed.append((o_ref[rows, :] * w_own + og_ref[rows, :] * w_got) / denom)
    attended = jnp.concatenate(mixed, axis=0).T.astype(jnp.bfloat16)
    out = hid_ref[...].astype(jnp.float32) + jnp.dot(
        attended, wo_ref[...], preferred_element_type=jnp.float32
    )
    out_ref[...] = out.astype(out_ref.dtype)


def finish(o_part, st_part, o_got, st_got, hidden, out_weight, heads, head_size):
    rows, width_out = hidden.shape
    width = heads * head_size
    whole = lambda i: (0, 0)
    return pl.pallas_call(
        functools.partial(finish_kernel, heads, head_size),
        grid=(1,),
        in_specs=[
            pl.BlockSpec((width, rows), whole),
            pl.BlockSpec((2 * heads, rows), whole),
            pl.BlockSpec((width, rows), whole),
            pl.BlockSpec((2 * heads, rows), whole),
            pl.BlockSpec((rows, width_out), whole),
            pl.BlockSpec((width, width_out), whole),
        ],
        out_specs=pl.BlockSpec((rows, width_out), whole),
        out_shape=jax.ShapeDtypeStruct((rows, width_out), jnp.bfloat16),
    )(o_part, st_part, o_got, st_got, hidden, out_weight)


def ring_gather_kernel(side, heads, head_size, x_ref, h_ref, wq_ref, wv_ref, scale_ref,
                       out_ref, qt_ref, wvt_ref, qo_ref, send_sem, recv_sem, local_sem, pair_sem):
    me = lax.axis_index("zx")
    z, x = me // side, me % side
    half = x_ref.shape[1]
    q = half // 2
    mesh_ids = pl.DeviceIdType.MESH

    def slot(stream, a, b):
        a = lax.rem(a + side, side)
        b = lax.rem(b + side, side)
        return b * side + a if stream == 0 else a * side + b

    own = [(x, z), (z, x)]
    barrier = pltpu.get_barrier_semaphore()
    for target in (slot(0, x + 1, z), slot(0, x - 1, z), slot(1, z + 1, x), slot(1, z - 1, x)):
        pl.semaphore_signal(barrier, inc=1, device_id={"zx": target}, device_id_type=mesh_ids)
    sibling = 1 - lax.axis_index("core")
    pl.semaphore_signal(barrier, inc=1, device_id={"core": sibling}, device_id_type=mesh_ids)
    pl.semaphore_wait(barrier, 5)
    local = pltpu.make_async_copy(x_ref, out_ref.at[me], local_sem)
    local.start()

    sends = []
    index = {}

    def send(key, src, view, target):
        idx = len(index)
        index[key] = idx
        copy = pltpu.make_async_remote_copy(
            src_ref=src, dst_ref=view, send_sem=send_sem.at[idx], recv_sem=recv_sem.at[idx],
            device_id={"zx": target}, device_id_type=mesh_ids,
        )
        copy.start()
        sends.append(copy)

    def recv(key, view, source):
        idx = index[key]
        pltpu.make_async_remote_copy(
            src_ref=view, dst_ref=view, send_sem=send_sem.at[idx], recv_sem=recv_sem.at[idx],
            device_id={"zx": source}, device_id_type=mesh_ids,
        ).wait_recv()

    def part(stream, a, b, lo=None):
        view = out_ref.at[slot(stream, a, b), stream]
        return view if lo is None else view.at[pl.ds(lo, q)]

    def send_row(st, k):
        a0, b0 = own[st]
        src = x_ref.at[st] if k == 0 else part(st, a0 + k, b0)
        send((st, 3, 1, k), src, part(st, a0 + k, b0), slot(st, a0, b0 + 1))
        send((st, 3, -1, k), src, part(st, a0 + k, b0), slot(st, a0, b0 - 1))

    for st in range(2):
        a0, b0 = own[st]
        send((st, 1, 1), x_ref.at[st], part(st, a0, b0), slot(st, a0 + 1, b0))
        send((st, 1, -1), x_ref.at[st], part(st, a0, b0), slot(st, a0 - 1, b0))
        send_row(st, 0)
    for st in range(2):
        a0, b0 = own[st]
        recv((st, 1, 1), part(st, a0 - 1, b0), slot(st, a0 - 1, b0))
        send((st, 2, 1), part(st, a0 - 1, b0, 0), part(st, a0 - 1, b0, 0), slot(st, a0 + 1, b0))
        send_row(st, side - 1)
        recv((st, 1, -1), part(st, a0 + 1, b0), slot(st, a0 + 1, b0))
        send((st, 2, -1), part(st, a0 + 1, b0, q), part(st, a0 + 1, b0, q), slot(st, a0 - 1, b0))
        send_row(st, 1)
    for st in range(2):
        a0, b0 = own[st]
        recv((st, 2, 1), part(st, a0 - 2, b0, 0), slot(st, a0 - 1, b0))
        recv((st, 2, -1), part(st, a0 + 2, b0, q), slot(st, a0 + 1, b0))
        for k in range(2, side - 1):
            send_row(st, k)
    for st in range(2):
        a0, b0 = own[st]
        for k in range(side):
            recv((st, 3, 1, k), part(st, a0 + k, b0 - 1), slot(st, a0, b0 - 1))
            recv((st, 3, -1, k), part(st, a0 + k, b0 + 1), slot(st, a0, b0 + 1))
            send((st, 4, 1, k), part(st, a0 + k, b0 - 1, 0), part(st, a0 + k, b0 - 1, 0), slot(st, a0, b0 + 1))
            send((st, 4, -1, k), part(st, a0 + k, b0 + 1, q), part(st, a0 + k, b0 + 1, q), slot(st, a0, b0 - 1))
    proj = jnp.dot(h_ref[...], wq_ref[...], preferred_element_type=jnp.float32)
    normed = []
    for h in range(heads):
        cols = slice(h * head_size, (h + 1) * head_size)
        part_q = proj[:, cols]
        mean_sq = jnp.mean(part_q * part_q, axis=1, keepdims=True)
        scale = jnp.full((1, head_size), scale_ref[h], jnp.float32) / math.sqrt(head_size)
        normed.append(part_q * lax.rsqrt(mean_sq + 1e-06) * scale)
    qt_ref[...] = jnp.concatenate(normed, axis=1).T.astype(qt_ref.dtype)
    wvt_ref[...] = wv_ref[...].astype(jnp.float32).T.astype(wvt_ref.dtype)
    pair = pltpu.make_async_remote_copy(
        src_ref=qt_ref, dst_ref=qo_ref, send_sem=pair_sem.at[0], recv_sem=pair_sem.at[1],
        device_id={"core": sibling}, device_id_type=mesh_ids,
    )
    pair.start()
    for st in range(2):
        a0, b0 = own[st]
        for k in range(side):
            recv((st, 4, 1, k), part(st, a0 + k, b0 - 2, 0), slot(st, a0, b0 - 1))
            recv((st, 4, -1, k), part(st, a0 + k, b0 + 2, q), slot(st, a0, b0 + 1))
    pair.wait_send()
    pair.wait_recv()
    local.wait()
    for copy in sends:
        copy.wait_send()


def gather_rows(block, qkv_weight, logit_scale, heads, head_size, axis):
    n = lax.axis_size(axis)
    side = math.isqrt(n)
    rows, width = block.shape
    channels, width_qkv = qkv_weight.shape
    width_all = width_qkv // 3
    copies = 2 * (2 + 2 + 4 * side)
    whole = lambda i: (0, 0)
    out, qt, wvt, qo = pl.pallas_call(
        functools.partial(ring_gather_kernel, side, heads, head_size),
        grid=(1,),
        in_specs=[
            pl.BlockSpec(memory_space=pl.ANY),
            pl.BlockSpec((rows, width), whole),
            pl.BlockSpec((channels, width_all), lambda i: (0, 0)),
            pl.BlockSpec((channels, width_all), lambda i: (0, 2)),
            pl.BlockSpec(memory_space=pltpu.SMEM),
        ],
        out_specs=[
            pl.BlockSpec(memory_space=pl.ANY),
            pl.BlockSpec((width_all, rows), whole),
            pl.BlockSpec((width_all, channels), whole),
            pl.BlockSpec(memory_space=pl.ANY),
        ],
        out_shape=[
            jax.ShapeDtypeStruct((n, 2, rows // 2, width), block.dtype),
            jax.ShapeDtypeStruct((width_all, rows), jnp.bfloat16),
            jax.ShapeDtypeStruct((width_all, channels), jnp.bfloat16),
            jax.ShapeDtypeStruct((width_all, rows), jnp.bfloat16),
        ],
        scratch_shapes=[
            pltpu.SemaphoreType.DMA((copies,)),
            pltpu.SemaphoreType.DMA((copies,)),
            pltpu.SemaphoreType.DMA,
            pltpu.SemaphoreType.DMA((2,)),
        ],
        compiler_params=pltpu.CompilerParams(collective_id=0, has_side_effects=True),
    )(block.reshape(2, rows // 2, width), block, qkv_weight, qkv_weight, logit_scale)
    return out.reshape(n * rows, width), qt, wvt, qo


def conv_gelu_kernel(taps, rows, halo, lo_ref, mid_ref, hi_ref, w_ref, o_ref, x_ref, acc_sc):
    j = pl.program_id(0)
    edge = lo_ref.shape[0]

    @pl.when(j == 0)
    def _():
        x_ref[:edge, :] = lo_ref[...]
        x_ref[edge : edge + mid_ref.shape[0], :] = mid_ref[...]
        x_ref[edge + mid_ref.shape[0] :, :] = hi_ref[...]

    product = jnp.dot(x_ref[...], w_ref[...], preferred_element_type=jnp.float32)
    for t in range(taps):

        @pl.when(j == t)
        def _():
            if t == 0:
                acc_sc[...] = product[t : t + rows]
            else:
                acc_sc[...] = acc_sc[...] + product[t : t + rows]

    @pl.when(j == taps - 1)
    def _():
        place = lax.axis_index(SEQ_AXES)
        last = lax.axis_size(SEQ_AXES) - 1
        row = lax.broadcasted_iota(jnp.int32, acc_sc.shape, 0)
        outside = jnp.logical_or(
            jnp.logical_and(place == 0, row < halo),
            jnp.logical_and(place == last, row >= rows - halo),
        )
        value = jax.nn.gelu(acc_sc[...])
        o_ref[...] = jnp.where(outside, 0.0, value).astype(o_ref.dtype)


def conv_gelu(low, block, high, weight, halo):
    taps, channels, width = weight.shape
    total = low.shape[0] + block.shape[0] + high.shape[0]
    rows = total - taps + 1
    whole = lambda j: (0, 0)
    return pl.pallas_call(
        functools.partial(conv_gelu_kernel, taps, rows, halo),
        grid=(taps,),
        in_specs=[
            pl.BlockSpec(low.shape, whole),
            pl.BlockSpec(block.shape, whole),
            pl.BlockSpec(high.shape, whole),
            pl.BlockSpec((None, channels, width), lambda j: (j, 0, 0)),
        ],
        out_specs=pl.BlockSpec((rows, width), whole),
        out_shape=jax.ShapeDtypeStruct((rows, width), jnp.bfloat16),
        scratch_shapes=[pltpu.VMEM((total, channels), block.dtype), pltpu.VMEM((rows, width), jnp.float32)],
        compiler_params=pltpu.CompilerParams(
            dimension_semantics=("arbitrary",), vmem_limit_bytes=24 * 1024 * 1024
        ),
        cost_estimate=pl.CostEstimate(
            flops=2 * taps * total * channels * width,
            transcendentals=rows * width,
            bytes_accessed=taps * channels * width * 2 + total * channels * 2 + rows * width * 2,
        ),
    )(low, block, high, weight)


def body(sequence_input, conv_first, conv_second, qkv_weight, out_weight, logit_scale):
    row_count = sequence_input.shape[0]
    low, high = halo_rows(sequence_input, 4)
    padded_first = conv_gelu(low, sequence_input, high, conv_first, 2)
    first_out = padded_first[2 : 2 + row_count]
    second = convolve(padded_first, conv_second, row_count)
    hidden = (first_out.astype(jnp.float32) + second).astype(jnp.bfloat16)
    head_count = logit_scale.shape[0]
    width_all = qkv_weight.shape[1] // 3
    head_size = width_all // head_count

    hidden_all, qt_own, wvt, qt_other = gather_rows(hidden, qkv_weight, logit_scale, head_count, head_size, "zx")
    attended = attend_partial(qt_own, qt_other, hidden_all, qkv_weight, wvt, head_count, head_size)
    return (
        hidden.astype(jnp.float32)
        + jnp.dot(attended, out_weight, preferred_element_type=jnp.float32)
    ).astype(jnp.bfloat16)


def solution(mesh):
    devices = np.asarray(mesh.devices)
    seq_size = mesh.shape["seq"]
    batch_size = mesh.shape["batch"]
    order = [mesh.axis_names.index("seq"), mesh.axis_names.index("batch")]
    devices = devices.transpose(order).reshape(seq_size // 2, 2, batch_size)
    split_mesh = Mesh(devices, ("zx", "core", "batch"))
    rows = P(("batch", "zx", "core"), None)
    in_specs = (rows, P(), P(), P(), P(), P())
    return jax.shard_map(body, mesh=split_mesh, in_specs=in_specs, out_specs=rows, check_vma=False)
```
